32 devices in a mesh: ctx: 16 (over z, y, core), fsdp: 2 (over x).
Axes of the slice: x: 2, y: 2, z: 4, core: 2. Of those that a mesh axis runs over, the one named last changes fastest.
Arguments:
- tokens: bfloat16 [4, 1024, 2048], P('fsdp', 'ctx'), may hold values from -6 to 6
- cotangent: bfloat16 [4, 1024, 2048], P('fsdp', 'ctx'), may hold values from -6 to 6
- q_weight: bfloat16 [2048, 2048], P(('ctx', 'fsdp')), may hold values from -0.125 to 0.125
- k_weight: bfloat16 [512, 2048], P(('ctx', 'fsdp')), may hold values from -0.125 to 0.125
- v_weight: bfloat16 [512, 2048], P(('ctx', 'fsdp')), may hold values from -0.125 to 0.125
- o_weight: bfloat16 [2048, 2048], P(('ctx', 'fsdp')), may hold values from -0.75 to 0.75
- gate_weight: bfloat16 [8192, 2048], P(('ctx', 'fsdp')), may hold values from -0.125 to 0.125
- up_weight: bfloat16 [8192, 2048], P(('ctx', 'fsdp')), may hold values from -0.125 to 0.125
- down_weight: bfloat16 [8192, 2048], P(('ctx', 'fsdp')), may hold values from -0.0625 to 0.0625
- attn_gain: float32 [2048], replicated, may hold values from 0.5 to 1.5
- ffn_gain: float32 [2048], replicated, may hold values from 0.5 to 1.5
- q_gain: float32 [64], replicated, may hold values from 0.1 to 1.9
- k_gain: float32 [64], replicated, may hold values from 0.1 to 1.9
- lengths: int32 [4], P('fsdp'), may hold values from 256 to 1024, as said below
- pair_order: int32 [16], replicated, may hold values from 0 to 15, each once
Outputs:
- block_out: bfloat16 [4, 1024, 2048], P('fsdp', 'ctx')
- grad_tokens: float32 [4, 1024, 2048], P('fsdp', 'ctx')
- grad_q_weight: float32 [2048, 2048], P(('ctx', 'fsdp'))
- grad_k_weight: float32 [512, 2048], P(('ctx', 'fsdp'))
- grad_v_weight: float32 [512, 2048], P(('ctx', 'fsdp'))
- grad_o_weight: float32 [2048, 2048], P(('ctx', 'fsdp'))
- grad_gate_weight: float32 [8192, 2048], P(('ctx', 'fsdp'))
- grad_up_weight: float32 [8192, 2048], P(('ctx', 'fsdp'))
- grad_down_weight: float32 [8192, 2048], P(('ctx', 'fsdp'))
- grad_attn_gain: float32 [2048], replicated
- grad_ffn_gain: float32 [2048], replicated
- grad_q_gain: float32 [64], replicated
- grad_k_gain: float32 [64], replicated
The draws below stay inside these ranges and needn't reach their ends.
Inputs may be any that keep to these rules, and one draw needn't show every extreme that they name: `lengths`: at least one sequence has all 1024 slots live. `pair_order`: each of 0 to 15 appears once.
All inputs are finite; a program needn't handle non-finite values.
Results may differ from the reference program's by a relative error of at most 0.02.
Values may be sent and summed in bfloat16 or wider, within the bound.
No kernel may reach another device: no remote copies, remote signals or barrier semaphores. Data moves between devices by JAX's collectives and lax.ppermute only.
A program may use at most 768 MiB of HBM per device.

```python
import math
import jax
import jax.numpy as jnp
from jax import lax

D = 2048
HEADS = 32
KV_HEADS = 8
HEAD_DIM = 64
FF = 8192
BLOCK = 32
PAIRS = 16
SLOTS = 1024
SEQS = 4
QW = 2048
KVW = 512


def draw_lengths(key, part):
    first, second = jax.random.split(key)
    values = jax.random.randint(first, (SEQS,), SLOTS // 4, SLOTS + 1)
    which = jax.random.randint(second, (), 0, SEQS)
    return jnp.where(jnp.arange(SEQS) == which, SLOTS, values).astype(jnp.int32)


def levels(rng, shape, cuts, smallest, top_value):
    loudness = 1.0
    for axis_at, parts in cuts:
        heights = jax.random.uniform(jax.random.fold_in(jax.random.fold_in(rng, 6), axis_at), (parts,), jnp.float32, smallest / len(cuts), top_value / len(cuts))
        loudness = loudness * jnp.repeat(jnp.exp(heights), shape[axis_at] // parts).reshape((-1,) + (1,) * (len(shape) - 1 - axis_at))
    return loudness


def noise(rng, shape, width, bound, cuts=(), kind=jnp.bfloat16):
    drawn = width * jax.random.normal(rng, shape, jnp.float32)
    if cuts:
        drawn = drawn * levels(rng, shape, cuts, -0.22, 0.18)
    return jnp.clip(drawn, -bound, bound).astype(kind)


def setup_inputs(seed: int = 0) -> dict:
    arg_keys = jax.random.split(jax.random.key(seed), 16)
    return {
        "tokens": noise(arg_keys[0], (SEQS, SLOTS, D), 1.0, 6.0, ((0, 2), (1, 16))),
        "cotangent": noise(arg_keys[1], (SEQS, SLOTS, D), 1.0, 6.0, ((0, 2), (1, 16))),
        "q_weight": noise(arg_keys[2], (QW, D), D ** -0.5, 0.125, ((0, 32),)),
        "k_weight": noise(arg_keys[3], (KVW, D), D ** -0.5, 0.125, ((0, 32),)),
        "v_weight": noise(arg_keys[4], (KVW, D), D ** -0.5, 0.125, ((0, 32),)),
        "o_weight": noise(arg_keys[5], (QW, D), (max(1, QW * 32 // SLOTS)) ** -0.5, 0.75, ((0, 32),)),
        "gate_weight": noise(arg_keys[6], (FF, D), D ** -0.5, 0.125, ((0, 32),)),
        "up_weight": noise(arg_keys[7], (FF, D), D ** -0.5, 0.125, ((0, 32),)),
        "down_weight": noise(arg_keys[8], (FF, D), FF ** -0.5, 0.0625, ((0, 32),)),
        "attn_gain": jnp.clip(1.0 + 0.1 * jax.random.normal(arg_keys[9], (D,), jnp.float32), 0.5, 1.5),
        "ffn_gain": jnp.clip(1.0 + 0.1 * jax.random.normal(arg_keys[10], (D,), jnp.float32), 0.5, 1.5),
        "q_gain": jnp.clip(1.0 + 0.18 * jax.random.normal(arg_keys[11], (HEAD_DIM,), jnp.float32), 0.1, 1.9),
        "k_gain": jnp.clip(1.0 + 0.18 * jax.random.normal(arg_keys[12], (HEAD_DIM,), jnp.float32), 0.1, 1.9),
        "lengths": draw_lengths(jax.random.fold_in(arg_keys[15], 71), 0),
        "pair_order": jax.random.permutation(arg_keys[14], PAIRS).astype(jnp.int32),
    }


EPS = 1e-05
THETA = 1000000.0
NEG = -1e+30
HIGH = lax.Precision.HIGHEST

@jax.custom_vjp
def low(v):
    return lax.optimization_barrier(v.astype(jnp.bfloat16)).astype(jnp.float32)

@jax.custom_vjp
def low_back(v):
    return v

def low_keep(v):
    return (low(v), None)

def low_pass(kept, grad):
    return (grad,)

def back_keep(v):
    return (v, None)

def back_low(kept, grad):
    return (low(grad),)
low.defvjp(low_keep, low_pass)
low_back.defvjp(back_keep, back_low)

def rms_scale(values):
    return lax.rsqrt(lax.optimization_barrier(jnp.mean(values * values, axis=-1, keepdims=True)) + EPS)

def rope_tables(positions):
    half = HEAD_DIM // 2
    freq = THETA ** (-(jnp.arange(half, dtype=jnp.float32) * 2.0 / HEAD_DIM))
    angle = positions.astype(jnp.float32)[:, None] * freq[None, :]
    return (jnp.cos(angle), jnp.sin(angle))

def rotate(values, cosine, sine):
    half = values.shape[-1] // 2
    first = values[..., :half]
    second = values[..., half:]
    return jnp.concatenate([first * cosine - second * sine, second * cosine + first * sine], axis=-1)

def slot_positions(pair_order, width_pair, first, count):
    slot = first + jnp.arange(count, dtype=jnp.int32)
    owner = slot // width_pair
    within = slot % width_pair
    half_blk = width_pair // 2
    pair = pair_order[owner]
    block_id = jnp.where(within < half_blk, pair, 2 * pair_order.shape[0] - 1 - pair)
    return (block_id * half_blk + within % half_blk).astype(jnp.int32)

def attend(q_rot, k_rot, v_low, positions, length):
    groups = HEADS // KV_HEADS
    q_blk = math.gcd(SLOTS, 512)
    keys = k_rot.transpose(1, 0, 2)
    values = v_low.reshape(SLOTS, KV_HEADS, HEAD_DIM).transpose(1, 0, 2)
    key_live = positions < length
    q_blocks = q_rot.reshape(SLOTS // q_blk, q_blk, KV_HEADS, groups, HEAD_DIM)
    pos_blocks = positions.reshape(SLOTS // q_blk, q_blk)

    def one_block(item):
        q_part, q_pos = item
        scores = jnp.einsum('qhgd,hjd->hgqj', q_part, keys, precision=HIGH) * HEAD_DIM ** (-0.5)
        scores = low_back(scores)
        allowed = (positions[None, :] <= q_pos[:, None]) & key_live[None, :]
        scores = jnp.where(allowed[None, None], scores, NEG)
        top = lax.optimization_barrier(jnp.max(scores, axis=-1, keepdims=True))
        lse = top + jnp.log(lax.optimization_barrier(jnp.sum(jnp.exp(scores - top), axis=-1, keepdims=True)))
        probs = low(jnp.exp(scores - lse))
        out = jnp.einsum('hgqj,hjd->qhgd', probs, values, precision=HIGH)
        return out.reshape(q_blk, HEADS * HEAD_DIM)
    return lax.map(jax.checkpoint(one_block), (q_blocks, pos_blocks)).reshape(SLOTS, HEADS * HEAD_DIM)

def layer(params, x_seq, positions, length):
    w_query, w_key, w_value, w_out, w_gate, w_up, w_down, attn_gain, ffn_gain, q_gain, k_gain = params
    live = (positions < length)[:, None]
    x_norm = low(x_seq * rms_scale(x_seq) * attn_gain)
    q_proj = low_back(jnp.dot(x_norm, w_query.T, precision=HIGH)).reshape(SLOTS, HEADS, HEAD_DIM)
    k_proj = low_back(jnp.dot(x_norm, w_key.T, precision=HIGH)).reshape(SLOTS, KV_HEADS, HEAD_DIM)
    v_low = low(low_back(jnp.dot(x_norm, w_value.T, precision=HIGH)))
    cosine, sine = rope_tables(positions)
    cosine = cosine[:, None, :]
    sine = sine[:, None, :]
    q_rot = low(rotate(q_proj * rms_scale(q_proj) * q_gain, cosine, sine))
    k_rot = low(rotate(k_proj * rms_scale(k_proj) * k_gain, cosine, sine))
    attn = low_back(low(attend(q_rot, k_rot, v_low, positions, length)))
    resid = x_seq + low_back(jnp.dot(attn, w_out, precision=HIGH))
    x_norm2 = low(resid * rms_scale(resid) * ffn_gain)
    gate_pre = low_back(jnp.dot(x_norm2, w_gate.T, precision=HIGH))
    up_pre = low_back(jnp.dot(x_norm2, w_up.T, precision=HIGH))
    hidden = low(jax.nn.silu(gate_pre) * up_pre)
    ffn_out = low_back(jnp.dot(hidden, w_down, precision=HIGH))
    return jnp.where(live, resid + ffn_out, 0.0)

def reference(tokens, cotangent, q_weight, k_weight, v_weight, o_weight, gate_weight, up_weight, down_weight, attn_gain, ffn_gain, q_gain, k_gain, lengths, pair_order):
    positions = slot_positions(pair_order, 2 * BLOCK, 0, SLOTS)
    params = tuple((w.astype(jnp.float32) for w in (q_weight, k_weight, v_weight, o_weight, gate_weight, up_weight, down_weight, attn_gain, ffn_gain, q_gain, k_gain)))

    def one_seq(summed, item):
        x_seq, cot_seq, length = item

        def inner(param_set, x_in):
            return layer(param_set, x_in, positions, length)
        out, pull = jax.vjp(inner, params, x_seq)
        grad_params, grad_x = pull(cot_seq)
        summed = jax.tree.map(lambda left, right: left + right, summed, grad_params)
        return (summed, (out.astype(jnp.bfloat16), grad_x))
    zero = jax.tree.map(jnp.zeros_like, params)
    summed, (outs, grads_x) = lax.scan(one_seq, zero, (tokens.astype(jnp.float32), cotangent.astype(jnp.float32), lengths))
    return (outs, grads_x, summed[0], summed[1], summed[2], summed[3], summed[4], summed[5], summed[6], summed[7], summed[8], summed[9], summed[10])
```

```python
import math

import jax
import jax.numpy as jnp
from jax import lax
from jax.experimental import pallas as pl
from jax.experimental.pallas import tpu as pltpu
from jax.sharding import PartitionSpec as P

D = 2048
HEADS = 32
KV_HEADS = 8
HEAD_DIM = 64
FF = 8192


EPS = 1e-05
THETA = 1000000.0
NEG = -1e30


def rms_scale(values):
    return lax.rsqrt(jnp.mean(values * values, axis=-1, keepdims=True) + EPS)


def rms_back(grad_normed, normed, scale_rows):
    return scale_rows * (
        grad_normed - normed * jnp.mean(grad_normed * normed, axis=-1, keepdims=True)
    )


def rope_tables(positions):
    half = HEAD_DIM // 2
    freq = THETA ** (-(jnp.arange(half, dtype=jnp.float32) * 2.0 / HEAD_DIM))
    angle = positions.astype(jnp.float32)[:, None] * freq[None, :]
    return (jnp.cos(angle), jnp.sin(angle))


def rotate(values, cosine, sine):
    half = values.shape[-1] // 2
    first = values[..., :half]
    second = values[..., half:]
    return jnp.concatenate(
        [first * cosine - second * sine, second * cosine + first * sine], axis=-1
    )


def slot_positions(pair_order, width_pair, first, count):
    slot = first + jnp.arange(count, dtype=jnp.int32)
    owner = slot // width_pair
    within = slot % width_pair
    half_blk = width_pair // 2
    pair = pair_order[owner]
    block_id = jnp.where(within < half_blk, pair, 2 * pair_order.shape[0] - 1 - pair)
    return block_id * half_blk + within % half_blk


def block_mask(query_pos, key_part, lengths):
    return (key_part[None, None, :] <= query_pos[None, :, None]) & (
        key_part[None, None, :] < lengths[:, None, None]
    )


def project(inputs, weight):
    return jnp.einsum("td,fd->tf", inputs, weight, preferred_element_type=jnp.float32)


def gate_grads(grad_hidden, gate_part, up_part):
    sigma = jax.nn.sigmoid(gate_part)
    grad_gate = grad_hidden * up_part * sigma * (1.0 + gate_part * (1.0 - sigma))
    grad_up = grad_hidden * gate_part * sigma
    return (grad_gate.astype(jnp.bfloat16), grad_up.astype(jnp.bfloat16))


def block_grads(q_rot, grad_o_low, lse, delta, k_blk, v_blk, allowed, scale):
    scores = (
        jnp.einsum("sqhgd,sjhd->sqhgj", q_rot, k_blk, preferred_element_type=jnp.float32) * scale
    )
    scores = jnp.where(allowed[:, :, None, None, :], scores, NEG)
    probs = jnp.exp(scores - lse[..., None])
    grad_probs = jnp.einsum(
        "sqhgd,sjhd->sqhgj", grad_o_low, v_blk, preferred_element_type=jnp.float32
    )
    grad_scores = (probs * (grad_probs - delta[..., None])).astype(jnp.bfloat16)
    return (probs, grad_scores)


def local(
    tokens,
    cotangent,
    q_weight,
    k_weight,
    v_weight,
    o_weight,
    gate_weight,
    up_weight,
    down_weight,
    attn_gain,
    ffn_gain,
    q_gain,
    k_gain,
    lengths,
    pair_order,
):
    seq_grp = tokens.shape[0]
    width_pair = tokens.shape[1]
    groups = HEADS // KV_HEADS
    q_width = HEADS * HEAD_DIM
    kv_width = KV_HEADS * HEAD_DIM
    scale = HEAD_DIM ** (-0.5)
    tok_rows = seq_grp * width_pair
    slots = width_pair * pair_order.shape[0]
    key_blk = math.gcd(slots, 512)
    key_count = slots // key_blk
    dev_count = lax.axis_size("ctx") * lax.axis_size("fsdp")
    local_pos = slot_positions(
        pair_order, width_pair, lax.axis_index("ctx") * width_pair, width_pair
    )
    key_pos = slot_positions(pair_order, width_pair, 0, slots)
    live_rows = (local_pos[None, :] < lengths[:, None]).reshape(tok_rows, 1)
    cosine, sine = rope_tables(local_pos)
    cosine = cosine[None, :, None, :]
    sine = sine[None, :, None, :]
    x_rows = tokens.astype(jnp.float32).reshape(tok_rows, D)
    scale_one = rms_scale(x_rows)
    normed_one = x_rows * scale_one
    x_norm = (normed_one * attn_gain).astype(jnp.bfloat16)
    w_query, w_key, w_value, w_out = (
        lax.all_gather(q_weight, ("ctx", "fsdp"), axis=0, tiled=True),
        lax.all_gather(k_weight, ("ctx", "fsdp"), axis=0, tiled=True),
        lax.all_gather(v_weight, ("ctx", "fsdp"), axis=0, tiled=True),
        lax.all_gather(o_weight, ("ctx", "fsdp"), axis=0, tiled=True),
    )
    q_proj = project(x_norm, w_query).reshape(seq_grp, width_pair, HEADS, HEAD_DIM)
    k_proj = project(x_norm, w_key).reshape(seq_grp, width_pair, KV_HEADS, HEAD_DIM)
    v_low = project(x_norm, w_value).astype(jnp.bfloat16).reshape(seq_grp, width_pair, kv_width)
    q_scale = rms_scale(q_proj)
    q_normed = q_proj * q_scale
    q_rot = (
        rotate(q_normed * q_gain, cosine, sine)
        .astype(jnp.bfloat16)
        .reshape(seq_grp, width_pair, KV_HEADS, groups, HEAD_DIM)
    )
    k_scale = rms_scale(k_proj)
    k_normed = k_proj * k_scale
    k_rot = (
        rotate(k_normed * k_gain, cosine, sine)
        .astype(jnp.bfloat16)
        .reshape(seq_grp, width_pair, kv_width)
    )
    k_all, v_all = (
        lax.all_gather(k_rot, "ctx", axis=1, tiled=True),
        lax.all_gather(v_low, "ctx", axis=1, tiled=True),
    )
    k_all = k_all.reshape(seq_grp, slots, KV_HEADS, HEAD_DIM)
    v_all = v_all.reshape(seq_grp, slots, KV_HEADS, HEAD_DIM)

    def key_slices(first, count):
        k_blk = lax.dynamic_slice_in_dim(k_all, first, count, 1)
        v_blk = lax.dynamic_slice_in_dim(v_all, first, count, 1)
        allowed = block_mask(local_pos, lax.dynamic_slice_in_dim(key_pos, first, count, 0), lengths)
        return (k_blk, v_blk, allowed)

    def forward_step(index, carry):
        top, total, summed = carry
        k_blk, v_blk, allowed = key_slices(index * key_blk, key_blk)
        scores = (
            jnp.einsum("sqhgd,sjhd->sqhgj", q_rot, k_blk, preferred_element_type=jnp.float32)
            * scale
        )
        scores = jnp.where(allowed[:, :, None, None, :], scores, NEG)
        new_top = jnp.maximum(top, jnp.max(scores, axis=-1))
        shrink = jnp.exp(top - new_top)
        probs = jnp.exp(scores - new_top[..., None])
        total = total * shrink + jnp.sum(probs, axis=-1)
        summed = summed * shrink[..., None] + jnp.einsum(
            "sqhgj,sjhd->sqhgd",
            probs.astype(jnp.bfloat16),
            v_blk,
            preferred_element_type=jnp.float32,
        )
        return (new_top, total, summed)

    stat_shape = (seq_grp, width_pair, KV_HEADS, groups)
    start_carry = (
        jnp.full(stat_shape, NEG, jnp.float32),
        jnp.zeros(stat_shape, jnp.float32),
        jnp.zeros(stat_shape + (HEAD_DIM,), jnp.float32),
    )
    top, total, summed = lax.fori_loop(0, key_count, forward_step, start_carry)
    lse = top + jnp.log(total)
    o_low = (summed / total[..., None]).astype(jnp.bfloat16)
    o_rows = o_low.reshape(tok_rows, q_width)
    resid = x_rows + jnp.einsum("tf,fd->td", o_rows, w_out, preferred_element_type=jnp.float32)
    scale_two = rms_scale(resid)
    normed_two = resid * scale_two
    x_norm2 = (normed_two * ffn_gain).astype(jnp.bfloat16)
    grad_out = jnp.where(live_rows, cotangent.astype(jnp.float32).reshape(tok_rows, D), 0.0)
    grad_low = grad_out.astype(jnp.bfloat16)
    pieces = (
        lax.all_gather(gate_weight, ("ctx", "fsdp"), axis=0, tiled=True),
        lax.all_gather(up_weight, ("ctx", "fsdp"), axis=0, tiled=True),
        lax.all_gather(down_weight, ("ctx", "fsdp"), axis=0, tiled=True),
    )
    gate_part = project(x_norm2, pieces[0])
    up_part = project(x_norm2, pieces[1])
    hidden_part = (jax.nn.silu(gate_part) * up_part).astype(jnp.bfloat16)
    out_sum = jnp.einsum("tf,fd->td", hidden_part, pieces[2], preferred_element_type=jnp.float32)
    gate_all = gate_part
    up_all = up_part
    hidden = (jax.nn.silu(gate_all) * up_all).astype(jnp.bfloat16)
    pieces = (
        lax.all_gather(gate_weight, ("ctx", "fsdp"), axis=0, tiled=True),
        lax.all_gather(up_weight, ("ctx", "fsdp"), axis=0, tiled=True),
        lax.all_gather(down_weight, ("ctx", "fsdp"), axis=0, tiled=True),
    )
    count = pieces[0].shape[0]
    gate_part = gate_all
    up_part = up_all
    grad_gate_part, grad_up_part = gate_grads(project(grad_low, pieces[2]), gate_part, up_part)
    grad_sum = jnp.einsum(
        "tf,fd->td", grad_gate_part, pieces[0], preferred_element_type=jnp.float32
    ) + jnp.einsum("tf,fd->td", grad_up_part, pieces[1], preferred_element_type=jnp.float32)
    gate_grad_all = grad_gate_part
    up_grad_all = grad_up_part
    block_out = (
        jnp.where(live_rows, resid + out_sum, 0.0)
        .astype(jnp.bfloat16)
        .reshape(seq_grp, width_pair, D)
    )
    ffn_dev = FF // dev_count
    owners = lax.axis_size(("ctx", "fsdp")) * (3 * ffn_dev) // (3 * ffn_dev)
    first = jnp.int32(0) // (3 * ffn_dev) * ffn_dev
    grad_gate_part = jnp.einsum(
        "tf,td->fd", gate_grad_all, x_norm2, preferred_element_type=jnp.float32
    )
    grad_up_part = jnp.einsum("tf,td->fd", up_grad_all, x_norm2, preferred_element_type=jnp.float32)
    grad_down_part = jnp.einsum("tf,td->fd", hidden, grad_low, preferred_element_type=jnp.float32)
    stacked = jnp.stack(
        [
            grad_gate_part.reshape(owners, ffn_dev, D),
            grad_up_part.reshape(owners, ffn_dev, D),
            grad_down_part.reshape(owners, ffn_dev, D),
        ],
        axis=1,
    )
    ffn_grads = lax.psum_scatter(
        stacked.reshape(lax.axis_size(("ctx", "fsdp")) * (3 * ffn_dev), D),
        ("ctx", "fsdp"),
        scatter_dimension=0,
        tiled=True,
    )
    grad_ffn_gain = jnp.sum(grad_sum * normed_two, axis=0)
    grad_resid = grad_out + rms_back(grad_sum * ffn_gain, normed_two, scale_two)
    grad_attn_low = grad_resid.astype(jnp.bfloat16)
    grad_o_low = (
        project(grad_attn_low, w_out)
        .astype(jnp.bfloat16)
        .reshape(seq_grp, width_pair, KV_HEADS, groups, HEAD_DIM)
    )
    delta = jnp.sum(grad_o_low.astype(jnp.float32) * o_low.astype(jnp.float32), axis=-1)
    dq_zero = jnp.zeros((seq_grp, width_pair, KV_HEADS, groups, HEAD_DIM), jnp.float32)
    kv_cols = seq_grp * 2 * kv_width

    def key_value_grads(probs, grad_scores):
        grad_k_blk = (
            jnp.einsum("sqhgj,sqhgd->jshd", grad_scores, q_rot, preferred_element_type=jnp.float32)
            * scale
        )
        grad_v_blk = jnp.einsum(
            "sqhgj,sqhgd->jshd",
            probs.astype(jnp.bfloat16),
            grad_o_low,
            preferred_element_type=jnp.float32,
        )
        return jnp.stack([grad_k_blk, grad_v_blk], axis=2).reshape(probs.shape[-1], kv_cols)

    def both_step(grad_q, index):
        k_blk, v_blk, allowed = key_slices(index * key_blk, key_blk)
        probs, grad_scores = block_grads(
            q_rot, grad_o_low, lse, delta, k_blk, v_blk, allowed, scale
        )
        grad_q = (
            grad_q
            + jnp.einsum(
                "sqhgj,sjhd->sqhgd", grad_scores, k_blk, preferred_element_type=jnp.float32
            )
            * scale
        )
        return (grad_q, key_value_grads(probs, grad_scores))

    grad_q_rot, kv_blocks = lax.scan(both_step, dq_zero, jnp.arange(key_count))
    kv_grad = lax.psum_scatter(
        kv_blocks.reshape(slots, kv_cols), "ctx", scatter_dimension=0, tiled=True
    )
    kv_grad = jnp.transpose(
        kv_grad.reshape(width_pair, seq_grp, 2, KV_HEADS, HEAD_DIM), (1, 0, 2, 3, 4)
    )
    grad_q_pre = rotate(grad_q_rot.reshape(seq_grp, width_pair, HEADS, HEAD_DIM), cosine, -sine)
    grad_k_pre = rotate(kv_grad[:, :, 0], cosine, -sine)
    grad_q_gain = jnp.sum(grad_q_pre * q_normed, axis=(0, 1, 2))
    grad_k_gain = jnp.sum(grad_k_pre * k_normed, axis=(0, 1, 2))
    grad_q_proj = (
        rms_back(grad_q_pre * q_gain, q_normed, q_scale)
        .reshape(tok_rows, q_width)
        .astype(jnp.bfloat16)
    )
    grad_k_proj = (
        rms_back(grad_k_pre * k_gain, k_normed, k_scale)
        .reshape(tok_rows, kv_width)
        .astype(jnp.bfloat16)
    )
    grad_v_proj = kv_grad[:, :, 1].reshape(tok_rows, kv_width).astype(jnp.bfloat16)
    grad_norm1 = jnp.einsum("tf,fd->td", grad_q_proj, w_query, preferred_element_type=jnp.float32)
    grad_norm1 = grad_norm1 + jnp.einsum(
        "tf,fd->td", grad_k_proj, w_key, preferred_element_type=jnp.float32
    )
    grad_norm1 = grad_norm1 + jnp.einsum(
        "tf,fd->td", grad_v_proj, w_value, preferred_element_type=jnp.float32
    )
    grad_attn_gain = jnp.sum(grad_norm1 * normed_one, axis=0)
    grad_tokens = (grad_resid + rms_back(grad_norm1 * attn_gain, normed_one, scale_one)).reshape(
        seq_grp, width_pair, D
    )
    q_dev = q_width // dev_count
    kv_dev = kv_width // dev_count
    per_dev = 2 * q_dev + 2 * kv_dev
    owners = lax.axis_size(("ctx", "fsdp")) * per_dev // per_dev

    def rows_of(grad_rows, inputs, each):
        return jnp.einsum(
            "tf,td->fd", grad_rows, inputs, preferred_element_type=jnp.float32
        ).reshape(owners, each, D)

    joined = jnp.concatenate(
        [
            rows_of(grad_q_proj, x_norm, q_dev),
            rows_of(grad_k_proj, x_norm, kv_dev),
            rows_of(grad_v_proj, x_norm, kv_dev),
            rows_of(o_rows, grad_attn_low, q_dev),
        ],
        axis=1,
    )
    attn_grads = lax.psum_scatter(
        joined.reshape(lax.axis_size(("ctx", "fsdp")) * per_dev, D),
        ("ctx", "fsdp"),
        scatter_dimension=0,
        tiled=True,
    )
    grad_attn_gain, grad_ffn_gain, grad_q_gain, grad_k_gain = lax.psum(
        (grad_attn_gain, grad_ffn_gain, grad_q_gain, grad_k_gain), ("ctx", "fsdp")
    )
    return (
        block_out,
        grad_tokens,
        attn_grads[:q_dev],
        attn_grads[q_dev : q_dev + kv_dev],
        attn_grads[q_dev + kv_dev : q_dev + 2 * kv_dev],
        attn_grads[q_dev + 2 * kv_dev :],
        ffn_grads[:ffn_dev],
        ffn_grads[ffn_dev : 2 * ffn_dev],
        ffn_grads[2 * ffn_dev :],
        grad_attn_gain,
        grad_ffn_gain,
        grad_q_gain,
        grad_k_gain,
    )


AXES = ("ctx", "fsdp")
RANKS = 16
LANES = 4 * HEAD_DIM
BF16 = jnp.bfloat16
F32 = jnp.float32
FAR = 1 << 30


def fits_split(mesh):
    return mesh.shape["ctx"] == RANKS and mesh.shape["fsdp"] == 2


def pairs_of(move):
    found = []
    for z in range(4):
        for y in range(2):
            for core in range(2):
                for x in range(2):
                    to = move(z, y, core, x)
                    if to is not None:
                        tz, ty, tcore, tx = to
                        found.append(
                            (z * 8 + y * 4 + core * 2 + x, tz * 8 + ty * 4 + tcore * 2 + tx)
                        )
    return found


SWAP_X = pairs_of(lambda z, y, c, x: (z, y, c, 1 - x))
SWAP_CORE = pairs_of(lambda z, y, c, x: (z, y, 1 - c, x))
SWAP_Y = pairs_of(lambda z, y, c, x: (z, 1 - y, c, x))
SWAP_Z0 = pairs_of(lambda z, y, c, x: (z ^ 1, y, c, x))
SWAP_Z1 = pairs_of(lambda z, y, c, x: (z ^ 2, y, c, x))
SWAP_MID = pairs_of(lambda z, y, c, x: (3 - z, y, c, x) if z in (1, 2) else None)
OUTWARD = pairs_of(lambda z, y, c, x: (z ^ 1, y, c, x) if z in (1, 2) else None)
INWARD = pairs_of(lambda z, y, c, x: (z ^ 1, y, c, x) if z in (0, 3) else None)
RELATIVE = tuple(kz * 4 + ky * 2 + kc for kc in range(2) for ky in range(2) for kz in range(4))


def send(value, pairs):
    return lax.ppermute(value, AXES, pairs)


def gather_blocks(piece):
    outer = jnp.logical_or(lax.axis_index("ctx") < 4, lax.axis_index("ctx") >= 12)
    near = send(piece, SWAP_Z0)
    mid_own = send(piece, SWAP_MID)
    across = [send(piece, SWAP_Y)]
    mid_near = send(near, SWAP_MID)
    out_own = send(mid_own, OUTWARD)
    across.append(send(near, SWAP_Y))
    two = jnp.where(outer, out_own, mid_near)
    out_near = send(mid_near, OUTWARD)
    across.append(send(two, SWAP_Y))
    three = jnp.where(outer, out_near, mid_own)
    across.append(send(three, SWAP_Y))
    half = [piece, near, two, three] + across
    other = [send(block, SWAP_CORE) for block in half]
    return jnp.concatenate(half + other, axis=0)


def add_low(left, right):
    return (left.astype(F32) + right.astype(F32)).astype(BF16)


def scatter_blocks(near_half, far_half):
    rows = near_half.shape[0] // 8
    summed = add_low(near_half, send(far_half, SWAP_CORE))
    blocks = [summed[j * rows : (j + 1) * rows] for j in range(8)]
    own = [None] * 4
    for kz in (3, 2, 1, 0):
        own[kz] = add_low(blocks[kz], send(blocks[4 + kz], SWAP_Y))
    to_two = add_low(own[2], send(own[3], INWARD))
    to_three = add_low(own[3], send(own[2], INWARD))
    to_near = add_low(own[1], send(to_two, SWAP_MID))
    mine = own[0].astype(F32) + send(to_three, SWAP_MID).astype(F32)
    return mine + send(to_near, SWAP_Z0).astype(F32)


def total_sum(value):
    for pairs in (SWAP_CORE, SWAP_X, SWAP_Y, SWAP_Z0, SWAP_Z1):
        value = value + send(value, pairs)
    return value


def head_sums():
    row = lax.broadcasted_iota(jnp.int32, (LANES, LANES), 0) // HEAD_DIM
    col = lax.broadcasted_iota(jnp.int32, (LANES, LANES), 1) // HEAD_DIM
    return jnp.where(row == col, 1.0 / HEAD_DIM, 0.0).astype(F32)


def head_mean(values):
    return jnp.dot(
        values, head_sums(), precision=lax.Precision.HIGHEST, preferred_element_type=F32
    )


def swap_halves(values):
    lane = lax.broadcasted_iota(jnp.int32, values.shape, 1)
    return jnp.where(
        lane % HEAD_DIM < HEAD_DIM // 2,
        pltpu.roll(values, LANES - HEAD_DIM // 2, 1),
        pltpu.roll(values, HEAD_DIM // 2, 1),
    )


def dot_lanes(left, right):
    return lax.dot_general(left, right, (((1,), (1,)), ((), ())), preferred_element_type=F32)


def allowed_of(length_ref, pos_col_ref, pos_row_ref):
    col = pos_col_ref[...]
    return jnp.where(col < length_ref[0], col, FAR) <= pos_row_ref[...]


def attend_kernel(
    length_ref, proj_ref, cos_ref, sin_ref, gain_ref, pos_col_ref, pos_row_ref,
    out_ref, lse_ref, rot_ref, val_ref,
):
    step = pl.program_id(0)
    block = out_ref.shape[0]

    @pl.when(step == 0)
    def _():
        proj = proj_ref[...]
        normed = proj * lax.rsqrt(head_mean(proj * proj) + EPS) * gain_ref[...]
        rotated = normed * cos_ref[...] + swap_halves(normed) * sin_ref[...]
        lane = lax.broadcasted_iota(jnp.int32, proj.shape, 1)
        rotated = jnp.where(lane < 2 * HEAD_DIM, rotated * HEAD_DIM**-0.5, rotated)
        rot_ref[...] = jnp.where(lane < 3 * HEAD_DIM, rotated, proj).astype(BF16)
        val_ref[:HEAD_DIM, :] = proj[:, 3 * HEAD_DIM :].T.astype(BF16)
        val_ref[HEAD_DIM:, :] = jnp.ones((16, proj.shape[0]), BF16)

    allowed = allowed_of(length_ref, pos_col_ref, pos_row_ref)
    keys = rot_ref[:, 2 * HEAD_DIM : 3 * HEAD_DIM]
    query = rot_ref[pl.ds(pl.multiple_of(step * block, block), block), : 2 * HEAD_DIM]
    outs = []
    for head in range(2):
        scores = dot_lanes(keys, query[:, head * HEAD_DIM : (head + 1) * HEAD_DIM])
        weights = jnp.where(allowed, jnp.exp(scores), 0.0).astype(BF16)
        summed = jnp.dot(val_ref[...], weights, preferred_element_type=F32)
        total = summed[HEAD_DIM : HEAD_DIM + 1]
        outs.append((summed[:HEAD_DIM] / total).T)
        lse_ref[head : head + 1, :] = jnp.log(total)
    out_ref[...] = jnp.concatenate(outs, axis=1).astype(BF16)


def attend(proj, cosine, sine, gain, positions, length):
    slots = proj.shape[0]
    block = 256
    full = lambda shape: pl.BlockSpec(shape, lambda i: (0, 0))
    return pl.pallas_call(
        attend_kernel,
        grid=(slots // block,),
        in_specs=[
            pl.BlockSpec(memory_space=pltpu.SMEM),
            full((slots, LANES)),
            full((slots, LANES)),
            full((slots, LANES)),
            full((1, LANES)),
            full((slots, 1)),
            pl.BlockSpec((1, block), lambda i: (0, i)),
        ],
        out_specs=[
            pl.BlockSpec((block, 2 * HEAD_DIM), lambda i: (i, 0)),
            pl.BlockSpec((2, block), lambda i: (0, i)),
            full((slots, LANES)),
        ],
        out_shape=[
            jax.ShapeDtypeStruct((slots, 2 * HEAD_DIM), BF16),
            jax.ShapeDtypeStruct((2, slots), F32),
            jax.ShapeDtypeStruct((slots, LANES), BF16),
        ],
        scratch_shapes=[pltpu.VMEM((HEAD_DIM + 16, slots), BF16)],
        name="attend",
    )(length, proj, cosine, sine, gain, positions[:, None], positions[None, :])


def attend_back_kernel(
    length_ref, rot_ref, grad_ref, out_ref, lse_ref, pos_col_ref, pos_row_ref, dq_ref, dkv_ref
):
    step = pl.program_id(0)
    block = dq_ref.shape[0]
    allowed = allowed_of(length_ref, pos_col_ref, pos_row_ref)
    keys = rot_ref[:, 2 * HEAD_DIM : 3 * HEAD_DIM]
    values = rot_ref[:, 3 * HEAD_DIM :]
    query = rot_ref[pl.ds(pl.multiple_of(step * block, block), block), : 2 * HEAD_DIM]
    grad = grad_ref[...]
    product = grad.astype(F32) * out_ref[...].astype(F32)
    ones = jnp.ones((8, HEAD_DIM), F32)
    grad_q, grad_k, grad_v = [], 0.0, 0.0
    for head in range(2):
        cut = slice(head * HEAD_DIM, (head + 1) * HEAD_DIM)
        delta = lax.dot_general(
            ones,
            product[:, cut],
            (((1,), (1,)), ((), ())),
            precision=lax.Precision.HIGHEST,
            preferred_element_type=F32,
        )[:1]
        scores = dot_lanes(keys, query[:, cut])
        probs = jnp.where(allowed, jnp.exp(scores - lse_ref[head : head + 1, :]), 0.0)
        grad_probs = dot_lanes(values, grad[:, cut])
        grad_scores = (probs * (grad_probs - delta)).astype(BF16)
        grad_v += jnp.dot(probs.astype(BF16), grad[:, cut], preferred_element_type=F32)
        grad_k += jnp.dot(grad_scores, query[:, cut], preferred_element_type=F32)
        grad_q.append(
            lax.dot_general(
                grad_scores, keys, (((0,), (0,)), ((), ())), preferred_element_type=F32
            )
        )
    dq_ref[...] = jnp.concatenate(grad_q, axis=1) * HEAD_DIM**-0.5
    both = jnp.concatenate([grad_k, grad_v], axis=1)

    @pl.when(step == 0)
    def _():
        dkv_ref[...] = both

    @pl.when(step > 0)
    def _():
        dkv_ref[...] += both


def attend_back(rotated, grad, out, lse, positions, length):
    slots = rotated.shape[0]
    block = 256
    full = lambda shape: pl.BlockSpec(shape, lambda i: (0, 0))
    rows = pl.BlockSpec((block, 2 * HEAD_DIM), lambda i: (i, 0))
    return pl.pallas_call(
        attend_back_kernel,
        grid=(slots // block,),
        in_specs=[
            pl.BlockSpec(memory_space=pltpu.SMEM),
            full((slots, LANES)),
            rows,
            rows,
            pl.BlockSpec((2, block), lambda i: (0, i)),
            full((slots, 1)),
            pl.BlockSpec((1, block), lambda i: (0, i)),
        ],
        out_specs=[rows, full((slots, 2 * HEAD_DIM))],
        out_shape=[
            jax.ShapeDtypeStruct((slots, 2 * HEAD_DIM), F32),
            jax.ShapeDtypeStruct((slots, 2 * HEAD_DIM), F32),
        ],
        name="attend_back",
    )(length, rotated, grad, out, lse, positions[:, None], positions[None, :])


def project_back_kernel(
    dq_ref, dkv_ref, other_ref, proj_ref, cos_ref, sin_ref, gain_ref, grad_ref, sum_ref
):
    step = pl.program_id(0)
    grad = jnp.concatenate([dq_ref[...], dkv_ref[...] + other_ref[...]], axis=1)
    proj = proj_ref[...]
    scale_rows = lax.rsqrt(head_mean(proj * proj) + EPS)
    normed = proj * scale_rows
    turned = grad * cos_ref[...] - swap_halves(grad) * sin_ref[...]
    gained = turned * gain_ref[...]
    back = scale_rows * (gained - normed * head_mean(gained * normed))
    lane = lax.broadcasted_iota(jnp.int32, proj.shape, 1)
    grad_ref[...] = jnp.where(lane < 3 * HEAD_DIM, back, grad).astype(BF16)
    sums = jnp.sum((turned * normed).reshape(-1, 8, LANES), axis=0)

    @pl.when(step == 0)
    def _():
        sum_ref[...] = sums

    @pl.when(step > 0)
    def _():
        sum_ref[...] += sums


def project_back(grad_q, grad_kv, other_kv, proj, cosine, sine, gain):
    slots = proj.shape[0]
    block = 256
    steps = slots // block
    half = pl.BlockSpec((block, 2 * HEAD_DIM), lambda i: (i, 0))
    rows = pl.BlockSpec((block, LANES), lambda i: (i, 0))
    return pl.pallas_call(
        project_back_kernel,
        grid=(steps,),
        in_specs=[
            half,
            half,
            pl.BlockSpec((block, 2 * HEAD_DIM), lambda i: ((i + steps // 2) % steps, 0)),
            rows,
            rows,
            rows,
            pl.BlockSpec((1, LANES), lambda i: (0, 0)),
        ],
        out_specs=[rows, pl.BlockSpec((8, LANES), lambda i: (0, 0))],
        out_shape=[
            jax.ShapeDtypeStruct((slots, LANES), BF16),
            jax.ShapeDtypeStruct((8, LANES), F32),
        ],
        name="project_back",
    )(grad_q, grad_kv, other_kv, proj, cosine, sine, gain)


def dot_rows(left, right):
    return lax.dot_general(left, right, (((0,), (0,)), ((), ())), preferred_element_type=F32)


def plain(left, right):
    return jnp.dot(left, right, preferred_element_type=F32)


def in_order(own, other, index):
    first = index == 0
    return jnp.concatenate([jnp.where(first, own, other), jnp.where(first, other, own)], axis=0)


def split_local(
    tokens, cotangent, q_weight, k_weight, v_weight, o_weight, gate_weight, up_weight,
    down_weight, attn_gain, ffn_gain, q_gain, k_gain, lengths, pair_order,
):
    seqs, width, _ = tokens.shape
    rank = lax.axis_index("ctx")
    side = lax.axis_index("fsdp")
    core = rank % 2
    chunks = range(seqs)
    q_rows, kv_rows, ff_rows = q_weight.shape[0], k_weight.shape[0], gate_weight.shape[0]

    kv_own = jnp.stack([k_weight, v_weight])
    kv_side = send(kv_own, SWAP_X)
    kv_half = jnp.concatenate(
        [jnp.where(side == 0, kv_own, kv_side), jnp.where(side == 0, kv_side, kv_own)], axis=1
    )
    kv_core = send(kv_half, SWAP_CORE)
    kv_full = jnp.concatenate(
        [jnp.where(core == 0, kv_half, kv_core), jnp.where(core == 0, kv_core, kv_half)], axis=1
    )
    w_attn = jnp.concatenate(
        [q_weight, send(q_weight, SWAP_X), kv_full[0], kv_full[1]], axis=0
    )
    x_rows = [tokens[s].astype(F32) for s in chunks]
    scale_one = [rms_scale(x) for x in x_rows]
    normed_one = [x * r for x, r in zip(x_rows, scale_one)]
    x_norm = [gather_blocks((n * attn_gain).astype(BF16)) for n in normed_one]

    w_out = jnp.concatenate([o_weight, send(o_weight, SWAP_X)], axis=0)
    gate_up = jnp.concatenate([gate_weight, up_weight], axis=0)
    w_gate_up = jnp.concatenate([gate_up, send(gate_up, SWAP_X)], axis=0)
    w_down = jnp.concatenate([down_weight, send(down_weight, SWAP_X)], axis=0)

    dealt = pair_order[rank ^ jnp.array(RELATIVE, jnp.int32)]
    within = jnp.arange(width, dtype=jnp.int32)
    half_blk = width // 2
    block_id = jnp.where(
        within[None, :] < half_blk, dealt[:, None], 2 * pair_order.shape[0] - 1 - dealt[:, None]
    )
    positions = (block_id * half_blk + within[None, :] % half_blk).reshape(-1)
    slots = positions.shape[0]
    cosine, sine = rope_tables(positions)
    plain_lanes = jnp.ones((slots, HEAD_DIM), F32)
    cosine = jnp.concatenate([cosine] * 6 + [plain_lanes], axis=1)
    sine = jnp.concatenate([-sine, sine] * 3 + [plain_lanes * 0.0], axis=1)
    gain_lanes = jnp.concatenate([q_gain, q_gain, k_gain, jnp.ones((HEAD_DIM,), F32)])[None, :]
    my_dealt = pair_order[rank]
    my_pos = (
        jnp.where(within < half_blk, my_dealt, 2 * pair_order.shape[0] - 1 - my_dealt) * half_blk
        + within % half_blk
    )
    live = [(my_pos < lengths[s])[:, None] for s in chunks]

    grad_out = [jnp.where(live[s], cotangent[s].astype(F32), 0.0) for s in chunks]
    grad_low = [gather_blocks(g.astype(BF16)) for g in grad_out]

    proj = [project(x_norm[s], w_attn) for s in chunks]
    heads = [
        attend(proj[s], cosine, sine, gain_lanes, positions, lengths[s : s + 1]) for s in chunks
    ]

    def partial_sums(rows, weight):
        cut = rows.shape[0] // 2
        far = plain(rows[cut:], weight).astype(BF16)
        near = plain(rows[:cut], weight).astype(BF16)
        return scatter_blocks(near, far)

    resid = [x_rows[s] + partial_sums(heads[s][0], w_out) for s in chunks]
    scale_two = [rms_scale(h) for h in resid]
    normed_two = [h * r for h, r in zip(resid, scale_two)]
    x_norm2 = [gather_blocks((n * ffn_gain).astype(BF16)) for n in normed_two]

    hidden, gate_up_grads = [], []
    for s in chunks:
        both = project(x_norm2[s], w_gate_up).reshape(slots, 2, 2, ff_rows)
        gate_part, up_part = both[:, :, 0], both[:, :, 1]
        hidden.append((jax.nn.silu(gate_part) * up_part).astype(BF16).reshape(slots, 2 * ff_rows))
        grad_hidden = project(grad_low[s], w_down).reshape(slots, 2, ff_rows)
        parts = gate_grads(grad_hidden, gate_part, up_part)
        gate_up_grads.append(jnp.stack(parts, axis=2).reshape(slots, 4 * ff_rows))
    grad_norm2 = [partial_sums(gate_up_grads[s], w_gate_up) for s in chunks]
    out_sum = [partial_sums(hidden[s], w_down) for s in chunks]
    block_out = jnp.stack(
        [jnp.where(live[s], resid[s] + out_sum[s], 0.0).astype(BF16) for s in chunks]
    )
    grad_ffn_gain = sum(jnp.sum(grad_norm2[s] * normed_two[s], axis=0) for s in chunks)
    grad_resid = [
        grad_out[s] + rms_back(grad_norm2[s] * ffn_gain, normed_two[s], scale_two[s])
        for s in chunks
    ]
    grad_attn_low = [gather_blocks(g.astype(BF16)) for g in grad_resid]

    def both_sides(full):
        own = full.shape[0] // 2
        return full[:own] + send(full[own:].astype(BF16), SWAP_X).astype(F32)

    gate_up_grad = both_sides(sum(dot_rows(gate_up_grads[s], x_norm2[s]) for s in chunks))
    down_grad = both_sides(sum(dot_rows(hidden[s], grad_low[s]) for s in chunks))

    grads, gain_sums = [], 0.0
    for s in chunks:
        grad_o = project(grad_attn_low[s], w_out).astype(BF16)
        out, lse, rotated = heads[s]
        grad_q, grad_kv = attend_back(rotated, grad_o, out, lse, positions, lengths[s : s + 1])
        grad_rows, sums = project_back(
            grad_q, grad_kv, send(grad_kv, SWAP_CORE), proj[s], cosine, sine, gain_lanes
        )
        grads.append(grad_rows)
        gain_sums = gain_sums + jnp.sum(sums, axis=0)
    row = jnp.arange(LANES)[:, None] // HEAD_DIM
    w_once = jnp.where((row < 2) | (row == 2 + core), w_attn, 0).astype(BF16)
    grad_norm1 = [partial_sums(grads[s], w_once) for s in chunks]
    o_grad = both_sides(sum(dot_rows(heads[s][0], grad_attn_low[s]) for s in chunks))
    attn_full = sum(dot_rows(grads[s], x_norm[s]) for s in chunks)
    kv_grads = attn_full[2 * q_rows :].reshape(2, 2, 2, kv_rows, D)
    kv_mine = jnp.where(core == 0, kv_grads[:, 0], kv_grads[:, 1])
    kv_stay = jnp.where(side == 0, kv_mine[:, 0], kv_mine[:, 1])
    kv_leave = jnp.where(side == 0, kv_mine[:, 1], kv_mine[:, 0])
    attn_grads = both_sides(
        jnp.concatenate(
            [
                attn_full[:q_rows],
                kv_stay.reshape(2 * kv_rows, D),
                attn_full[q_rows : 2 * q_rows],
                kv_leave.reshape(2 * kv_rows, D),
            ],
            axis=0,
        )
    )
    grad_tokens = jnp.stack(
        [
            grad_resid[s] + rms_back(grad_norm1[s] * attn_gain, normed_one[s], scale_one[s])
            for s in chunks
        ]
    )
    owned = jnp.concatenate([q_weight, k_weight, v_weight], axis=0).astype(F32)
    grad_attn_gain = jnp.sum(owned * attn_grads, axis=0) / attn_gain
    gains = total_sum(
        jnp.concatenate(
            [
                grad_attn_gain,
                grad_ffn_gain,
                gain_sums[:HEAD_DIM] + gain_sums[HEAD_DIM : 2 * HEAD_DIM],
                0.5 * gain_sums[2 * HEAD_DIM : 3 * HEAD_DIM],
            ]
        )
    )
    return (
        block_out,
        grad_tokens,
        attn_grads[:q_rows],
        attn_grads[q_rows : q_rows + kv_rows],
        attn_grads[q_rows + kv_rows :],
        o_grad,
        gate_up_grad[:ff_rows],
        gate_up_grad[ff_rows:],
        down_grad,
        gains[:D],
        gains[D : 2 * D],
        gains[2 * D : 2 * D + HEAD_DIM],
        gains[2 * D + HEAD_DIM :],
    )


def solution(mesh):
    body = split_local if fits_split(mesh) else local
    in_specs = (
        P("fsdp", "ctx", None),
        P("fsdp", "ctx", None),
        P(("ctx", "fsdp"), None),
        P(("ctx", "fsdp"), None),
        P(("ctx", "fsdp"), None),
        P(("ctx", "fsdp"), None),
        P(("ctx", "fsdp"), None),
        P(("ctx", "fsdp"), None),
        P(("ctx", "fsdp"), None),
        P(),
        P(),
        P(),
        P(),
        P("fsdp"),
        P(),
    )
    out_specs = (
        P("fsdp", "ctx", None),
        P("fsdp", "ctx", None),
        P(("ctx", "fsdp"), None),
        P(("ctx", "fsdp"), None),
        P(("ctx", "fsdp"), None),
        P(("ctx", "fsdp"), None),
        P(("ctx", "fsdp"), None),
        P(("ctx", "fsdp"), None),
        P(("ctx", "fsdp"), None),
        P(),
        P(),
        P(),
        P(),
    )
    return jax.shard_map(body, mesh=mesh, in_specs=in_specs, out_specs=out_specs, check_vma=False)
```

```python
import math

import jax
import jax.numpy as jnp
from jax import lax
from jax.experimental import pallas as pl
from jax.experimental.pallas import tpu as pltpu
from jax.sharding import PartitionSpec as P

D = 2048
HEADS = 32
KV_HEADS = 8
HEAD_DIM = 64
FF = 8192


EPS = 1e-05
THETA = 1000000.0
NEG = -1e30


def rms_scale(values):
    return lax.rsqrt(jnp.mean(values * values, axis=-1, keepdims=True) + EPS)


def rms_back(grad_normed, normed, scale_rows):
    return scale_rows * (
        grad_normed - normed * jnp.mean(grad_normed * normed, axis=-1, keepdims=True)
    )


def rope_tables(positions):
    half = HEAD_DIM // 2
    freq = THETA ** (-(jnp.arange(half, dtype=jnp.float32) * 2.0 / HEAD_DIM))
    angle = positions.astype(jnp.float32)[:, None] * freq[None, :]
    return (jnp.cos(angle), jnp.sin(angle))


def rotate(values, cosine, sine):
    half = values.shape[-1] // 2
    first = values[..., :half]
    second = values[..., half:]
    return jnp.concatenate(
        [first * cosine - second * sine, second * cosine + first * sine], axis=-1
    )


def slot_positions(pair_order, width_pair, first, count):
    slot = first + jnp.arange(count, dtype=jnp.int32)
    owner = slot // width_pair
    within = slot % width_pair
    half_blk = width_pair // 2
    pair = pair_order[owner]
    block_id = jnp.where(within < half_blk, pair, 2 * pair_order.shape[0] - 1 - pair)
    return block_id * half_blk + within % half_blk


def block_mask(query_pos, key_part, lengths):
    return (key_part[None, None, :] <= query_pos[None, :, None]) & (
        key_part[None, None, :] < lengths[:, None, None]
    )


def project(inputs, weight):
    return jnp.einsum("td,fd->tf", inputs, weight, preferred_element_type=jnp.float32)


def gate_grads(grad_hidden, gate_part, up_part):
    sigma = jax.nn.sigmoid(gate_part)
    grad_gate = grad_hidden * up_part * sigma * (1.0 + gate_part * (1.0 - sigma))
    grad_up = grad_hidden * gate_part * sigma
    return (grad_gate.astype(jnp.bfloat16), grad_up.astype(jnp.bfloat16))


def block_grads(q_rot, grad_o_low, lse, delta, k_blk, v_blk, allowed, scale):
    scores = (
        jnp.einsum("sqhgd,sjhd->sqhgj", q_rot, k_blk, preferred_element_type=jnp.float32) * scale
    )
    scores = jnp.where(allowed[:, :, None, None, :], scores, NEG)
    probs = jnp.exp(scores - lse[..., None])
    grad_probs = jnp.einsum(
        "sqhgd,sjhd->sqhgj", grad_o_low, v_blk, preferred_element_type=jnp.float32
    )
    grad_scores = (probs * (grad_probs - delta[..., None])).astype(jnp.bfloat16)
    return (probs, grad_scores)


def local(
    tokens,
    cotangent,
    q_weight,
    k_weight,
    v_weight,
    o_weight,
    gate_weight,
    up_weight,
    down_weight,
    attn_gain,
    ffn_gain,
    q_gain,
    k_gain,
    lengths,
    pair_order,
):
    seq_grp = tokens.shape[0]
    width_pair = tokens.shape[1]
    groups = HEADS // KV_HEADS
    q_width = HEADS * HEAD_DIM
    kv_width = KV_HEADS * HEAD_DIM
    scale = HEAD_DIM ** (-0.5)
    tok_rows = seq_grp * width_pair
    slots = width_pair * pair_order.shape[0]
    key_blk = math.gcd(slots, 512)
    key_count = slots // key_blk
    dev_count = lax.axis_size("ctx") * lax.axis_size("fsdp")
    local_pos = slot_positions(
        pair_order, width_pair, lax.axis_index("ctx") * width_pair, width_pair
    )
    key_pos = slot_positions(pair_order, width_pair, 0, slots)
    live_rows = (local_pos[None, :] < lengths[:, None]).reshape(tok_rows, 1)
    cosine, sine = rope_tables(local_pos)
    cosine = cosine[None, :, None, :]
    sine = sine[None, :, None, :]
    x_rows = tokens.astype(jnp.float32).reshape(tok_rows, D)
    scale_one = rms_scale(x_rows)
    normed_one = x_rows * scale_one
    x_norm = (normed_one * attn_gain).astype(jnp.bfloat16)
    w_query, w_key, w_value, w_out = (
        lax.all_gather(q_weight, ("ctx", "fsdp"), axis=0, tiled=True),
        lax.all_gather(k_weight, ("ctx", "fsdp"), axis=0, tiled=True),
        lax.all_gather(v_weight, ("ctx", "fsdp"), axis=0, tiled=True),
        lax.all_gather(o_weight, ("ctx", "fsdp"), axis=0, tiled=True),
    )
    q_proj = project(x_norm, w_query).reshape(seq_grp, width_pair, HEADS, HEAD_DIM)
    k_proj = project(x_norm, w_key).reshape(seq_grp, width_pair, KV_HEADS, HEAD_DIM)
    v_low = project(x_norm, w_value).astype(jnp.bfloat16).reshape(seq_grp, width_pair, kv_width)
    q_scale = rms_scale(q_proj)
    q_normed = q_proj * q_scale
    q_rot = (
        rotate(q_normed * q_gain, cosine, sine)
        .astype(jnp.bfloat16)
        .reshape(seq_grp, width_pair, KV_HEADS, groups, HEAD_DIM)
    )
    k_scale = rms_scale(k_proj)
    k_normed = k_proj * k_scale
    k_rot = (
        rotate(k_normed * k_gain, cosine, sine)
        .astype(jnp.bfloat16)
        .reshape(seq_grp, width_pair, kv_width)
    )
    k_all, v_all = (
        lax.all_gather(k_rot, "ctx", axis=1, tiled=True),
        lax.all_gather(v_low, "ctx", axis=1, tiled=True),
    )
    k_all = k_all.reshape(seq_grp, slots, KV_HEADS, HEAD_DIM)
    v_all = v_all.reshape(seq_grp, slots, KV_HEADS, HEAD_DIM)

    def key_slices(first, count):
        k_blk = lax.dynamic_slice_in_dim(k_all, first, count, 1)
        v_blk = lax.dynamic_slice_in_dim(v_all, first, count, 1)
        allowed = block_mask(local_pos, lax.dynamic_slice_in_dim(key_pos, first, count, 0), lengths)
        return (k_blk, v_blk, allowed)

    def forward_step(index, carry):
        top, total, summed = carry
        k_blk, v_blk, allowed = key_slices(index * key_blk, key_blk)
        scores = (
            jnp.einsum("sqhgd,sjhd->sqhgj", q_rot, k_blk, preferred_element_type=jnp.float32)
            * scale
        )
        scores = jnp.where(allowed[:, :, None, None, :], scores, NEG)
        new_top = jnp.maximum(top, jnp.max(scores, axis=-1))
        shrink = jnp.exp(top - new_top)
        probs = jnp.exp(scores - new_top[..., None])
        total = total * shrink + jnp.sum(probs, axis=-1)
        summed = summed * shrink[..., None] + jnp.einsum(
            "sqhgj,sjhd->sqhgd",
            probs.astype(jnp.bfloat16),
            v_blk,
            preferred_element_type=jnp.float32,
        )
        return (new_top, total, summed)

    stat_shape = (seq_grp, width_pair, KV_HEADS, groups)
    start_carry = (
        jnp.full(stat_shape, NEG, jnp.float32),
        jnp.zeros(stat_shape, jnp.float32),
        jnp.zeros(stat_shape + (HEAD_DIM,), jnp.float32),
    )
    top, total, summed = lax.fori_loop(0, key_count, forward_step, start_carry)
    lse = top + jnp.log(total)
    o_low = (summed / total[..., None]).astype(jnp.bfloat16)
    o_rows = o_low.reshape(tok_rows, q_width)
    resid = x_rows + jnp.einsum("tf,fd->td", o_rows, w_out, preferred_element_type=jnp.float32)
    scale_two = rms_scale(resid)
    normed_two = resid * scale_two
    x_norm2 = (normed_two * ffn_gain).astype(jnp.bfloat16)
    grad_out = jnp.where(live_rows, cotangent.astype(jnp.float32).reshape(tok_rows, D), 0.0)
    grad_low = grad_out.astype(jnp.bfloat16)
    pieces = (
        lax.all_gather(gate_weight, ("ctx", "fsdp"), axis=0, tiled=True),
        lax.all_gather(up_weight, ("ctx", "fsdp"), axis=0, tiled=True),
        lax.all_gather(down_weight, ("ctx", "fsdp"), axis=0, tiled=True),
    )
    gate_part = project(x_norm2, pieces[0])
    up_part = project(x_norm2, pieces[1])
    hidden_part = (jax.nn.silu(gate_part) * up_part).astype(jnp.bfloat16)
    out_sum = jnp.einsum("tf,fd->td", hidden_part, pieces[2], preferred_element_type=jnp.float32)
    gate_all = gate_part
    up_all = up_part
    hidden = (jax.nn.silu(gate_all) * up_all).astype(jnp.bfloat16)
    pieces = (
        lax.all_gather(gate_weight, ("ctx", "fsdp"), axis=0, tiled=True),
        lax.all_gather(up_weight, ("ctx", "fsdp"), axis=0, tiled=True),
        lax.all_gather(down_weight, ("ctx", "fsdp"), axis=0, tiled=True),
    )
    count = pieces[0].shape[0]
    gate_part = gate_all
    up_part = up_all
    grad_gate_part, grad_up_part = gate_grads(project(grad_low, pieces[2]), gate_part, up_part)
    grad_sum = jnp.einsum(
        "tf,fd->td", grad_gate_part, pieces[0], preferred_element_type=jnp.float32
    ) + jnp.einsum("tf,fd->td", grad_up_part, pieces[1], preferred_element_type=jnp.float32)
    gate_grad_all = grad_gate_part
    up_grad_all = grad_up_part
    block_out = (
        jnp.where(live_rows, resid + out_sum, 0.0)
        .astype(jnp.bfloat16)
        .reshape(seq_grp, width_pair, D)
    )
    ffn_dev = FF // dev_count
    owners = lax.axis_size(("ctx", "fsdp")) * (3 * ffn_dev) // (3 * ffn_dev)
    first = jnp.int32(0) // (3 * ffn_dev) * ffn_dev
    grad_gate_part = jnp.einsum(
        "tf,td->fd", gate_grad_all, x_norm2, preferred_element_type=jnp.float32
    )
    grad_up_part = jnp.einsum("tf,td->fd", up_grad_all, x_norm2, preferred_element_type=jnp.float32)
    grad_down_part = jnp.einsum("tf,td->fd", hidden, grad_low, preferred_element_type=jnp.float32)
    stacked = jnp.stack(
        [
            grad_gate_part.reshape(owners, ffn_dev, D),
            grad_up_part.reshape(owners, ffn_dev, D),
            grad_down_part.reshape(owners, ffn_dev, D),
        ],
        axis=1,
    )
    ffn_grads = lax.psum_scatter(
        stacked.reshape(lax.axis_size(("ctx", "fsdp")) * (3 * ffn_dev), D),
        ("ctx", "fsdp"),
        scatter_dimension=0,
        tiled=True,
    )
    grad_ffn_gain = jnp.sum(grad_sum * normed_two, axis=0)
    grad_resid = grad_out + rms_back(grad_sum * ffn_gain, normed_two, scale_two)
    grad_attn_low = grad_resid.astype(jnp.bfloat16)
    grad_o_low = (
        project(grad_attn_low, w_out)
        .astype(jnp.bfloat16)
        .reshape(seq_grp, width_pair, KV_HEADS, groups, HEAD_DIM)
    )
    delta = jnp.sum(grad_o_low.astype(jnp.float32) * o_low.astype(jnp.float32), axis=-1)
    dq_zero = jnp.zeros((seq_grp, width_pair, KV_HEADS, groups, HEAD_DIM), jnp.float32)
    kv_cols = seq_grp * 2 * kv_width

    def key_value_grads(probs, grad_scores):
        grad_k_blk = (
            jnp.einsum("sqhgj,sqhgd->jshd", grad_scores, q_rot, preferred_element_type=jnp.float32)
            * scale
        )
        grad_v_blk = jnp.einsum(
            "sqhgj,sqhgd->jshd",
            probs.astype(jnp.bfloat16),
            grad_o_low,
            preferred_element_type=jnp.float32,
        )
        return jnp.stack([grad_k_blk, grad_v_blk], axis=2).reshape(probs.shape[-1], kv_cols)

    def both_step(grad_q, index):
        k_blk, v_blk, allowed = key_slices(index * key_blk, key_blk)
        probs, grad_scores = block_grads(
            q_rot, grad_o_low, lse, delta, k_blk, v_blk, allowed, scale
        )
        grad_q = (
            grad_q
            + jnp.einsum(
                "sqhgj,sjhd->sqhgd", grad_scores, k_blk, preferred_element_type=jnp.float32
            )
            * scale
        )
        return (grad_q, key_value_grads(probs, grad_scores))

    grad_q_rot, kv_blocks = lax.scan(both_step, dq_zero, jnp.arange(key_count))
    kv_grad = lax.psum_scatter(
        kv_blocks.reshape(slots, kv_cols), "ctx", scatter_dimension=0, tiled=True
    )
    kv_grad = jnp.transpose(
        kv_grad.reshape(width_pair, seq_grp, 2, KV_HEADS, HEAD_DIM), (1, 0, 2, 3, 4)
    )
    grad_q_pre = rotate(grad_q_rot.reshape(seq_grp, width_pair, HEADS, HEAD_DIM), cosine, -sine)
    grad_k_pre = rotate(kv_grad[:, :, 0], cosine, -sine)
    grad_q_gain = jnp.sum(grad_q_pre * q_normed, axis=(0, 1, 2))
    grad_k_gain = jnp.sum(grad_k_pre * k_normed, axis=(0, 1, 2))
    grad_q_proj = (
        rms_back(grad_q_pre * q_gain, q_normed, q_scale)
        .reshape(tok_rows, q_width)
        .astype(jnp.bfloat16)
    )
    grad_k_proj = (
        rms_back(grad_k_pre * k_gain, k_normed, k_scale)
        .reshape(tok_rows, kv_width)
        .astype(jnp.bfloat16)
    )
    grad_v_proj = kv_grad[:, :, 1].reshape(tok_rows, kv_width).astype(jnp.bfloat16)
    grad_norm1 = jnp.einsum("tf,fd->td", grad_q_proj, w_query, preferred_element_type=jnp.float32)
    grad_norm1 = grad_norm1 + jnp.einsum(
        "tf,fd->td", grad_k_proj, w_key, preferred_element_type=jnp.float32
    )
    grad_norm1 = grad_norm1 + jnp.einsum(
        "tf,fd->td", grad_v_proj, w_value, preferred_element_type=jnp.float32
    )
    grad_attn_gain = jnp.sum(grad_norm1 * normed_one, axis=0)
    grad_tokens = (grad_resid + rms_back(grad_norm1 * attn_gain, normed_one, scale_one)).reshape(
        seq_grp, width_pair, D
    )
    q_dev = q_width // dev_count
    kv_dev = kv_width // dev_count
    per_dev = 2 * q_dev + 2 * kv_dev
    owners = lax.axis_size(("ctx", "fsdp")) * per_dev // per_dev

    def rows_of(grad_rows, inputs, each):
        return jnp.einsum(
            "tf,td->fd", grad_rows, inputs, preferred_element_type=jnp.float32
        ).reshape(owners, each, D)

    joined = jnp.concatenate(
        [
            rows_of(grad_q_proj, x_norm, q_dev),
            rows_of(grad_k_proj, x_norm, kv_dev),
            rows_of(grad_v_proj, x_norm, kv_dev),
            rows_of(o_rows, grad_attn_low, q_dev),
        ],
        axis=1,
    )
    attn_grads = lax.psum_scatter(
        joined.reshape(lax.axis_size(("ctx", "fsdp")) * per_dev, D),
        ("ctx", "fsdp"),
        scatter_dimension=0,
        tiled=True,
    )
    grad_attn_gain, grad_ffn_gain, grad_q_gain, grad_k_gain = lax.psum(
        (grad_attn_gain, grad_ffn_gain, grad_q_gain, grad_k_gain), ("ctx", "fsdp")
    )
    return (
        block_out,
        grad_tokens,
        attn_grads[:q_dev],
        attn_grads[q_dev : q_dev + kv_dev],
        attn_grads[q_dev + kv_dev : q_dev + 2 * kv_dev],
        attn_grads[q_dev + 2 * kv_dev :],
        ffn_grads[:ffn_dev],
        ffn_grads[ffn_dev : 2 * ffn_dev],
        ffn_grads[2 * ffn_dev :],
        grad_attn_gain,
        grad_ffn_gain,
        grad_q_gain,
        grad_k_gain,
    )


AXES = ("ctx", "fsdp")
RANKS = 16
LANES = 4 * HEAD_DIM
BF16 = jnp.bfloat16
F32 = jnp.float32
FAR = 1 << 30


def fits_split(mesh):
    return mesh.shape["ctx"] == RANKS and mesh.shape["fsdp"] == 2


CYCLE = ((0, 0), (1, 0), (2, 0), (3, 0), (3, 1), (2, 1), (1, 1), (0, 1))
CHIPS = len(CYCLE)
DISTANCES = (4, 3, -3, 2, -2, 1, -1, 0)


def index_of(z, y, core, x):
    return z * 8 + y * 4 + core * 2 + x


def pairs_of(move):
    places = [(z, y, c, x) for z in range(4) for y in range(2) for c in range(2) for x in range(2)]
    return [(index_of(*place), index_of(*move(*place))) for place in places]


def along_cycle(step):
    def move(z, y, core, x):
        return (*CYCLE[(CYCLE.index((z, y)) + step) % CHIPS], core, x)

    return pairs_of(move)


SWAP_X = pairs_of(lambda z, y, c, x: (z, y, c, 1 - x))
SWAP_CORE = pairs_of(lambda z, y, c, x: (z, y, 1 - c, x))
SWAP_Y = pairs_of(lambda z, y, c, x: (z, 1 - y, c, x))
SWAP_Z0 = pairs_of(lambda z, y, c, x: (z ^ 1, y, c, x))
SWAP_Z1 = pairs_of(lambda z, y, c, x: (z ^ 2, y, c, x))
AHEAD = along_cycle(1)
BEHIND = along_cycle(-1)


def block_owners(rank):
    place = jnp.array([CYCLE.index((chip // 2, chip % 2)) for chip in range(CHIPS)], jnp.int32)
    chips = jnp.array([2 * z + y for z, y in CYCLE], jnp.int32)
    around = (place[rank // 2] + jnp.array(DISTANCES, jnp.int32)) % CHIPS
    core = rank % 2
    return jnp.concatenate([chips[around] * 2 + core, chips[around] * 2 + 1 - core])


def send(value, pairs):
    return lax.ppermute(value, AXES, pairs)


def gather_blocks(piece):
    half = piece.shape[0] // 2
    back1, front1 = send(piece, AHEAD), send(piece, BEHIND)
    back2, front2 = send(back1, AHEAD), send(front1, BEHIND)
    back3, front3 = send(back2, AHEAD), send(front2, BEHIND)
    back4, front4 = send(back3[:half], AHEAD), send(front3[half:], BEHIND)
    mine = [back4, front4, front3, back3, front2, back2, front1, back1, piece]
    other = [send(block, SWAP_CORE) for block in mine]
    return jnp.concatenate(mine + other, axis=0)


def add_low(left, right):
    return (left.astype(F32) + right.astype(F32)).astype(BF16)


def scatter_blocks(mine, other):
    rows = mine.shape[0] // CHIPS
    half = rows // 2
    cuts = (0, rows, 3 * rows, 5 * rows, 7 * rows, 8 * rows)
    parts = [
        add_low(mine[lo:hi], send(other[lo:hi], SWAP_CORE)) for lo, hi in zip(cuts[:-1], cuts[1:])
    ]
    back, front = send(parts[0][:half], AHEAD), send(parts[0][half:], BEHIND)
    to_front, to_back = parts[1][:rows], parts[1][rows:]
    back, front = (
        send(jnp.concatenate([add_low(to_front[:half], back), to_front[half:]]), AHEAD),
        send(jnp.concatenate([to_back[:half], add_low(to_back[half:], front)]), BEHIND),
    )
    for part in parts[2:4]:
        back, front = (
            send(add_low(part[:rows], back), AHEAD),
            send(add_low(part[rows:], front), BEHIND),
        )
    return parts[4].astype(F32) + back.astype(F32) + front.astype(F32)


def total_sum(value):
    for pairs in (SWAP_CORE, SWAP_X, SWAP_Y, SWAP_Z0, SWAP_Z1):
        value = value + send(value, pairs)
    return value


def head_sums():
    row = lax.broadcasted_iota(jnp.int32, (LANES, LANES), 0) // HEAD_DIM
    col = lax.broadcasted_iota(jnp.int32, (LANES, LANES), 1) // HEAD_DIM
    return jnp.where(row == col, 1.0 / HEAD_DIM, 0.0).astype(F32)


def head_mean(values):
    return jnp.dot(
        values, head_sums(), precision=lax.Precision.HIGHEST, preferred_element_type=F32
    )


def swap_halves(values):
    lane = lax.broadcasted_iota(jnp.int32, values.shape, 1)
    return jnp.where(
        lane % HEAD_DIM < HEAD_DIM // 2,
        pltpu.roll(values, LANES - HEAD_DIM // 2, 1),
        pltpu.roll(values, HEAD_DIM // 2, 1),
    )


def dot_lanes(left, right):
    return lax.dot_general(left, right, (((1,), (1,)), ((), ())), preferred_element_type=F32)


def allowed_of(length, pos_col_ref, pos_row_ref):
    col = pos_col_ref[...]
    return jnp.where(col < length, col, FAR) <= pos_row_ref[...]


def rows_of_ref(ref):
    value = ref[...]
    return value.reshape(-1, value.shape[-1])


def attend_kernel(
    length_ref, proj_ref, cos_ref, sin_ref, gain_ref, pos_col_ref, pos_row_ref,
    out_ref, lse_ref, rot_ref, val_ref, kept_ref,
):
    seq, step = pl.program_id(0), pl.program_id(1)
    block = lse_ref.shape[-1]

    @pl.when(step == 0)
    def _():
        proj = rows_of_ref(proj_ref)
        normed = proj * lax.rsqrt(head_mean(proj * proj) + EPS) * gain_ref[...]
        rotated = normed * cos_ref[...] + swap_halves(normed) * sin_ref[...]
        lane = lax.broadcasted_iota(jnp.int32, proj.shape, 1)
        rotated = jnp.where(lane < 2 * HEAD_DIM, rotated * HEAD_DIM**-0.5, rotated)
        kept = jnp.where(lane < 3 * HEAD_DIM, rotated, proj).astype(BF16)
        kept_ref[...] = kept
        rot_ref[...] = kept.reshape(rot_ref.shape)
        val_ref[:HEAD_DIM, :] = proj[:, 3 * HEAD_DIM :].T.astype(BF16)
        val_ref[HEAD_DIM:, :] = jnp.ones((16, proj.shape[0]), BF16)

    allowed = allowed_of(length_ref[seq], pos_col_ref, pos_row_ref)
    keys = kept_ref[:, 2 * HEAD_DIM : 3 * HEAD_DIM]
    query = kept_ref[pl.ds(pl.multiple_of(step * block, block), block), : 2 * HEAD_DIM]
    outs = []
    for head in range(2):
        scores = dot_lanes(keys, query[:, head * HEAD_DIM : (head + 1) * HEAD_DIM])
        weights = jnp.where(allowed, jnp.exp(scores), 0.0).astype(BF16)
        summed = jnp.dot(val_ref[...], weights, preferred_element_type=F32)
        total = summed[HEAD_DIM : HEAD_DIM + 1]
        outs.append((summed[:HEAD_DIM] / total).T)
        lse_ref[0, head : head + 1, :] = jnp.log(total)
    out_ref[...] = jnp.concatenate(outs, axis=1).astype(BF16).reshape(out_ref.shape)


def fixed(shape):
    return pl.BlockSpec(shape, lambda s, i: (0,) * len(shape))


def of_seq(blocks, width, lanes):
    return pl.BlockSpec((blocks, 1, width, lanes), lambda s, i: (0, s, 0, 0))


def of_step(blocks, width, lanes):
    return pl.BlockSpec((blocks, 1, width, lanes), lambda s, i: (i, s, 0, 0))


STEPS = 4


def attend(proj, cosine, sine, gain, positions, lengths):
    blocks, seqs, width, _ = proj.shape
    slots = blocks * width
    part = slots // STEPS
    return pl.pallas_call(
        attend_kernel,
        grid=(seqs, STEPS),
        in_specs=[
            pl.BlockSpec(memory_space=pltpu.SMEM),
            of_seq(blocks, width, LANES),
            fixed((slots, LANES)),
            fixed((slots, LANES)),
            fixed((1, LANES)),
            fixed((slots, 1)),
            pl.BlockSpec((1, part), lambda s, i: (0, i)),
        ],
        out_specs=[
            of_step(blocks // STEPS, width, 2 * HEAD_DIM),
            pl.BlockSpec((1, 2, part), lambda s, i: (s, 0, i)),
            of_seq(blocks, width, LANES),
        ],
        out_shape=[
            jax.ShapeDtypeStruct((blocks, seqs, width, 2 * HEAD_DIM), BF16),
            jax.ShapeDtypeStruct((seqs, 2, slots), F32),
            jax.ShapeDtypeStruct((blocks, seqs, width, LANES), BF16),
        ],
        scratch_shapes=[
            pltpu.VMEM((HEAD_DIM + 16, slots), BF16),
            pltpu.VMEM((slots, LANES), BF16),
        ],
        name="attend",
    )(lengths, proj, cosine, sine, gain, positions[:, None], positions[None, :])


def attend_back_kernel(
    length_ref, rot_ref, query_ref, grad_ref, out_ref, lse_ref, pos_col_ref, pos_row_ref,
    dq_ref, dkv_ref, sum_ref,
):
    seq, step = pl.program_id(0), pl.program_id(1)
    allowed = allowed_of(length_ref[seq], pos_col_ref, pos_row_ref)
    rotated = rows_of_ref(rot_ref)
    keys = rotated[:, 2 * HEAD_DIM : 3 * HEAD_DIM]
    values = rotated[:, 3 * HEAD_DIM :]
    query = rows_of_ref(query_ref)
    grad = rows_of_ref(grad_ref)
    product = grad.astype(F32) * rows_of_ref(out_ref).astype(F32)
    ones = jnp.ones((8, HEAD_DIM), F32)
    grad_q, grad_k, grad_v = [], 0.0, 0.0
    for head in range(2):
        cut = slice(head * HEAD_DIM, (head + 1) * HEAD_DIM)
        delta = lax.dot_general(
            ones,
            product[:, cut],
            (((1,), (1,)), ((), ())),
            precision=lax.Precision.HIGHEST,
            preferred_element_type=F32,
        )[:1]
        scores = dot_lanes(keys, query[:, cut])
        probs = jnp.where(allowed, jnp.exp(scores - lse_ref[0, head : head + 1, :]), 0.0)
        grad_probs = dot_lanes(values, grad[:, cut])
        grad_scores = (probs * (grad_probs - delta)).astype(BF16)
        grad_v += jnp.dot(probs.astype(BF16), grad[:, cut], preferred_element_type=F32)
        grad_k += jnp.dot(grad_scores, query[:, cut], preferred_element_type=F32)
        grad_q.append(
            lax.dot_general(
                grad_scores, keys, (((0,), (0,)), ((), ())), preferred_element_type=F32
            )
        )
    dq_ref[...] = (jnp.concatenate(grad_q, axis=1) * HEAD_DIM**-0.5).reshape(dq_ref.shape)
    both = jnp.concatenate([grad_k, grad_v], axis=1)

    @pl.when(step == 0)
    def _():
        sum_ref[...] = both

    @pl.when(step > 0)
    def _():
        sum_ref[...] += both

    @pl.when(step == STEPS - 1)
    def _():
        dkv_ref[...] = sum_ref[...].reshape(dkv_ref.shape)


def attend_back(rotated, grad, out, lse, positions, lengths):
    blocks, seqs, width, _ = rotated.shape
    slots = blocks * width
    part = slots // STEPS
    rows = of_step(blocks // STEPS, width, 2 * HEAD_DIM)
    return pl.pallas_call(
        attend_back_kernel,
        grid=(seqs, STEPS),
        in_specs=[
            pl.BlockSpec(memory_space=pltpu.SMEM),
            of_seq(blocks, width, LANES),
            rows,
            rows,
            rows,
            pl.BlockSpec((1, 2, part), lambda s, i: (s, 0, i)),
            fixed((slots, 1)),
            pl.BlockSpec((1, part), lambda s, i: (0, i)),
        ],
        out_specs=[rows, of_seq(blocks, width, 2 * HEAD_DIM)],
        out_shape=[
            jax.ShapeDtypeStruct((blocks, seqs, width, 2 * HEAD_DIM), F32),
            jax.ShapeDtypeStruct((blocks, seqs, width, 2 * HEAD_DIM), F32),
        ],
        scratch_shapes=[pltpu.VMEM((slots, 2 * HEAD_DIM), F32)],
        name="attend_back",
    )(lengths, rotated, rotated, grad, out, lse, positions[:, None], positions[None, :])


def project_back_kernel(
    dq_ref, dkv_ref, other_ref, proj_ref, cos_ref, sin_ref, gain_ref, grad_ref, sum_ref
):
    first = jnp.logical_and(pl.program_id(0) == 0, pl.program_id(1) == 0)
    grad = jnp.concatenate(
        [rows_of_ref(dq_ref), rows_of_ref(dkv_ref) + rows_of_ref(other_ref)], axis=1
    )
    proj = rows_of_ref(proj_ref)
    scale_rows = lax.rsqrt(head_mean(proj * proj) + EPS)
    normed = proj * scale_rows
    turned = grad * cos_ref[...] - swap_halves(grad) * sin_ref[...]
    gained = turned * gain_ref[...]
    back = scale_rows * (gained - normed * head_mean(gained * normed))
    lane = lax.broadcasted_iota(jnp.int32, proj.shape, 1)
    grad_ref[...] = jnp.where(lane < 3 * HEAD_DIM, back, grad).astype(BF16).reshape(grad_ref.shape)
    sums = jnp.sum((turned * normed).reshape(-1, 8, LANES), axis=0)

    @pl.when(first)
    def _():
        sum_ref[...] = sums

    @pl.when(jnp.logical_not(first))
    def _():
        sum_ref[...] += sums


def project_back(grad_q, grad_kv, other_kv, proj, cosine, sine, gain):
    blocks, seqs, width, _ = proj.shape
    some = blocks // STEPS
    half = of_step(some, width, 2 * HEAD_DIM)
    turned = pl.BlockSpec(
        (some, 1, width, 2 * HEAD_DIM), lambda s, i: ((i + STEPS // 2) % STEPS, s, 0, 0)
    )
    rows = of_step(some, width, LANES)
    table = pl.BlockSpec((some * width, LANES), lambda s, i: (i, 0))
    return pl.pallas_call(
        project_back_kernel,
        grid=(seqs, STEPS),
        in_specs=[half, half, turned, rows, table, table, fixed((1, LANES))],
        out_specs=[rows, fixed((8, LANES))],
        out_shape=[
            jax.ShapeDtypeStruct((blocks, seqs, width, LANES), BF16),
            jax.ShapeDtypeStruct((8, LANES), F32),
        ],
        name="project_back",
    )(grad_q, grad_kv, other_kv, proj, cosine, sine, gain)


def dot_rows(left, right):
    return lax.dot_general(left, right, (((0,), (0,)), ((), ())), preferred_element_type=F32)


def plain(left, right):
    return jnp.dot(left, right, preferred_element_type=F32)


def in_order(own, other, index):
    first = index == 0
    return jnp.concatenate([jnp.where(first, own, other), jnp.where(first, other, own)], axis=0)


def split_local(
    tokens, cotangent, q_weight, k_weight, v_weight, o_weight, gate_weight, up_weight,
    down_weight, attn_gain, ffn_gain, q_gain, k_gain, lengths, pair_order,
):
    seqs, width, _ = tokens.shape
    rank = lax.axis_index("ctx")
    side = lax.axis_index("fsdp")
    core = rank % 2
    mine = seqs * width
    q_rows, kv_rows, ff_rows = q_weight.shape[0], k_weight.shape[0], gate_weight.shape[0]

    x_rows = tokens.astype(F32).reshape(mine, D)
    scale_one = rms_scale(x_rows)
    normed_one = x_rows * scale_one
    x_norm = gather_blocks((normed_one * attn_gain).astype(BF16))

    kv_own = jnp.stack([k_weight, v_weight])
    kv_side = send(kv_own, SWAP_X)
    kv_half = jnp.concatenate(
        [jnp.where(side == 0, kv_own, kv_side), jnp.where(side == 0, kv_side, kv_own)], axis=1
    )
    kv_core = send(kv_half, SWAP_CORE)
    kv_full = jnp.concatenate(
        [jnp.where(core == 0, kv_half, kv_core), jnp.where(core == 0, kv_core, kv_half)], axis=1
    )
    w_attn = jnp.concatenate(
        [q_weight, send(q_weight, SWAP_X), kv_full[0], kv_full[1]], axis=0
    )
    w_out = jnp.concatenate([o_weight, send(o_weight, SWAP_X)], axis=0)
    gate_up = jnp.concatenate([gate_weight, up_weight], axis=0)
    w_gate_up = jnp.concatenate([gate_up, send(gate_up, SWAP_X)], axis=0)
    w_down = jnp.concatenate([down_weight, send(down_weight, SWAP_X)], axis=0)

    owners = block_owners(rank)
    blocks = owners.shape[0]
    within = jnp.arange(width, dtype=jnp.int32)
    half_blk = width // 2

    def positions_of(dealt):
        block_id = jnp.where(
            within[None, :] < half_blk, dealt[:, None], 2 * pair_order.shape[0] - 1 - dealt[:, None]
        )
        return (block_id * half_blk + within[None, :] % half_blk).reshape(-1)

    positions = positions_of(pair_order[owners])
    slots = positions.shape[0]
    cosine, sine = rope_tables(positions)
    plain_lanes = jnp.ones((slots, HEAD_DIM), F32)
    cosine = jnp.concatenate([cosine] * 6 + [plain_lanes], axis=1)
    sine = jnp.concatenate([-sine, sine] * 3 + [plain_lanes * 0.0], axis=1)
    gain_lanes = jnp.concatenate([q_gain, q_gain, k_gain, jnp.ones((HEAD_DIM,), F32)])[None, :]
    my_pos = positions_of(pair_order[rank][None])
    live = (my_pos[None, :] < lengths[:, None]).reshape(mine, 1)

    grad_out = jnp.where(live, cotangent.astype(F32).reshape(mine, D), 0.0)
    grad_low = gather_blocks(grad_out.astype(BF16))

    proj = project(x_norm, w_attn).reshape(blocks, seqs, width, LANES)
    out, lse, rotated = attend(proj, cosine, sine, gain_lanes, positions, lengths)
    out_rows = out.reshape(blocks * mine, 2 * HEAD_DIM)

    def partial_sums(rows, weight):
        cut = rows.shape[0] // 2
        other = plain(rows[cut:], weight).astype(BF16)
        own = plain(rows[:cut], weight).astype(BF16)
        return scatter_blocks(own, other)

    resid = x_rows + partial_sums(out_rows, w_out)
    scale_two = rms_scale(resid)
    normed_two = resid * scale_two
    x_norm2 = gather_blocks((normed_two * ffn_gain).astype(BF16))

    both = project(x_norm2, w_gate_up)
    gate_part = jnp.concatenate([both[:, :ff_rows], both[:, 2 * ff_rows : 3 * ff_rows]], axis=1)
    up_part = jnp.concatenate([both[:, ff_rows : 2 * ff_rows], both[:, 3 * ff_rows :]], axis=1)
    hidden = (jax.nn.silu(gate_part) * up_part).astype(BF16)
    gate_low, up_low = gate_grads(project(grad_low, w_down), gate_part, up_part)
    gate_up_low = jnp.concatenate(
        [gate_low[:, :ff_rows], up_low[:, :ff_rows], gate_low[:, ff_rows:], up_low[:, ff_rows:]],
        axis=1,
    )
    grad_norm2 = partial_sums(gate_up_low, w_gate_up)
    out_sum = partial_sums(hidden, w_down)
    block_out = (
        jnp.where(live, resid + out_sum, 0.0).astype(BF16).reshape(seqs, width, D)
    )
    grad_ffn_gain = jnp.sum(grad_norm2 * normed_two, axis=0)
    grad_resid = grad_out + rms_back(grad_norm2 * ffn_gain, normed_two, scale_two)
    grad_attn_low = gather_blocks(grad_resid.astype(BF16))

    def both_sides(full):
        own = full.shape[0] // 2
        return full[:own] + send(full[own:].astype(BF16), SWAP_X).astype(F32)

    gate_up_grad = both_sides(dot_rows(gate_up_low, x_norm2))
    down_grad = both_sides(dot_rows(hidden, grad_low))

    grad_o = project(grad_attn_low, w_out).astype(BF16).reshape(out.shape)
    grad_q, grad_kv = attend_back(rotated, grad_o, out, lse, positions, lengths)
    grad_rows, gain_sums = project_back(
        grad_q, grad_kv, send(grad_kv, SWAP_CORE), proj, cosine, sine, gain_lanes
    )
    grad_rows = grad_rows.reshape(blocks * mine, LANES)
    gain_sums = jnp.sum(gain_sums, axis=0)
    row = jnp.arange(LANES)[:, None] // HEAD_DIM
    w_once = jnp.where((row < 2) | (row == 2 + core), w_attn, 0).astype(BF16)
    grad_norm1 = partial_sums(grad_rows, w_once)
    o_grad = both_sides(dot_rows(out_rows, grad_attn_low))
    attn_full = dot_rows(grad_rows, x_norm)
    kv_grads = attn_full[2 * q_rows :].reshape(2, 2, 2, kv_rows, D)
    kv_mine = jnp.where(core == 0, kv_grads[:, 0], kv_grads[:, 1])
    kv_stay = jnp.where(side == 0, kv_mine[:, 0], kv_mine[:, 1])
    kv_leave = jnp.where(side == 0, kv_mine[:, 1], kv_mine[:, 0])
    attn_grads = both_sides(
        jnp.concatenate(
            [
                attn_full[:q_rows],
                kv_stay.reshape(2 * kv_rows, D),
                attn_full[q_rows : 2 * q_rows],
                kv_leave.reshape(2 * kv_rows, D),
            ],
            axis=0,
        )
    )
    grad_tokens = (grad_resid + rms_back(grad_norm1 * attn_gain, normed_one, scale_one)).reshape(
        seqs, width, D
    )
    owned = jnp.concatenate([q_weight, k_weight, v_weight], axis=0).astype(F32)
    grad_attn_gain = jnp.sum(owned * attn_grads, axis=0) / attn_gain
    gains = total_sum(
        jnp.concatenate(
            [
                grad_attn_gain,
                grad_ffn_gain,
                gain_sums[:HEAD_DIM] + gain_sums[HEAD_DIM : 2 * HEAD_DIM],
                0.5 * gain_sums[2 * HEAD_DIM : 3 * HEAD_DIM],
            ]
        )
    )
    return (
        block_out,
        grad_tokens,
        attn_grads[:q_rows],
        attn_grads[q_rows : q_rows + kv_rows],
        attn_grads[q_rows + kv_rows :],
        o_grad,
        gate_up_grad[:ff_rows],
        gate_up_grad[ff_rows:],
        down_grad,
        gains[:D],
        gains[D : 2 * D],
        gains[2 * D : 2 * D + HEAD_DIM],
        gains[2 * D + HEAD_DIM :],
    )


def solution(mesh):
    body = split_local if fits_split(mesh) else local
    in_specs = (
        P("fsdp", "ctx", None),
        P("fsdp", "ctx", None),
        P(("ctx", "fsdp"), None),
        P(("ctx", "fsdp"), None),
        P(("ctx", "fsdp"), None),
        P(("ctx", "fsdp"), None),
        P(("ctx", "fsdp"), None),
        P(("ctx", "fsdp"), None),
        P(("ctx", "fsdp"), None),
        P(),
        P(),
        P(),
        P(),
        P("fsdp"),
        P(),
    )
    out_specs = (
        P("fsdp", "ctx", None),
        P("fsdp", "ctx", None),
        P(("ctx", "fsdp"), None),
        P(("ctx", "fsdp"), None),
        P(("ctx", "fsdp"), None),
        P(("ctx", "fsdp"), None),
        P(("ctx", "fsdp"), None),
        P(("ctx", "fsdp"), None),
        P(("ctx", "fsdp"), None),
        P(),
        P(),
        P(),
        P(),
    )
    return jax.shard_map(body, mesh=mesh, in_specs=in_specs, out_specs=out_specs, check_vma=False)
```

```python
import math

import jax
import jax.numpy as jnp
from jax import lax
from jax.experimental import pallas as pl
from jax.experimental.pallas import tpu as pltpu
from jax.sharding import PartitionSpec as P

D = 2048
HEADS = 32
KV_HEADS = 8
HEAD_DIM = 64
FF = 8192


EPS = 1e-05
THETA = 1000000.0
NEG = -1e30


def rms_scale(values):
    return lax.rsqrt(jnp.mean(values * values, axis=-1, keepdims=True) + EPS)


def rms_back(grad_normed, normed, scale_rows):
    return scale_rows * (
        grad_normed - normed * jnp.mean(grad_normed * normed, axis=-1, keepdims=True)
    )


def rope_tables(positions):
    half = HEAD_DIM // 2
    freq = THETA ** (-(jnp.arange(half, dtype=jnp.float32) * 2.0 / HEAD_DIM))
    angle = positions.astype(jnp.float32)[:, None] * freq[None, :]
    return (jnp.cos(angle), jnp.sin(angle))


def rotate(values, cosine, sine):
    half = values.shape[-1] // 2
    first = values[..., :half]
    second = values[..., half:]
    return jnp.concatenate(
        [first * cosine - second * sine, second * cosine + first * sine], axis=-1
    )


def slot_positions(pair_order, width_pair, first, count):
    slot = first + jnp.arange(count, dtype=jnp.int32)
    owner = slot // width_pair
    within = slot % width_pair
    half_blk = width_pair // 2
    pair = pair_order[owner]
    block_id = jnp.where(within < half_blk, pair, 2 * pair_order.shape[0] - 1 - pair)
    return block_id * half_blk + within % half_blk


def block_mask(query_pos, key_part, lengths):
    return (key_part[None, None, :] <= query_pos[None, :, None]) & (
        key_part[None, None, :] < lengths[:, None, None]
    )


def project(inputs, weight):
    return jnp.einsum("td,fd->tf", inputs, weight, preferred_element_type=jnp.float32)


def gate_grads(grad_hidden, gate_part, up_part):
    sigma = jax.nn.sigmoid(gate_part)
    grad_gate = grad_hidden * up_part * sigma * (1.0 + gate_part * (1.0 - sigma))
    grad_up = grad_hidden * gate_part * sigma
    return (grad_gate.astype(jnp.bfloat16), grad_up.astype(jnp.bfloat16))


def block_grads(q_rot, grad_o_low, lse, delta, k_blk, v_blk, allowed, scale):
    scores = (
        jnp.einsum("sqhgd,sjhd->sqhgj", q_rot, k_blk, preferred_element_type=jnp.float32) * scale
    )
    scores = jnp.where(allowed[:, :, None, None, :], scores, NEG)
    probs = jnp.exp(scores - lse[..., None])
    grad_probs = jnp.einsum(
        "sqhgd,sjhd->sqhgj", grad_o_low, v_blk, preferred_element_type=jnp.float32
    )
    grad_scores = (probs * (grad_probs - delta[..., None])).astype(jnp.bfloat16)
    return (probs, grad_scores)


def local(
    tokens,
    cotangent,
    q_weight,
    k_weight,
    v_weight,
    o_weight,
    gate_weight,
    up_weight,
    down_weight,
    attn_gain,
    ffn_gain,
    q_gain,
    k_gain,
    lengths,
    pair_order,
):
    seq_grp = tokens.shape[0]
    width_pair = tokens.shape[1]
    groups = HEADS // KV_HEADS
    q_width = HEADS * HEAD_DIM
    kv_width = KV_HEADS * HEAD_DIM
    scale = HEAD_DIM ** (-0.5)
    tok_rows = seq_grp * width_pair
    slots = width_pair * pair_order.shape[0]
    key_blk = math.gcd(slots, 512)
    key_count = slots // key_blk
    dev_count = lax.axis_size("ctx") * lax.axis_size("fsdp")
    local_pos = slot_positions(
        pair_order, width_pair, lax.axis_index("ctx") * width_pair, width_pair
    )
    key_pos = slot_positions(pair_order, width_pair, 0, slots)
    live_rows = (local_pos[None, :] < lengths[:, None]).reshape(tok_rows, 1)
    cosine, sine = rope_tables(local_pos)
    cosine = cosine[None, :, None, :]
    sine = sine[None, :, None, :]
    x_rows = tokens.astype(jnp.float32).reshape(tok_rows, D)
    scale_one = rms_scale(x_rows)
    normed_one = x_rows * scale_one
    x_norm = (normed_one * attn_gain).astype(jnp.bfloat16)
    w_query, w_key, w_value, w_out = (
        lax.all_gather(q_weight, ("ctx", "fsdp"), axis=0, tiled=True),
        lax.all_gather(k_weight, ("ctx", "fsdp"), axis=0, tiled=True),
        lax.all_gather(v_weight, ("ctx", "fsdp"), axis=0, tiled=True),
        lax.all_gather(o_weight, ("ctx", "fsdp"), axis=0, tiled=True),
    )
    q_proj = project(x_norm, w_query).reshape(seq_grp, width_pair, HEADS, HEAD_DIM)
    k_proj = project(x_norm, w_key).reshape(seq_grp, width_pair, KV_HEADS, HEAD_DIM)
    v_low = project(x_norm, w_value).astype(jnp.bfloat16).reshape(seq_grp, width_pair, kv_width)
    q_scale = rms_scale(q_proj)
    q_normed = q_proj * q_scale
    q_rot = (
        rotate(q_normed * q_gain, cosine, sine)
        .astype(jnp.bfloat16)
        .reshape(seq_grp, width_pair, KV_HEADS, groups, HEAD_DIM)
    )
    k_scale = rms_scale(k_proj)
    k_normed = k_proj * k_scale
    k_rot = (
        rotate(k_normed * k_gain, cosine, sine)
        .astype(jnp.bfloat16)
        .reshape(seq_grp, width_pair, kv_width)
    )
    k_all, v_all = (
        lax.all_gather(k_rot, "ctx", axis=1, tiled=True),
        lax.all_gather(v_low, "ctx", axis=1, tiled=True),
    )
    k_all = k_all.reshape(seq_grp, slots, KV_HEADS, HEAD_DIM)
    v_all = v_all.reshape(seq_grp, slots, KV_HEADS, HEAD_DIM)

    def key_slices(first, count):
        k_blk = lax.dynamic_slice_in_dim(k_all, first, count, 1)
        v_blk = lax.dynamic_slice_in_dim(v_all, first, count, 1)
        allowed = block_mask(local_pos, lax.dynamic_slice_in_dim(key_pos, first, count, 0), lengths)
        return (k_blk, v_blk, allowed)

    def forward_step(index, carry):
        top, total, summed = carry
        k_blk, v_blk, allowed = key_slices(index * key_blk, key_blk)
        scores = (
            jnp.einsum("sqhgd,sjhd->sqhgj", q_rot, k_blk, preferred_element_type=jnp.float32)
            * scale
        )
        scores = jnp.where(allowed[:, :, None, None, :], scores, NEG)
        new_top = jnp.maximum(top, jnp.max(scores, axis=-1))
        shrink = jnp.exp(top - new_top)
        probs = jnp.exp(scores - new_top[..., None])
        total = total * shrink + jnp.sum(probs, axis=-1)
        summed = summed * shrink[..., None] + jnp.einsum(
            "sqhgj,sjhd->sqhgd",
            probs.astype(jnp.bfloat16),
            v_blk,
            preferred_element_type=jnp.float32,
        )
        return (new_top, total, summed)

    stat_shape = (seq_grp, width_pair, KV_HEADS, groups)
    start_carry = (
        jnp.full(stat_shape, NEG, jnp.float32),
        jnp.zeros(stat_shape, jnp.float32),
        jnp.zeros(stat_shape + (HEAD_DIM,), jnp.float32),
    )
    top, total, summed = lax.fori_loop(0, key_count, forward_step, start_carry)
    lse = top + jnp.log(total)
    o_low = (summed / total[..., None]).astype(jnp.bfloat16)
    o_rows = o_low.reshape(tok_rows, q_width)
    resid = x_rows + jnp.einsum("tf,fd->td", o_rows, w_out, preferred_element_type=jnp.float32)
    scale_two = rms_scale(resid)
    normed_two = resid * scale_two
    x_norm2 = (normed_two * ffn_gain).astype(jnp.bfloat16)
    grad_out = jnp.where(live_rows, cotangent.astype(jnp.float32).reshape(tok_rows, D), 0.0)
    grad_low = grad_out.astype(jnp.bfloat16)
    pieces = (
        lax.all_gather(gate_weight, ("ctx", "fsdp"), axis=0, tiled=True),
        lax.all_gather(up_weight, ("ctx", "fsdp"), axis=0, tiled=True),
        lax.all_gather(down_weight, ("ctx", "fsdp"), axis=0, tiled=True),
    )
    gate_part = project(x_norm2, pieces[0])
    up_part = project(x_norm2, pieces[1])
    hidden_part = (jax.nn.silu(gate_part) * up_part).astype(jnp.bfloat16)
    out_sum = jnp.einsum("tf,fd->td", hidden_part, pieces[2], preferred_element_type=jnp.float32)
    gate_all = gate_part
    up_all = up_part
    hidden = (jax.nn.silu(gate_all) * up_all).astype(jnp.bfloat16)
    pieces = (
        lax.all_gather(gate_weight, ("ctx", "fsdp"), axis=0, tiled=True),
        lax.all_gather(up_weight, ("ctx", "fsdp"), axis=0, tiled=True),
        lax.all_gather(down_weight, ("ctx", "fsdp"), axis=0, tiled=True),
    )
    count = pieces[0].shape[0]
    gate_part = gate_all
    up_part = up_all
    grad_gate_part, grad_up_part = gate_grads(project(grad_low, pieces[2]), gate_part, up_part)
    grad_sum = jnp.einsum(
        "tf,fd->td", grad_gate_part, pieces[0], preferred_element_type=jnp.float32
    ) + jnp.einsum("tf,fd->td", grad_up_part, pieces[1], preferred_element_type=jnp.float32)
    gate_grad_all = grad_gate_part
    up_grad_all = grad_up_part
    block_out = (
        jnp.where(live_rows, resid + out_sum, 0.0)
        .astype(jnp.bfloat16)
        .reshape(seq_grp, width_pair, D)
    )
    ffn_dev = FF // dev_count
    owners = lax.axis_size(("ctx", "fsdp")) * (3 * ffn_dev) // (3 * ffn_dev)
    first = jnp.int32(0) // (3 * ffn_dev) * ffn_dev
    grad_gate_part = jnp.einsum(
        "tf,td->fd", gate_grad_all, x_norm2, preferred_element_type=jnp.float32
    )
    grad_up_part = jnp.einsum("tf,td->fd", up_grad_all, x_norm2, preferred_element_type=jnp.float32)
    grad_down_part = jnp.einsum("tf,td->fd", hidden, grad_low, preferred_element_type=jnp.float32)
    stacked = jnp.stack(
        [
            grad_gate_part.reshape(owners, ffn_dev, D),
            grad_up_part.reshape(owners, ffn_dev, D),
            grad_down_part.reshape(owners, ffn_dev, D),
        ],
        axis=1,
    )
    ffn_grads = lax.psum_scatter(
        stacked.reshape(lax.axis_size(("ctx", "fsdp")) * (3 * ffn_dev), D),
        ("ctx", "fsdp"),
        scatter_dimension=0,
        tiled=True,
    )
    grad_ffn_gain = jnp.sum(grad_sum * normed_two, axis=0)
    grad_resid = grad_out + rms_back(grad_sum * ffn_gain, normed_two, scale_two)
    grad_attn_low = grad_resid.astype(jnp.bfloat16)
    grad_o_low = (
        project(grad_attn_low, w_out)
        .astype(jnp.bfloat16)
        .reshape(seq_grp, width_pair, KV_HEADS, groups, HEAD_DIM)
    )
    delta = jnp.sum(grad_o_low.astype(jnp.float32) * o_low.astype(jnp.float32), axis=-1)
    dq_zero = jnp.zeros((seq_grp, width_pair, KV_HEADS, groups, HEAD_DIM), jnp.float32)
    kv_cols = seq_grp * 2 * kv_width

    def key_value_grads(probs, grad_scores):
        grad_k_blk = (
            jnp.einsum("sqhgj,sqhgd->jshd", grad_scores, q_rot, preferred_element_type=jnp.float32)
            * scale
        )
        grad_v_blk = jnp.einsum(
            "sqhgj,sqhgd->jshd",
            probs.astype(jnp.bfloat16),
            grad_o_low,
            preferred_element_type=jnp.float32,
        )
        return jnp.stack([grad_k_blk, grad_v_blk], axis=2).reshape(probs.shape[-1], kv_cols)

    def both_step(grad_q, index):
        k_blk, v_blk, allowed = key_slices(index * key_blk, key_blk)
        probs, grad_scores = block_grads(
            q_rot, grad_o_low, lse, delta, k_blk, v_blk, allowed, scale
        )
        grad_q = (
            grad_q
            + jnp.einsum(
                "sqhgj,sjhd->sqhgd", grad_scores, k_blk, preferred_element_type=jnp.float32
            )
            * scale
        )
        return (grad_q, key_value_grads(probs, grad_scores))

    grad_q_rot, kv_blocks = lax.scan(both_step, dq_zero, jnp.arange(key_count))
    kv_grad = lax.psum_scatter(
        kv_blocks.reshape(slots, kv_cols), "ctx", scatter_dimension=0, tiled=True
    )
    kv_grad = jnp.transpose(
        kv_grad.reshape(width_pair, seq_grp, 2, KV_HEADS, HEAD_DIM), (1, 0, 2, 3, 4)
    )
    grad_q_pre = rotate(grad_q_rot.reshape(seq_grp, width_pair, HEADS, HEAD_DIM), cosine, -sine)
    grad_k_pre = rotate(kv_grad[:, :, 0], cosine, -sine)
    grad_q_gain = jnp.sum(grad_q_pre * q_normed, axis=(0, 1, 2))
    grad_k_gain = jnp.sum(grad_k_pre * k_normed, axis=(0, 1, 2))
    grad_q_proj = (
        rms_back(grad_q_pre * q_gain, q_normed, q_scale)
        .reshape(tok_rows, q_width)
        .astype(jnp.bfloat16)
    )
    grad_k_proj = (
        rms_back(grad_k_pre * k_gain, k_normed, k_scale)
        .reshape(tok_rows, kv_width)
        .astype(jnp.bfloat16)
    )
    grad_v_proj = kv_grad[:, :, 1].reshape(tok_rows, kv_width).astype(jnp.bfloat16)
    grad_norm1 = jnp.einsum("tf,fd->td", grad_q_proj, w_query, preferred_element_type=jnp.float32)
    grad_norm1 = grad_norm1 + jnp.einsum(
        "tf,fd->td", grad_k_proj, w_key, preferred_element_type=jnp.float32
    )
    grad_norm1 = grad_norm1 + jnp.einsum(
        "tf,fd->td", grad_v_proj, w_value, preferred_element_type=jnp.float32
    )
    grad_attn_gain = jnp.sum(grad_norm1 * normed_one, axis=0)
    grad_tokens = (grad_resid + rms_back(grad_norm1 * attn_gain, normed_one, scale_one)).reshape(
        seq_grp, width_pair, D
    )
    q_dev = q_width // dev_count
    kv_dev = kv_width // dev_count
    per_dev = 2 * q_dev + 2 * kv_dev
    owners = lax.axis_size(("ctx", "fsdp")) * per_dev // per_dev

    def rows_of(grad_rows, inputs, each):
        return jnp.einsum(
            "tf,td->fd", grad_rows, inputs, preferred_element_type=jnp.float32
        ).reshape(owners, each, D)

    joined = jnp.concatenate(
        [
            rows_of(grad_q_proj, x_norm, q_dev),
            rows_of(grad_k_proj, x_norm, kv_dev),
            rows_of(grad_v_proj, x_norm, kv_dev),
            rows_of(o_rows, grad_attn_low, q_dev),
        ],
        axis=1,
    )
    attn_grads = lax.psum_scatter(
        joined.reshape(lax.axis_size(("ctx", "fsdp")) * per_dev, D),
        ("ctx", "fsdp"),
        scatter_dimension=0,
        tiled=True,
    )
    grad_attn_gain, grad_ffn_gain, grad_q_gain, grad_k_gain = lax.psum(
        (grad_attn_gain, grad_ffn_gain, grad_q_gain, grad_k_gain), ("ctx", "fsdp")
    )
    return (
        block_out,
        grad_tokens,
        attn_grads[:q_dev],
        attn_grads[q_dev : q_dev + kv_dev],
        attn_grads[q_dev + kv_dev : q_dev + 2 * kv_dev],
        attn_grads[q_dev + 2 * kv_dev :],
        ffn_grads[:ffn_dev],
        ffn_grads[ffn_dev : 2 * ffn_dev],
        ffn_grads[2 * ffn_dev :],
        grad_attn_gain,
        grad_ffn_gain,
        grad_q_gain,
        grad_k_gain,
    )


AXES = ("ctx", "fsdp")
RANKS = 16
LANES = 4 * HEAD_DIM
BF16 = jnp.bfloat16
F32 = jnp.float32
FAR = 1 << 30


def fits_split(mesh):
    return mesh.shape["ctx"] == RANKS and mesh.shape["fsdp"] == 2


CYCLE = ((0, 0), (1, 0), (2, 0), (3, 0), (3, 1), (2, 1), (1, 1), (0, 1))
CHIPS = len(CYCLE)
DISTANCES = (4, 3, -3, 2, -2, 1, -1, 0)


def index_of(z, y, core, x):
    return z * 8 + y * 4 + core * 2 + x


def pairs_of(move):
    places = [(z, y, c, x) for z in range(4) for y in range(2) for c in range(2) for x in range(2)]
    return [(index_of(*place), index_of(*move(*place))) for place in places]


def along_cycle(step):
    def move(z, y, core, x):
        return (*CYCLE[(CYCLE.index((z, y)) + step) % CHIPS], core, x)

    return pairs_of(move)


SWAP_X = pairs_of(lambda z, y, c, x: (z, y, c, 1 - x))
SWAP_CORE = pairs_of(lambda z, y, c, x: (z, y, 1 - c, x))
SWAP_Y = pairs_of(lambda z, y, c, x: (z, 1 - y, c, x))
SWAP_Z0 = pairs_of(lambda z, y, c, x: (z ^ 1, y, c, x))
SWAP_Z1 = pairs_of(lambda z, y, c, x: (z ^ 2, y, c, x))
AHEAD = along_cycle(1)
BEHIND = along_cycle(-1)


def block_owners(rank):
    place = jnp.array([CYCLE.index((chip // 2, chip % 2)) for chip in range(CHIPS)], jnp.int32)
    chips = jnp.array([2 * z + y for z, y in CYCLE], jnp.int32)
    around = (place[rank // 2] + jnp.array(DISTANCES, jnp.int32)) % CHIPS
    core = rank % 2
    return jnp.concatenate([chips[around] * 2 + core, chips[around] * 2 + 1 - core])


def send(value, pairs):
    return lax.ppermute(value, AXES, pairs)


def gather_blocks(piece):
    half = piece.shape[0] // 2
    back1, front1 = send(piece, AHEAD), send(piece, BEHIND)
    back2, front2 = send(back1, AHEAD), send(front1, BEHIND)
    back3, front3 = send(back2, AHEAD), send(front2, BEHIND)
    back4, front4 = send(back3[:half], AHEAD), send(front3[half:], BEHIND)
    mine = [back4, front4, front3, back3, front2, back2, front1, back1, piece]
    other = [send(block, SWAP_CORE) for block in mine]
    return jnp.concatenate(mine + other, axis=0)


def add_low(left, right):
    return (left.astype(F32) + right.astype(F32)).astype(BF16)


def scatter_blocks(mine, other):
    rows = mine.shape[0] // CHIPS
    half = rows // 2
    cuts = (0, rows, 3 * rows, 5 * rows, 7 * rows, 8 * rows)
    parts = [
        add_low(mine[lo:hi], send(other[lo:hi], SWAP_CORE)) for lo, hi in zip(cuts[:-1], cuts[1:])
    ]
    back, front = send(parts[0][:half], AHEAD), send(parts[0][half:], BEHIND)
    to_front, to_back = parts[1][:rows], parts[1][rows:]
    back, front = (
        send(jnp.concatenate([add_low(to_front[:half], back), to_front[half:]]), AHEAD),
        send(jnp.concatenate([to_back[:half], add_low(to_back[half:], front)]), BEHIND),
    )
    for part in parts[2:4]:
        back, front = (
            send(add_low(part[:rows], back), AHEAD),
            send(add_low(part[rows:], front), BEHIND),
        )
    return parts[4].astype(F32) + back.astype(F32) + front.astype(F32)


def total_sum(value):
    for pairs in (SWAP_CORE, SWAP_X, SWAP_Y, SWAP_Z0, SWAP_Z1):
        value = value + send(value, pairs)
    return value


def head_sums():
    row = lax.broadcasted_iota(jnp.int32, (LANES, LANES), 0) // HEAD_DIM
    col = lax.broadcasted_iota(jnp.int32, (LANES, LANES), 1) // HEAD_DIM
    return jnp.where(row == col, 1.0 / HEAD_DIM, 0.0).astype(BF16)


def head_mean(values):
    high = values.astype(BF16)
    rest = (values - high.astype(F32)).astype(BF16)
    sums = head_sums()
    return plain(high, sums) + plain(rest, sums)


def swap_halves(values):
    lane = lax.broadcasted_iota(jnp.int32, values.shape, 1)
    return jnp.where(
        lane % HEAD_DIM < HEAD_DIM // 2,
        pltpu.roll(values, LANES - HEAD_DIM // 2, 1),
        pltpu.roll(values, HEAD_DIM // 2, 1),
    )


def dot_lanes(left, right):
    return lax.dot_general(left, right, (((1,), (1,)), ((), ())), preferred_element_type=F32)


def allowed_of(length, pos_col_ref, pos_row_ref):
    col = pos_col_ref[...]
    return jnp.where(col < length, col, FAR) <= pos_row_ref[...]


def rows_of_ref(ref):
    value = ref[...]
    return value.reshape(-1, value.shape[-1])


def attend_kernel(
    length_ref, proj_ref, cos_ref, sin_ref, gain_ref, pos_col_ref, pos_row_ref,
    out_ref, lse_ref, rot_ref, val_ref,
):
    step = pl.program_id(0)
    block = lse_ref.shape[-1]

    @pl.when(step == 0)
    def _():
        proj = rows_of_ref(proj_ref)
        normed = proj * lax.rsqrt(head_mean(proj * proj) + EPS) * gain_ref[...]
        rotated = normed * cos_ref[...] + swap_halves(normed) * sin_ref[...]
        lane = lax.broadcasted_iota(jnp.int32, proj.shape, 1)
        rotated = jnp.where(lane < 2 * HEAD_DIM, rotated * HEAD_DIM**-0.5, rotated)
        rot_ref[...] = jnp.where(lane < 3 * HEAD_DIM, rotated, proj).astype(BF16)
        val_ref[:HEAD_DIM, :] = proj[:, 3 * HEAD_DIM :].T.astype(BF16)
        val_ref[HEAD_DIM:, :] = jnp.ones((16, proj.shape[0]), BF16)

    allowed = allowed_of(length_ref[0], pos_col_ref, pos_row_ref)
    keys = rot_ref[:, 2 * HEAD_DIM : 3 * HEAD_DIM]
    query = rot_ref[pl.ds(pl.multiple_of(step * block, block), block), : 2 * HEAD_DIM]
    outs = []
    for head in range(2):
        scores = dot_lanes(keys, query[:, head * HEAD_DIM : (head + 1) * HEAD_DIM])
        weights = jnp.where(allowed, jnp.exp(scores), 0.0).astype(BF16)
        summed = jnp.dot(val_ref[...], weights, preferred_element_type=F32)
        total = summed[HEAD_DIM : HEAD_DIM + 1]
        outs.append((summed[:HEAD_DIM] / total).T)
        lse_ref[head : head + 1, :] = jnp.log(total)
    out_ref[...] = jnp.concatenate(outs, axis=1).astype(BF16).reshape(out_ref.shape)


def fixed(shape):
    return pl.BlockSpec(shape, lambda i: (0,) * len(shape))


def of_seq(seq, blocks, width, lanes):
    return pl.BlockSpec((blocks, 1, width, lanes), lambda i: (0, seq, 0, 0))


def part_of_seq(seq, blocks, width, lanes):
    return pl.BlockSpec((blocks, 1, width, lanes), lambda i: (i, seq, 0, 0))


def cost_of(microseconds):
    return pl.CostEstimate(
        flops=int(microseconds * 6e8), transcendentals=0, bytes_accessed=int(microseconds * 2.5e6)
    )


STEPS = 4


def attend(seq, proj, cosine, sine, gain, positions, lengths):
    blocks, _, width, _ = proj.shape
    slots = blocks * width
    part = slots // STEPS
    return pl.pallas_call(
        attend_kernel,
        grid=(STEPS,),
        in_specs=[
            pl.BlockSpec(memory_space=pltpu.SMEM),
            of_seq(seq, blocks, width, LANES),
            fixed((slots, LANES)),
            fixed((slots, LANES)),
            fixed((1, LANES)),
            fixed((slots, 1)),
            pl.BlockSpec((1, part), lambda i: (0, i)),
        ],
        out_specs=[
            part_of_seq(0, blocks // STEPS, width, 2 * HEAD_DIM),
            pl.BlockSpec((2, part), lambda i: (0, i)),
            fixed((slots, LANES)),
        ],
        out_shape=[
            jax.ShapeDtypeStruct((blocks, 1, width, 2 * HEAD_DIM), BF16),
            jax.ShapeDtypeStruct((2, slots), F32),
            jax.ShapeDtypeStruct((slots, LANES), BF16),
        ],
        scratch_shapes=[pltpu.VMEM((HEAD_DIM + 16, slots), BF16)],
        cost_estimate=cost_of(8),
        name="attend",
    )(lengths[seq : seq + 1], proj, cosine, sine, gain, positions[:, None], positions[None, :])


def attend_back_kernel(
    length_ref, rot_ref, query_ref, grad_ref, out_ref, lse_ref, pos_col_ref, pos_row_ref,
    dq_ref, dkv_ref,
):
    step = pl.program_id(0)
    allowed = allowed_of(length_ref[0], pos_col_ref, pos_row_ref)
    keys = rot_ref[:, 2 * HEAD_DIM : 3 * HEAD_DIM]
    values = rot_ref[:, 3 * HEAD_DIM :]
    query = query_ref[:, : 2 * HEAD_DIM]
    grad = rows_of_ref(grad_ref)
    product = grad.astype(F32) * rows_of_ref(out_ref).astype(F32)
    ones = jnp.ones((8, HEAD_DIM), F32)
    grad_q, grad_k, grad_v = [], 0.0, 0.0
    for head in range(2):
        cut = slice(head * HEAD_DIM, (head + 1) * HEAD_DIM)
        delta = lax.dot_general(
            ones,
            product[:, cut],
            (((1,), (1,)), ((), ())),
            precision=lax.Precision.HIGHEST,
            preferred_element_type=F32,
        )[:1]
        scores = dot_lanes(keys, query[:, cut])
        probs = jnp.where(allowed, jnp.exp(scores - lse_ref[head : head + 1, :]), 0.0)
        grad_probs = dot_lanes(values, grad[:, cut])
        grad_scores = (probs * (grad_probs - delta)).astype(BF16)
        grad_v += jnp.dot(probs.astype(BF16), grad[:, cut], preferred_element_type=F32)
        grad_k += jnp.dot(grad_scores, query[:, cut], preferred_element_type=F32)
        grad_q.append(
            lax.dot_general(
                grad_scores, keys, (((0,), (0,)), ((), ())), preferred_element_type=F32
            )
        )
    dq_ref[...] = jnp.concatenate(grad_q, axis=1) * HEAD_DIM**-0.5
    both = jnp.concatenate([grad_k, grad_v], axis=1)

    @pl.when(step == 0)
    def _():
        dkv_ref[...] = both

    @pl.when(step > 0)
    def _():
        dkv_ref[...] += both


def attend_back(seq, rotated, grad, out, lse, positions, lengths):
    blocks, _, width, _ = grad.shape
    slots = blocks * width
    part = slots // STEPS
    return pl.pallas_call(
        attend_back_kernel,
        grid=(STEPS,),
        in_specs=[
            pl.BlockSpec(memory_space=pltpu.SMEM),
            fixed((slots, LANES)),
            pl.BlockSpec((part, LANES), lambda i: (i, 0)),
            part_of_seq(seq, blocks // STEPS, width, 2 * HEAD_DIM),
            part_of_seq(0, blocks // STEPS, width, 2 * HEAD_DIM),
            pl.BlockSpec((2, part), lambda i: (0, i)),
            fixed((slots, 1)),
            pl.BlockSpec((1, part), lambda i: (0, i)),
        ],
        out_specs=[
            pl.BlockSpec((part, 2 * HEAD_DIM), lambda i: (i, 0)),
            fixed((slots, 2 * HEAD_DIM)),
        ],
        out_shape=[jax.ShapeDtypeStruct((slots, 2 * HEAD_DIM), F32)] * 2,
        cost_estimate=cost_of(10),
        name="attend_back",
    )(
        lengths[seq : seq + 1], rotated, rotated, grad, out, lse,
        positions[:, None], positions[None, :],
    )


def project_back_kernel(
    dq_ref, dkv_ref, other_ref, proj_ref, cos_ref, sin_ref, gain_ref, grad_ref, sum_ref
):
    step = pl.program_id(0)
    grad = jnp.concatenate([dq_ref[...], dkv_ref[...] + other_ref[...]], axis=1)
    proj = rows_of_ref(proj_ref)
    scale_rows = lax.rsqrt(head_mean(proj * proj) + EPS)
    normed = proj * scale_rows
    turned = grad * cos_ref[...] - swap_halves(grad) * sin_ref[...]
    gained = turned * gain_ref[...]
    back = scale_rows * (gained - normed * head_mean(gained * normed))
    lane = lax.broadcasted_iota(jnp.int32, proj.shape, 1)
    grad_ref[...] = jnp.where(lane < 3 * HEAD_DIM, back, grad).astype(BF16).reshape(grad_ref.shape)
    sums = jnp.sum((turned * normed).reshape(-1, 8, LANES), axis=0)

    @pl.when(step == 0)
    def _():
        sum_ref[...] = sums

    @pl.when(step > 0)
    def _():
        sum_ref[...] += sums


def project_back(seq, grad_q, grad_kv, other_kv, proj, cosine, sine, gain):
    blocks, _, width, _ = proj.shape
    some = blocks // STEPS
    part = some * width
    half = pl.BlockSpec((part, 2 * HEAD_DIM), lambda i: (i, 0))
    turned = pl.BlockSpec((part, 2 * HEAD_DIM), lambda i: ((i + STEPS // 2) % STEPS, 0))
    table = pl.BlockSpec((part, LANES), lambda i: (i, 0))
    return pl.pallas_call(
        project_back_kernel,
        grid=(STEPS,),
        in_specs=[
            half, half, turned, part_of_seq(seq, some, width, LANES), table, table,
            fixed((1, LANES)),
        ],
        out_specs=[part_of_seq(0, some, width, LANES), fixed((8, LANES))],
        out_shape=[
            jax.ShapeDtypeStruct((blocks, 1, width, LANES), BF16),
            jax.ShapeDtypeStruct((8, LANES), F32),
        ],
        cost_estimate=cost_of(3),
        name="project_back",
    )(grad_q, grad_kv, other_kv, proj, cosine, sine, gain)


def dot_rows(left, right):
    return lax.dot_general(left, right, (((0,), (0,)), ((), ())), preferred_element_type=F32)


def plain(left, right):
    return jnp.dot(left, right, preferred_element_type=F32)


def in_order(own, other, index):
    first = index == 0
    return jnp.concatenate([jnp.where(first, own, other), jnp.where(first, other, own)], axis=0)


def split_local(
    tokens, cotangent, q_weight, k_weight, v_weight, o_weight, gate_weight, up_weight,
    down_weight, attn_gain, ffn_gain, q_gain, k_gain, lengths, pair_order,
):
    seqs, width, _ = tokens.shape
    rank = lax.axis_index("ctx")
    side = lax.axis_index("fsdp")
    core = rank % 2
    mine = seqs * width
    q_rows, kv_rows, ff_rows = q_weight.shape[0], k_weight.shape[0], gate_weight.shape[0]

    x_rows = tokens.astype(F32).reshape(mine, D)
    scale_one = rms_scale(x_rows)
    normed_one = x_rows * scale_one
    x_norm = gather_blocks((normed_one * attn_gain).astype(BF16))

    kv_own = jnp.stack([k_weight, v_weight])
    kv_side = send(kv_own, SWAP_X)
    kv_half = jnp.concatenate(
        [jnp.where(side == 0, kv_own, kv_side), jnp.where(side == 0, kv_side, kv_own)], axis=1
    )
    kv_core = send(kv_half, SWAP_CORE)
    kv_full = jnp.concatenate(
        [jnp.where(core == 0, kv_half, kv_core), jnp.where(core == 0, kv_core, kv_half)], axis=1
    )
    w_attn = jnp.concatenate(
        [q_weight, send(q_weight, SWAP_X), kv_full[0], kv_full[1]], axis=0
    )
    w_out = jnp.concatenate([o_weight, send(o_weight, SWAP_X)], axis=0)
    ff_own = jnp.concatenate([gate_weight, up_weight, down_weight], axis=0)
    ff_side = send(ff_own, SWAP_X)
    w_gate_up = jnp.concatenate([ff_own[: 2 * ff_rows], ff_side[: 2 * ff_rows]], axis=0)
    w_down = jnp.concatenate([down_weight, ff_side[2 * ff_rows :]], axis=0)

    owners = block_owners(rank)
    blocks = owners.shape[0]
    within = jnp.arange(width, dtype=jnp.int32)
    half_blk = width // 2

    def positions_of(dealt):
        block_id = jnp.where(
            within[None, :] < half_blk, dealt[:, None], 2 * pair_order.shape[0] - 1 - dealt[:, None]
        )
        return (block_id * half_blk + within[None, :] % half_blk).reshape(-1)

    positions = positions_of(pair_order[owners])
    slots = positions.shape[0]
    cosine, sine = rope_tables(positions)
    plain_lanes = jnp.ones((slots, HEAD_DIM), F32)
    cosine = jnp.concatenate([cosine] * 6 + [plain_lanes], axis=1)
    sine = jnp.concatenate([-sine, sine] * 3 + [plain_lanes * 0.0], axis=1)
    gain_lanes = jnp.concatenate([q_gain, q_gain, k_gain, jnp.ones((HEAD_DIM,), F32)])[None, :]
    my_pos = positions_of(pair_order[rank][None])
    live = (my_pos[None, :] < lengths[:, None]).reshape(mine, 1)

    grad_out = jnp.where(live, cotangent.astype(F32).reshape(mine, D), 0.0)
    x_norm, grad_piece = lax.optimization_barrier((x_norm, grad_out.astype(BF16)))
    grad_low = gather_blocks(grad_piece)

    proj = project(x_norm, w_attn).reshape(blocks, seqs, width, LANES)
    heads = [
        attend(s, proj, cosine, sine, gain_lanes, positions, lengths) for s in range(seqs)
    ]
    out_rows = jnp.concatenate([out for out, _, _ in heads], axis=1)
    out_rows = out_rows.reshape(blocks * mine, 2 * HEAD_DIM)

    def partials(rows, weight):
        cut = rows.shape[0] // 2
        other = plain(rows[cut:], weight).astype(BF16)
        own = plain(rows[:cut], weight).astype(BF16)
        return (own, other)

    def partial_sums(rows, weight):
        return scatter_blocks(*partials(rows, weight))

    resid = x_rows + partial_sums(out_rows, w_out)
    scale_two = rms_scale(resid)
    normed_two = resid * scale_two
    x_norm2 = gather_blocks((normed_two * ffn_gain).astype(BF16))

    both = project(x_norm2, w_gate_up)
    gate_part = jnp.concatenate([both[:, :ff_rows], both[:, 2 * ff_rows : 3 * ff_rows]], axis=1)
    up_part = jnp.concatenate([both[:, ff_rows : 2 * ff_rows], both[:, 3 * ff_rows :]], axis=1)
    hidden = (jax.nn.silu(gate_part) * up_part).astype(BF16)
    gate_low, up_low = gate_grads(project(grad_low, w_down), gate_part, up_part)
    gate_up_low = jnp.concatenate(
        [gate_low[:, :ff_rows], up_low[:, :ff_rows], gate_low[:, ff_rows:], up_low[:, ff_rows:]],
        axis=1,
    )
    grad_norm2 = partial_sums(gate_up_low, w_gate_up)
    out_parts = partials(hidden, w_down)
    grad_ffn_gain = jnp.sum(grad_norm2 * normed_two, axis=0)
    grad_resid = grad_out + rms_back(grad_norm2 * ffn_gain, normed_two, scale_two)
    grad_attn_low = gather_blocks(grad_resid.astype(BF16))
    grad_attn_low, out_parts = lax.optimization_barrier((grad_attn_low, out_parts))
    out_sum = scatter_blocks(*out_parts)
    block_out = (
        jnp.where(live, resid + out_sum, 0.0).astype(BF16).reshape(seqs, width, D)
    )

    def sent_aside(full):
        own = full.shape[0] // 2
        return (full[:own], send(full[own:].astype(BF16), SWAP_X))

    gate_up_full = dot_rows(gate_up_low, x_norm2)
    down_full = dot_rows(hidden, grad_low)
    gate_up_stay, gate_up_come = sent_aside(gate_up_full)
    down_stay, down_come = sent_aside(down_full)

    grad_o = project(grad_attn_low, w_out).astype(BF16).reshape(blocks, seqs, width, 2 * HEAD_DIM)
    grads, gain_sums = [], 0.0
    for s, (out, lse, rotated) in enumerate(heads):
        grad_q, grad_kv = attend_back(s, rotated, grad_o, out, lse, positions, lengths)
        rows, sums = project_back(
            s, grad_q, grad_kv, send(grad_kv, SWAP_CORE), proj, cosine, sine, gain_lanes
        )
        grads.append(rows)
        gain_sums = gain_sums + jnp.sum(sums, axis=0)
    grad_rows = jnp.concatenate(grads, axis=1).reshape(blocks * mine, LANES)
    grad_rows, gate_up_come, down_come = lax.optimization_barrier(
        (grad_rows, gate_up_come, down_come)
    )
    gate_up_grad = gate_up_stay + gate_up_come.astype(F32)
    down_grad = down_stay + down_come.astype(F32)
    row = jnp.arange(LANES)[:, None] // HEAD_DIM
    w_once = jnp.where((row < 2) | (row == 2 + core), w_attn, 0).astype(BF16)
    grad_norm1 = partial_sums(grad_rows, w_once)
    o_stay, o_come = sent_aside(dot_rows(out_rows, grad_attn_low))
    o_grad = o_stay + o_come.astype(F32)
    attn_full = dot_rows(grad_rows, x_norm)
    kv_grads = attn_full[2 * q_rows :].reshape(2, 2, 2, kv_rows, D)
    kv_mine = jnp.where(core == 0, kv_grads[:, 0], kv_grads[:, 1])
    kv_stay = jnp.where(side == 0, kv_mine[:, 0], kv_mine[:, 1])
    kv_leave = jnp.where(side == 0, kv_mine[:, 1], kv_mine[:, 0])
    attn_stay, attn_come = sent_aside(
        jnp.concatenate(
            [
                attn_full[:q_rows],
                kv_stay.reshape(2 * kv_rows, D),
                attn_full[q_rows : 2 * q_rows],
                kv_leave.reshape(2 * kv_rows, D),
            ],
            axis=0,
        )
    )
    attn_grads = attn_stay + attn_come.astype(F32)
    grad_tokens = (grad_resid + rms_back(grad_norm1 * attn_gain, normed_one, scale_one)).reshape(
        seqs, width, D
    )
    owned = jnp.concatenate([q_weight, k_weight, v_weight], axis=0).astype(F32)
    grad_attn_gain = jnp.sum(owned * attn_grads, axis=0) / attn_gain
    gains = total_sum(
        jnp.concatenate(
            [
                grad_attn_gain,
                grad_ffn_gain,
                gain_sums[:HEAD_DIM] + gain_sums[HEAD_DIM : 2 * HEAD_DIM],
                0.5 * gain_sums[2 * HEAD_DIM : 3 * HEAD_DIM],
            ]
        )
    )
    return (
        block_out,
        grad_tokens,
        attn_grads[:q_rows],
        attn_grads[q_rows : q_rows + kv_rows],
        attn_grads[q_rows + kv_rows :],
        o_grad,
        gate_up_grad[:ff_rows],
        gate_up_grad[ff_rows:],
        down_grad,
        gains[:D],
        gains[D : 2 * D],
        gains[2 * D : 2 * D + HEAD_DIM],
        gains[2 * D + HEAD_DIM :],
    )


def solution(mesh):
    body = split_local if fits_split(mesh) else local
    in_specs = (
        P("fsdp", "ctx", None),
        P("fsdp", "ctx", None),
        P(("ctx", "fsdp"), None),
        P(("ctx", "fsdp"), None),
        P(("ctx", "fsdp"), None),
        P(("ctx", "fsdp"), None),
        P(("ctx", "fsdp"), None),
        P(("ctx", "fsdp"), None),
        P(("ctx", "fsdp"), None),
        P(),
        P(),
        P(),
        P(),
        P("fsdp"),
        P(),
    )
    out_specs = (
        P("fsdp", "ctx", None),
        P("fsdp", "ctx", None),
        P(("ctx", "fsdp"), None),
        P(("ctx", "fsdp"), None),
        P(("ctx", "fsdp"), None),
        P(("ctx", "fsdp"), None),
        P(("ctx", "fsdp"), None),
        P(("ctx", "fsdp"), None),
        P(("ctx", "fsdp"), None),
        P(),
        P(),
        P(),
        P(),
    )
    return jax.shard_map(body, mesh=mesh, in_specs=in_specs, out_specs=out_specs, check_vma=False)
```

```python
import functools
import math

import jax
import jax.numpy as jnp
from jax import lax
from jax.experimental import pallas as pl
from jax.experimental.pallas import tpu as pltpu
from jax.sharding import PartitionSpec as P

D = 2048
HEADS = 32
KV_HEADS = 8
HEAD_DIM = 64
FF = 8192


EPS = 1e-05
THETA = 1000000.0
NEG = -1e30


def rms_scale(values):
    return lax.rsqrt(jnp.mean(values * values, axis=-1, keepdims=True) + EPS)


def rms_back(grad_normed, normed, scale_rows):
    return scale_rows * (
        grad_normed - normed * jnp.mean(grad_normed * normed, axis=-1, keepdims=True)
    )


def rope_tables(positions):
    half = HEAD_DIM // 2
    freq = THETA ** (-(jnp.arange(half, dtype=jnp.float32) * 2.0 / HEAD_DIM))
    angle = positions.astype(jnp.float32)[:, None] * freq[None, :]
    return (jnp.cos(angle), jnp.sin(angle))


def rotate(values, cosine, sine):
    half = values.shape[-1] // 2
    first = values[..., :half]
    second = values[..., half:]
    return jnp.concatenate(
        [first * cosine - second * sine, second * cosine + first * sine], axis=-1
    )


def slot_positions(pair_order, width_pair, first, count):
    slot = first + jnp.arange(count, dtype=jnp.int32)
    owner = slot // width_pair
    within = slot % width_pair
    half_blk = width_pair // 2
    pair = pair_order[owner]
    block_id = jnp.where(within < half_blk, pair, 2 * pair_order.shape[0] - 1 - pair)
    return block_id * half_blk + within % half_blk


def block_mask(query_pos, key_part, lengths):
    return (key_part[None, None, :] <= query_pos[None, :, None]) & (
        key_part[None, None, :] < lengths[:, None, None]
    )


def project(inputs, weight):
    return jnp.einsum("td,fd->tf", inputs, weight, preferred_element_type=jnp.float32)


def gate_grads(grad_hidden, gate_part, up_part):
    sigma = jax.nn.sigmoid(gate_part)
    grad_gate = grad_hidden * up_part * sigma * (1.0 + gate_part * (1.0 - sigma))
    grad_up = grad_hidden * gate_part * sigma
    return (grad_gate.astype(jnp.bfloat16), grad_up.astype(jnp.bfloat16))


def block_grads(q_rot, grad_o_low, lse, delta, k_blk, v_blk, allowed, scale):
    scores = (
        jnp.einsum("sqhgd,sjhd->sqhgj", q_rot, k_blk, preferred_element_type=jnp.float32) * scale
    )
    scores = jnp.where(allowed[:, :, None, None, :], scores, NEG)
    probs = jnp.exp(scores - lse[..., None])
    grad_probs = jnp.einsum(
        "sqhgd,sjhd->sqhgj", grad_o_low, v_blk, preferred_element_type=jnp.float32
    )
    grad_scores = (probs * (grad_probs - delta[..., None])).astype(jnp.bfloat16)
    return (probs, grad_scores)


def local(
    tokens,
    cotangent,
    q_weight,
    k_weight,
    v_weight,
    o_weight,
    gate_weight,
    up_weight,
    down_weight,
    attn_gain,
    ffn_gain,
    q_gain,
    k_gain,
    lengths,
    pair_order,
):
    seq_grp = tokens.shape[0]
    width_pair = tokens.shape[1]
    groups = HEADS // KV_HEADS
    q_width = HEADS * HEAD_DIM
    kv_width = KV_HEADS * HEAD_DIM
    scale = HEAD_DIM ** (-0.5)
    tok_rows = seq_grp * width_pair
    slots = width_pair * pair_order.shape[0]
    key_blk = math.gcd(slots, 512)
    key_count = slots // key_blk
    dev_count = lax.axis_size("ctx") * lax.axis_size("fsdp")
    local_pos = slot_positions(
        pair_order, width_pair, lax.axis_index("ctx") * width_pair, width_pair
    )
    key_pos = slot_positions(pair_order, width_pair, 0, slots)
    live_rows = (local_pos[None, :] < lengths[:, None]).reshape(tok_rows, 1)
    cosine, sine = rope_tables(local_pos)
    cosine = cosine[None, :, None, :]
    sine = sine[None, :, None, :]
    x_rows = tokens.astype(jnp.float32).reshape(tok_rows, D)
    scale_one = rms_scale(x_rows)
    normed_one = x_rows * scale_one
    x_norm = (normed_one * attn_gain).astype(jnp.bfloat16)
    w_query, w_key, w_value, w_out = (
        lax.all_gather(q_weight, ("ctx", "fsdp"), axis=0, tiled=True),
        lax.all_gather(k_weight, ("ctx", "fsdp"), axis=0, tiled=True),
        lax.all_gather(v_weight, ("ctx", "fsdp"), axis=0, tiled=True),
        lax.all_gather(o_weight, ("ctx", "fsdp"), axis=0, tiled=True),
    )
    q_proj = project(x_norm, w_query).reshape(seq_grp, width_pair, HEADS, HEAD_DIM)
    k_proj = project(x_norm, w_key).reshape(seq_grp, width_pair, KV_HEADS, HEAD_DIM)
    v_low = project(x_norm, w_value).astype(jnp.bfloat16).reshape(seq_grp, width_pair, kv_width)
    q_scale = rms_scale(q_proj)
    q_normed = q_proj * q_scale
    q_rot = (
        rotate(q_normed * q_gain, cosine, sine)
        .astype(jnp.bfloat16)
        .reshape(seq_grp, width_pair, KV_HEADS, groups, HEAD_DIM)
    )
    k_scale = rms_scale(k_proj)
    k_normed = k_proj * k_scale
    k_rot = (
        rotate(k_normed * k_gain, cosine, sine)
        .astype(jnp.bfloat16)
        .reshape(seq_grp, width_pair, kv_width)
    )
    k_all, v_all = (
        lax.all_gather(k_rot, "ctx", axis=1, tiled=True),
        lax.all_gather(v_low, "ctx", axis=1, tiled=True),
    )
    k_all = k_all.reshape(seq_grp, slots, KV_HEADS, HEAD_DIM)
    v_all = v_all.reshape(seq_grp, slots, KV_HEADS, HEAD_DIM)

    def key_slices(first, count):
        k_blk = lax.dynamic_slice_in_dim(k_all, first, count, 1)
        v_blk = lax.dynamic_slice_in_dim(v_all, first, count, 1)
        allowed = block_mask(local_pos, lax.dynamic_slice_in_dim(key_pos, first, count, 0), lengths)
        return (k_blk, v_blk, allowed)

    def forward_step(index, carry):
        top, total, summed = carry
        k_blk, v_blk, allowed = key_slices(index * key_blk, key_blk)
        scores = (
            jnp.einsum("sqhgd,sjhd->sqhgj", q_rot, k_blk, preferred_element_type=jnp.float32)
            * scale
        )
        scores = jnp.where(allowed[:, :, None, None, :], scores, NEG)
        new_top = jnp.maximum(top, jnp.max(scores, axis=-1))
        shrink = jnp.exp(top - new_top)
        probs = jnp.exp(scores - new_top[..., None])
        total = total * shrink + jnp.sum(probs, axis=-1)
        summed = summed * shrink[..., None] + jnp.einsum(
            "sqhgj,sjhd->sqhgd",
            probs.astype(jnp.bfloat16),
            v_blk,
            preferred_element_type=jnp.float32,
        )
        return (new_top, total, summed)

    stat_shape = (seq_grp, width_pair, KV_HEADS, groups)
    start_carry = (
        jnp.full(stat_shape, NEG, jnp.float32),
        jnp.zeros(stat_shape, jnp.float32),
        jnp.zeros(stat_shape + (HEAD_DIM,), jnp.float32),
    )
    top, total, summed = lax.fori_loop(0, key_count, forward_step, start_carry)
    lse = top + jnp.log(total)
    o_low = (summed / total[..., None]).astype(jnp.bfloat16)
    o_rows = o_low.reshape(tok_rows, q_width)
    resid = x_rows + jnp.einsum("tf,fd->td", o_rows, w_out, preferred_element_type=jnp.float32)
    scale_two = rms_scale(resid)
    normed_two = resid * scale_two
    x_norm2 = (normed_two * ffn_gain).astype(jnp.bfloat16)
    grad_out = jnp.where(live_rows, cotangent.astype(jnp.float32).reshape(tok_rows, D), 0.0)
    grad_low = grad_out.astype(jnp.bfloat16)
    pieces = (
        lax.all_gather(gate_weight, ("ctx", "fsdp"), axis=0, tiled=True),
        lax.all_gather(up_weight, ("ctx", "fsdp"), axis=0, tiled=True),
        lax.all_gather(down_weight, ("ctx", "fsdp"), axis=0, tiled=True),
    )
    gate_part = project(x_norm2, pieces[0])
    up_part = project(x_norm2, pieces[1])
    hidden_part = (jax.nn.silu(gate_part) * up_part).astype(jnp.bfloat16)
    out_sum = jnp.einsum("tf,fd->td", hidden_part, pieces[2], preferred_element_type=jnp.float32)
    gate_all = gate_part
    up_all = up_part
    hidden = (jax.nn.silu(gate_all) * up_all).astype(jnp.bfloat16)
    pieces = (
        lax.all_gather(gate_weight, ("ctx", "fsdp"), axis=0, tiled=True),
        lax.all_gather(up_weight, ("ctx", "fsdp"), axis=0, tiled=True),
        lax.all_gather(down_weight, ("ctx", "fsdp"), axis=0, tiled=True),
    )
    count = pieces[0].shape[0]
    gate_part = gate_all
    up_part = up_all
    grad_gate_part, grad_up_part = gate_grads(project(grad_low, pieces[2]), gate_part, up_part)
    grad_sum = jnp.einsum(
        "tf,fd->td", grad_gate_part, pieces[0], preferred_element_type=jnp.float32
    ) + jnp.einsum("tf,fd->td", grad_up_part, pieces[1], preferred_element_type=jnp.float32)
    gate_grad_all = grad_gate_part
    up_grad_all = grad_up_part
    block_out = (
        jnp.where(live_rows, resid + out_sum, 0.0)
        .astype(jnp.bfloat16)
        .reshape(seq_grp, width_pair, D)
    )
    ffn_dev = FF // dev_count
    owners = lax.axis_size(("ctx", "fsdp")) * (3 * ffn_dev) // (3 * ffn_dev)
    first = jnp.int32(0) // (3 * ffn_dev) * ffn_dev
    grad_gate_part = jnp.einsum(
        "tf,td->fd", gate_grad_all, x_norm2, preferred_element_type=jnp.float32
    )
    grad_up_part = jnp.einsum("tf,td->fd", up_grad_all, x_norm2, preferred_element_type=jnp.float32)
    grad_down_part = jnp.einsum("tf,td->fd", hidden, grad_low, preferred_element_type=jnp.float32)
    stacked = jnp.stack(
        [
            grad_gate_part.reshape(owners, ffn_dev, D),
            grad_up_part.reshape(owners, ffn_dev, D),
            grad_down_part.reshape(owners, ffn_dev, D),
        ],
        axis=1,
    )
    ffn_grads = lax.psum_scatter(
        stacked.reshape(lax.axis_size(("ctx", "fsdp")) * (3 * ffn_dev), D),
        ("ctx", "fsdp"),
        scatter_dimension=0,
        tiled=True,
    )
    grad_ffn_gain = jnp.sum(grad_sum * normed_two, axis=0)
    grad_resid = grad_out + rms_back(grad_sum * ffn_gain, normed_two, scale_two)
    grad_attn_low = grad_resid.astype(jnp.bfloat16)
    grad_o_low = (
        project(grad_attn_low, w_out)
        .astype(jnp.bfloat16)
        .reshape(seq_grp, width_pair, KV_HEADS, groups, HEAD_DIM)
    )
    delta = jnp.sum(grad_o_low.astype(jnp.float32) * o_low.astype(jnp.float32), axis=-1)
    dq_zero = jnp.zeros((seq_grp, width_pair, KV_HEADS, groups, HEAD_DIM), jnp.float32)
    kv_cols = seq_grp * 2 * kv_width

    def key_value_grads(probs, grad_scores):
        grad_k_blk = (
            jnp.einsum("sqhgj,sqhgd->jshd", grad_scores, q_rot, preferred_element_type=jnp.float32)
            * scale
        )
        grad_v_blk = jnp.einsum(
            "sqhgj,sqhgd->jshd",
            probs.astype(jnp.bfloat16),
            grad_o_low,
            preferred_element_type=jnp.float32,
        )
        return jnp.stack([grad_k_blk, grad_v_blk], axis=2).reshape(probs.shape[-1], kv_cols)

    def both_step(grad_q, index):
        k_blk, v_blk, allowed = key_slices(index * key_blk, key_blk)
        probs, grad_scores = block_grads(
            q_rot, grad_o_low, lse, delta, k_blk, v_blk, allowed, scale
        )
        grad_q = (
            grad_q
            + jnp.einsum(
                "sqhgj,sjhd->sqhgd", grad_scores, k_blk, preferred_element_type=jnp.float32
            )
            * scale
        )
        return (grad_q, key_value_grads(probs, grad_scores))

    grad_q_rot, kv_blocks = lax.scan(both_step, dq_zero, jnp.arange(key_count))
    kv_grad = lax.psum_scatter(
        kv_blocks.reshape(slots, kv_cols), "ctx", scatter_dimension=0, tiled=True
    )
    kv_grad = jnp.transpose(
        kv_grad.reshape(width_pair, seq_grp, 2, KV_HEADS, HEAD_DIM), (1, 0, 2, 3, 4)
    )
    grad_q_pre = rotate(grad_q_rot.reshape(seq_grp, width_pair, HEADS, HEAD_DIM), cosine, -sine)
    grad_k_pre = rotate(kv_grad[:, :, 0], cosine, -sine)
    grad_q_gain = jnp.sum(grad_q_pre * q_normed, axis=(0, 1, 2))
    grad_k_gain = jnp.sum(grad_k_pre * k_normed, axis=(0, 1, 2))
    grad_q_proj = (
        rms_back(grad_q_pre * q_gain, q_normed, q_scale)
        .reshape(tok_rows, q_width)
        .astype(jnp.bfloat16)
    )
    grad_k_proj = (
        rms_back(grad_k_pre * k_gain, k_normed, k_scale)
        .reshape(tok_rows, kv_width)
        .astype(jnp.bfloat16)
    )
    grad_v_proj = kv_grad[:, :, 1].reshape(tok_rows, kv_width).astype(jnp.bfloat16)
    grad_norm1 = jnp.einsum("tf,fd->td", grad_q_proj, w_query, preferred_element_type=jnp.float32)
    grad_norm1 = grad_norm1 + jnp.einsum(
        "tf,fd->td", grad_k_proj, w_key, preferred_element_type=jnp.float32
    )
    grad_norm1 = grad_norm1 + jnp.einsum(
        "tf,fd->td", grad_v_proj, w_value, preferred_element_type=jnp.float32
    )
    grad_attn_gain = jnp.sum(grad_norm1 * normed_one, axis=0)
    grad_tokens = (grad_resid + rms_back(grad_norm1 * attn_gain, normed_one, scale_one)).reshape(
        seq_grp, width_pair, D
    )
    q_dev = q_width // dev_count
    kv_dev = kv_width // dev_count
    per_dev = 2 * q_dev + 2 * kv_dev
    owners = lax.axis_size(("ctx", "fsdp")) * per_dev // per_dev

    def rows_of(grad_rows, inputs, each):
        return jnp.einsum(
            "tf,td->fd", grad_rows, inputs, preferred_element_type=jnp.float32
        ).reshape(owners, each, D)

    joined = jnp.concatenate(
        [
            rows_of(grad_q_proj, x_norm, q_dev),
            rows_of(grad_k_proj, x_norm, kv_dev),
            rows_of(grad_v_proj, x_norm, kv_dev),
            rows_of(o_rows, grad_attn_low, q_dev),
        ],
        axis=1,
    )
    attn_grads = lax.psum_scatter(
        joined.reshape(lax.axis_size(("ctx", "fsdp")) * per_dev, D),
        ("ctx", "fsdp"),
        scatter_dimension=0,
        tiled=True,
    )
    grad_attn_gain, grad_ffn_gain, grad_q_gain, grad_k_gain = lax.psum(
        (grad_attn_gain, grad_ffn_gain, grad_q_gain, grad_k_gain), ("ctx", "fsdp")
    )
    return (
        block_out,
        grad_tokens,
        attn_grads[:q_dev],
        attn_grads[q_dev : q_dev + kv_dev],
        attn_grads[q_dev + kv_dev : q_dev + 2 * kv_dev],
        attn_grads[q_dev + 2 * kv_dev :],
        ffn_grads[:ffn_dev],
        ffn_grads[ffn_dev : 2 * ffn_dev],
        ffn_grads[2 * ffn_dev :],
        grad_attn_gain,
        grad_ffn_gain,
        grad_q_gain,
        grad_k_gain,
    )


AXES = ("ctx", "fsdp")
RANKS = 16
LANES = 4 * HEAD_DIM
BF16 = jnp.bfloat16
F32 = jnp.float32
FAR = 1 << 30


def fits_split(mesh):
    return mesh.shape["ctx"] == RANKS and mesh.shape["fsdp"] == 2


CYCLE = ((0, 0), (1, 0), (2, 0), (3, 0), (3, 1), (2, 1), (1, 1), (0, 1))
CHIPS = len(CYCLE)
DISTANCES = (4, 3, -3, 2, -2, 1, -1, 0)


def index_of(z, y, core, x):
    return z * 8 + y * 4 + core * 2 + x


def pairs_of(move):
    places = [(z, y, c, x) for z in range(4) for y in range(2) for c in range(2) for x in range(2)]
    return [(index_of(*place), index_of(*move(*place))) for place in places]


def along_cycle(step):
    def move(z, y, core, x):
        return (*CYCLE[(CYCLE.index((z, y)) + step) % CHIPS], core, x)

    return pairs_of(move)


SWAP_X = pairs_of(lambda z, y, c, x: (z, y, c, 1 - x))
SWAP_CORE = pairs_of(lambda z, y, c, x: (z, y, 1 - c, x))
SWAP_Y = pairs_of(lambda z, y, c, x: (z, 1 - y, c, x))
SWAP_Z0 = pairs_of(lambda z, y, c, x: (z ^ 1, y, c, x))
SWAP_Z1 = pairs_of(lambda z, y, c, x: (z ^ 2, y, c, x))
AHEAD = along_cycle(1)
BEHIND = along_cycle(-1)


def block_owners(rank):
    place = jnp.array([CYCLE.index((chip // 2, chip % 2)) for chip in range(CHIPS)], jnp.int32)
    chips = jnp.array([2 * z + y for z, y in CYCLE], jnp.int32)
    around = (place[rank // 2] + jnp.array(DISTANCES, jnp.int32)) % CHIPS
    core = rank % 2
    return jnp.concatenate([chips[around] * 2 + core, chips[around] * 2 + 1 - core])


def send(value, pairs):
    return lax.ppermute(value, AXES, pairs)


def tie(values, *others):
    return lax.optimization_barrier((values, others))[0]


def nothing(hold):
    return ()


def collect_kernel(starts, *refs):
    count = len(starts)
    pieces, whole, sems = refs[:count], refs[-2], refs[-1]
    copies = [
        pltpu.make_async_copy(piece, whole.at[pl.ds(start, piece.shape[0])], sems.at[i])
        for i, (piece, start) in enumerate(zip(pieces, starts))
    ]
    for copy in copies:
        copy.start()
    for copy in copies:
        copy.wait()


def collect(pieces, starts, whole):
    inner = functools.partial(collect_kernel, starts)
    given = isinstance(whole, jax.Array)
    anywhere = pl.BlockSpec(memory_space=pl.ANY)
    return pl.pallas_call(
        inner,
        in_specs=[anywhere] * (len(pieces) + given),
        out_specs=anywhere,
        out_shape=jax.ShapeDtypeStruct(whole.shape, whole.dtype),
        scratch_shapes=[pltpu.SemaphoreType.DMA((len(pieces),))],
        input_output_aliases={len(pieces): 0} if given else {},
        cost_estimate=cost_of(0.3 * len(pieces)),
        name="collect",
    )(*pieces, *([whole] if given else []))


def gather_blocks(piece, slots=(nothing,) * 4):
    rows = piece.shape[0]
    half = rows // 2
    back, front = [piece], [piece]
    for step, slot in enumerate(slots):
        to_ahead, to_behind = back[-1], front[-1]
        if step == 3:
            to_ahead, to_behind = to_ahead[:half], to_behind[half:]
        come = (send(to_ahead, AHEAD), send(to_behind, BEHIND))
        before = (back[-1], front[-1])
        done = slot(lambda *xs: tie(xs, before) if step else xs)
        come = tie(come, *done)
        back.append(come[0])
        front.append(come[1])
    late = [back[4], front[4]]
    late_starts = (0, half)
    early = [front[3], back[3], front[2], back[2], front[1], back[1], piece]
    early_starts = tuple(rows * (1 + i) for i in range(len(early)))
    across = CHIPS * rows
    full = jax.ShapeDtypeStruct((2 * across, piece.shape[1]), piece.dtype)
    whole = collect(
        early + [send(block, SWAP_CORE) for block in early],
        early_starts + tuple(across + start for start in early_starts),
        full,
    )
    return collect(
        late + [send(block, SWAP_CORE) for block in late],
        late_starts + tuple(across + start for start in late_starts),
        whole,
    )


def add_low(left, right):
    return (left.astype(F32) + right.astype(F32)).astype(BF16)


def partial_sums(rows, weight):
    own, other = jnp.split(rows, 2)
    cut = 3 * (own.shape[0] // CHIPS)
    halves = []
    for part in (slice(0, cut), slice(cut, None)):
        come = send(plain(other[part], weight).astype(BF16), SWAP_CORE)
        halves.append((own[part], come))
    return tuple((plain(mine, weight) + come.astype(F32)).astype(BF16) for mine, come in halves)


def scatter_blocks(first, rest, slots=(nothing,) * 4):
    rows = first.shape[0] // 3
    half = rows // 2
    come = (send(first[:half], AHEAD), send(first[half:rows], BEHIND))
    come = tie(come, *slots[0](lambda *xs: xs))
    ahead, behind = first[rows : 2 * rows], first[2 * rows :]
    leave = (
        jnp.concatenate([add_low(ahead[:half], come[0]), ahead[half:]]),
        jnp.concatenate([behind[:half], add_low(behind[half:], come[1])]),
    )
    for step in (1, 2, 3):
        before = leave
        come = (send(leave[0], AHEAD), send(leave[1], BEHIND))
        come = tie(come, *slots[step](lambda *xs: tie(xs, before)))
        at = (step - 1) * 2 * rows
        if step < 3:
            leave = (
                add_low(rest[at : at + rows], come[0]),
                add_low(rest[at + rows : at + 2 * rows], come[1]),
            )
    return rest[4 * rows :].astype(F32) + come[0].astype(F32) + come[1].astype(F32)


def total_sum(value):
    for pairs in (SWAP_CORE, SWAP_X, SWAP_Y, SWAP_Z0, SWAP_Z1):
        value = value + send(value, pairs)
    return value


def head_sums():
    row = lax.broadcasted_iota(jnp.int32, (LANES, LANES), 0) // HEAD_DIM
    col = lax.broadcasted_iota(jnp.int32, (LANES, LANES), 1) // HEAD_DIM
    return jnp.where(row == col, 1.0 / HEAD_DIM, 0.0).astype(BF16)


def head_mean(values):
    high = values.astype(BF16)
    rest = (values - high.astype(F32)).astype(BF16)
    sums = head_sums()
    return plain(high, sums) + plain(rest, sums)


def swap_halves(values):
    lane = lax.broadcasted_iota(jnp.int32, values.shape, 1)
    return jnp.where(
        lane % HEAD_DIM < HEAD_DIM // 2,
        pltpu.roll(values, LANES - HEAD_DIM // 2, 1),
        pltpu.roll(values, HEAD_DIM // 2, 1),
    )


def twice(ref):
    return jnp.concatenate([ref[...]] * 2, axis=1)


def dot_lanes(left, right):
    return lax.dot_general(left, right, (((1,), (1,)), ((), ())), preferred_element_type=F32)


def allowed_of(length, pos_col_ref, pos_row_ref):
    col = pos_col_ref[...]
    return jnp.where(col < length, col, FAR) <= pos_row_ref[...]


def rows_of_ref(ref):
    value = ref[...]
    return value.reshape(-1, value.shape[-1])


def attend_kernel(
    length_ref, proj_ref, cos_ref, sin_ref, gain_ref, pos_col_ref, pos_row_ref,
    out_ref, lse_ref, rot_ref, val_ref,
):
    step = pl.program_id(0)
    block = lse_ref.shape[-1]

    @pl.when(step == 0)
    def _():
        proj = rows_of_ref(proj_ref)
        normed = proj * lax.rsqrt(head_mean(proj * proj) + EPS) * gain_ref[...]
        rotated = normed * twice(cos_ref) + swap_halves(normed) * twice(sin_ref)
        lane = lax.broadcasted_iota(jnp.int32, proj.shape, 1)
        rotated = jnp.where(lane < 2 * HEAD_DIM, rotated * HEAD_DIM**-0.5, rotated)
        rot_ref[...] = jnp.where(lane < 3 * HEAD_DIM, rotated, proj).astype(BF16)
        val_ref[:HEAD_DIM, :] = proj[:, 3 * HEAD_DIM :].T.astype(BF16)
        val_ref[HEAD_DIM:, :] = jnp.ones((16, proj.shape[0]), BF16)

    allowed = allowed_of(length_ref[0], pos_col_ref, pos_row_ref)
    keys = rot_ref[:, 2 * HEAD_DIM : 3 * HEAD_DIM]
    query = rot_ref[pl.ds(pl.multiple_of(step * block, block), block), : 2 * HEAD_DIM]
    outs = []
    for head in range(2):
        scores = dot_lanes(keys, query[:, head * HEAD_DIM : (head + 1) * HEAD_DIM])
        weights = jnp.where(allowed, jnp.exp(scores), 0.0).astype(BF16)
        summed = jnp.dot(val_ref[...], weights, preferred_element_type=F32)
        total = summed[HEAD_DIM : HEAD_DIM + 1]
        outs.append((summed[:HEAD_DIM] / total).T)
        lse_ref[head : head + 1, :] = jnp.log(total)
    out_ref[...] = jnp.concatenate(outs, axis=1).astype(BF16).reshape(out_ref.shape)


def fixed(shape):
    return pl.BlockSpec(shape, lambda i: (0,) * len(shape))


def of_seq(seq, blocks, width, lanes):
    return pl.BlockSpec((blocks, 1, width, lanes), lambda i: (0, seq, 0, 0))


def part_of_seq(seq, blocks, width, lanes):
    return pl.BlockSpec((blocks, 1, width, lanes), lambda i: (i, seq, 0, 0))


def cost_of(microseconds):
    return pl.CostEstimate(
        flops=int(microseconds * 6e8), transcendentals=0, bytes_accessed=int(microseconds * 2.5e6)
    )


STEPS = 4


def attend(seq, proj, cosine, sine, gain, positions, lengths):
    blocks, _, width, _ = proj.shape
    slots = blocks * width
    part = slots // STEPS
    return pl.pallas_call(
        attend_kernel,
        grid=(STEPS,),
        in_specs=[
            pl.BlockSpec(memory_space=pltpu.SMEM),
            of_seq(seq, blocks, width, LANES),
            fixed((slots, LANES // 2)),
            fixed((slots, LANES // 2)),
            fixed((1, LANES)),
            fixed((slots, 1)),
            pl.BlockSpec((1, part), lambda i: (0, i)),
        ],
        out_specs=[
            part_of_seq(0, blocks // STEPS, width, 2 * HEAD_DIM),
            pl.BlockSpec((2, part), lambda i: (0, i)),
            fixed((slots, LANES)),
        ],
        out_shape=[
            jax.ShapeDtypeStruct((blocks, 1, width, 2 * HEAD_DIM), BF16),
            jax.ShapeDtypeStruct((2, slots), F32),
            jax.ShapeDtypeStruct((slots, LANES), BF16),
        ],
        scratch_shapes=[pltpu.VMEM((HEAD_DIM + 16, slots), BF16)],
        cost_estimate=cost_of(8),
        name="attend",
    )(lengths[seq : seq + 1], proj, cosine, sine, gain, positions[:, None], positions[None, :])


def attend_back_kernel(
    length_ref, rot_ref, query_ref, grad_ref, out_ref, lse_ref, pos_col_ref, pos_row_ref,
    dq_ref, dkv_ref,
):
    step = pl.program_id(0)
    allowed = allowed_of(length_ref[0], pos_col_ref, pos_row_ref)
    keys = rot_ref[:, 2 * HEAD_DIM : 3 * HEAD_DIM]
    values = rot_ref[:, 3 * HEAD_DIM :]
    query = query_ref[:, : 2 * HEAD_DIM]
    grad = rows_of_ref(grad_ref)
    product = grad.astype(F32) * rows_of_ref(out_ref).astype(F32)
    ones = jnp.ones((8, HEAD_DIM), F32)
    grad_q, grad_k, grad_v = [], 0.0, 0.0
    for head in range(2):
        cut = slice(head * HEAD_DIM, (head + 1) * HEAD_DIM)
        delta = lax.dot_general(
            ones,
            product[:, cut],
            (((1,), (1,)), ((), ())),
            precision=lax.Precision.HIGHEST,
            preferred_element_type=F32,
        )[:1]
        scores = dot_lanes(keys, query[:, cut])
        probs = jnp.where(allowed, jnp.exp(scores - lse_ref[head : head + 1, :]), 0.0)
        grad_probs = dot_lanes(values, grad[:, cut])
        grad_scores = (probs * (grad_probs - delta)).astype(BF16)
        grad_v += jnp.dot(probs.astype(BF16), grad[:, cut], preferred_element_type=F32)
        grad_k += jnp.dot(grad_scores, query[:, cut], preferred_element_type=F32)
        grad_q.append(
            lax.dot_general(
                grad_scores, keys, (((0,), (0,)), ((), ())), preferred_element_type=F32
            )
        )
    dq_ref[...] = jnp.concatenate(grad_q, axis=1) * HEAD_DIM**-0.5
    both = jnp.concatenate([grad_k, grad_v], axis=1)

    @pl.when(step == 0)
    def _():
        dkv_ref[...] = both

    @pl.when(step > 0)
    def _():
        dkv_ref[...] += both


def attend_back(seq, rotated, grad, out, lse, positions, lengths):
    blocks, _, width, _ = grad.shape
    slots = blocks * width
    part = slots // STEPS
    return pl.pallas_call(
        attend_back_kernel,
        grid=(STEPS,),
        in_specs=[
            pl.BlockSpec(memory_space=pltpu.SMEM),
            fixed((slots, LANES)),
            pl.BlockSpec((part, LANES), lambda i: (i, 0)),
            part_of_seq(seq, blocks // STEPS, width, 2 * HEAD_DIM),
            part_of_seq(0, blocks // STEPS, width, 2 * HEAD_DIM),
            pl.BlockSpec((2, part), lambda i: (0, i)),
            fixed((slots, 1)),
            pl.BlockSpec((1, part), lambda i: (0, i)),
        ],
        out_specs=[
            pl.BlockSpec((part, 2 * HEAD_DIM), lambda i: (i, 0)),
            fixed((slots, 2 * HEAD_DIM)),
        ],
        out_shape=[jax.ShapeDtypeStruct((slots, 2 * HEAD_DIM), F32)] * 2,
        cost_estimate=cost_of(10),
        name="attend_back",
    )(
        lengths[seq : seq + 1], rotated, rotated, grad, out, lse,
        positions[:, None], positions[None, :],
    )


def project_back_kernel(
    dq_ref, dkv_ref, other_ref, proj_ref, cos_ref, sin_ref, gain_ref, grad_ref, sum_ref
):
    step = pl.program_id(0)
    grad = jnp.concatenate([dq_ref[...], dkv_ref[...] + other_ref[...]], axis=1)
    proj = rows_of_ref(proj_ref)
    scale_rows = lax.rsqrt(head_mean(proj * proj) + EPS)
    normed = proj * scale_rows
    turned = grad * twice(cos_ref) - swap_halves(grad) * twice(sin_ref)
    gained = turned * gain_ref[...]
    back = scale_rows * (gained - normed * head_mean(gained * normed))
    lane = lax.broadcasted_iota(jnp.int32, proj.shape, 1)
    grad_ref[...] = jnp.where(lane < 3 * HEAD_DIM, back, grad).astype(BF16).reshape(grad_ref.shape)
    sums = jnp.sum((turned * normed).reshape(-1, 8, LANES), axis=0)

    @pl.when(step == 0)
    def _():
        sum_ref[...] = sums

    @pl.when(step > 0)
    def _():
        sum_ref[...] += sums


def project_back(seq, grad_q, grad_kv, other_kv, proj, cosine, sine, gain):
    blocks, _, width, _ = proj.shape
    some = blocks // STEPS
    part = some * width
    half = pl.BlockSpec((part, 2 * HEAD_DIM), lambda i: (i, 0))
    turned = pl.BlockSpec((part, 2 * HEAD_DIM), lambda i: ((i + STEPS // 2) % STEPS, 0))
    table = pl.BlockSpec((part, LANES // 2), lambda i: (i, 0))
    return pl.pallas_call(
        project_back_kernel,
        grid=(STEPS,),
        in_specs=[
            half, half, turned, part_of_seq(seq, some, width, LANES), table, table,
            fixed((1, LANES)),
        ],
        out_specs=[part_of_seq(0, some, width, LANES), fixed((8, LANES))],
        out_shape=[
            jax.ShapeDtypeStruct((blocks, 1, width, LANES), BF16),
            jax.ShapeDtypeStruct((8, LANES), F32),
        ],
        cost_estimate=cost_of(3),
        name="project_back",
    )(grad_q, grad_kv, other_kv, proj, cosine, sine, gain)


def dot_rows(left, right):
    return lax.dot_general(left, right, (((0,), (0,)), ((), ())), preferred_element_type=F32)


def plain(left, right):
    return jnp.dot(left, right, preferred_element_type=F32)


def in_order(own, other, index):
    first = index == 0
    return jnp.concatenate([jnp.where(first, own, other), jnp.where(first, other, own)], axis=0)


def split_local(
    tokens, cotangent, q_weight, k_weight, v_weight, o_weight, gate_weight, up_weight,
    down_weight, attn_gain, ffn_gain, q_gain, k_gain, lengths, pair_order,
):
    seqs, width, _ = tokens.shape
    rank = lax.axis_index("ctx")
    side = lax.axis_index("fsdp")
    core = rank % 2
    mine = seqs * width
    q_rows, kv_rows, ff_rows = q_weight.shape[0], k_weight.shape[0], gate_weight.shape[0]

    x_rows = tokens.astype(F32).reshape(mine, D)
    scale_one = rms_scale(x_rows)
    normed_one = x_rows * scale_one
    kept = {}

    owners = block_owners(rank)
    blocks = owners.shape[0]
    within = jnp.arange(width, dtype=jnp.int32)
    half_blk = width // 2

    def positions_of(dealt):
        block_id = jnp.where(
            within[None, :] < half_blk, dealt[:, None], 2 * pair_order.shape[0] - 1 - dealt[:, None]
        )
        return (block_id * half_blk + within[None, :] % half_blk).reshape(-1)

    def tables(hold):
        positions = positions_of(pair_order[owners])
        cosine, sine = rope_tables(positions)
        kept["positions"] = positions
        kept["tables"] = (
            jnp.concatenate([cosine] * 4, axis=1),
            jnp.concatenate([-sine, sine] * 2, axis=1),
        )
        return kept["tables"]

    def attention_weights(hold):
        kv_own = jnp.stack([k_weight, v_weight])
        kv_side = send(kv_own, SWAP_X)
        kv_half = jnp.concatenate(
            [jnp.where(side == 0, kv_own, kv_side), jnp.where(side == 0, kv_side, kv_own)], axis=1
        )
        kv_core = send(kv_half, SWAP_CORE)
        kv_full = jnp.concatenate(
            [jnp.where(core == 0, kv_half, kv_core), jnp.where(core == 0, kv_core, kv_half)], axis=1
        )
        kept["w_attn"] = jnp.concatenate(
            [q_weight, send(q_weight, SWAP_X), kv_full[0], kv_full[1]], axis=0
        )
        return (kept["w_attn"],)

    def other_weights(hold):
        own = jnp.concatenate([o_weight, *hold(gate_weight, up_weight, down_weight)], axis=0)
        kept["own"], kept["aside"] = own, send(own, SWAP_X)
        return (own,)

    x_norm = gather_blocks(
        (normed_one * attn_gain).astype(BF16), (tables, attention_weights, other_weights, nothing)
    )
    positions, (cosine, sine), w_attn = kept["positions"], kept["tables"], kept["w_attn"]
    gain_lanes = jnp.concatenate([q_gain, q_gain, k_gain, jnp.ones((HEAD_DIM,), F32)])[None, :]
    my_pos = positions_of(pair_order[rank][None])
    live = (my_pos[None, :] < lengths[:, None]).reshape(mine, 1)

    grad_out = jnp.where(live, cotangent.astype(F32).reshape(mine, D), 0.0)
    proj = project(x_norm, w_attn).reshape(blocks, seqs, width, LANES)
    heads = [
        attend(s, proj, cosine, sine, gain_lanes, positions, lengths) for s in range(seqs)
    ]
    grad_low = gather_blocks(
        tie(grad_out.astype(BF16), x_norm),
        (lambda hold: (proj,), lambda hold: heads[0][:1], lambda hold: heads[1][:1], nothing),
    )
    out_rows = jnp.concatenate([out for out, _, _ in heads], axis=1)
    out_rows = out_rows.reshape(blocks * mine, 2 * HEAD_DIM)

    own, aside = kept["own"], kept["aside"]
    w_out = jnp.concatenate([o_weight, aside[:q_rows]], axis=0)
    w_gate_up = jnp.concatenate(
        [own[q_rows : q_rows + 2 * ff_rows], aside[q_rows : q_rows + 2 * ff_rows]], axis=0
    )
    w_down = jnp.concatenate([down_weight, aside[q_rows + 2 * ff_rows :]], axis=0)

    resid = x_rows + scatter_blocks(*partial_sums(out_rows, w_out))
    scale_two = rms_scale(resid)
    normed_two = resid * scale_two

    def hidden_grads(hold):
        kept["grad_hidden"] = project(*hold(grad_low, w_down))
        return (kept["grad_hidden"],)

    x_norm2 = gather_blocks(
        (normed_two * ffn_gain).astype(BF16), (hidden_grads, nothing, nothing, nothing)
    )
    both = project(x_norm2, w_gate_up)
    gate_part = jnp.concatenate([both[:, :ff_rows], both[:, 2 * ff_rows : 3 * ff_rows]], axis=1)
    up_part = jnp.concatenate([both[:, ff_rows : 2 * ff_rows], both[:, 3 * ff_rows :]], axis=1)
    hidden = (jax.nn.silu(gate_part) * up_part).astype(BF16)
    gate_low, up_low = gate_grads(kept["grad_hidden"], gate_part, up_part)
    gate_up_low = jnp.concatenate(
        [gate_low[:, :ff_rows], up_low[:, :ff_rows], gate_low[:, ff_rows:], up_low[:, ff_rows:]],
        axis=1,
    )

    def sent_aside(full):
        stay = full.shape[0] // 2
        return (full[:stay], send(full[stay:].astype(BF16), SWAP_X))

    def hidden_sums(hold):
        kept["out_parts"] = partial_sums(*hold(hidden, w_down))
        return kept["out_parts"]

    def gate_up_grads(hold):
        kept["gate_up"] = dot_rows(*hold(gate_up_low, x_norm2))
        return (kept["gate_up"],)

    def down_grads(hold):
        kept["down"] = dot_rows(*hold(hidden, grad_low))
        return (kept["down"],)

    grad_norm2 = scatter_blocks(
        *partial_sums(gate_up_low, w_gate_up), (nothing, hidden_sums, gate_up_grads, down_grads)
    )
    gate_up_stay, gate_up_come = sent_aside(kept["gate_up"])
    down_stay, down_come = sent_aside(kept["down"])
    grad_ffn_gain = jnp.sum(grad_norm2 * normed_two, axis=0)
    grad_resid = grad_out + rms_back(grad_norm2 * ffn_gain, normed_two, scale_two)
    grad_attn_low = gather_blocks(grad_resid.astype(BF16))

    grad_o = project(grad_attn_low, w_out).astype(BF16).reshape(blocks, seqs, width, 2 * HEAD_DIM)
    grads, gain_sums, back_out = [], 0.0, []
    for s, (out, lse, rotated) in enumerate(heads):
        grad_q, grad_kv = attend_back(s, rotated, grad_o, out, lse, positions, lengths)
        rows, sums = project_back(
            s, grad_q, grad_kv, send(grad_kv, SWAP_CORE), proj, cosine, sine, gain_lanes
        )
        back_out.append(grad_q)
        grads.append(rows)
        gain_sums = gain_sums + jnp.sum(sums, axis=0)
    out_sum = scatter_blocks(
        *tie(kept["out_parts"], grad_attn_low),
        (
            lambda hold: (grad_o,),
            lambda hold: (back_out[0],),
            lambda hold: (back_out[1],),
            lambda hold: grads,
        ),
    )
    block_out = (
        jnp.where(live, resid + out_sum, 0.0).astype(BF16).reshape(seqs, width, D)
    )
    grad_rows = jnp.concatenate(grads, axis=1).reshape(blocks * mine, LANES)
    row = jnp.arange(LANES)[:, None] // HEAD_DIM
    w_once = jnp.where((row < 2) | (row == 2 + core), w_attn, 0).astype(BF16)

    def out_grads(hold):
        kept["o_full"] = dot_rows(*hold(out_rows, grad_attn_low))
        return (kept["o_full"],)

    def attention_grads(hold):
        full = dot_rows(*hold(grad_rows, x_norm))
        kv_grads = full[2 * q_rows :].reshape(2, 2, 2, kv_rows, D)
        kv_mine = jnp.where(core == 0, kv_grads[:, 0], kv_grads[:, 1])
        kv_stay = jnp.where(side == 0, kv_mine[:, 0], kv_mine[:, 1])
        kv_leave = jnp.where(side == 0, kv_mine[:, 1], kv_mine[:, 0])
        stay = jnp.concatenate([full[:q_rows], kv_stay.reshape(2 * kv_rows, D)])
        leave = jnp.concatenate([full[q_rows : 2 * q_rows], kv_leave.reshape(2 * kv_rows, D)])
        kept["attn"] = (stay, send(leave.astype(BF16), SWAP_X))
        return (stay,)

    def feed_forward_sums(hold):
        stay = hold(gate_up_stay, gate_up_come, down_stay, down_come)
        kept["ff"] = (stay[0] + stay[1].astype(F32), stay[2] + stay[3].astype(F32))
        return kept["ff"]

    grad_norm1 = scatter_blocks(
        *partial_sums(grad_rows, w_once),
        (nothing, attention_grads, out_grads, feed_forward_sums),
    )
    gate_up_grad, down_grad = kept["ff"]
    o_stay, o_come = sent_aside(kept["o_full"])
    o_grad = o_stay + o_come.astype(F32)
    attn_stay, attn_come = kept["attn"]
    attn_grads = attn_stay + attn_come.astype(F32)
    grad_tokens = (grad_resid + rms_back(grad_norm1 * attn_gain, normed_one, scale_one)).reshape(
        seqs, width, D
    )
    owned = jnp.concatenate([q_weight, k_weight, v_weight], axis=0).astype(F32)
    grad_attn_gain = jnp.sum(owned * attn_grads, axis=0) / attn_gain
    gains = total_sum(
        jnp.concatenate(
            [
                grad_attn_gain,
                grad_ffn_gain,
                gain_sums[:HEAD_DIM] + gain_sums[HEAD_DIM : 2 * HEAD_DIM],
                0.5 * gain_sums[2 * HEAD_DIM : 3 * HEAD_DIM],
            ]
        )
    )
    return (
        block_out,
        grad_tokens,
        attn_grads[:q_rows],
        attn_grads[q_rows : q_rows + kv_rows],
        attn_grads[q_rows + kv_rows :],
        o_grad,
        gate_up_grad[:ff_rows],
        gate_up_grad[ff_rows:],
        down_grad,
        gains[:D],
        gains[D : 2 * D],
        gains[2 * D : 2 * D + HEAD_DIM],
        gains[2 * D + HEAD_DIM :],
    )


def solution(mesh):
    body = split_local if fits_split(mesh) else local
    in_specs = (
        P("fsdp", "ctx", None),
        P("fsdp", "ctx", None),
        P(("ctx", "fsdp"), None),
        P(("ctx", "fsdp"), None),
        P(("ctx", "fsdp"), None),
        P(("ctx", "fsdp"), None),
        P(("ctx", "fsdp"), None),
        P(("ctx", "fsdp"), None),
        P(("ctx", "fsdp"), None),
        P(),
        P(),
        P(),
        P(),
        P("fsdp"),
        P(),
    )
    out_specs = (
        P("fsdp", "ctx", None),
        P("fsdp", "ctx", None),
        P(("ctx", "fsdp"), None),
        P(("ctx", "fsdp"), None),
        P(("ctx", "fsdp"), None),
        P(("ctx", "fsdp"), None),
        P(("ctx", "fsdp"), None),
        P(("ctx", "fsdp"), None),
        P(("ctx", "fsdp"), None),
        P(),
        P(),
        P(),
        P(),
    )
    return jax.shard_map(body, mesh=mesh, in_specs=in_specs, out_specs=out_specs, check_vma=False)
```

```python
import functools
import math

import jax
import jax.numpy as jnp
from jax import lax
from jax.experimental import pallas as pl
from jax.experimental.pallas import tpu as pltpu
from jax.sharding import PartitionSpec as P

D = 2048
HEADS = 32
KV_HEADS = 8
HEAD_DIM = 64
FF = 8192


EPS = 1e-05
THETA = 1000000.0
NEG = -1e30


def rms_scale(values):
    return lax.rsqrt(jnp.mean(values * values, axis=-1, keepdims=True) + EPS)


def rms_back(grad_normed, normed, scale_rows):
    return scale_rows * (
        grad_normed - normed * jnp.mean(grad_normed * normed, axis=-1, keepdims=True)
    )


def rope_tables(positions):
    half = HEAD_DIM // 2
    freq = THETA ** (-(jnp.arange(half, dtype=jnp.float32) * 2.0 / HEAD_DIM))
    angle = positions.astype(jnp.float32)[:, None] * freq[None, :]
    return (jnp.cos(angle), jnp.sin(angle))


def rotate(values, cosine, sine):
    half = values.shape[-1] // 2
    first = values[..., :half]
    second = values[..., half:]
    return jnp.concatenate(
        [first * cosine - second * sine, second * cosine + first * sine], axis=-1
    )


def slot_positions(pair_order, width_pair, first, count):
    slot = first + jnp.arange(count, dtype=jnp.int32)
    owner = slot // width_pair
    within = slot % width_pair
    half_blk = width_pair // 2
    pair = pair_order[owner]
    block_id = jnp.where(within < half_blk, pair, 2 * pair_order.shape[0] - 1 - pair)
    return block_id * half_blk + within % half_blk


def block_mask(query_pos, key_part, lengths):
    return (key_part[None, None, :] <= query_pos[None, :, None]) & (
        key_part[None, None, :] < lengths[:, None, None]
    )


def project(inputs, weight):
    return jnp.einsum("td,fd->tf", inputs, weight, preferred_element_type=jnp.float32)


def gate_grads(grad_hidden, gate_part, up_part):
    sigma = jax.nn.sigmoid(gate_part)
    grad_gate = grad_hidden * up_part * sigma * (1.0 + gate_part * (1.0 - sigma))
    grad_up = grad_hidden * gate_part * sigma
    return (grad_gate.astype(jnp.bfloat16), grad_up.astype(jnp.bfloat16))


def block_grads(q_rot, grad_o_low, lse, delta, k_blk, v_blk, allowed, scale):
    scores = (
        jnp.einsum("sqhgd,sjhd->sqhgj", q_rot, k_blk, preferred_element_type=jnp.float32) * scale
    )
    scores = jnp.where(allowed[:, :, None, None, :], scores, NEG)
    probs = jnp.exp(scores - lse[..., None])
    grad_probs = jnp.einsum(
        "sqhgd,sjhd->sqhgj", grad_o_low, v_blk, preferred_element_type=jnp.float32
    )
    grad_scores = (probs * (grad_probs - delta[..., None])).astype(jnp.bfloat16)
    return (probs, grad_scores)


def local(
    tokens,
    cotangent,
    q_weight,
    k_weight,
    v_weight,
    o_weight,
    gate_weight,
    up_weight,
    down_weight,
    attn_gain,
    ffn_gain,
    q_gain,
    k_gain,
    lengths,
    pair_order,
):
    seq_grp = tokens.shape[0]
    width_pair = tokens.shape[1]
    groups = HEADS // KV_HEADS
    q_width = HEADS * HEAD_DIM
    kv_width = KV_HEADS * HEAD_DIM
    scale = HEAD_DIM ** (-0.5)
    tok_rows = seq_grp * width_pair
    slots = width_pair * pair_order.shape[0]
    key_blk = math.gcd(slots, 512)
    key_count = slots // key_blk
    dev_count = lax.axis_size("ctx") * lax.axis_size("fsdp")
    local_pos = slot_positions(
        pair_order, width_pair, lax.axis_index("ctx") * width_pair, width_pair
    )
    key_pos = slot_positions(pair_order, width_pair, 0, slots)
    live_rows = (local_pos[None, :] < lengths[:, None]).reshape(tok_rows, 1)
    cosine, sine = rope_tables(local_pos)
    cosine = cosine[None, :, None, :]
    sine = sine[None, :, None, :]
    x_rows = tokens.astype(jnp.float32).reshape(tok_rows, D)
    scale_one = rms_scale(x_rows)
    normed_one = x_rows * scale_one
    x_norm = (normed_one * attn_gain).astype(jnp.bfloat16)
    w_query, w_key, w_value, w_out = (
        lax.all_gather(q_weight, ("ctx", "fsdp"), axis=0, tiled=True),
        lax.all_gather(k_weight, ("ctx", "fsdp"), axis=0, tiled=True),
        lax.all_gather(v_weight, ("ctx", "fsdp"), axis=0, tiled=True),
        lax.all_gather(o_weight, ("ctx", "fsdp"), axis=0, tiled=True),
    )
    q_proj = project(x_norm, w_query).reshape(seq_grp, width_pair, HEADS, HEAD_DIM)
    k_proj = project(x_norm, w_key).reshape(seq_grp, width_pair, KV_HEADS, HEAD_DIM)
    v_low = project(x_norm, w_value).astype(jnp.bfloat16).reshape(seq_grp, width_pair, kv_width)
    q_scale = rms_scale(q_proj)
    q_normed = q_proj * q_scale
    q_rot = (
        rotate(q_normed * q_gain, cosine, sine)
        .astype(jnp.bfloat16)
        .reshape(seq_grp, width_pair, KV_HEADS, groups, HEAD_DIM)
    )
    k_scale = rms_scale(k_proj)
    k_normed = k_proj * k_scale
    k_rot = (
        rotate(k_normed * k_gain, cosine, sine)
        .astype(jnp.bfloat16)
        .reshape(seq_grp, width_pair, kv_width)
    )
    k_all, v_all = (
        lax.all_gather(k_rot, "ctx", axis=1, tiled=True),
        lax.all_gather(v_low, "ctx", axis=1, tiled=True),
    )
    k_all = k_all.reshape(seq_grp, slots, KV_HEADS, HEAD_DIM)
    v_all = v_all.reshape(seq_grp, slots, KV_HEADS, HEAD_DIM)

    def key_slices(first, count):
        k_blk = lax.dynamic_slice_in_dim(k_all, first, count, 1)
        v_blk = lax.dynamic_slice_in_dim(v_all, first, count, 1)
        allowed = block_mask(local_pos, lax.dynamic_slice_in_dim(key_pos, first, count, 0), lengths)
        return (k_blk, v_blk, allowed)

    def forward_step(index, carry):
        top, total, summed = carry
        k_blk, v_blk, allowed = key_slices(index * key_blk, key_blk)
        scores = (
            jnp.einsum("sqhgd,sjhd->sqhgj", q_rot, k_blk, preferred_element_type=jnp.float32)
            * scale
        )
        scores = jnp.where(allowed[:, :, None, None, :], scores, NEG)
        new_top = jnp.maximum(top, jnp.max(scores, axis=-1))
        shrink = jnp.exp(top - new_top)
        probs = jnp.exp(scores - new_top[..., None])
        total = total * shrink + jnp.sum(probs, axis=-1)
        summed = summed * shrink[..., None] + jnp.einsum(
            "sqhgj,sjhd->sqhgd",
            probs.astype(jnp.bfloat16),
            v_blk,
            preferred_element_type=jnp.float32,
        )
        return (new_top, total, summed)

    stat_shape = (seq_grp, width_pair, KV_HEADS, groups)
    start_carry = (
        jnp.full(stat_shape, NEG, jnp.float32),
        jnp.zeros(stat_shape, jnp.float32),
        jnp.zeros(stat_shape + (HEAD_DIM,), jnp.float32),
    )
    top, total, summed = lax.fori_loop(0, key_count, forward_step, start_carry)
    lse = top + jnp.log(total)
    o_low = (summed / total[..., None]).astype(jnp.bfloat16)
    o_rows = o_low.reshape(tok_rows, q_width)
    resid = x_rows + jnp.einsum("tf,fd->td", o_rows, w_out, preferred_element_type=jnp.float32)
    scale_two = rms_scale(resid)
    normed_two = resid * scale_two
    x_norm2 = (normed_two * ffn_gain).astype(jnp.bfloat16)
    grad_out = jnp.where(live_rows, cotangent.astype(jnp.float32).reshape(tok_rows, D), 0.0)
    grad_low = grad_out.astype(jnp.bfloat16)
    pieces = (
        lax.all_gather(gate_weight, ("ctx", "fsdp"), axis=0, tiled=True),
        lax.all_gather(up_weight, ("ctx", "fsdp"), axis=0, tiled=True),
        lax.all_gather(down_weight, ("ctx", "fsdp"), axis=0, tiled=True),
    )
    gate_part = project(x_norm2, pieces[0])
    up_part = project(x_norm2, pieces[1])
    hidden_part = (jax.nn.silu(gate_part) * up_part).astype(jnp.bfloat16)
    out_sum = jnp.einsum("tf,fd->td", hidden_part, pieces[2], preferred_element_type=jnp.float32)
    gate_all = gate_part
    up_all = up_part
    hidden = (jax.nn.silu(gate_all) * up_all).astype(jnp.bfloat16)
    pieces = (
        lax.all_gather(gate_weight, ("ctx", "fsdp"), axis=0, tiled=True),
        lax.all_gather(up_weight, ("ctx", "fsdp"), axis=0, tiled=True),
        lax.all_gather(down_weight, ("ctx", "fsdp"), axis=0, tiled=True),
    )
    count = pieces[0].shape[0]
    gate_part = gate_all
    up_part = up_all
    grad_gate_part, grad_up_part = gate_grads(project(grad_low, pieces[2]), gate_part, up_part)
    grad_sum = jnp.einsum(
        "tf,fd->td", grad_gate_part, pieces[0], preferred_element_type=jnp.float32
    ) + jnp.einsum("tf,fd->td", grad_up_part, pieces[1], preferred_element_type=jnp.float32)
    gate_grad_all = grad_gate_part
    up_grad_all = grad_up_part
    block_out = (
        jnp.where(live_rows, resid + out_sum, 0.0)
        .astype(jnp.bfloat16)
        .reshape(seq_grp, width_pair, D)
    )
    ffn_dev = FF // dev_count
    owners = lax.axis_size(("ctx", "fsdp")) * (3 * ffn_dev) // (3 * ffn_dev)
    first = jnp.int32(0) // (3 * ffn_dev) * ffn_dev
    grad_gate_part = jnp.einsum(
        "tf,td->fd", gate_grad_all, x_norm2, preferred_element_type=jnp.float32
    )
    grad_up_part = jnp.einsum("tf,td->fd", up_grad_all, x_norm2, preferred_element_type=jnp.float32)
    grad_down_part = jnp.einsum("tf,td->fd", hidden, grad_low, preferred_element_type=jnp.float32)
    stacked = jnp.stack(
        [
            grad_gate_part.reshape(owners, ffn_dev, D),
            grad_up_part.reshape(owners, ffn_dev, D),
            grad_down_part.reshape(owners, ffn_dev, D),
        ],
        axis=1,
    )
    ffn_grads = lax.psum_scatter(
        stacked.reshape(lax.axis_size(("ctx", "fsdp")) * (3 * ffn_dev), D),
        ("ctx", "fsdp"),
        scatter_dimension=0,
        tiled=True,
    )
    grad_ffn_gain = jnp.sum(grad_sum * normed_two, axis=0)
    grad_resid = grad_out + rms_back(grad_sum * ffn_gain, normed_two, scale_two)
    grad_attn_low = grad_resid.astype(jnp.bfloat16)
    grad_o_low = (
        project(grad_attn_low, w_out)
        .astype(jnp.bfloat16)
        .reshape(seq_grp, width_pair, KV_HEADS, groups, HEAD_DIM)
    )
    delta = jnp.sum(grad_o_low.astype(jnp.float32) * o_low.astype(jnp.float32), axis=-1)
    dq_zero = jnp.zeros((seq_grp, width_pair, KV_HEADS, groups, HEAD_DIM), jnp.float32)
    kv_cols = seq_grp * 2 * kv_width

    def key_value_grads(probs, grad_scores):
        grad_k_blk = (
            jnp.einsum("sqhgj,sqhgd->jshd", grad_scores, q_rot, preferred_element_type=jnp.float32)
            * scale
        )
        grad_v_blk = jnp.einsum(
            "sqhgj,sqhgd->jshd",
            probs.astype(jnp.bfloat16),
            grad_o_low,
            preferred_element_type=jnp.float32,
        )
        return jnp.stack([grad_k_blk, grad_v_blk], axis=2).reshape(probs.shape[-1], kv_cols)

    def both_step(grad_q, index):
        k_blk, v_blk, allowed = key_slices(index * key_blk, key_blk)
        probs, grad_scores = block_grads(
            q_rot, grad_o_low, lse, delta, k_blk, v_blk, allowed, scale
        )
        grad_q = (
            grad_q
            + jnp.einsum(
                "sqhgj,sjhd->sqhgd", grad_scores, k_blk, preferred_element_type=jnp.float32
            )
            * scale
        )
        return (grad_q, key_value_grads(probs, grad_scores))

    grad_q_rot, kv_blocks = lax.scan(both_step, dq_zero, jnp.arange(key_count))
    kv_grad = lax.psum_scatter(
        kv_blocks.reshape(slots, kv_cols), "ctx", scatter_dimension=0, tiled=True
    )
    kv_grad = jnp.transpose(
        kv_grad.reshape(width_pair, seq_grp, 2, KV_HEADS, HEAD_DIM), (1, 0, 2, 3, 4)
    )
    grad_q_pre = rotate(grad_q_rot.reshape(seq_grp, width_pair, HEADS, HEAD_DIM), cosine, -sine)
    grad_k_pre = rotate(kv_grad[:, :, 0], cosine, -sine)
    grad_q_gain = jnp.sum(grad_q_pre * q_normed, axis=(0, 1, 2))
    grad_k_gain = jnp.sum(grad_k_pre * k_normed, axis=(0, 1, 2))
    grad_q_proj = (
        rms_back(grad_q_pre * q_gain, q_normed, q_scale)
        .reshape(tok_rows, q_width)
        .astype(jnp.bfloat16)
    )
    grad_k_proj = (
        rms_back(grad_k_pre * k_gain, k_normed, k_scale)
        .reshape(tok_rows, kv_width)
        .astype(jnp.bfloat16)
    )
    grad_v_proj = kv_grad[:, :, 1].reshape(tok_rows, kv_width).astype(jnp.bfloat16)
    grad_norm1 = jnp.einsum("tf,fd->td", grad_q_proj, w_query, preferred_element_type=jnp.float32)
    grad_norm1 = grad_norm1 + jnp.einsum(
        "tf,fd->td", grad_k_proj, w_key, preferred_element_type=jnp.float32
    )
    grad_norm1 = grad_norm1 + jnp.einsum(
        "tf,fd->td", grad_v_proj, w_value, preferred_element_type=jnp.float32
    )
    grad_attn_gain = jnp.sum(grad_norm1 * normed_one, axis=0)
    grad_tokens = (grad_resid + rms_back(grad_norm1 * attn_gain, normed_one, scale_one)).reshape(
        seq_grp, width_pair, D
    )
    q_dev = q_width // dev_count
    kv_dev = kv_width // dev_count
    per_dev = 2 * q_dev + 2 * kv_dev
    owners = lax.axis_size(("ctx", "fsdp")) * per_dev // per_dev

    def rows_of(grad_rows, inputs, each):
        return jnp.einsum(
            "tf,td->fd", grad_rows, inputs, preferred_element_type=jnp.float32
        ).reshape(owners, each, D)

    joined = jnp.concatenate(
        [
            rows_of(grad_q_proj, x_norm, q_dev),
            rows_of(grad_k_proj, x_norm, kv_dev),
            rows_of(grad_v_proj, x_norm, kv_dev),
            rows_of(o_rows, grad_attn_low, q_dev),
        ],
        axis=1,
    )
    attn_grads = lax.psum_scatter(
        joined.reshape(lax.axis_size(("ctx", "fsdp")) * per_dev, D),
        ("ctx", "fsdp"),
        scatter_dimension=0,
        tiled=True,
    )
    grad_attn_gain, grad_ffn_gain, grad_q_gain, grad_k_gain = lax.psum(
        (grad_attn_gain, grad_ffn_gain, grad_q_gain, grad_k_gain), ("ctx", "fsdp")
    )
    return (
        block_out,
        grad_tokens,
        attn_grads[:q_dev],
        attn_grads[q_dev : q_dev + kv_dev],
        attn_grads[q_dev + kv_dev : q_dev + 2 * kv_dev],
        attn_grads[q_dev + 2 * kv_dev :],
        ffn_grads[:ffn_dev],
        ffn_grads[ffn_dev : 2 * ffn_dev],
        ffn_grads[2 * ffn_dev :],
        grad_attn_gain,
        grad_ffn_gain,
        grad_q_gain,
        grad_k_gain,
    )


AXES = ("ctx", "fsdp")
RANKS = 16
LANES = 4 * HEAD_DIM
BF16 = jnp.bfloat16
F32 = jnp.float32
FAR = 1 << 30


def fits_split(mesh):
    return mesh.shape["ctx"] == RANKS and mesh.shape["fsdp"] == 2


CYCLE = ((0, 0), (1, 0), (2, 0), (3, 0), (3, 1), (2, 1), (1, 1), (0, 1))
CHIPS = len(CYCLE)
DISTANCES = (4, 3, -3, 2, -2, 1, -1, 0)


def index_of(z, y, core, x):
    return z * 8 + y * 4 + core * 2 + x


def pairs_of(move):
    places = [(z, y, c, x) for z in range(4) for y in range(2) for c in range(2) for x in range(2)]
    return [(index_of(*place), index_of(*move(*place))) for place in places]


def along_cycle(step):
    def move(z, y, core, x):
        return (*CYCLE[(CYCLE.index((z, y)) + step) % CHIPS], core, x)

    return pairs_of(move)


SWAP_X = pairs_of(lambda z, y, c, x: (z, y, c, 1 - x))
SWAP_CORE = pairs_of(lambda z, y, c, x: (z, y, 1 - c, x))
SWAP_Y = pairs_of(lambda z, y, c, x: (z, 1 - y, c, x))
SWAP_Z0 = pairs_of(lambda z, y, c, x: (z ^ 1, y, c, x))
SWAP_Z1 = pairs_of(lambda z, y, c, x: (z ^ 2, y, c, x))
AHEAD = along_cycle(1)
BEHIND = along_cycle(-1)


def block_owners(rank):
    place = jnp.array([CYCLE.index((chip // 2, chip % 2)) for chip in range(CHIPS)], jnp.int32)
    chips = jnp.array([2 * z + y for z, y in CYCLE], jnp.int32)
    around = (place[rank // 2] + jnp.array(DISTANCES, jnp.int32)) % CHIPS
    core = rank % 2
    return jnp.concatenate([chips[around] * 2 + core, chips[around] * 2 + 1 - core])


def send(value, pairs):
    return lax.ppermute(value, AXES, pairs)


def tie(values, *others):
    return lax.optimization_barrier((values, others))[0]


def nothing(hold):
    return ()


def collect_kernel(starts, *refs):
    count = len(starts)
    pieces, (whole, held, come_sems, leave_sems) = refs[:count], refs[-4:]
    coming, leaving, at = [], [], 0
    for i, (piece, start) in enumerate(zip(pieces, starts)):
        part = held.at[pl.ds(at, piece.shape[0])]
        at += piece.shape[0]
        coming.append(pltpu.make_async_copy(piece, part, come_sems.at[i]))
        place = whole.at[pl.ds(start, piece.shape[0])]
        leaving.append(pltpu.make_async_copy(part, place, leave_sems.at[i]))
    for copy in coming:
        copy.start()
    for come, leave in zip(coming, leaving):
        come.wait()
        leave.start()
    for copy in leaving:
        copy.wait()


def collect(pieces, starts, whole):
    inner = functools.partial(collect_kernel, starts)
    given = isinstance(whole, jax.Array)
    anywhere = pl.BlockSpec(memory_space=pl.ANY)
    rows = sum(piece.shape[0] for piece in pieces)
    return pl.pallas_call(
        inner,
        in_specs=[anywhere] * (len(pieces) + given),
        out_specs=anywhere,
        out_shape=jax.ShapeDtypeStruct(whole.shape, whole.dtype),
        scratch_shapes=[
            pltpu.VMEM((rows, whole.shape[1]), whole.dtype),
            pltpu.SemaphoreType.DMA((len(pieces),)),
            pltpu.SemaphoreType.DMA((len(pieces),)),
        ],
        input_output_aliases={len(pieces): 0} if given else {},
        cost_estimate=cost_of(0.3 * len(pieces)),
        name="collect",
    )(*pieces, *([whole] if given else []))


def gather_blocks(piece, slots=(nothing,) * 4):
    rows = piece.shape[0]
    half = rows // 2
    back, front = [piece], [piece]
    for step, slot in enumerate(slots):
        to_ahead, to_behind = back[-1], front[-1]
        if step == 3:
            to_ahead, to_behind = to_ahead[:half], to_behind[half:]
        come = (send(to_ahead, AHEAD), send(to_behind, BEHIND))
        before = (back[-1], front[-1])
        done = slot(lambda *xs: tie(xs, before) if step else xs)
        come = tie(come, *done)
        back.append(come[0])
        front.append(come[1])
    late = [back[4], front[4]]
    late_starts = (0, half)
    early = [front[3], back[3], front[2], back[2], front[1], back[1], piece]
    early_starts = tuple(rows * (1 + i) for i in range(len(early)))
    across = CHIPS * rows
    full = jax.ShapeDtypeStruct((2 * across, piece.shape[1]), piece.dtype)
    whole = collect(
        early + [send(block, SWAP_CORE) for block in early],
        early_starts + tuple(across + start for start in early_starts),
        full,
    )
    return collect(
        late + [send(block, SWAP_CORE) for block in late],
        late_starts + tuple(across + start for start in late_starts),
        whole,
    )


def add_low(left, right):
    return (left.astype(F32) + right.astype(F32)).astype(BF16)


def partial_sums(rows, weight):
    own, other = jnp.split(rows, 2)
    cut = 3 * (own.shape[0] // CHIPS)
    halves = []
    for part in (slice(0, cut), slice(cut, None)):
        come = send(plain(other[part], weight).astype(BF16), SWAP_CORE)
        halves.append((own[part], come))
    return tuple((plain(mine, weight) + come.astype(F32)).astype(BF16) for mine, come in halves)


def scatter_blocks(first, rest, slots=(nothing,) * 4):
    rows = first.shape[0] // 3
    half = rows // 2
    come = (send(first[:half], AHEAD), send(first[half:rows], BEHIND))
    come = tie(come, *slots[0](lambda *xs: xs))
    ahead, behind = first[rows : 2 * rows], first[2 * rows :]
    leave = (
        jnp.concatenate([add_low(ahead[:half], come[0]), ahead[half:]]),
        jnp.concatenate([behind[:half], add_low(behind[half:], come[1])]),
    )
    for step in (1, 2, 3):
        before = leave
        come = (send(leave[0], AHEAD), send(leave[1], BEHIND))
        come = tie(come, *slots[step](lambda *xs: tie(xs, before)))
        at = (step - 1) * 2 * rows
        if step < 3:
            leave = (
                add_low(rest[at : at + rows], come[0]),
                add_low(rest[at + rows : at + 2 * rows], come[1]),
            )
    return rest[4 * rows :].astype(F32) + come[0].astype(F32) + come[1].astype(F32)


def total_sum(value):
    for pairs in (SWAP_CORE, SWAP_X, SWAP_Y, SWAP_Z0, SWAP_Z1):
        value = value + send(value, pairs)
    return value


def head_sums():
    row = lax.broadcasted_iota(jnp.int32, (LANES, LANES), 0) // HEAD_DIM
    col = lax.broadcasted_iota(jnp.int32, (LANES, LANES), 1) // HEAD_DIM
    return jnp.where(row == col, 1.0 / HEAD_DIM, 0.0).astype(BF16)


def head_mean(values):
    high = values.astype(BF16)
    rest = (values - high.astype(F32)).astype(BF16)
    sums = head_sums()
    return plain(high, sums) + plain(rest, sums)


def swap_halves(values):
    lane = lax.broadcasted_iota(jnp.int32, values.shape, 1)
    return jnp.where(
        lane % HEAD_DIM < HEAD_DIM // 2,
        pltpu.roll(values, LANES - HEAD_DIM // 2, 1),
        pltpu.roll(values, HEAD_DIM // 2, 1),
    )


def twice(ref):
    return jnp.concatenate([ref[...]] * 2, axis=1)


def dot_lanes(left, right):
    return lax.dot_general(left, right, (((1,), (1,)), ((), ())), preferred_element_type=F32)


def allowed_of(length, pos_col_ref, pos_row_ref):
    col = pos_col_ref[...]
    return jnp.where(col < length, col, FAR) <= pos_row_ref[...]


def rows_of_ref(ref):
    value = ref[...]
    return value.reshape(-1, value.shape[-1])


def attend_kernel(
    length_ref, proj_ref, cos_ref, sin_ref, gain_ref, pos_col_ref, pos_row_ref,
    out_ref, lse_ref, rot_ref, val_ref,
):
    step = pl.program_id(0)
    block = lse_ref.shape[-1]

    @pl.when(step == 0)
    def _():
        proj = rows_of_ref(proj_ref)
        normed = proj * lax.rsqrt(head_mean(proj * proj) + EPS) * gain_ref[...]
        rotated = normed * twice(cos_ref) + swap_halves(normed) * twice(sin_ref)
        lane = lax.broadcasted_iota(jnp.int32, proj.shape, 1)
        rotated = jnp.where(lane < 2 * HEAD_DIM, rotated * HEAD_DIM**-0.5, rotated)
        rot_ref[...] = jnp.where(lane < 3 * HEAD_DIM, rotated, proj).astype(BF16)
        val_ref[:HEAD_DIM, :] = proj[:, 3 * HEAD_DIM :].T.astype(BF16)
        val_ref[HEAD_DIM:, :] = jnp.ones((16, proj.shape[0]), BF16)

    allowed = allowed_of(length_ref[0], pos_col_ref, pos_row_ref)
    keys = rot_ref[:, 2 * HEAD_DIM : 3 * HEAD_DIM]
    query = rot_ref[pl.ds(pl.multiple_of(step * block, block), block), : 2 * HEAD_DIM]
    outs = []
    for head in range(2):
        scores = dot_lanes(keys, query[:, head * HEAD_DIM : (head + 1) * HEAD_DIM])
        weights = jnp.where(allowed, jnp.exp(scores), 0.0).astype(BF16)
        summed = jnp.dot(val_ref[...], weights, preferred_element_type=F32)
        total = summed[HEAD_DIM : HEAD_DIM + 1]
        outs.append((summed[:HEAD_DIM] / total).T)
        lse_ref[head : head + 1, :] = jnp.log(total)
    out_ref[...] = jnp.concatenate(outs, axis=1).astype(BF16).reshape(out_ref.shape)


def fixed(shape):
    return pl.BlockSpec(shape, lambda i: (0,) * len(shape))


def of_seq(seq, blocks, width, lanes):
    return pl.BlockSpec((blocks, 1, width, lanes), lambda i: (0, seq, 0, 0))


def part_of_seq(seq, blocks, width, lanes):
    return pl.BlockSpec((blocks, 1, width, lanes), lambda i: (i, seq, 0, 0))


def cost_of(microseconds):
    return pl.CostEstimate(
        flops=int(microseconds * 6e8), transcendentals=0, bytes_accessed=int(microseconds * 2.5e6)
    )


STEPS = 4


def attend(seq, proj, cosine, sine, gain, positions, lengths):
    blocks, _, width, _ = proj.shape
    slots = blocks * width
    part = slots // STEPS
    return pl.pallas_call(
        attend_kernel,
        grid=(STEPS,),
        in_specs=[
            pl.BlockSpec(memory_space=pltpu.SMEM),
            of_seq(seq, blocks, width, LANES),
            fixed((slots, LANES // 2)),
            fixed((slots, LANES // 2)),
            fixed((1, LANES)),
            fixed((slots, 1)),
            pl.BlockSpec((1, part), lambda i: (0, i)),
        ],
        out_specs=[
            part_of_seq(0, blocks // STEPS, width, 2 * HEAD_DIM),
            pl.BlockSpec((2, part), lambda i: (0, i)),
            fixed((slots, LANES)),
        ],
        out_shape=[
            jax.ShapeDtypeStruct((blocks, 1, width, 2 * HEAD_DIM), BF16),
            jax.ShapeDtypeStruct((2, slots), F32),
            jax.ShapeDtypeStruct((slots, LANES), BF16),
        ],
        scratch_shapes=[pltpu.VMEM((HEAD_DIM + 16, slots), BF16)],
        cost_estimate=cost_of(8),
        name="attend",
    )(lengths[seq : seq + 1], proj, cosine, sine, gain, positions[:, None], positions[None, :])


def attend_back_kernel(
    length_ref, rot_ref, query_ref, grad_ref, out_ref, lse_ref, pos_col_ref, pos_row_ref,
    dq_ref, dkv_ref,
):
    step = pl.program_id(0)
    allowed = allowed_of(length_ref[0], pos_col_ref, pos_row_ref)
    keys = rot_ref[:, 2 * HEAD_DIM : 3 * HEAD_DIM]
    values = rot_ref[:, 3 * HEAD_DIM :]
    query = query_ref[:, : 2 * HEAD_DIM]
    grad = rows_of_ref(grad_ref)
    product = grad.astype(F32) * rows_of_ref(out_ref).astype(F32)
    ones = jnp.ones((8, HEAD_DIM), F32)
    grad_q, grad_k, grad_v = [], 0.0, 0.0
    for head in range(2):
        cut = slice(head * HEAD_DIM, (head + 1) * HEAD_DIM)
        delta = lax.dot_general(
            ones,
            product[:, cut],
            (((1,), (1,)), ((), ())),
            precision=lax.Precision.HIGHEST,
            preferred_element_type=F32,
        )[:1]
        scores = dot_lanes(keys, query[:, cut])
        probs = jnp.where(allowed, jnp.exp(scores - lse_ref[head : head + 1, :]), 0.0)
        grad_probs = dot_lanes(values, grad[:, cut])
        grad_scores = (probs * (grad_probs - delta)).astype(BF16)
        grad_v += jnp.dot(probs.astype(BF16), grad[:, cut], preferred_element_type=F32)
        grad_k += jnp.dot(grad_scores, query[:, cut], preferred_element_type=F32)
        grad_q.append(
            lax.dot_general(
                grad_scores, keys, (((0,), (0,)), ((), ())), preferred_element_type=F32
            )
        )
    dq_ref[...] = jnp.concatenate(grad_q, axis=1) * HEAD_DIM**-0.5
    both = jnp.concatenate([grad_k, grad_v], axis=1)

    @pl.when(step == 0)
    def _():
        dkv_ref[...] = both

    @pl.when(step > 0)
    def _():
        dkv_ref[...] += both


def attend_back(seq, rotated, grad, out, lse, positions, lengths):
    blocks, _, width, _ = grad.shape
    slots = blocks * width
    part = slots // STEPS
    return pl.pallas_call(
        attend_back_kernel,
        grid=(STEPS,),
        in_specs=[
            pl.BlockSpec(memory_space=pltpu.SMEM),
            fixed((slots, LANES)),
            pl.BlockSpec((part, LANES), lambda i: (i, 0)),
            part_of_seq(seq, blocks // STEPS, width, 2 * HEAD_DIM),
            part_of_seq(0, blocks // STEPS, width, 2 * HEAD_DIM),
            pl.BlockSpec((2, part), lambda i: (0, i)),
            fixed((slots, 1)),
            pl.BlockSpec((1, part), lambda i: (0, i)),
        ],
        out_specs=[
            pl.BlockSpec((part, 2 * HEAD_DIM), lambda i: (i, 0)),
            fixed((slots, 2 * HEAD_DIM)),
        ],
        out_shape=[jax.ShapeDtypeStruct((slots, 2 * HEAD_DIM), F32)] * 2,
        cost_estimate=cost_of(10),
        name="attend_back",
    )(
        lengths[seq : seq + 1], rotated, rotated, grad, out, lse,
        positions[:, None], positions[None, :],
    )


def project_back_kernel(
    dq_ref, dkv_ref, other_ref, proj_ref, cos_ref, sin_ref, gain_ref, grad_ref, sum_ref
):
    step = pl.program_id(0)
    grad = jnp.concatenate([dq_ref[...], dkv_ref[...] + other_ref[...]], axis=1)
    proj = rows_of_ref(proj_ref)
    scale_rows = lax.rsqrt(head_mean(proj * proj) + EPS)
    normed = proj * scale_rows
    turned = grad * twice(cos_ref) - swap_halves(grad) * twice(sin_ref)
    gained = turned * gain_ref[...]
    back = scale_rows * (gained - normed * head_mean(gained * normed))
    lane = lax.broadcasted_iota(jnp.int32, proj.shape, 1)
    grad_ref[...] = jnp.where(lane < 3 * HEAD_DIM, back, grad).astype(BF16).reshape(grad_ref.shape)
    sums = jnp.sum((turned * normed).reshape(-1, 8, LANES), axis=0)

    @pl.when(step == 0)
    def _():
        sum_ref[...] = sums

    @pl.when(step > 0)
    def _():
        sum_ref[...] += sums


def project_back(seq, grad_q, grad_kv, other_kv, proj, cosine, sine, gain):
    blocks, _, width, _ = proj.shape
    some = blocks // STEPS
    part = some * width
    half = pl.BlockSpec((part, 2 * HEAD_DIM), lambda i: (i, 0))
    turned = pl.BlockSpec((part, 2 * HEAD_DIM), lambda i: ((i + STEPS // 2) % STEPS, 0))
    table = pl.BlockSpec((part, LANES // 2), lambda i: (i, 0))
    return pl.pallas_call(
        project_back_kernel,
        grid=(STEPS,),
        in_specs=[
            half, half, turned, part_of_seq(seq, some, width, LANES), table, table,
            fixed((1, LANES)),
        ],
        out_specs=[part_of_seq(0, some, width, LANES), fixed((8, LANES))],
        out_shape=[
            jax.ShapeDtypeStruct((blocks, 1, width, LANES), BF16),
            jax.ShapeDtypeStruct((8, LANES), F32),
        ],
        cost_estimate=cost_of(3),
        name="project_back",
    )(grad_q, grad_kv, other_kv, proj, cosine, sine, gain)


def dot_rows(left, right):
    return lax.dot_general(left, right, (((0,), (0,)), ((), ())), preferred_element_type=F32)


def plain(left, right):
    return jnp.dot(left, right, preferred_element_type=F32)


def in_order(own, other, index):
    first = index == 0
    return jnp.concatenate([jnp.where(first, own, other), jnp.where(first, other, own)], axis=0)


def split_local(
    tokens, cotangent, q_weight, k_weight, v_weight, o_weight, gate_weight, up_weight,
    down_weight, attn_gain, ffn_gain, q_gain, k_gain, lengths, pair_order,
):
    seqs, width, _ = tokens.shape
    rank = lax.axis_index("ctx")
    side = lax.axis_index("fsdp")
    core = rank % 2
    mine = seqs * width
    q_rows, kv_rows, ff_rows = q_weight.shape[0], k_weight.shape[0], gate_weight.shape[0]

    x_rows = tokens.astype(F32).reshape(mine, D)
    scale_one = rms_scale(x_rows)
    normed_one = x_rows * scale_one
    kept = {}

    owners = block_owners(rank)
    blocks = owners.shape[0]
    within = jnp.arange(width, dtype=jnp.int32)
    half_blk = width // 2

    def positions_of(dealt):
        block_id = jnp.where(
            within[None, :] < half_blk, dealt[:, None], 2 * pair_order.shape[0] - 1 - dealt[:, None]
        )
        return (block_id * half_blk + within[None, :] % half_blk).reshape(-1)

    def tables(hold):
        positions = positions_of(pair_order[owners])
        cosine, sine = rope_tables(positions)
        kept["positions"] = positions
        kept["tables"] = (
            jnp.concatenate([cosine] * 4, axis=1),
            jnp.concatenate([-sine, sine] * 2, axis=1),
        )
        return kept["tables"]

    def attention_weights(hold):
        kv_own = jnp.stack([k_weight, v_weight])
        kv_side = send(kv_own, SWAP_X)
        kv_half = jnp.concatenate(
            [jnp.where(side == 0, kv_own, kv_side), jnp.where(side == 0, kv_side, kv_own)], axis=1
        )
        kv_core = send(kv_half, SWAP_CORE)
        kv_full = jnp.concatenate(
            [jnp.where(core == 0, kv_half, kv_core), jnp.where(core == 0, kv_core, kv_half)], axis=1
        )
        kept["w_attn"] = jnp.concatenate(
            [q_weight, send(q_weight, SWAP_X), kv_full[0], kv_full[1]], axis=0
        )
        return (kept["w_attn"],)

    def other_weights(hold):
        own = jnp.concatenate([o_weight, *hold(gate_weight, up_weight, down_weight)], axis=0)
        kept["own"], kept["aside"] = own, send(own, SWAP_X)
        return (own,)

    x_norm = gather_blocks(
        (normed_one * attn_gain).astype(BF16), (tables, attention_weights, other_weights, nothing)
    )
    positions, (cosine, sine), w_attn = kept["positions"], kept["tables"], kept["w_attn"]
    gain_lanes = jnp.concatenate([q_gain, q_gain, k_gain, jnp.ones((HEAD_DIM,), F32)])[None, :]
    my_pos = positions_of(pair_order[rank][None])
    live = (my_pos[None, :] < lengths[:, None]).reshape(mine, 1)

    grad_out = jnp.where(live, cotangent.astype(F32).reshape(mine, D), 0.0)
    proj = project(x_norm, w_attn).reshape(blocks, seqs, width, LANES)
    heads = [
        attend(s, proj, cosine, sine, gain_lanes, positions, lengths) for s in range(seqs)
    ]
    grad_low = gather_blocks(
        tie(grad_out.astype(BF16), x_norm),
        (lambda hold: (proj,), lambda hold: heads[0][:1], lambda hold: heads[1][:1], nothing),
    )
    out_rows = jnp.concatenate([out for out, _, _ in heads], axis=1)
    out_rows = out_rows.reshape(blocks * mine, 2 * HEAD_DIM)

    own, aside = kept["own"], kept["aside"]
    w_out = jnp.concatenate([o_weight, aside[:q_rows]], axis=0)
    w_gate_up = jnp.concatenate(
        [own[q_rows : q_rows + 2 * ff_rows], aside[q_rows : q_rows + 2 * ff_rows]], axis=0
    )
    w_down = jnp.concatenate([down_weight, aside[q_rows + 2 * ff_rows :]], axis=0)

    resid = x_rows + scatter_blocks(*partial_sums(out_rows, w_out))
    scale_two = rms_scale(resid)
    normed_two = resid * scale_two

    def hidden_grads(hold):
        kept["grad_hidden"] = project(*hold(grad_low, w_down))
        return (kept["grad_hidden"],)

    x_norm2 = gather_blocks(
        (normed_two * ffn_gain).astype(BF16), (hidden_grads, nothing, nothing, nothing)
    )
    both = project(x_norm2, w_gate_up)
    gate_part = jnp.concatenate([both[:, :ff_rows], both[:, 2 * ff_rows : 3 * ff_rows]], axis=1)
    up_part = jnp.concatenate([both[:, ff_rows : 2 * ff_rows], both[:, 3 * ff_rows :]], axis=1)
    hidden = (jax.nn.silu(gate_part) * up_part).astype(BF16)
    gate_low, up_low = gate_grads(kept["grad_hidden"], gate_part, up_part)
    gate_up_low = jnp.concatenate(
        [gate_low[:, :ff_rows], up_low[:, :ff_rows], gate_low[:, ff_rows:], up_low[:, ff_rows:]],
        axis=1,
    )

    def sent_aside(full):
        stay = full.shape[0] // 2
        return (full[:stay], send(full[stay:].astype(BF16), SWAP_X))

    def hidden_sums(hold):
        kept["out_parts"] = partial_sums(*hold(hidden, w_down))
        return kept["out_parts"]

    def gate_up_grads(hold):
        kept["gate_up"] = dot_rows(*hold(gate_up_low, x_norm2))
        return (kept["gate_up"],)

    def down_grads(hold):
        kept["down"] = dot_rows(*hold(hidden, grad_low))
        return (kept["down"],)

    grad_norm2 = scatter_blocks(
        *partial_sums(gate_up_low, w_gate_up), (nothing, hidden_sums, gate_up_grads, down_grads)
    )
    gate_up_stay, gate_up_come = sent_aside(kept["gate_up"])
    down_stay, down_come = sent_aside(kept["down"])
    grad_ffn_gain = jnp.sum(grad_norm2 * normed_two, axis=0)
    grad_resid = grad_out + rms_back(grad_norm2 * ffn_gain, normed_two, scale_two)
    grad_attn_low = gather_blocks(grad_resid.astype(BF16))

    grad_o = project(grad_attn_low, w_out).astype(BF16).reshape(blocks, seqs, width, 2 * HEAD_DIM)
    grads, gain_sums, back_out = [], 0.0, []
    for s, (out, lse, rotated) in enumerate(heads):
        grad_q, grad_kv = attend_back(s, rotated, grad_o, out, lse, positions, lengths)
        rows, sums = project_back(
            s, grad_q, grad_kv, send(grad_kv, SWAP_CORE), proj, cosine, sine, gain_lanes
        )
        back_out.append(grad_q)
        grads.append(rows)
        gain_sums = gain_sums + jnp.sum(sums, axis=0)
    out_sum = scatter_blocks(
        *tie(kept["out_parts"], grad_attn_low),
        (
            lambda hold: (grad_o,),
            lambda hold: (back_out[0],),
            lambda hold: (back_out[1],),
            lambda hold: grads,
        ),
    )
    block_out = (
        jnp.where(live, resid + out_sum, 0.0).astype(BF16).reshape(seqs, width, D)
    )
    grad_rows = jnp.concatenate(grads, axis=1).reshape(blocks * mine, LANES)
    row = jnp.arange(LANES)[:, None] // HEAD_DIM
    w_once = jnp.where((row < 2) | (row == 2 + core), w_attn, 0).astype(BF16)

    def out_grads(hold):
        kept["o_full"] = dot_rows(*hold(out_rows, grad_attn_low))
        return (kept["o_full"],)

    def attention_grads(hold):
        full = dot_rows(*hold(grad_rows, x_norm))
        kv_grads = full[2 * q_rows :].reshape(2, 2, 2, kv_rows, D)
        kv_mine = jnp.where(core == 0, kv_grads[:, 0], kv_grads[:, 1])
        kv_stay = jnp.where(side == 0, kv_mine[:, 0], kv_mine[:, 1])
        kv_leave = jnp.where(side == 0, kv_mine[:, 1], kv_mine[:, 0])
        stay = jnp.concatenate([full[:q_rows], kv_stay.reshape(2 * kv_rows, D)])
        leave = jnp.concatenate([full[q_rows : 2 * q_rows], kv_leave.reshape(2 * kv_rows, D)])
        kept["attn"] = (stay, send(leave.astype(BF16), SWAP_X))
        return (stay,)

    def feed_forward_sums(hold):
        stay = hold(gate_up_stay, gate_up_come, down_stay, down_come)
        kept["ff"] = (stay[0] + stay[1].astype(F32), stay[2] + stay[3].astype(F32))
        return kept["ff"]

    grad_norm1 = scatter_blocks(
        *partial_sums(grad_rows, w_once),
        (nothing, attention_grads, out_grads, feed_forward_sums),
    )
    gate_up_grad, down_grad = kept["ff"]
    o_stay, o_come = sent_aside(kept["o_full"])
    o_grad = o_stay + o_come.astype(F32)
    attn_stay, attn_come = kept["attn"]
    attn_grads = attn_stay + attn_come.astype(F32)
    grad_tokens = (grad_resid + rms_back(grad_norm1 * attn_gain, normed_one, scale_one)).reshape(
        seqs, width, D
    )
    owned = jnp.concatenate([q_weight, k_weight, v_weight], axis=0).astype(F32)
    grad_attn_gain = jnp.sum(owned * attn_grads, axis=0) / attn_gain
    gains = total_sum(
        jnp.concatenate(
            [
                grad_attn_gain,
                grad_ffn_gain,
                gain_sums[:HEAD_DIM] + gain_sums[HEAD_DIM : 2 * HEAD_DIM],
                0.5 * gain_sums[2 * HEAD_DIM : 3 * HEAD_DIM],
            ]
        )
    )
    return (
        block_out,
        grad_tokens,
        attn_grads[:q_rows],
        attn_grads[q_rows : q_rows + kv_rows],
        attn_grads[q_rows + kv_rows :],
        o_grad,
        gate_up_grad[:ff_rows],
        gate_up_grad[ff_rows:],
        down_grad,
        gains[:D],
        gains[D : 2 * D],
        gains[2 * D : 2 * D + HEAD_DIM],
        gains[2 * D + HEAD_DIM :],
    )


def solution(mesh):
    body = split_local if fits_split(mesh) else local
    in_specs = (
        P("fsdp", "ctx", None),
        P("fsdp", "ctx", None),
        P(("ctx", "fsdp"), None),
        P(("ctx", "fsdp"), None),
        P(("ctx", "fsdp"), None),
        P(("ctx", "fsdp"), None),
        P(("ctx", "fsdp"), None),
        P(("ctx", "fsdp"), None),
        P(("ctx", "fsdp"), None),
        P(),
        P(),
        P(),
        P(),
        P("fsdp"),
        P(),
    )
    out_specs = (
        P("fsdp", "ctx", None),
        P("fsdp", "ctx", None),
        P(("ctx", "fsdp"), None),
        P(("ctx", "fsdp"), None),
        P(("ctx", "fsdp"), None),
        P(("ctx", "fsdp"), None),
        P(("ctx", "fsdp"), None),
        P(("ctx", "fsdp"), None),
        P(("ctx", "fsdp"), None),
        P(),
        P(),
        P(),
        P(),
    )
    return jax.shard_map(body, mesh=mesh, in_specs=in_specs, out_specs=out_specs, check_vma=False)
```

```python
import functools
import math

import jax
import jax.numpy as jnp
from jax import lax
from jax.experimental import pallas as pl
from jax.experimental.pallas import tpu as pltpu
from jax.sharding import PartitionSpec as P

D = 2048
HEADS = 32
KV_HEADS = 8
HEAD_DIM = 64
FF = 8192


EPS = 1e-05
THETA = 1000000.0
NEG = -1e30


def rms_scale(values):
    return lax.rsqrt(jnp.mean(values * values, axis=-1, keepdims=True) + EPS)


def rms_back(grad_normed, normed, scale_rows):
    return scale_rows * (
        grad_normed - normed * jnp.mean(grad_normed * normed, axis=-1, keepdims=True)
    )


def rope_tables(positions):
    half = HEAD_DIM // 2
    freq = THETA ** (-(jnp.arange(half, dtype=jnp.float32) * 2.0 / HEAD_DIM))
    angle = positions.astype(jnp.float32)[:, None] * freq[None, :]
    return (jnp.cos(angle), jnp.sin(angle))


def rotate(values, cosine, sine):
    half = values.shape[-1] // 2
    first = values[..., :half]
    second = values[..., half:]
    return jnp.concatenate(
        [first * cosine - second * sine, second * cosine + first * sine], axis=-1
    )


def slot_positions(pair_order, width_pair, first, count):
    slot = first + jnp.arange(count, dtype=jnp.int32)
    owner = slot // width_pair
    within = slot % width_pair
    half_blk = width_pair // 2
    pair = pair_order[owner]
    block_id = jnp.where(within < half_blk, pair, 2 * pair_order.shape[0] - 1 - pair)
    return block_id * half_blk + within % half_blk


def block_mask(query_pos, key_part, lengths):
    return (key_part[None, None, :] <= query_pos[None, :, None]) & (
        key_part[None, None, :] < lengths[:, None, None]
    )


def project(inputs, weight):
    return jnp.einsum("td,fd->tf", inputs, weight, preferred_element_type=jnp.float32)


def gate_grads(grad_hidden, gate_part, up_part):
    sigma = jax.nn.sigmoid(gate_part)
    grad_gate = grad_hidden * up_part * sigma * (1.0 + gate_part * (1.0 - sigma))
    grad_up = grad_hidden * gate_part * sigma
    return (grad_gate.astype(jnp.bfloat16), grad_up.astype(jnp.bfloat16))


def block_grads(q_rot, grad_o_low, lse, delta, k_blk, v_blk, allowed, scale):
    scores = (
        jnp.einsum("sqhgd,sjhd->sqhgj", q_rot, k_blk, preferred_element_type=jnp.float32) * scale
    )
    scores = jnp.where(allowed[:, :, None, None, :], scores, NEG)
    probs = jnp.exp(scores - lse[..., None])
    grad_probs = jnp.einsum(
        "sqhgd,sjhd->sqhgj", grad_o_low, v_blk, preferred_element_type=jnp.float32
    )
    grad_scores = (probs * (grad_probs - delta[..., None])).astype(jnp.bfloat16)
    return (probs, grad_scores)


def local(
    tokens,
    cotangent,
    q_weight,
    k_weight,
    v_weight,
    o_weight,
    gate_weight,
    up_weight,
    down_weight,
    attn_gain,
    ffn_gain,
    q_gain,
    k_gain,
    lengths,
    pair_order,
):
    seq_grp = tokens.shape[0]
    width_pair = tokens.shape[1]
    groups = HEADS // KV_HEADS
    q_width = HEADS * HEAD_DIM
    kv_width = KV_HEADS * HEAD_DIM
    scale = HEAD_DIM ** (-0.5)
    tok_rows = seq_grp * width_pair
    slots = width_pair * pair_order.shape[0]
    key_blk = math.gcd(slots, 512)
    key_count = slots // key_blk
    dev_count = lax.axis_size("ctx") * lax.axis_size("fsdp")
    local_pos = slot_positions(
        pair_order, width_pair, lax.axis_index("ctx") * width_pair, width_pair
    )
    key_pos = slot_positions(pair_order, width_pair, 0, slots)
    live_rows = (local_pos[None, :] < lengths[:, None]).reshape(tok_rows, 1)
    cosine, sine = rope_tables(local_pos)
    cosine = cosine[None, :, None, :]
    sine = sine[None, :, None, :]
    x_rows = tokens.astype(jnp.float32).reshape(tok_rows, D)
    scale_one = rms_scale(x_rows)
    normed_one = x_rows * scale_one
    x_norm = (normed_one * attn_gain).astype(jnp.bfloat16)
    w_query, w_key, w_value, w_out = (
        lax.all_gather(q_weight, ("ctx", "fsdp"), axis=0, tiled=True),
        lax.all_gather(k_weight, ("ctx", "fsdp"), axis=0, tiled=True),
        lax.all_gather(v_weight, ("ctx", "fsdp"), axis=0, tiled=True),
        lax.all_gather(o_weight, ("ctx", "fsdp"), axis=0, tiled=True),
    )
    q_proj = project(x_norm, w_query).reshape(seq_grp, width_pair, HEADS, HEAD_DIM)
    k_proj = project(x_norm, w_key).reshape(seq_grp, width_pair, KV_HEADS, HEAD_DIM)
    v_low = project(x_norm, w_value).astype(jnp.bfloat16).reshape(seq_grp, width_pair, kv_width)
    q_scale = rms_scale(q_proj)
    q_normed = q_proj * q_scale
    q_rot = (
        rotate(q_normed * q_gain, cosine, sine)
        .astype(jnp.bfloat16)
        .reshape(seq_grp, width_pair, KV_HEADS, groups, HEAD_DIM)
    )
    k_scale = rms_scale(k_proj)
    k_normed = k_proj * k_scale
    k_rot = (
        rotate(k_normed * k_gain, cosine, sine)
        .astype(jnp.bfloat16)
        .reshape(seq_grp, width_pair, kv_width)
    )
    k_all, v_all = (
        lax.all_gather(k_rot, "ctx", axis=1, tiled=True),
        lax.all_gather(v_low, "ctx", axis=1, tiled=True),
    )
    k_all = k_all.reshape(seq_grp, slots, KV_HEADS, HEAD_DIM)
    v_all = v_all.reshape(seq_grp, slots, KV_HEADS, HEAD_DIM)

    def key_slices(first, count):
        k_blk = lax.dynamic_slice_in_dim(k_all, first, count, 1)
        v_blk = lax.dynamic_slice_in_dim(v_all, first, count, 1)
        allowed = block_mask(local_pos, lax.dynamic_slice_in_dim(key_pos, first, count, 0), lengths)
        return (k_blk, v_blk, allowed)

    def forward_step(index, carry):
        top, total, summed = carry
        k_blk, v_blk, allowed = key_slices(index * key_blk, key_blk)
        scores = (
            jnp.einsum("sqhgd,sjhd->sqhgj", q_rot, k_blk, preferred_element_type=jnp.float32)
            * scale
        )
        scores = jnp.where(allowed[:, :, None, None, :], scores, NEG)
        new_top = jnp.maximum(top, jnp.max(scores, axis=-1))
        shrink = jnp.exp(top - new_top)
        probs = jnp.exp(scores - new_top[..., None])
        total = total * shrink + jnp.sum(probs, axis=-1)
        summed = summed * shrink[..., None] + jnp.einsum(
            "sqhgj,sjhd->sqhgd",
            probs.astype(jnp.bfloat16),
            v_blk,
            preferred_element_type=jnp.float32,
        )
        return (new_top, total, summed)

    stat_shape = (seq_grp, width_pair, KV_HEADS, groups)
    start_carry = (
        jnp.full(stat_shape, NEG, jnp.float32),
        jnp.zeros(stat_shape, jnp.float32),
        jnp.zeros(stat_shape + (HEAD_DIM,), jnp.float32),
    )
    top, total, summed = lax.fori_loop(0, key_count, forward_step, start_carry)
    lse = top + jnp.log(total)
    o_low = (summed / total[..., None]).astype(jnp.bfloat16)
    o_rows = o_low.reshape(tok_rows, q_width)
    resid = x_rows + jnp.einsum("tf,fd->td", o_rows, w_out, preferred_element_type=jnp.float32)
    scale_two = rms_scale(resid)
    normed_two = resid * scale_two
    x_norm2 = (normed_two * ffn_gain).astype(jnp.bfloat16)
    grad_out = jnp.where(live_rows, cotangent.astype(jnp.float32).reshape(tok_rows, D), 0.0)
    grad_low = grad_out.astype(jnp.bfloat16)
    pieces = (
        lax.all_gather(gate_weight, ("ctx", "fsdp"), axis=0, tiled=True),
        lax.all_gather(up_weight, ("ctx", "fsdp"), axis=0, tiled=True),
        lax.all_gather(down_weight, ("ctx", "fsdp"), axis=0, tiled=True),
    )
    gate_part = project(x_norm2, pieces[0])
    up_part = project(x_norm2, pieces[1])
    hidden_part = (jax.nn.silu(gate_part) * up_part).astype(jnp.bfloat16)
    out_sum = jnp.einsum("tf,fd->td", hidden_part, pieces[2], preferred_element_type=jnp.float32)
    gate_all = gate_part
    up_all = up_part
    hidden = (jax.nn.silu(gate_all) * up_all).astype(jnp.bfloat16)
    pieces = (
        lax.all_gather(gate_weight, ("ctx", "fsdp"), axis=0, tiled=True),
        lax.all_gather(up_weight, ("ctx", "fsdp"), axis=0, tiled=True),
        lax.all_gather(down_weight, ("ctx", "fsdp"), axis=0, tiled=True),
    )
    count = pieces[0].shape[0]
    gate_part = gate_all
    up_part = up_all
    grad_gate_part, grad_up_part = gate_grads(project(grad_low, pieces[2]), gate_part, up_part)
    grad_sum = jnp.einsum(
        "tf,fd->td", grad_gate_part, pieces[0], preferred_element_type=jnp.float32
    ) + jnp.einsum("tf,fd->td", grad_up_part, pieces[1], preferred_element_type=jnp.float32)
    gate_grad_all = grad_gate_part
    up_grad_all = grad_up_part
    block_out = (
        jnp.where(live_rows, resid + out_sum, 0.0)
        .astype(jnp.bfloat16)
        .reshape(seq_grp, width_pair, D)
    )
    ffn_dev = FF // dev_count
    owners = lax.axis_size(("ctx", "fsdp")) * (3 * ffn_dev) // (3 * ffn_dev)
    first = jnp.int32(0) // (3 * ffn_dev) * ffn_dev
    grad_gate_part = jnp.einsum(
        "tf,td->fd", gate_grad_all, x_norm2, preferred_element_type=jnp.float32
    )
    grad_up_part = jnp.einsum("tf,td->fd", up_grad_all, x_norm2, preferred_element_type=jnp.float32)
    grad_down_part = jnp.einsum("tf,td->fd", hidden, grad_low, preferred_element_type=jnp.float32)
    stacked = jnp.stack(
        [
            grad_gate_part.reshape(owners, ffn_dev, D),
            grad_up_part.reshape(owners, ffn_dev, D),
            grad_down_part.reshape(owners, ffn_dev, D),
        ],
        axis=1,
    )
    ffn_grads = lax.psum_scatter(
        stacked.reshape(lax.axis_size(("ctx", "fsdp")) * (3 * ffn_dev), D),
        ("ctx", "fsdp"),
        scatter_dimension=0,
        tiled=True,
    )
    grad_ffn_gain = jnp.sum(grad_sum * normed_two, axis=0)
    grad_resid = grad_out + rms_back(grad_sum * ffn_gain, normed_two, scale_two)
    grad_attn_low = grad_resid.astype(jnp.bfloat16)
    grad_o_low = (
        project(grad_attn_low, w_out)
        .astype(jnp.bfloat16)
        .reshape(seq_grp, width_pair, KV_HEADS, groups, HEAD_DIM)
    )
    delta = jnp.sum(grad_o_low.astype(jnp.float32) * o_low.astype(jnp.float32), axis=-1)
    dq_zero = jnp.zeros((seq_grp, width_pair, KV_HEADS, groups, HEAD_DIM), jnp.float32)
    kv_cols = seq_grp * 2 * kv_width

    def key_value_grads(probs, grad_scores):
        grad_k_blk = (
            jnp.einsum("sqhgj,sqhgd->jshd", grad_scores, q_rot, preferred_element_type=jnp.float32)
            * scale
        )
        grad_v_blk = jnp.einsum(
            "sqhgj,sqhgd->jshd",
            probs.astype(jnp.bfloat16),
            grad_o_low,
            preferred_element_type=jnp.float32,
        )
        return jnp.stack([grad_k_blk, grad_v_blk], axis=2).reshape(probs.shape[-1], kv_cols)

    def both_step(grad_q, index):
        k_blk, v_blk, allowed = key_slices(index * key_blk, key_blk)
        probs, grad_scores = block_grads(
            q_rot, grad_o_low, lse, delta, k_blk, v_blk, allowed, scale
        )
        grad_q = (
            grad_q
            + jnp.einsum(
                "sqhgj,sjhd->sqhgd", grad_scores, k_blk, preferred_element_type=jnp.float32
            )
            * scale
        )
        return (grad_q, key_value_grads(probs, grad_scores))

    grad_q_rot, kv_blocks = lax.scan(both_step, dq_zero, jnp.arange(key_count))
    kv_grad = lax.psum_scatter(
        kv_blocks.reshape(slots, kv_cols), "ctx", scatter_dimension=0, tiled=True
    )
    kv_grad = jnp.transpose(
        kv_grad.reshape(width_pair, seq_grp, 2, KV_HEADS, HEAD_DIM), (1, 0, 2, 3, 4)
    )
    grad_q_pre = rotate(grad_q_rot.reshape(seq_grp, width_pair, HEADS, HEAD_DIM), cosine, -sine)
    grad_k_pre = rotate(kv_grad[:, :, 0], cosine, -sine)
    grad_q_gain = jnp.sum(grad_q_pre * q_normed, axis=(0, 1, 2))
    grad_k_gain = jnp.sum(grad_k_pre * k_normed, axis=(0, 1, 2))
    grad_q_proj = (
        rms_back(grad_q_pre * q_gain, q_normed, q_scale)
        .reshape(tok_rows, q_width)
        .astype(jnp.bfloat16)
    )
    grad_k_proj = (
        rms_back(grad_k_pre * k_gain, k_normed, k_scale)
        .reshape(tok_rows, kv_width)
        .astype(jnp.bfloat16)
    )
    grad_v_proj = kv_grad[:, :, 1].reshape(tok_rows, kv_width).astype(jnp.bfloat16)
    grad_norm1 = jnp.einsum("tf,fd->td", grad_q_proj, w_query, preferred_element_type=jnp.float32)
    grad_norm1 = grad_norm1 + jnp.einsum(
        "tf,fd->td", grad_k_proj, w_key, preferred_element_type=jnp.float32
    )
    grad_norm1 = grad_norm1 + jnp.einsum(
        "tf,fd->td", grad_v_proj, w_value, preferred_element_type=jnp.float32
    )
    grad_attn_gain = jnp.sum(grad_norm1 * normed_one, axis=0)
    grad_tokens = (grad_resid + rms_back(grad_norm1 * attn_gain, normed_one, scale_one)).reshape(
        seq_grp, width_pair, D
    )
    q_dev = q_width // dev_count
    kv_dev = kv_width // dev_count
    per_dev = 2 * q_dev + 2 * kv_dev
    owners = lax.axis_size(("ctx", "fsdp")) * per_dev // per_dev

    def rows_of(grad_rows, inputs, each):
        return jnp.einsum(
            "tf,td->fd", grad_rows, inputs, preferred_element_type=jnp.float32
        ).reshape(owners, each, D)

    joined = jnp.concatenate(
        [
            rows_of(grad_q_proj, x_norm, q_dev),
            rows_of(grad_k_proj, x_norm, kv_dev),
            rows_of(grad_v_proj, x_norm, kv_dev),
            rows_of(o_rows, grad_attn_low, q_dev),
        ],
        axis=1,
    )
    attn_grads = lax.psum_scatter(
        joined.reshape(lax.axis_size(("ctx", "fsdp")) * per_dev, D),
        ("ctx", "fsdp"),
        scatter_dimension=0,
        tiled=True,
    )
    grad_attn_gain, grad_ffn_gain, grad_q_gain, grad_k_gain = lax.psum(
        (grad_attn_gain, grad_ffn_gain, grad_q_gain, grad_k_gain), ("ctx", "fsdp")
    )
    return (
        block_out,
        grad_tokens,
        attn_grads[:q_dev],
        attn_grads[q_dev : q_dev + kv_dev],
        attn_grads[q_dev + kv_dev : q_dev + 2 * kv_dev],
        attn_grads[q_dev + 2 * kv_dev :],
        ffn_grads[:ffn_dev],
        ffn_grads[ffn_dev : 2 * ffn_dev],
        ffn_grads[2 * ffn_dev :],
        grad_attn_gain,
        grad_ffn_gain,
        grad_q_gain,
        grad_k_gain,
    )


AXES = ("ctx", "fsdp")
RANKS = 16
LANES = 4 * HEAD_DIM
BF16 = jnp.bfloat16
F32 = jnp.float32
FAR = 1 << 30


def fits_split(mesh):
    return mesh.shape["ctx"] == RANKS and mesh.shape["fsdp"] == 2


CYCLE = ((0, 0), (1, 0), (2, 0), (3, 0), (3, 1), (2, 1), (1, 1), (0, 1))
CHIPS = len(CYCLE)
DISTANCES = (4, 3, -3, 2, -2, 1, -1, 0)


def index_of(z, y, core, x):
    return z * 8 + y * 4 + core * 2 + x


def pairs_of(move):
    places = [(z, y, c, x) for z in range(4) for y in range(2) for c in range(2) for x in range(2)]
    return [(index_of(*place), index_of(*move(*place))) for place in places]


def along_cycle(step):
    def move(z, y, core, x):
        return (*CYCLE[(CYCLE.index((z, y)) + step) % CHIPS], core, x)

    return pairs_of(move)


SWAP_X = pairs_of(lambda z, y, c, x: (z, y, c, 1 - x))
SWAP_CORE = pairs_of(lambda z, y, c, x: (z, y, 1 - c, x))
SWAP_Y = pairs_of(lambda z, y, c, x: (z, 1 - y, c, x))
SWAP_Z0 = pairs_of(lambda z, y, c, x: (z ^ 1, y, c, x))
SWAP_Z1 = pairs_of(lambda z, y, c, x: (z ^ 2, y, c, x))
AHEAD = along_cycle(1)
BEHIND = along_cycle(-1)


def block_owners(rank):
    place = jnp.array([CYCLE.index((chip // 2, chip % 2)) for chip in range(CHIPS)], jnp.int32)
    chips = jnp.array([2 * z + y for z, y in CYCLE], jnp.int32)
    around = (place[rank // 2] + jnp.array(DISTANCES, jnp.int32)) % CHIPS
    core = rank % 2
    return jnp.concatenate([chips[around] * 2 + core, chips[around] * 2 + 1 - core])


def send(value, pairs):
    return lax.ppermute(value, AXES, pairs)


def window(moves, inputs=(), work=None):
    values, inputs = lax.optimization_barrier((tuple(v for v, _ in moves), tuple(inputs)))
    come = tuple(send(v, pairs) for v, (_, pairs) in zip(values, moves))
    done = work(*inputs) if work else ()
    return lax.optimization_barrier((come, done))


def idle(run):
    run()


def collect_kernel(starts, *refs):
    count = len(starts)
    pieces, (whole, held, come_sems, leave_sems) = refs[:count], refs[-4:]
    coming, leaving, at = [], [], 0
    for i, (piece, start) in enumerate(zip(pieces, starts)):
        part = held.at[pl.ds(at, piece.shape[0])]
        at += piece.shape[0]
        coming.append(pltpu.make_async_copy(piece, part, come_sems.at[i]))
        place = whole.at[pl.ds(start, piece.shape[0])]
        leaving.append(pltpu.make_async_copy(part, place, leave_sems.at[i]))
    for copy in coming:
        copy.start()
    for come, leave in zip(coming, leaving):
        come.wait()
        leave.start()
    for copy in leaving:
        copy.wait()


def collect(pieces, starts, whole):
    inner = functools.partial(collect_kernel, starts)
    given = isinstance(whole, jax.Array)
    anywhere = pl.BlockSpec(memory_space=pl.ANY)
    rows = sum(piece.shape[0] for piece in pieces)
    return pl.pallas_call(
        inner,
        in_specs=[anywhere] * (len(pieces) + given),
        out_specs=anywhere,
        out_shape=jax.ShapeDtypeStruct(whole.shape, whole.dtype),
        scratch_shapes=[
            pltpu.VMEM((rows, whole.shape[1]), whole.dtype),
            pltpu.SemaphoreType.DMA((len(pieces),)),
            pltpu.SemaphoreType.DMA((len(pieces),)),
        ],
        input_output_aliases={len(pieces): 0} if given else {},
        cost_estimate=cost_of(0.3 * len(pieces)),
        name="collect",
    )(*pieces, *([whole] if given else []))


def gather_blocks(piece, slots=(idle,) * 4):
    rows = piece.shape[0]
    half = rows // 2
    across = CHIPS * rows
    back, front = [piece], [piece]
    other = {}
    for step, slot in enumerate(slots):
        leave = (back[-1], front[-1])
        if step == 3:
            leave = (back[-1][:half], front[-1][half:])

        def run(inputs=(), work=None, moves=()):
            both = [(leave[0], AHEAD), (leave[1], BEHIND), *moves]
            come, done = window(both, inputs, work)
            back.append(come[0])
            front.append(come[1])
            return come[2:], done

        slot(run)

    def stage(steps, whole):
        parts, starts = [], []
        for step in steps:
            if step == 0:
                found = [(piece, across - rows)]
            elif step == 4:
                found = [(back[4], 0), (front[4], half)]
            else:
                at = (7 - 2 * step) * rows
                found = [(front[step], at), (back[step], at + rows)]
            for part, start in found:
                parts += [part, send(part, SWAP_CORE)]
                starts += [start, across + start]
        return collect(parts, tuple(starts), whole)

    whole = stage((0, 1, 2, 3), jax.ShapeDtypeStruct((2 * across, piece.shape[1]), piece.dtype))
    return stage((4,), whole)


def add_low(left, right):
    return (left.astype(F32) + right.astype(F32)).astype(BF16)


def partial_sums(rows, weight):
    own, other = jnp.split(rows, 2)
    cut = 3 * (own.shape[0] // CHIPS)
    first = send(plain(other[:cut], weight).astype(BF16), SWAP_CORE)
    rest = send(plain(other[cut:], weight).astype(BF16), SWAP_CORE)
    first = (plain(own[:cut], weight) + first.astype(F32)).astype(BF16)
    return first, (own[cut:], weight, rest)


def rest_of(own, weight, come):
    return (plain(own, weight) + come.astype(F32)).astype(BF16)


def scatter_blocks(first, rest, slots=(idle,) * 4):
    rows = first.shape[0] // 3
    half = rows // 2
    state = {"rest": rest}

    def stepper(leave, given, own_work):
        def run(inputs=(), work=None, moves=()):
            both = [(leave[0], AHEAD), (leave[1], BEHIND), *moves]
            count = len(given)

            def all_work(*xs):
                mine = (own_work(*xs[:count]),) if count else ()
                return mine + tuple(work(*xs[count:]) if work else ())

            come, done = window(both, tuple(given) + tuple(inputs), all_work)
            state["come"] = come[:2]
            if count:
                state["rest"] = done[0]
                done = done[1:]
            return come[2:], done

        return run

    given = rest if isinstance(rest, tuple) else ()
    slots[0](stepper((first[:half], first[half:rows]), given, rest_of))
    ahead, behind = first[rows : 2 * rows], first[2 * rows :]
    come, rest = state["come"], state["rest"]
    leave = (
        jnp.concatenate([add_low(ahead[:half], come[0]), ahead[half:]]),
        jnp.concatenate([behind[:half], add_low(behind[half:], come[1])]),
    )
    for step in (1, 2, 3):
        slots[step](stepper(leave, (), None))
        come = state["come"]
        at = (step - 1) * 2 * rows
        if step < 3:
            leave = (
                add_low(rest[at : at + rows], come[0]),
                add_low(rest[at + rows : at + 2 * rows], come[1]),
            )
    return rest[4 * rows :].astype(F32) + come[0].astype(F32) + come[1].astype(F32)


def total_sum(value):
    for pairs in (SWAP_CORE, SWAP_X, SWAP_Y, SWAP_Z0, SWAP_Z1):
        value = value + send(value, pairs)
    return value


def head_sums():
    row = lax.broadcasted_iota(jnp.int32, (LANES, LANES), 0) // HEAD_DIM
    col = lax.broadcasted_iota(jnp.int32, (LANES, LANES), 1) // HEAD_DIM
    return jnp.where(row == col, 1.0 / HEAD_DIM, 0.0).astype(BF16)


def head_mean(values):
    high = values.astype(BF16)
    rest = (values - high.astype(F32)).astype(BF16)
    sums = head_sums()
    return plain(high, sums) + plain(rest, sums)


def swap_halves(values):
    lane = lax.broadcasted_iota(jnp.int32, values.shape, 1)
    return jnp.where(
        lane % HEAD_DIM < HEAD_DIM // 2,
        pltpu.roll(values, LANES - HEAD_DIM // 2, 1),
        pltpu.roll(values, HEAD_DIM // 2, 1),
    )


def twice(ref):
    return jnp.concatenate([ref[...]] * 2, axis=1)


def dot_lanes(left, right):
    return lax.dot_general(left, right, (((1,), (1,)), ((), ())), preferred_element_type=F32)


def allowed_of(length, pos_col_ref, pos_row_ref):
    col = pos_col_ref[...]
    return jnp.where(col < length, col, FAR) <= pos_row_ref[...]


def rows_of_ref(ref):
    value = ref[...]
    return value.reshape(-1, value.shape[-1])


def attend_kernel(
    length_ref, proj_ref, cos_ref, sin_ref, gain_ref, pos_col_ref, pos_row_ref,
    out_ref, lse_ref, rot_ref, val_ref,
):
    step = pl.program_id(0)
    block = lse_ref.shape[-1]

    @pl.when(step == 0)
    def _():
        proj = rows_of_ref(proj_ref)
        normed = proj * lax.rsqrt(head_mean(proj * proj) + EPS) * gain_ref[...]
        rotated = normed * twice(cos_ref) + swap_halves(normed) * twice(sin_ref)
        lane = lax.broadcasted_iota(jnp.int32, proj.shape, 1)
        rotated = jnp.where(lane < 2 * HEAD_DIM, rotated * HEAD_DIM**-0.5, rotated)
        rot_ref[...] = jnp.where(lane < 3 * HEAD_DIM, rotated, proj).astype(BF16)
        val_ref[:HEAD_DIM, :] = proj[:, 3 * HEAD_DIM :].T.astype(BF16)
        val_ref[HEAD_DIM:, :] = jnp.ones((16, proj.shape[0]), BF16)

    allowed = allowed_of(length_ref[0], pos_col_ref, pos_row_ref)
    keys = rot_ref[:, 2 * HEAD_DIM : 3 * HEAD_DIM]
    query = rot_ref[pl.ds(pl.multiple_of(step * block, block), block), : 2 * HEAD_DIM]
    outs = []
    for head in range(2):
        scores = dot_lanes(keys, query[:, head * HEAD_DIM : (head + 1) * HEAD_DIM])
        weights = jnp.where(allowed, jnp.exp(scores), 0.0).astype(BF16)
        summed = jnp.dot(val_ref[...], weights, preferred_element_type=F32)
        total = summed[HEAD_DIM : HEAD_DIM + 1]
        outs.append((summed[:HEAD_DIM] / total).T)
        lse_ref[head : head + 1, :] = jnp.log(total)
    out_ref[...] = jnp.concatenate(outs, axis=1).astype(BF16).reshape(out_ref.shape)


def fixed(shape):
    return pl.BlockSpec(shape, lambda i: (0,) * len(shape))


def of_seq(seq, blocks, width, lanes):
    return pl.BlockSpec((blocks, 1, width, lanes), lambda i: (0, seq, 0, 0))


def part_of_seq(seq, blocks, width, lanes):
    return pl.BlockSpec((blocks, 1, width, lanes), lambda i: (i, seq, 0, 0))


def cost_of(microseconds):
    return pl.CostEstimate(
        flops=int(microseconds * 6e8), transcendentals=0, bytes_accessed=int(microseconds * 2.5e6)
    )


STEPS = 4


def attend(seq, proj, cosine, sine, gain, positions, lengths):
    blocks, _, width, _ = proj.shape
    slots = blocks * width
    part = slots // STEPS
    return pl.pallas_call(
        attend_kernel,
        grid=(STEPS,),
        in_specs=[
            pl.BlockSpec(memory_space=pltpu.SMEM),
            of_seq(seq, blocks, width, LANES),
            fixed((slots, LANES // 2)),
            fixed((slots, LANES // 2)),
            fixed((1, LANES)),
            fixed((slots, 1)),
            pl.BlockSpec((1, part), lambda i: (0, i)),
        ],
        out_specs=[
            part_of_seq(0, blocks // STEPS, width, 2 * HEAD_DIM),
            pl.BlockSpec((2, part), lambda i: (0, i)),
            fixed((slots, LANES)),
        ],
        out_shape=[
            jax.ShapeDtypeStruct((blocks, 1, width, 2 * HEAD_DIM), BF16),
            jax.ShapeDtypeStruct((2, slots), F32),
            jax.ShapeDtypeStruct((slots, LANES), BF16),
        ],
        scratch_shapes=[pltpu.VMEM((HEAD_DIM + 16, slots), BF16)],
        cost_estimate=cost_of(8),
        name="attend",
    )(lengths[seq : seq + 1], proj, cosine, sine, gain, positions[:, None], positions[None, :])


def attend_back_kernel(
    length_ref, rot_ref, query_ref, grad_ref, out_ref, lse_ref, pos_col_ref, pos_row_ref,
    dq_ref, dkv_ref,
):
    step = pl.program_id(0)
    allowed = allowed_of(length_ref[0], pos_col_ref, pos_row_ref)
    keys = rot_ref[:, 2 * HEAD_DIM : 3 * HEAD_DIM]
    values = rot_ref[:, 3 * HEAD_DIM :]
    query = query_ref[:, : 2 * HEAD_DIM]
    grad = rows_of_ref(grad_ref)
    product = grad.astype(F32) * rows_of_ref(out_ref).astype(F32)
    ones = jnp.ones((8, HEAD_DIM), F32)
    grad_q, grad_k, grad_v = [], 0.0, 0.0
    for head in range(2):
        cut = slice(head * HEAD_DIM, (head + 1) * HEAD_DIM)
        delta = lax.dot_general(
            ones,
            product[:, cut],
            (((1,), (1,)), ((), ())),
            precision=lax.Precision.HIGHEST,
            preferred_element_type=F32,
        )[:1]
        scores = dot_lanes(keys, query[:, cut])
        probs = jnp.where(allowed, jnp.exp(scores - lse_ref[head : head + 1, :]), 0.0)
        grad_probs = dot_lanes(values, grad[:, cut])
        grad_scores = (probs * (grad_probs - delta)).astype(BF16)
        grad_v += jnp.dot(probs.astype(BF16), grad[:, cut], preferred_element_type=F32)
        grad_k += jnp.dot(grad_scores, query[:, cut], preferred_element_type=F32)
        grad_q.append(
            lax.dot_general(
                grad_scores, keys, (((0,), (0,)), ((), ())), preferred_element_type=F32
            )
        )
    dq_ref[...] = jnp.concatenate(grad_q, axis=1) * HEAD_DIM**-0.5
    both = jnp.concatenate([grad_k, grad_v], axis=1)

    @pl.when(step == 0)
    def _():
        dkv_ref[...] = both

    @pl.when(step > 0)
    def _():
        dkv_ref[...] += both


def attend_back(seq, rotated, grad, out, lse, positions, lengths):
    blocks, _, width, _ = grad.shape
    slots = blocks * width
    part = slots // STEPS
    return pl.pallas_call(
        attend_back_kernel,
        grid=(STEPS,),
        in_specs=[
            pl.BlockSpec(memory_space=pltpu.SMEM),
            fixed((slots, LANES)),
            pl.BlockSpec((part, LANES), lambda i: (i, 0)),
            part_of_seq(seq, blocks // STEPS, width, 2 * HEAD_DIM),
            part_of_seq(0, blocks // STEPS, width, 2 * HEAD_DIM),
            pl.BlockSpec((2, part), lambda i: (0, i)),
            fixed((slots, 1)),
            pl.BlockSpec((1, part), lambda i: (0, i)),
        ],
        out_specs=[
            pl.BlockSpec((part, 2 * HEAD_DIM), lambda i: (i, 0)),
            fixed((slots, 2 * HEAD_DIM)),
        ],
        out_shape=[jax.ShapeDtypeStruct((slots, 2 * HEAD_DIM), F32)] * 2,
        cost_estimate=cost_of(10),
        name="attend_back",
    )(
        lengths[seq : seq + 1], rotated, rotated, grad, out, lse,
        positions[:, None], positions[None, :],
    )


def project_back_kernel(
    dq_ref, dkv_ref, other_ref, proj_ref, cos_ref, sin_ref, gain_ref, grad_ref, sum_ref
):
    step = pl.program_id(0)
    grad = jnp.concatenate([dq_ref[...], dkv_ref[...] + other_ref[...]], axis=1)
    proj = rows_of_ref(proj_ref)
    scale_rows = lax.rsqrt(head_mean(proj * proj) + EPS)
    normed = proj * scale_rows
    turned = grad * twice(cos_ref) - swap_halves(grad) * twice(sin_ref)
    gained = turned * gain_ref[...]
    back = scale_rows * (gained - normed * head_mean(gained * normed))
    lane = lax.broadcasted_iota(jnp.int32, proj.shape, 1)
    grad_ref[...] = jnp.where(lane < 3 * HEAD_DIM, back, grad).astype(BF16).reshape(grad_ref.shape)
    sums = jnp.sum((turned * normed).reshape(-1, 8, LANES), axis=0)

    @pl.when(step == 0)
    def _():
        sum_ref[...] = sums

    @pl.when(step > 0)
    def _():
        sum_ref[...] += sums


def project_back(seq, grad_q, grad_kv, other_kv, proj, cosine, sine, gain):
    blocks, _, width, _ = proj.shape
    some = blocks // STEPS
    part = some * width
    half = pl.BlockSpec((part, 2 * HEAD_DIM), lambda i: (i, 0))
    turned = pl.BlockSpec((part, 2 * HEAD_DIM), lambda i: ((i + STEPS // 2) % STEPS, 0))
    table = pl.BlockSpec((part, LANES // 2), lambda i: (i, 0))
    return pl.pallas_call(
        project_back_kernel,
        grid=(STEPS,),
        in_specs=[
            half, half, turned, part_of_seq(seq, some, width, LANES), table, table,
            fixed((1, LANES)),
        ],
        out_specs=[part_of_seq(0, some, width, LANES), fixed((8, LANES))],
        out_shape=[
            jax.ShapeDtypeStruct((blocks, 1, width, LANES), BF16),
            jax.ShapeDtypeStruct((8, LANES), F32),
        ],
        cost_estimate=cost_of(3),
        name="project_back",
    )(grad_q, grad_kv, other_kv, proj, cosine, sine, gain)


def dot_rows(left, right):
    return lax.dot_general(left, right, (((0,), (0,)), ((), ())), preferred_element_type=F32)


def plain(left, right):
    return jnp.dot(left, right, preferred_element_type=F32)


def in_order(own, other, index):
    first = index == 0
    return jnp.concatenate([jnp.where(first, own, other), jnp.where(first, other, own)], axis=0)


def split_local(
    tokens, cotangent, q_weight, k_weight, v_weight, o_weight, gate_weight, up_weight,
    down_weight, attn_gain, ffn_gain, q_gain, k_gain, lengths, pair_order,
):
    seqs, width, _ = tokens.shape
    rank = lax.axis_index("ctx")
    side = lax.axis_index("fsdp")
    core = rank % 2
    mine = seqs * width
    q_rows, kv_rows, ff_rows = q_weight.shape[0], k_weight.shape[0], gate_weight.shape[0]

    x_rows = tokens.astype(F32).reshape(mine, D)
    scale_one = rms_scale(x_rows)
    normed_one = x_rows * scale_one
    kept = {}

    owners = block_owners(rank)
    blocks = owners.shape[0]
    within = jnp.arange(width, dtype=jnp.int32)
    half_blk = width // 2

    def positions_of(dealt):
        block_id = jnp.where(
            within[None, :] < half_blk, dealt[:, None], 2 * pair_order.shape[0] - 1 - dealt[:, None]
        )
        return (block_id * half_blk + within[None, :] % half_blk).reshape(-1)

    def tables(order):
        found = positions_of(order[owners])
        cosine, sine = rope_tables(found)
        return (
            found,
            jnp.concatenate([cosine] * 4, axis=1),
            jnp.concatenate([-sine, sine] * 2, axis=1),
        )

    cut = ff_rows // 2
    ff_own = [w[at : at + cut] for w in (gate_weight, up_weight, down_weight) for at in (0, cut)]
    ff_side = []

    def moving(index):
        return [(ff_own[index], SWAP_X)]

    def slot_tables(run):
        moves = [(jnp.stack([k_weight, v_weight]), SWAP_X), (q_weight, SWAP_X)]
        kept["side"], kept["tables"] = run((pair_order,), tables, moves)

    def attention_weights(kv_side, q_side):
        kv_own = jnp.stack([k_weight, v_weight])
        kv_half = jnp.concatenate(
            [jnp.where(side == 0, kv_own, kv_side), jnp.where(side == 0, kv_side, kv_own)], axis=1
        )
        kv_core = send(kv_half, SWAP_CORE)
        kv_full = jnp.concatenate(
            [jnp.where(core == 0, kv_half, kv_core), jnp.where(core == 0, kv_core, kv_half)], axis=1
        )
        return (jnp.concatenate([q_weight, q_side, kv_full[0], kv_full[1]], axis=0),)

    def slot_weights(run):
        (o_side,), (kept["w_attn"],) = run(
            kept["side"], attention_weights, [(o_weight, SWAP_X)]
        )
        kept["w_out"] = jnp.concatenate([o_weight, o_side], axis=0)

    def slot_move(index):
        def slot(run):
            (come,), _ = run(moves=moving(index))
            ff_side.append(come)

        return slot

    x_norm = gather_blocks(
        (normed_one * attn_gain).astype(BF16), (slot_tables, slot_weights, slot_move(0), idle)
    )
    positions, cosine, sine = kept["tables"]
    w_attn, w_out = kept["w_attn"], kept["w_out"]
    gain_lanes = jnp.concatenate([q_gain, q_gain, k_gain, jnp.ones((HEAD_DIM,), F32)])[None, :]
    my_pos = positions_of(pair_order[rank][None])
    live = (my_pos[None, :] < lengths[:, None]).reshape(mine, 1)
    grad_out = jnp.where(live, cotangent.astype(F32).reshape(mine, D), 0.0)

    heads = []

    def slot_project(run):
        work = lambda x, w: (project(x, w).reshape(blocks, seqs, width, LANES),)
        (come,), (kept["proj"],) = run((x_norm, w_attn), work, moving(1))
        ff_side.append(come)

    def slot_attend(seq):
        def slot(run):
            work = lambda proj: attend(seq, proj, cosine, sine, gain_lanes, positions, lengths)
            (come,), found = run((kept["proj"],), work, moving(2 + seq))
            ff_side.append(come)
            heads.append(found)

        return slot

    def slot_out(run):
        def work(*outs):
            rows = jnp.concatenate(outs, axis=1).reshape(blocks * mine, 2 * HEAD_DIM)
            return rows, *partial_sums(rows, w_out)

        _, (kept["out_rows"], *kept["resid"]) = run([found[0] for found in heads], work)

    grad_low = gather_blocks(
        grad_out.astype(BF16), (slot_project, slot_attend(0), slot_attend(1), slot_out)
    )
    out_rows, proj = kept["out_rows"], kept["proj"]

    def slot_collect(run):
        (come,), (kept["grad_low"],) = run((grad_low,), lambda x: (x,), moving(4))
        ff_side.append(come)

    def slot_down(run):
        (come,), _ = run(moves=moving(5))
        ff_side.append(come)

    resid = x_rows + scatter_blocks(*kept["resid"], (idle, slot_collect, slot_down, idle))
    grad_low = kept["grad_low"]
    w_gate_up = jnp.concatenate([*ff_own[:4], *ff_side[:4]], axis=0)
    w_down = jnp.concatenate([*ff_own[4:], *ff_side[4:]], axis=0)
    scale_two = rms_scale(resid)
    normed_two = resid * scale_two

    def slot_hidden(run):
        _, (kept["grad_hidden"],) = run((grad_low, w_down), lambda g, w: (project(g, w),))

    def slot_join(run):
        _, (kept["w_gate_up"],) = run((w_gate_up,), lambda w: (w,))

    x_norm2 = gather_blocks(
        (normed_two * ffn_gain).astype(BF16), (slot_hidden, slot_join, idle, idle)
    )
    w_gate_up = kept["w_gate_up"]
    both = project(x_norm2, w_gate_up)
    gate_part = jnp.concatenate([both[:, :ff_rows], both[:, 2 * ff_rows : 3 * ff_rows]], axis=1)
    up_part = jnp.concatenate([both[:, ff_rows : 2 * ff_rows], both[:, 3 * ff_rows :]], axis=1)
    hidden = (jax.nn.silu(gate_part) * up_part).astype(BF16)
    gate_low, up_low = gate_grads(kept["grad_hidden"], gate_part, up_part)
    gate_up_low = jnp.concatenate(
        [gate_low[:, :ff_rows], up_low[:, :ff_rows], gate_low[:, ff_rows:], up_low[:, ff_rows:]],
        axis=1,
    )

    def slot_sums(run):
        work = lambda h, w: partial_sums(h, w)
        _, kept["out_parts"] = run((hidden, w_down), work)

    def leaving(full):
        stay, leave = jnp.split(full, 2)
        return stay, *jnp.split(leave.astype(BF16), leave.shape[0] // cut)

    def slot_gate_up(run):
        _, kept["gate_up"] = run((gate_up_low, x_norm2), lambda g, x: leaving(dot_rows(g, x)))

    def slot_down_grads(run):
        _, kept["down"] = run((hidden, grad_low), lambda h, g: leaving(dot_rows(h, g)))

    grad_norm2 = scatter_blocks(
        *partial_sums(gate_up_low, w_gate_up),
        (idle, slot_sums, slot_gate_up, slot_down_grads),
    )
    pieces = [*kept["gate_up"][1:], *kept["down"][1:]]
    came = []
    grad_ffn_gain = jnp.sum(grad_norm2 * normed_two, axis=0)
    grad_resid = grad_out + rms_back(grad_norm2 * ffn_gain, normed_two, scale_two)

    def slot_aside(index):
        def slot(run):
            (come,), _ = run(moves=[(pieces[index], SWAP_X)])
            came.append(come)

        return slot

    grad_attn_low = gather_blocks(
        grad_resid.astype(BF16), (slot_aside(0), slot_aside(1), slot_aside(2), idle)
    )

    def slot_grad_o(run):
        work = lambda x, w: (
            project(x, w).astype(BF16).reshape(blocks, seqs, width, 2 * HEAD_DIM),
        )
        _, (kept["grad_o"],) = run((grad_attn_low, w_out), work)

    def slot_attend_back(seq):
        def slot(run):
            out, lse, rotated = heads[seq]
            work = lambda g: attend_back(seq, rotated, g, out, lse, positions, lengths)
            (come,), found = run((kept["grad_o"],), work, [(pieces[3 + seq], SWAP_X)])
            came.append(come)
            kept["back", seq] = found

        return slot

    def slot_project_back(run):
        def work(*found):
            grads, sums = [], 0.0
            for s in range(seqs):
                grad_q, grad_kv = found[2 * s : 2 * s + 2]
                rows, part = project_back(
                    s, grad_q, grad_kv, send(grad_kv, SWAP_CORE), proj, cosine, sine, gain_lanes
                )
                grads.append(rows)
                sums = sums + jnp.sum(part, axis=0)
            return jnp.concatenate(grads, axis=1).reshape(blocks * mine, LANES), sums

        (come,), (kept["grad_rows"], kept["gain_sums"]) = run(
            [x for s in range(seqs) for x in kept["back", s]], work, [(pieces[5], SWAP_X)]
        )
        came.append(come)

    out_sum = scatter_blocks(
        *kept["out_parts"],
        (slot_grad_o, slot_attend_back(0), slot_attend_back(1), slot_project_back),
    )
    grad_rows, gain_sums = kept["grad_rows"], kept["gain_sums"]
    row = jnp.arange(LANES)[:, None] // HEAD_DIM
    w_once = jnp.where((row < 2) | (row == 2 + core), w_attn, 0).astype(BF16)

    def attention_grads(grads, inputs):
        full = dot_rows(grads, inputs)
        kv_grads = full[2 * q_rows :].reshape(2, 2, 2, kv_rows, D)
        kv_mine = jnp.where(core == 0, kv_grads[:, 0], kv_grads[:, 1])
        kv_stay = jnp.where(side == 0, kv_mine[:, 0], kv_mine[:, 1])
        kv_leave = jnp.where(side == 0, kv_mine[:, 1], kv_mine[:, 0])
        stay = jnp.concatenate([full[:q_rows], kv_stay.reshape(2 * kv_rows, D)])
        leave = jnp.concatenate([full[q_rows : 2 * q_rows], kv_leave.reshape(2 * kv_rows, D)])
        return stay, leave.astype(BF16)

    def slot_attn_grads(run):
        _, kept["attn"] = run((grad_rows, x_norm), attention_grads)

    def slot_out_grads(run):
        def work(rows, grad):
            stay, leave = jnp.split(dot_rows(rows, grad), 2)
            return stay, leave.astype(BF16)

        (kept["attn_come"],), kept["o"] = run(
            (out_rows, grad_attn_low), work, [(kept["attn"][1], SWAP_X)]
        )

    def slot_finish(run):
        def work(*xs):
            gate_up, down = xs[:2]
            gate_up = gate_up + jnp.concatenate(xs[2:6]).astype(F32)
            down = down + jnp.concatenate(xs[6:8]).astype(F32)
            block = jnp.where(live, resid + xs[8], 0.0).astype(BF16).reshape(seqs, width, D)
            return gate_up, down, block

        (kept["o_come"],), kept["finish"] = run(
            (kept["gate_up"][0], kept["down"][0], *came, out_sum), work, [(kept["o"][1], SWAP_X)]
        )

    grad_norm1 = scatter_blocks(
        *partial_sums(grad_rows, w_once),
        (idle, slot_attn_grads, slot_out_grads, slot_finish),
    )
    gate_up_grad, down_grad, block_out = kept["finish"]
    o_grad = kept["o"][0] + kept["o_come"].astype(F32)
    attn_grads = kept["attn"][0] + kept["attn_come"].astype(F32)
    grad_tokens = (grad_resid + rms_back(grad_norm1 * attn_gain, normed_one, scale_one)).reshape(
        seqs, width, D
    )
    owned = jnp.concatenate([q_weight, k_weight, v_weight], axis=0).astype(F32)
    grad_attn_gain = jnp.sum(owned * attn_grads, axis=0) / attn_gain
    gains = total_sum(
        jnp.concatenate(
            [
                grad_attn_gain,
                grad_ffn_gain,
                gain_sums[:HEAD_DIM] + gain_sums[HEAD_DIM : 2 * HEAD_DIM],
                0.5 * gain_sums[2 * HEAD_DIM : 3 * HEAD_DIM],
            ]
        )
    )
    return (
        block_out,
        grad_tokens,
        attn_grads[:q_rows],
        attn_grads[q_rows : q_rows + kv_rows],
        attn_grads[q_rows + kv_rows :],
        o_grad,
        gate_up_grad[:ff_rows],
        gate_up_grad[ff_rows:],
        down_grad,
        gains[:D],
        gains[D : 2 * D],
        gains[2 * D : 2 * D + HEAD_DIM],
        gains[2 * D + HEAD_DIM :],
    )


def solution(mesh):
    body = split_local if fits_split(mesh) else local
    in_specs = (
        P("fsdp", "ctx", None),
        P("fsdp", "ctx", None),
        P(("ctx", "fsdp"), None),
        P(("ctx", "fsdp"), None),
        P(("ctx", "fsdp"), None),
        P(("ctx", "fsdp"), None),
        P(("ctx", "fsdp"), None),
        P(("ctx", "fsdp"), None),
        P(("ctx", "fsdp"), None),
        P(),
        P(),
        P(),
        P(),
        P("fsdp"),
        P(),
    )
    out_specs = (
        P("fsdp", "ctx", None),
        P("fsdp", "ctx", None),
        P(("ctx", "fsdp"), None),
        P(("ctx", "fsdp"), None),
        P(("ctx", "fsdp"), None),
        P(("ctx", "fsdp"), None),
        P(("ctx", "fsdp"), None),
        P(("ctx", "fsdp"), None),
        P(("ctx", "fsdp"), None),
        P(),
        P(),
        P(),
        P(),
    )
    return jax.shard_map(body, mesh=mesh, in_specs=in_specs, out_specs=out_specs, check_vma=False)
```

```python
import functools
import math

import jax
import jax.numpy as jnp
from jax import lax
from jax.experimental import pallas as pl
from jax.experimental.pallas import tpu as pltpu
from jax.sharding import PartitionSpec as P

D = 2048
HEADS = 32
KV_HEADS = 8
HEAD_DIM = 64
FF = 8192


EPS = 1e-05
THETA = 1000000.0
NEG = -1e30


def rms_scale(values):
    return lax.rsqrt(jnp.mean(values * values, axis=-1, keepdims=True) + EPS)


def rms_back(grad_normed, normed, scale_rows):
    return scale_rows * (
        grad_normed - normed * jnp.mean(grad_normed * normed, axis=-1, keepdims=True)
    )


def rope_tables(positions):
    half = HEAD_DIM // 2
    freq = THETA ** (-(jnp.arange(half, dtype=jnp.float32) * 2.0 / HEAD_DIM))
    angle = positions.astype(jnp.float32)[:, None] * freq[None, :]
    return (jnp.cos(angle), jnp.sin(angle))


def rotate(values, cosine, sine):
    half = values.shape[-1] // 2
    first = values[..., :half]
    second = values[..., half:]
    return jnp.concatenate(
        [first * cosine - second * sine, second * cosine + first * sine], axis=-1
    )


def slot_positions(pair_order, width_pair, first, count):
    slot = first + jnp.arange(count, dtype=jnp.int32)
    owner = slot // width_pair
    within = slot % width_pair
    half_blk = width_pair // 2
    pair = pair_order[owner]
    block_id = jnp.where(within < half_blk, pair, 2 * pair_order.shape[0] - 1 - pair)
    return block_id * half_blk + within % half_blk


def block_mask(query_pos, key_part, lengths):
    return (key_part[None, None, :] <= query_pos[None, :, None]) & (
        key_part[None, None, :] < lengths[:, None, None]
    )


def project(inputs, weight):
    return jnp.einsum("td,fd->tf", inputs, weight, preferred_element_type=jnp.float32)


def gate_grads(grad_hidden, gate_part, up_part):
    sigma = jax.nn.sigmoid(gate_part)
    grad_gate = grad_hidden * up_part * sigma * (1.0 + gate_part * (1.0 - sigma))
    grad_up = grad_hidden * gate_part * sigma
    return (grad_gate.astype(jnp.bfloat16), grad_up.astype(jnp.bfloat16))


def block_grads(q_rot, grad_o_low, lse, delta, k_blk, v_blk, allowed, scale):
    scores = (
        jnp.einsum("sqhgd,sjhd->sqhgj", q_rot, k_blk, preferred_element_type=jnp.float32) * scale
    )
    scores = jnp.where(allowed[:, :, None, None, :], scores, NEG)
    probs = jnp.exp(scores - lse[..., None])
    grad_probs = jnp.einsum(
        "sqhgd,sjhd->sqhgj", grad_o_low, v_blk, preferred_element_type=jnp.float32
    )
    grad_scores = (probs * (grad_probs - delta[..., None])).astype(jnp.bfloat16)
    return (probs, grad_scores)


def local(
    tokens,
    cotangent,
    q_weight,
    k_weight,
    v_weight,
    o_weight,
    gate_weight,
    up_weight,
    down_weight,
    attn_gain,
    ffn_gain,
    q_gain,
    k_gain,
    lengths,
    pair_order,
):
    seq_grp = tokens.shape[0]
    width_pair = tokens.shape[1]
    groups = HEADS // KV_HEADS
    q_width = HEADS * HEAD_DIM
    kv_width = KV_HEADS * HEAD_DIM
    scale = HEAD_DIM ** (-0.5)
    tok_rows = seq_grp * width_pair
    slots = width_pair * pair_order.shape[0]
    key_blk = math.gcd(slots, 512)
    key_count = slots // key_blk
    dev_count = lax.axis_size("ctx") * lax.axis_size("fsdp")
    local_pos = slot_positions(
        pair_order, width_pair, lax.axis_index("ctx") * width_pair, width_pair
    )
    key_pos = slot_positions(pair_order, width_pair, 0, slots)
    live_rows = (local_pos[None, :] < lengths[:, None]).reshape(tok_rows, 1)
    cosine, sine = rope_tables(local_pos)
    cosine = cosine[None, :, None, :]
    sine = sine[None, :, None, :]
    x_rows = tokens.astype(jnp.float32).reshape(tok_rows, D)
    scale_one = rms_scale(x_rows)
    normed_one = x_rows * scale_one
    x_norm = (normed_one * attn_gain).astype(jnp.bfloat16)
    w_query, w_key, w_value, w_out = (
        lax.all_gather(q_weight, ("ctx", "fsdp"), axis=0, tiled=True),
        lax.all_gather(k_weight, ("ctx", "fsdp"), axis=0, tiled=True),
        lax.all_gather(v_weight, ("ctx", "fsdp"), axis=0, tiled=True),
        lax.all_gather(o_weight, ("ctx", "fsdp"), axis=0, tiled=True),
    )
    q_proj = project(x_norm, w_query).reshape(seq_grp, width_pair, HEADS, HEAD_DIM)
    k_proj = project(x_norm, w_key).reshape(seq_grp, width_pair, KV_HEADS, HEAD_DIM)
    v_low = project(x_norm, w_value).astype(jnp.bfloat16).reshape(seq_grp, width_pair, kv_width)
    q_scale = rms_scale(q_proj)
    q_normed = q_proj * q_scale
    q_rot = (
        rotate(q_normed * q_gain, cosine, sine)
        .astype(jnp.bfloat16)
        .reshape(seq_grp, width_pair, KV_HEADS, groups, HEAD_DIM)
    )
    k_scale = rms_scale(k_proj)
    k_normed = k_proj * k_scale
    k_rot = (
        rotate(k_normed * k_gain, cosine, sine)
        .astype(jnp.bfloat16)
        .reshape(seq_grp, width_pair, kv_width)
    )
    k_all, v_all = (
        lax.all_gather(k_rot, "ctx", axis=1, tiled=True),
        lax.all_gather(v_low, "ctx", axis=1, tiled=True),
    )
    k_all = k_all.reshape(seq_grp, slots, KV_HEADS, HEAD_DIM)
    v_all = v_all.reshape(seq_grp, slots, KV_HEADS, HEAD_DIM)

    def key_slices(first, count):
        k_blk = lax.dynamic_slice_in_dim(k_all, first, count, 1)
        v_blk = lax.dynamic_slice_in_dim(v_all, first, count, 1)
        allowed = block_mask(local_pos, lax.dynamic_slice_in_dim(key_pos, first, count, 0), lengths)
        return (k_blk, v_blk, allowed)

    def forward_step(index, carry):
        top, total, summed = carry
        k_blk, v_blk, allowed = key_slices(index * key_blk, key_blk)
        scores = (
            jnp.einsum("sqhgd,sjhd->sqhgj", q_rot, k_blk, preferred_element_type=jnp.float32)
            * scale
        )
        scores = jnp.where(allowed[:, :, None, None, :], scores, NEG)
        new_top = jnp.maximum(top, jnp.max(scores, axis=-1))
        shrink = jnp.exp(top - new_top)
        probs = jnp.exp(scores - new_top[..., None])
        total = total * shrink + jnp.sum(probs, axis=-1)
        summed = summed * shrink[..., None] + jnp.einsum(
            "sqhgj,sjhd->sqhgd",
            probs.astype(jnp.bfloat16),
            v_blk,
            preferred_element_type=jnp.float32,
        )
        return (new_top, total, summed)

    stat_shape = (seq_grp, width_pair, KV_HEADS, groups)
    start_carry = (
        jnp.full(stat_shape, NEG, jnp.float32),
        jnp.zeros(stat_shape, jnp.float32),
        jnp.zeros(stat_shape + (HEAD_DIM,), jnp.float32),
    )
    top, total, summed = lax.fori_loop(0, key_count, forward_step, start_carry)
    lse = top + jnp.log(total)
    o_low = (summed / total[..., None]).astype(jnp.bfloat16)
    o_rows = o_low.reshape(tok_rows, q_width)
    resid = x_rows + jnp.einsum("tf,fd->td", o_rows, w_out, preferred_element_type=jnp.float32)
    scale_two = rms_scale(resid)
    normed_two = resid * scale_two
    x_norm2 = (normed_two * ffn_gain).astype(jnp.bfloat16)
    grad_out = jnp.where(live_rows, cotangent.astype(jnp.float32).reshape(tok_rows, D), 0.0)
    grad_low = grad_out.astype(jnp.bfloat16)
    pieces = (
        lax.all_gather(gate_weight, ("ctx", "fsdp"), axis=0, tiled=True),
        lax.all_gather(up_weight, ("ctx", "fsdp"), axis=0, tiled=True),
        lax.all_gather(down_weight, ("ctx", "fsdp"), axis=0, tiled=True),
    )
    gate_part = project(x_norm2, pieces[0])
    up_part = project(x_norm2, pieces[1])
    hidden_part = (jax.nn.silu(gate_part) * up_part).astype(jnp.bfloat16)
    out_sum = jnp.einsum("tf,fd->td", hidden_part, pieces[2], preferred_element_type=jnp.float32)
    gate_all = gate_part
    up_all = up_part
    hidden = (jax.nn.silu(gate_all) * up_all).astype(jnp.bfloat16)
    pieces = (
        lax.all_gather(gate_weight, ("ctx", "fsdp"), axis=0, tiled=True),
        lax.all_gather(up_weight, ("ctx", "fsdp"), axis=0, tiled=True),
        lax.all_gather(down_weight, ("ctx", "fsdp"), axis=0, tiled=True),
    )
    count = pieces[0].shape[0]
    gate_part = gate_all
    up_part = up_all
    grad_gate_part, grad_up_part = gate_grads(project(grad_low, pieces[2]), gate_part, up_part)
    grad_sum = jnp.einsum(
        "tf,fd->td", grad_gate_part, pieces[0], preferred_element_type=jnp.float32
    ) + jnp.einsum("tf,fd->td", grad_up_part, pieces[1], preferred_element_type=jnp.float32)
    gate_grad_all = grad_gate_part
    up_grad_all = grad_up_part
    block_out = (
        jnp.where(live_rows, resid + out_sum, 0.0)
        .astype(jnp.bfloat16)
        .reshape(seq_grp, width_pair, D)
    )
    ffn_dev = FF // dev_count
    owners = lax.axis_size(("ctx", "fsdp")) * (3 * ffn_dev) // (3 * ffn_dev)
    first = jnp.int32(0) // (3 * ffn_dev) * ffn_dev
    grad_gate_part = jnp.einsum(
        "tf,td->fd", gate_grad_all, x_norm2, preferred_element_type=jnp.float32
    )
    grad_up_part = jnp.einsum("tf,td->fd", up_grad_all, x_norm2, preferred_element_type=jnp.float32)
    grad_down_part = jnp.einsum("tf,td->fd", hidden, grad_low, preferred_element_type=jnp.float32)
    stacked = jnp.stack(
        [
            grad_gate_part.reshape(owners, ffn_dev, D),
            grad_up_part.reshape(owners, ffn_dev, D),
            grad_down_part.reshape(owners, ffn_dev, D),
        ],
        axis=1,
    )
    ffn_grads = lax.psum_scatter(
        stacked.reshape(lax.axis_size(("ctx", "fsdp")) * (3 * ffn_dev), D),
        ("ctx", "fsdp"),
        scatter_dimension=0,
        tiled=True,
    )
    grad_ffn_gain = jnp.sum(grad_sum * normed_two, axis=0)
    grad_resid = grad_out + rms_back(grad_sum * ffn_gain, normed_two, scale_two)
    grad_attn_low = grad_resid.astype(jnp.bfloat16)
    grad_o_low = (
        project(grad_attn_low, w_out)
        .astype(jnp.bfloat16)
        .reshape(seq_grp, width_pair, KV_HEADS, groups, HEAD_DIM)
    )
    delta = jnp.sum(grad_o_low.astype(jnp.float32) * o_low.astype(jnp.float32), axis=-1)
    dq_zero = jnp.zeros((seq_grp, width_pair, KV_HEADS, groups, HEAD_DIM), jnp.float32)
    kv_cols = seq_grp * 2 * kv_width

    def key_value_grads(probs, grad_scores):
        grad_k_blk = (
            jnp.einsum("sqhgj,sqhgd->jshd", grad_scores, q_rot, preferred_element_type=jnp.float32)
            * scale
        )
        grad_v_blk = jnp.einsum(
            "sqhgj,sqhgd->jshd",
            probs.astype(jnp.bfloat16),
            grad_o_low,
            preferred_element_type=jnp.float32,
        )
        return jnp.stack([grad_k_blk, grad_v_blk], axis=2).reshape(probs.shape[-1], kv_cols)

    def both_step(grad_q, index):
        k_blk, v_blk, allowed = key_slices(index * key_blk, key_blk)
        probs, grad_scores = block_grads(
            q_rot, grad_o_low, lse, delta, k_blk, v_blk, allowed, scale
        )
        grad_q = (
            grad_q
            + jnp.einsum(
                "sqhgj,sjhd->sqhgd", grad_scores, k_blk, preferred_element_type=jnp.float32
            )
            * scale
        )
        return (grad_q, key_value_grads(probs, grad_scores))

    grad_q_rot, kv_blocks = lax.scan(both_step, dq_zero, jnp.arange(key_count))
    kv_grad = lax.psum_scatter(
        kv_blocks.reshape(slots, kv_cols), "ctx", scatter_dimension=0, tiled=True
    )
    kv_grad = jnp.transpose(
        kv_grad.reshape(width_pair, seq_grp, 2, KV_HEADS, HEAD_DIM), (1, 0, 2, 3, 4)
    )
    grad_q_pre = rotate(grad_q_rot.reshape(seq_grp, width_pair, HEADS, HEAD_DIM), cosine, -sine)
    grad_k_pre = rotate(kv_grad[:, :, 0], cosine, -sine)
    grad_q_gain = jnp.sum(grad_q_pre * q_normed, axis=(0, 1, 2))
    grad_k_gain = jnp.sum(grad_k_pre * k_normed, axis=(0, 1, 2))
    grad_q_proj = (
        rms_back(grad_q_pre * q_gain, q_normed, q_scale)
        .reshape(tok_rows, q_width)
        .astype(jnp.bfloat16)
    )
    grad_k_proj = (
        rms_back(grad_k_pre * k_gain, k_normed, k_scale)
        .reshape(tok_rows, kv_width)
        .astype(jnp.bfloat16)
    )
    grad_v_proj = kv_grad[:, :, 1].reshape(tok_rows, kv_width).astype(jnp.bfloat16)
    grad_norm1 = jnp.einsum("tf,fd->td", grad_q_proj, w_query, preferred_element_type=jnp.float32)
    grad_norm1 = grad_norm1 + jnp.einsum(
        "tf,fd->td", grad_k_proj, w_key, preferred_element_type=jnp.float32
    )
    grad_norm1 = grad_norm1 + jnp.einsum(
        "tf,fd->td", grad_v_proj, w_value, preferred_element_type=jnp.float32
    )
    grad_attn_gain = jnp.sum(grad_norm1 * normed_one, axis=0)
    grad_tokens = (grad_resid + rms_back(grad_norm1 * attn_gain, normed_one, scale_one)).reshape(
        seq_grp, width_pair, D
    )
    q_dev = q_width // dev_count
    kv_dev = kv_width // dev_count
    per_dev = 2 * q_dev + 2 * kv_dev
    owners = lax.axis_size(("ctx", "fsdp")) * per_dev // per_dev

    def rows_of(grad_rows, inputs, each):
        return jnp.einsum(
            "tf,td->fd", grad_rows, inputs, preferred_element_type=jnp.float32
        ).reshape(owners, each, D)

    joined = jnp.concatenate(
        [
            rows_of(grad_q_proj, x_norm, q_dev),
            rows_of(grad_k_proj, x_norm, kv_dev),
            rows_of(grad_v_proj, x_norm, kv_dev),
            rows_of(o_rows, grad_attn_low, q_dev),
        ],
        axis=1,
    )
    attn_grads = lax.psum_scatter(
        joined.reshape(lax.axis_size(("ctx", "fsdp")) * per_dev, D),
        ("ctx", "fsdp"),
        scatter_dimension=0,
        tiled=True,
    )
    grad_attn_gain, grad_ffn_gain, grad_q_gain, grad_k_gain = lax.psum(
        (grad_attn_gain, grad_ffn_gain, grad_q_gain, grad_k_gain), ("ctx", "fsdp")
    )
    return (
        block_out,
        grad_tokens,
        attn_grads[:q_dev],
        attn_grads[q_dev : q_dev + kv_dev],
        attn_grads[q_dev + kv_dev : q_dev + 2 * kv_dev],
        attn_grads[q_dev + 2 * kv_dev :],
        ffn_grads[:ffn_dev],
        ffn_grads[ffn_dev : 2 * ffn_dev],
        ffn_grads[2 * ffn_dev :],
        grad_attn_gain,
        grad_ffn_gain,
        grad_q_gain,
        grad_k_gain,
    )


AXES = ("ctx", "fsdp")
RANKS = 16
LANES = 4 * HEAD_DIM
BF16 = jnp.bfloat16
F32 = jnp.float32
NEVER = 1 << 30


def fits_split(mesh):
    return mesh.shape["ctx"] == RANKS and mesh.shape["fsdp"] == 2


CYCLE = ((0, 0), (1, 0), (2, 0), (3, 0), (3, 1), (2, 1), (1, 1), (0, 1))
CHIPS = len(CYCLE)
NEAR = (2, -2, 1, -1, 0)
FAR = (4, 3, -3)


def index_of(z, y, core, x):
    return z * 8 + y * 4 + core * 2 + x


def pairs_of(move):
    places = [(z, y, c, x) for z in range(4) for y in range(2) for c in range(2) for x in range(2)]
    return [(index_of(*place), index_of(*move(*place))) for place in places]


def along_cycle(step):
    def move(z, y, core, x):
        return (*CYCLE[(CYCLE.index((z, y)) + step) % CHIPS], core, x)

    return pairs_of(move)


SWAP_X = pairs_of(lambda z, y, c, x: (z, y, c, 1 - x))
SWAP_CORE = pairs_of(lambda z, y, c, x: (z, y, 1 - c, x))
SWAP_Y = pairs_of(lambda z, y, c, x: (z, 1 - y, c, x))
SWAP_Z0 = pairs_of(lambda z, y, c, x: (z ^ 1, y, c, x))
SWAP_Z1 = pairs_of(lambda z, y, c, x: (z ^ 2, y, c, x))
SWAP_Z = pairs_of(lambda z, y, c, x: (3 - z, y, c, x))
AHEAD = along_cycle(1)
BEHIND = along_cycle(-1)


def block_owners(rank):
    place = jnp.array([CYCLE.index((chip // 2, chip % 2)) for chip in range(CHIPS)], jnp.int32)
    chips = jnp.array([2 * z + y for z, y in CYCLE], jnp.int32)
    around = jnp.array(NEAR + NEAR + FAR + FAR, jnp.int32)
    turn = jnp.array((0,) * 5 + (1,) * 5 + (0,) * 3 + (1,) * 3, jnp.int32)
    return chips[(place[rank // 2] + around) % CHIPS] * 2 + (rank % 2) ^ turn


def send(value, pairs):
    return lax.ppermute(value, AXES, pairs)


def window(moves, inputs=(), work=None):
    values, inputs = lax.optimization_barrier((tuple(v for v, _ in moves), tuple(inputs)))
    come = tuple(send(v, pairs) for v, (_, pairs) in zip(values, moves))
    done = work(*inputs) if work else ()
    return lax.optimization_barrier((come, done))


def idle(run):
    run()


def collect_kernel(starts, *refs):
    count = len(starts)
    pieces, (whole, held, come_sems, leave_sems) = refs[:count], refs[-4:]
    coming, leaving, at = [], [], 0
    for i, (piece, start) in enumerate(zip(pieces, starts)):
        part = held.at[pl.ds(at, piece.shape[0])]
        at += piece.shape[0]
        coming.append(pltpu.make_async_copy(piece, part, come_sems.at[i]))
        place = whole.at[pl.ds(start, piece.shape[0])]
        leaving.append(pltpu.make_async_copy(part, place, leave_sems.at[i]))
    for copy in coming:
        copy.start()
    for come, leave in zip(coming, leaving):
        come.wait()
        leave.start()
    for copy in leaving:
        copy.wait()


def collect(pieces, starts, whole):
    inner = functools.partial(collect_kernel, starts)
    given = isinstance(whole, jax.Array)
    anywhere = pl.BlockSpec(memory_space=pl.ANY)
    rows = sum(piece.shape[0] for piece in pieces)
    return pl.pallas_call(
        inner,
        in_specs=[anywhere] * (len(pieces) + given),
        out_specs=anywhere,
        out_shape=jax.ShapeDtypeStruct(whole.shape, whole.dtype),
        scratch_shapes=[
            pltpu.VMEM((rows, whole.shape[1]), whole.dtype),
            pltpu.SemaphoreType.DMA((len(pieces),)),
            pltpu.SemaphoreType.DMA((len(pieces),)),
        ],
        input_output_aliases={len(pieces): 0} if given else {},
        cost_estimate=cost_of(0.3 * len(pieces)),
        name="collect",
    )(*pieces, *([whole] if given else []))


def gather_blocks(piece, slots):
    rows = piece.shape[0]
    half = rows // 2
    back, front = [piece], [piece]
    near = None
    for step, slot in enumerate(slots):
        leave = (back[-1], front[-1])
        if step == 3:
            leave = (back[-1][:half], front[-1][half:])

        def run(inputs=(), work=None, moves=()):
            both = [(leave[0], AHEAD), (leave[1], BEHIND), *moves]
            come, done = window(both, inputs, work)
            back.append(come[0])
            front.append(come[1])
            return come[2:], done

        if step == 1:
            found = [front[1], back[1], piece]
            early = [send(block, SWAP_CORE) for block in found]
        if step < 2:
            slot(run)
        elif step == 2:
            blocks = [front[2], back[2], *found]

            def join(*blocks_early):
                mine, other = blocks_early[:5], blocks_early[5:]
                other = [send(block, SWAP_CORE) for block in mine[:2]] + list(other)
                starts = tuple(i * rows for i in range(10))
                shape = jax.ShapeDtypeStruct((10 * rows, piece.shape[1]), piece.dtype)
                return collect([*mine, *other], starts, shape)

            near = slot(run, [*blocks, *early], join)
        else:
            slot(run, near)
    mine = [back[4], front[4], front[3], back[3]]
    starts = (0, half, rows, 2 * rows)
    across = 3 * rows
    far = collect(
        mine + [send(block, SWAP_CORE) for block in mine],
        starts + tuple(across + start for start in starts),
        jax.ShapeDtypeStruct((2 * across, piece.shape[1]), piece.dtype),
    )
    return near, far


def join_slot(run, blocks, join):
    _, (near,) = run(blocks, lambda *xs: (join(*xs),))
    return near


def add_low(left, right):
    return (left.astype(F32) + right.astype(F32)).astype(BF16)


def partial_sums(near, far, weight):
    cut, rest = far.shape[0] // 2, near.shape[0] // 2
    first_come = send(plain(far[cut:], weight).astype(BF16), SWAP_CORE)
    rest_come = send(plain(near[rest:], weight).astype(BF16), SWAP_CORE)
    first = (plain(far[:cut], weight) + first_come.astype(F32)).astype(BF16)
    return first, (near[:rest], weight, rest_come)


def rest_of(own, weight, come):
    return (plain(own, weight) + come.astype(F32)).astype(BF16)


def scatter_blocks(first, rest, slots=(idle,) * 4):
    rows = first.shape[0] // 3
    half = rows // 2
    state = {"rest": rest}

    def stepper(leave, given, own_work):
        def run(inputs=(), work=None, moves=()):
            both = [(leave[0], AHEAD), (leave[1], BEHIND), *moves]
            count = len(given)

            def all_work(*xs):
                mine = (own_work(*xs[:count]),) if count else ()
                return mine + tuple(work(*xs[count:]) if work else ())

            come, done = window(both, tuple(given) + tuple(inputs), all_work)
            state["come"] = come[:2]
            if count:
                state["rest"] = done[0]
                done = done[1:]
            return come[2:], done

        return run

    given = rest if isinstance(rest, tuple) else ()
    slots[0](stepper((first[:half], first[half:rows]), given, rest_of))
    ahead, behind = first[rows : 2 * rows], first[2 * rows :]
    come, rest = state["come"], state["rest"]
    leave = (
        jnp.concatenate([add_low(ahead[:half], come[0]), ahead[half:]]),
        jnp.concatenate([behind[:half], add_low(behind[half:], come[1])]),
    )
    for step in (1, 2, 3):
        slots[step](stepper(leave, (), None))
        come = state["come"]
        at = (step - 1) * 2 * rows
        if step < 3:
            leave = (
                add_low(rest[at : at + rows], come[0]),
                add_low(rest[at + rows : at + 2 * rows], come[1]),
            )
    return rest[4 * rows :].astype(F32) + come[0].astype(F32) + come[1].astype(F32)


def head_sums():
    row = lax.broadcasted_iota(jnp.int32, (LANES, LANES), 0) // HEAD_DIM
    col = lax.broadcasted_iota(jnp.int32, (LANES, LANES), 1) // HEAD_DIM
    return jnp.where(row == col, 1.0 / HEAD_DIM, 0.0).astype(BF16)


def head_mean(values):
    high = values.astype(BF16)
    rest = (values - high.astype(F32)).astype(BF16)
    sums = head_sums()
    return plain(high, sums) + plain(rest, sums)


def swap_halves(values):
    lane = lax.broadcasted_iota(jnp.int32, values.shape, 1)
    return jnp.where(
        lane % HEAD_DIM < HEAD_DIM // 2,
        pltpu.roll(values, LANES - HEAD_DIM // 2, 1),
        pltpu.roll(values, HEAD_DIM // 2, 1),
    )


def twice(ref):
    return jnp.concatenate([ref[...]] * 2, axis=1)


def dot_lanes(left, right):
    return lax.dot_general(left, right, (((1,), (1,)), ((), ())), preferred_element_type=F32)


def allowed_of(length, pos_col_ref, pos_row_ref):
    col = pos_col_ref[...]
    return jnp.where(col < length, col, NEVER) <= pos_row_ref[...]


def rows_of_ref(ref):
    value = ref[...]
    return value.reshape(-1, value.shape[-1])


def attend_kernel(
    length_ref, proj_ref, cos_ref, sin_ref, gain_ref, pos_col_ref, pos_row_ref,
    out_ref, lse_ref, rot_ref, val_ref,
):
    step = pl.program_id(0)
    block = lse_ref.shape[-1]

    @pl.when(step == 0)
    def _():
        proj = rows_of_ref(proj_ref)
        normed = proj * lax.rsqrt(head_mean(proj * proj) + EPS) * gain_ref[...]
        rotated = normed * twice(cos_ref) + swap_halves(normed) * twice(sin_ref)
        lane = lax.broadcasted_iota(jnp.int32, proj.shape, 1)
        rotated = jnp.where(lane < 2 * HEAD_DIM, rotated * HEAD_DIM**-0.5, rotated)
        rot_ref[...] = jnp.where(lane < 3 * HEAD_DIM, rotated, proj).astype(BF16)
        val_ref[:HEAD_DIM, :] = proj[:, 3 * HEAD_DIM :].T.astype(BF16)
        val_ref[HEAD_DIM:, :] = jnp.ones((16, proj.shape[0]), BF16)

    allowed = allowed_of(length_ref[0], pos_col_ref, pos_row_ref)
    keys = rot_ref[:, 2 * HEAD_DIM : 3 * HEAD_DIM]
    query = rot_ref[pl.ds(pl.multiple_of(step * block, block), block), : 2 * HEAD_DIM]
    outs = []
    for head in range(2):
        scores = dot_lanes(keys, query[:, head * HEAD_DIM : (head + 1) * HEAD_DIM])
        weights = jnp.where(allowed, jnp.exp(scores), 0.0).astype(BF16)
        summed = jnp.dot(val_ref[...], weights, preferred_element_type=F32)
        total = summed[HEAD_DIM : HEAD_DIM + 1]
        outs.append((summed[:HEAD_DIM] / total).T)
        lse_ref[head : head + 1, :] = jnp.log(total)
    out_ref[...] = jnp.concatenate(outs, axis=1).astype(BF16).reshape(out_ref.shape)


def fixed(shape):
    return pl.BlockSpec(shape, lambda i: (0,) * len(shape))


def of_seq(seq, blocks, width, lanes):
    return pl.BlockSpec((blocks, 1, width, lanes), lambda i: (0, seq, 0, 0))


def part_of_seq(seq, blocks, width, lanes):
    return pl.BlockSpec((blocks, 1, width, lanes), lambda i: (i, seq, 0, 0))


def cost_of(microseconds):
    return pl.CostEstimate(
        flops=int(microseconds * 6e8), transcendentals=0, bytes_accessed=int(microseconds * 2.5e6)
    )


STEPS = 4


def attend(seq, proj, cosine, sine, gain, positions, lengths):
    blocks, _, width, _ = proj.shape
    slots = blocks * width
    part = slots // STEPS
    return pl.pallas_call(
        attend_kernel,
        grid=(STEPS,),
        in_specs=[
            pl.BlockSpec(memory_space=pltpu.SMEM),
            of_seq(seq, blocks, width, LANES),
            fixed((slots, LANES // 2)),
            fixed((slots, LANES // 2)),
            fixed((1, LANES)),
            fixed((slots, 1)),
            pl.BlockSpec((1, part), lambda i: (0, i)),
        ],
        out_specs=[
            part_of_seq(0, blocks // STEPS, width, 2 * HEAD_DIM),
            pl.BlockSpec((2, part), lambda i: (0, i)),
            fixed((slots, LANES)),
        ],
        out_shape=[
            jax.ShapeDtypeStruct((blocks, 1, width, 2 * HEAD_DIM), BF16),
            jax.ShapeDtypeStruct((2, slots), F32),
            jax.ShapeDtypeStruct((slots, LANES), BF16),
        ],
        scratch_shapes=[pltpu.VMEM((HEAD_DIM + 16, slots), BF16)],
        cost_estimate=cost_of(8),
        name="attend",
    )(lengths[seq : seq + 1], proj, cosine, sine, gain, positions[:, None], positions[None, :])


def attend_back_kernel(
    length_ref, rot_ref, query_ref, grad_ref, out_ref, lse_ref, pos_col_ref, pos_row_ref,
    dq_ref, dkv_ref,
):
    step = pl.program_id(0)
    allowed = allowed_of(length_ref[0], pos_col_ref, pos_row_ref)
    keys = rot_ref[:, 2 * HEAD_DIM : 3 * HEAD_DIM]
    values = rot_ref[:, 3 * HEAD_DIM :]
    query = query_ref[:, : 2 * HEAD_DIM]
    grad = rows_of_ref(grad_ref)
    product = grad.astype(F32) * rows_of_ref(out_ref).astype(F32)
    ones = jnp.ones((8, HEAD_DIM), F32)
    grad_q, grad_k, grad_v = [], 0.0, 0.0
    for head in range(2):
        cut = slice(head * HEAD_DIM, (head + 1) * HEAD_DIM)
        delta = lax.dot_general(
            ones,
            product[:, cut],
            (((1,), (1,)), ((), ())),
            precision=lax.Precision.HIGHEST,
            preferred_element_type=F32,
        )[:1]
        scores = dot_lanes(keys, query[:, cut])
        probs = jnp.where(allowed, jnp.exp(scores - lse_ref[head : head + 1, :]), 0.0)
        grad_probs = dot_lanes(values, grad[:, cut])
        grad_scores = (probs * (grad_probs - delta)).astype(BF16)
        grad_v += jnp.dot(probs.astype(BF16), grad[:, cut], preferred_element_type=F32)
        grad_k += jnp.dot(grad_scores, query[:, cut], preferred_element_type=F32)
        grad_q.append(
            lax.dot_general(
                grad_scores, keys, (((0,), (0,)), ((), ())), preferred_element_type=F32
            )
        )
    dq_ref[...] = jnp.concatenate(grad_q, axis=1) * HEAD_DIM**-0.5
    both = jnp.concatenate([grad_k, grad_v], axis=1)

    @pl.when(step == 0)
    def _():
        dkv_ref[...] = both

    @pl.when(step > 0)
    def _():
        dkv_ref[...] += both


def attend_back(seq, rotated, grad, out, lse, positions, lengths):
    blocks, _, width, _ = grad.shape
    slots = blocks * width
    part = slots // STEPS
    return pl.pallas_call(
        attend_back_kernel,
        grid=(STEPS,),
        in_specs=[
            pl.BlockSpec(memory_space=pltpu.SMEM),
            fixed((slots, LANES)),
            pl.BlockSpec((part, LANES), lambda i: (i, 0)),
            part_of_seq(seq, blocks // STEPS, width, 2 * HEAD_DIM),
            part_of_seq(0, blocks // STEPS, width, 2 * HEAD_DIM),
            pl.BlockSpec((2, part), lambda i: (0, i)),
            fixed((slots, 1)),
            pl.BlockSpec((1, part), lambda i: (0, i)),
        ],
        out_specs=[
            pl.BlockSpec((part, 2 * HEAD_DIM), lambda i: (i, 0)),
            fixed((slots, 2 * HEAD_DIM)),
        ],
        out_shape=[jax.ShapeDtypeStruct((slots, 2 * HEAD_DIM), F32)] * 2,
        cost_estimate=cost_of(10),
        name="attend_back",
    )(
        lengths[seq : seq + 1], rotated, rotated, grad, out, lse,
        positions[:, None], positions[None, :],
    )


def project_back_kernel(
    dq_ref, dkv_ref, other_ref, proj_ref, cos_ref, sin_ref, gain_ref, grad_ref, sum_ref
):
    slots = dq_ref.shape[0]
    near, far = slots // 16 * len(NEAR), slots // 16 * len(FAR)
    cuts = [(near, near), (0, near), (2 * near + far, far), (2 * near, far)]
    other = jnp.concatenate([other_ref[at : at + size] for at, size in cuts], axis=0)
    grad = jnp.concatenate([dq_ref[...], dkv_ref[...] + other], axis=1)
    proj = rows_of_ref(proj_ref)
    scale_rows = lax.rsqrt(head_mean(proj * proj) + EPS)
    normed = proj * scale_rows
    turned = grad * twice(cos_ref) - swap_halves(grad) * twice(sin_ref)
    gained = turned * gain_ref[...]
    back = scale_rows * (gained - normed * head_mean(gained * normed))
    lane = lax.broadcasted_iota(jnp.int32, proj.shape, 1)
    grad_ref[...] = jnp.where(lane < 3 * HEAD_DIM, back, grad).astype(BF16).reshape(grad_ref.shape)
    sum_ref[...] = jnp.sum((turned * normed).reshape(-1, 8, LANES), axis=0)


def project_back(seq, grad_q, grad_kv, other_kv, proj, cosine, sine, gain):
    blocks, _, width, _ = proj.shape
    slots = blocks * width
    half = fixed((slots, 2 * HEAD_DIM))
    table = fixed((slots, LANES // 2))
    return pl.pallas_call(
        project_back_kernel,
        grid=(1,),
        in_specs=[
            half, half, half, of_seq(seq, blocks, width, LANES), table, table, fixed((1, LANES))
        ],
        out_specs=[of_seq(0, blocks, width, LANES), fixed((8, LANES))],
        out_shape=[
            jax.ShapeDtypeStruct((blocks, 1, width, LANES), BF16),
            jax.ShapeDtypeStruct((8, LANES), F32),
        ],
        cost_estimate=cost_of(4),
        name="project_back",
    )(grad_q, grad_kv, other_kv, proj, cosine, sine, gain)


def dot_rows(left, right):
    return lax.dot_general(left, right, (((0,), (0,)), ((), ())), preferred_element_type=F32)


def plain(left, right):
    return jnp.dot(left, right, preferred_element_type=F32)


def in_order(own, other, index):
    first = index == 0
    return jnp.concatenate([jnp.where(first, own, other), jnp.where(first, other, own)], axis=0)


def split_local(
    tokens, cotangent, q_weight, k_weight, v_weight, o_weight, gate_weight, up_weight,
    down_weight, attn_gain, ffn_gain, q_gain, k_gain, lengths, pair_order,
):
    seqs, width, _ = tokens.shape
    rank = lax.axis_index("ctx")
    side = lax.axis_index("fsdp")
    core = rank % 2
    mine = seqs * width
    q_rows, kv_rows, ff_rows = q_weight.shape[0], k_weight.shape[0], gate_weight.shape[0]

    x_rows = tokens.astype(F32).reshape(mine, D)
    scale_one = rms_scale(x_rows)
    normed_one = x_rows * scale_one
    kept = {}

    owners = block_owners(rank)
    blocks = owners.shape[0]
    within = jnp.arange(width, dtype=jnp.int32)
    half_blk = width // 2

    def positions_of(dealt):
        block_id = jnp.where(
            within[None, :] < half_blk, dealt[:, None], 2 * pair_order.shape[0] - 1 - dealt[:, None]
        )
        return (block_id * half_blk + within[None, :] % half_blk).reshape(-1)

    def tables(order):
        found = positions_of(order[owners])
        cosine, sine = rope_tables(found)
        return (
            found,
            jnp.concatenate([cosine] * 4, axis=1),
            jnp.concatenate([-sine, sine] * 2, axis=1),
        )

    cut = ff_rows // 2
    ff_own = [w[at : at + cut] for w in (gate_weight, up_weight, down_weight) for at in (0, cut)]
    ff_side = []

    def moving(index):
        return [(ff_own[index], SWAP_X)]

    def slot_tables(run):
        def work(order):
            return tables(order), tuple(send(w, SWAP_X) for w in (q_weight, k_weight, v_weight))

        _, (kept["tables"], kept["side"]) = run((pair_order,), work)

    def attention_weights(q_side, k_side, v_side):
        kv_own, kv_side = jnp.stack([k_weight, v_weight]), jnp.stack([k_side, v_side])
        kv_half = jnp.concatenate(
            [jnp.where(side == 0, kv_own, kv_side), jnp.where(side == 0, kv_side, kv_own)], axis=1
        )
        kv_core = send(kv_half, SWAP_CORE)
        kv_full = jnp.concatenate(
            [jnp.where(core == 0, kv_half, kv_core), jnp.where(core == 0, kv_core, kv_half)], axis=1
        )
        return (jnp.concatenate([q_weight, q_side, kv_full[0], kv_full[1]], axis=0),)

    def slot_weights(run):
        (o_side,), (kept["w_attn"],) = run(
            kept["side"], attention_weights, [(o_weight, SWAP_X)]
        )
        kept["w_out"] = jnp.concatenate([o_weight, o_side], axis=0)

    def slot_join_move(index):
        def slot(run, blocks, join):
            (come,), (near,) = run(blocks, lambda *xs: (join(*xs),), moving(index))
            ff_side.append(come)
            return near

        return slot

    def slot_project(run, near):
        _, (kept["proj_near"], kept["x_near"]) = run(
            (near, kept["w_attn"]), lambda x, w: (project(x, w), x)
        )

    _, x_far = gather_blocks(
        (normed_one * attn_gain).astype(BF16),
        (slot_tables, slot_weights, slot_join_move(0), slot_project),
    )
    x_near = kept["x_near"]
    positions, cosine, sine = kept["tables"]
    w_attn, w_out = kept["w_attn"], kept["w_out"]
    proj = jnp.concatenate([kept["proj_near"], project(x_far, w_attn)], axis=0)
    proj = proj.reshape(blocks, seqs, width, LANES)
    cut_rows = x_near.shape[0]
    gain_lanes = jnp.concatenate([q_gain, q_gain, k_gain, jnp.ones((HEAD_DIM,), F32)])[None, :]
    my_pos = positions_of(pair_order[rank][None])
    live = (my_pos[None, :] < lengths[:, None]).reshape(mine, 1)
    grad_out = jnp.where(live, cotangent.astype(F32).reshape(mine, D), 0.0)

    heads = []

    def slot_attend(seq):
        def slot(run):
            work = lambda p: attend(seq, p, cosine, sine, gain_lanes, positions, lengths)
            (come,), found = run((kept.get("proj", proj),), work, moving(1 + seq))
            ff_side.append(come)
            heads.append(found)

        return slot

    def slot_out(run, blocks, join):
        def work(*outs):
            rows = jnp.concatenate(outs, axis=1).reshape(-1, 2 * HEAD_DIM)
            return rows, *partial_sums(rows[:cut_rows], rows[cut_rows:], w_out)

        (come,), (kept["out_rows"], *kept["resid"]) = run(
            [found[0] for found in heads], work, moving(3)
        )
        ff_side.append(come)
        return blocks, join

    def slot_late_join(run, near):
        found, join = near
        _, (kept["grad_near"],) = run(found, lambda *xs: (join(*xs),))

    _, grad_far = gather_blocks(
        grad_out.astype(BF16), (slot_attend(0), slot_attend(1), slot_out, slot_late_join)
    )
    out_rows = kept["out_rows"]

    def slot_grad(run):
        (come,), (kept["grad_far"],) = run((grad_far,), lambda x: (x,), moving(4))
        ff_side.append(come)

    def slot_down(run):
        (come,), _ = run(moves=moving(5))
        ff_side.append(come)

    def slot_gate_up_weights(run):
        _, (kept["w_gate_up"],) = run(
            (*ff_own[:4], *ff_side[:4]), lambda *xs: (jnp.concatenate(xs, axis=0),)
        )

    resid = x_rows + scatter_blocks(
        *kept["resid"], (idle, slot_grad, slot_down, slot_gate_up_weights)
    )
    grad_near, grad_far = kept["grad_near"], kept["grad_far"]
    w_gate_up = kept["w_gate_up"]
    w_down = jnp.concatenate([*ff_own[4:], *ff_side[4:]], axis=0)
    scale_two = rms_scale(resid)
    normed_two = resid * scale_two

    def slot_hidden(name, grad):
        def slot(run):
            _, (kept[name],) = run((grad, w_down), lambda g, w: (project(g, w),))

        return slot

    def feed_forward(inputs, grad_hidden):
        both = project(inputs, w_gate_up)
        gate_part = jnp.concatenate([both[:, :ff_rows], both[:, 2 * ff_rows : 3 * ff_rows]], axis=1)
        up_part = jnp.concatenate([both[:, ff_rows : 2 * ff_rows], both[:, 3 * ff_rows :]], axis=1)
        hidden = (jax.nn.silu(gate_part) * up_part).astype(BF16)
        gate_low, up_low = gate_grads(grad_hidden, gate_part, up_part)
        grads = [gate_low[:, :ff_rows], up_low[:, :ff_rows], gate_low[:, ff_rows:], up_low[:, ff_rows:]]
        return hidden, jnp.concatenate(grads, axis=1)

    def slot_feed(run, near):
        _, (kept["hidden"], kept["gate_up_low"], kept["x2_near"]) = run(
            (near, kept["hidden_near"]), lambda x, g: (*feed_forward(x, g), x)
        )

    _, x2_far = gather_blocks(
        (normed_two * ffn_gain).astype(BF16),
        (
            slot_hidden("hidden_near", grad_near),
            slot_hidden("hidden_far", grad_far),
            join_slot,
            slot_feed,
        ),
    )
    x2_near = kept["x2_near"]
    hidden_near, low_near = kept["hidden"], kept["gate_up_low"]
    hidden_far, low_far = feed_forward(x2_far, kept["hidden_far"])

    def slot_sums(run):
        _, kept["out_parts"] = run((hidden_near, hidden_far, w_down), partial_sums)

    def both_parts(*parts):
        near, far, right_near, right_far = parts
        return dot_rows(near, right_near) + dot_rows(far, right_far)

    half_ff = 2 * ff_rows

    def slot_leave(run):
        def work(*parts):
            gate_up = both_parts(parts[0][:, half_ff:], parts[1][:, half_ff:], *parts[2:4])
            return jnp.split(gate_up.astype(BF16), 4)

        _, kept["gate_up_leave"] = run((low_near, low_far, x2_near, x2_far), work)

    def slot_down_leave(run):
        def work(*parts):
            down = both_parts(parts[0][:, ff_rows:], parts[1][:, ff_rows:], *parts[2:4])
            return jnp.split(down.astype(BF16), 2)

        _, kept["down_leave"] = run((hidden_near, hidden_far, grad_near, grad_far), work)

    grad_norm2 = scatter_blocks(
        *partial_sums(low_near, low_far, w_gate_up),
        (idle, slot_sums, slot_leave, slot_down_leave),
    )
    pieces = [*kept["gate_up_leave"], *kept["down_leave"]]
    came = []
    grad_ffn_gain = jnp.sum(grad_norm2 * normed_two, axis=0)
    grad_resid = grad_out + rms_back(grad_norm2 * ffn_gain, normed_two, scale_two)

    def slot_gate_up_stay(run):
        def work(*parts):
            return (both_parts(parts[0][:, :half_ff], parts[1][:, :half_ff], *parts[2:4]),)

        (come,), (kept["gate_up"],) = run(
            (low_near, low_far, x2_near, x2_far), work, [(pieces[0], SWAP_X)]
        )
        came.append(come)

    def slot_down_stay(run):
        def work(*parts):
            return (both_parts(parts[0][:, :ff_rows], parts[1][:, :ff_rows], *parts[2:4]),)

        (come,), (kept["down"],) = run(
            (hidden_near, hidden_far, grad_near, grad_far), work, [(pieces[1], SWAP_X)]
        )
        came.append(come)

    def slot_join_aside(run, blocks, join):
        (come,), (near,) = run(blocks, lambda *xs: (join(*xs),), [(pieces[2], SWAP_X)])
        came.append(come)
        return near

    def grad_heads(grad, weight):
        return project(grad, weight).astype(BF16)

    def slot_grad_heads(run, near):
        _, (kept["heads_near"], kept["da_near"]) = run(
            (near, w_out), lambda x, w: (grad_heads(x, w), x)
        )

    _, da_far = gather_blocks(
        grad_resid.astype(BF16),
        (slot_gate_up_stay, slot_down_stay, slot_join_aside, slot_grad_heads),
    )
    da_near = kept["da_near"]

    def slot_grad_o(run):
        def work(near, x, w):
            rows = jnp.concatenate([near, grad_heads(x, w)], axis=0)
            return (rows.reshape(blocks, seqs, width, 2 * HEAD_DIM),)

        _, (kept["grad_o"],) = run((kept["heads_near"], da_far, w_out), work)

    def slot_attend_back(seq):
        def slot(run):
            out, lse, rotated = heads[seq]
            work = lambda g: attend_back(seq, rotated, g, out, lse, positions, lengths)
            (come,), found = run((kept["grad_o"],), work, [(pieces[3 + seq], SWAP_X)])
            came.append(come)
            kept["back", seq] = found

        return slot

    def slot_project_back(run):
        def work(*found):
            grads, sums = [], 0.0
            for s in range(seqs):
                grad_q, grad_kv = found[2 * s : 2 * s + 2]
                rows, part = project_back(
                    s, grad_q, grad_kv, send(grad_kv, SWAP_CORE), proj, cosine, sine, gain_lanes
                )
                grads.append(rows)
                sums = sums + jnp.sum(part, axis=0)
            return jnp.concatenate(grads, axis=1).reshape(blocks * mine, LANES), sums

        (come,), (kept["grad_rows"], kept["gain_sums"]) = run(
            [x for s in range(seqs) for x in kept["back", s]], work, [(pieces[5], SWAP_X)]
        )
        came.append(come)

    out_sum = scatter_blocks(
        *kept["out_parts"],
        (slot_grad_o, slot_attend_back(0), slot_attend_back(1), slot_project_back),
    )
    grad_rows, gain_sums = kept["grad_rows"], kept["gain_sums"]
    row = jnp.arange(LANES)[:, None] // HEAD_DIM
    w_once = jnp.where((row < 2) | (row == 2 + core), w_attn, 0).astype(BF16)

    def slot_attn_grads(run):
        def work(grads, near, far):
            full = both_parts(grads[:cut_rows], grads[cut_rows:], near, far)
            kv_grads = full[2 * q_rows :].reshape(2, 2, 2, kv_rows, D)
            kv_mine = jnp.where(core == 0, kv_grads[:, 0], kv_grads[:, 1])
            kv_stay = jnp.where(side == 0, kv_mine[:, 0], kv_mine[:, 1])
            kv_leave = jnp.where(side == 0, kv_mine[:, 1], kv_mine[:, 0])
            stay = jnp.concatenate([full[:q_rows], kv_stay.reshape(2 * kv_rows, D)])
            leave = jnp.concatenate([full[q_rows : 2 * q_rows], kv_leave.reshape(2 * kv_rows, D)])
            return stay, leave.astype(BF16)

        _, kept["attn"] = run((grad_rows, x_near, x_far), work)

    def slot_out_grads(run):
        def work(rows, near, far):
            stay, leave = jnp.split(both_parts(rows[:cut_rows], rows[cut_rows:], near, far), 2)
            return stay, leave.astype(BF16)

        (kept["attn_come"],), kept["o"] = run(
            (out_rows, da_near, da_far), work, [(kept["attn"][1], SWAP_X)]
        )

    def slot_finish(run):
        def work(attn_stay, attn_come, gate_up, down, f_sum, *xs):
            attn_grads = attn_stay + attn_come.astype(F32)
            owned = jnp.concatenate([q_weight, k_weight, v_weight], axis=0).astype(F32)
            gains = jnp.concatenate(
                [
                    jnp.sum(owned * attn_grads, axis=0) / attn_gain,
                    grad_ffn_gain,
                    gain_sums[:HEAD_DIM] + gain_sums[HEAD_DIM : 2 * HEAD_DIM],
                    0.5 * gain_sums[2 * HEAD_DIM : 3 * HEAD_DIM],
                ]
            )
            gains = gains + send(gains, SWAP_CORE)
            gains = gains + send(gains, SWAP_X)
            gate_up = gate_up + jnp.concatenate(xs[:4]).astype(F32)
            down = down + jnp.concatenate(xs[4:]).astype(F32)
            block = jnp.where(live, resid + f_sum, 0.0).astype(BF16).reshape(seqs, width, D)
            return gains, attn_grads, gate_up, down, block

        (kept["o_come"],), kept["finish"] = run(
            (*kept["attn"][:1], kept["attn_come"], kept["gate_up"], kept["down"], out_sum, *came),
            work,
            [(kept["o"][1], SWAP_X)],
        )

    def slot_gains(run):
        gains = kept["finish"][0]
        (come,), kept["o_grad"] = run(
            (*kept["o"][:1], kept["o_come"]),
            lambda stay, come: (stay + come.astype(F32),),
            [(gains, SWAP_Y)],
        )
        gains = gains + come
        kept["gains"] = (gains + send(gains, SWAP_Z0)) + (
            send(gains, SWAP_Z1) + send(gains, SWAP_Z)
        )

    grad_norm1 = scatter_blocks(
        *partial_sums(grad_rows[:cut_rows], grad_rows[cut_rows:], w_once),
        (slot_attn_grads, slot_out_grads, slot_finish, slot_gains),
    )
    _, attn_grads, gate_up_grad, down_grad, block_out = kept["finish"]
    (o_grad,) = kept["o_grad"]
    gains = kept["gains"]
    grad_tokens = (grad_resid + rms_back(grad_norm1 * attn_gain, normed_one, scale_one)).reshape(
        seqs, width, D
    )
    return (
        block_out,
        grad_tokens,
        attn_grads[:q_rows],
        attn_grads[q_rows : q_rows + kv_rows],
        attn_grads[q_rows + kv_rows :],
        o_grad,
        gate_up_grad[:ff_rows],
        gate_up_grad[ff_rows:],
        down_grad,
        gains[:D],
        gains[D : 2 * D],
        gains[2 * D : 2 * D + HEAD_DIM],
        gains[2 * D + HEAD_DIM :],
    )


def solution(mesh):
    body = split_local if fits_split(mesh) else local
    in_specs = (
        P("fsdp", "ctx", None),
        P("fsdp", "ctx", None),
        P(("ctx", "fsdp"), None),
        P(("ctx", "fsdp"), None),
        P(("ctx", "fsdp"), None),
        P(("ctx", "fsdp"), None),
        P(("ctx", "fsdp"), None),
        P(("ctx", "fsdp"), None),
        P(("ctx", "fsdp"), None),
        P(),
        P(),
        P(),
        P(),
        P("fsdp"),
        P(),
    )
    out_specs = (
        P("fsdp", "ctx", None),
        P("fsdp", "ctx", None),
        P(("ctx", "fsdp"), None),
        P(("ctx", "fsdp"), None),
        P(("ctx", "fsdp"), None),
        P(("ctx", "fsdp"), None),
        P(("ctx", "fsdp"), None),
        P(("ctx", "fsdp"), None),
        P(("ctx", "fsdp"), None),
        P(),
        P(),
        P(),
        P(),
    )
    return jax.shard_map(body, mesh=mesh, in_specs=in_specs, out_specs=out_specs, check_vma=False)
```

```python
import functools
import math

import jax
import jax.numpy as jnp
from jax import lax
from jax.experimental import pallas as pl
from jax.experimental.pallas import tpu as pltpu
from jax.sharding import PartitionSpec as P

D = 2048
HEADS = 32
KV_HEADS = 8
HEAD_DIM = 64
FF = 8192


EPS = 1e-05
THETA = 1000000.0
NEG = -1e30


def rms_scale(values):
    return lax.rsqrt(jnp.mean(values * values, axis=-1, keepdims=True) + EPS)


def rms_back(grad_normed, normed, scale_rows):
    return scale_rows * (
        grad_normed - normed * jnp.mean(grad_normed * normed, axis=-1, keepdims=True)
    )


def rope_tables(positions):
    half = HEAD_DIM // 2
    freq = THETA ** (-(jnp.arange(half, dtype=jnp.float32) * 2.0 / HEAD_DIM))
    angle = positions.astype(jnp.float32)[:, None] * freq[None, :]
    return (jnp.cos(angle), jnp.sin(angle))


def rotate(values, cosine, sine):
    half = values.shape[-1] // 2
    first = values[..., :half]
    second = values[..., half:]
    return jnp.concatenate(
        [first * cosine - second * sine, second * cosine + first * sine], axis=-1
    )


def slot_positions(pair_order, width_pair, first, count):
    slot = first + jnp.arange(count, dtype=jnp.int32)
    owner = slot // width_pair
    within = slot % width_pair
    half_blk = width_pair // 2
    pair = pair_order[owner]
    block_id = jnp.where(within < half_blk, pair, 2 * pair_order.shape[0] - 1 - pair)
    return block_id * half_blk + within % half_blk


def block_mask(query_pos, key_part, lengths):
    return (key_part[None, None, :] <= query_pos[None, :, None]) & (
        key_part[None, None, :] < lengths[:, None, None]
    )


def project(inputs, weight):
    return jnp.einsum("td,fd->tf", inputs, weight, preferred_element_type=jnp.float32)


def gate_grads(grad_hidden, gate_part, up_part):
    sigma = jax.nn.sigmoid(gate_part)
    grad_gate = grad_hidden * up_part * sigma * (1.0 + gate_part * (1.0 - sigma))
    grad_up = grad_hidden * gate_part * sigma
    return (grad_gate.astype(jnp.bfloat16), grad_up.astype(jnp.bfloat16))


def block_grads(q_rot, grad_o_low, lse, delta, k_blk, v_blk, allowed, scale):
    scores = (
        jnp.einsum("sqhgd,sjhd->sqhgj", q_rot, k_blk, preferred_element_type=jnp.float32) * scale
    )
    scores = jnp.where(allowed[:, :, None, None, :], scores, NEG)
    probs = jnp.exp(scores - lse[..., None])
    grad_probs = jnp.einsum(
        "sqhgd,sjhd->sqhgj", grad_o_low, v_blk, preferred_element_type=jnp.float32
    )
    grad_scores = (probs * (grad_probs - delta[..., None])).astype(jnp.bfloat16)
    return (probs, grad_scores)


def local(
    tokens,
    cotangent,
    q_weight,
    k_weight,
    v_weight,
    o_weight,
    gate_weight,
    up_weight,
    down_weight,
    attn_gain,
    ffn_gain,
    q_gain,
    k_gain,
    lengths,
    pair_order,
):
    seq_grp = tokens.shape[0]
    width_pair = tokens.shape[1]
    groups = HEADS // KV_HEADS
    q_width = HEADS * HEAD_DIM
    kv_width = KV_HEADS * HEAD_DIM
    scale = HEAD_DIM ** (-0.5)
    tok_rows = seq_grp * width_pair
    slots = width_pair * pair_order.shape[0]
    key_blk = math.gcd(slots, 512)
    key_count = slots // key_blk
    dev_count = lax.axis_size("ctx") * lax.axis_size("fsdp")
    local_pos = slot_positions(
        pair_order, width_pair, lax.axis_index("ctx") * width_pair, width_pair
    )
    key_pos = slot_positions(pair_order, width_pair, 0, slots)
    live_rows = (local_pos[None, :] < lengths[:, None]).reshape(tok_rows, 1)
    cosine, sine = rope_tables(local_pos)
    cosine = cosine[None, :, None, :]
    sine = sine[None, :, None, :]
    x_rows = tokens.astype(jnp.float32).reshape(tok_rows, D)
    scale_one = rms_scale(x_rows)
    normed_one = x_rows * scale_one
    x_norm = (normed_one * attn_gain).astype(jnp.bfloat16)
    w_query, w_key, w_value, w_out = (
        lax.all_gather(q_weight, ("ctx", "fsdp"), axis=0, tiled=True),
        lax.all_gather(k_weight, ("ctx", "fsdp"), axis=0, tiled=True),
        lax.all_gather(v_weight, ("ctx", "fsdp"), axis=0, tiled=True),
        lax.all_gather(o_weight, ("ctx", "fsdp"), axis=0, tiled=True),
    )
    q_proj = project(x_norm, w_query).reshape(seq_grp, width_pair, HEADS, HEAD_DIM)
    k_proj = project(x_norm, w_key).reshape(seq_grp, width_pair, KV_HEADS, HEAD_DIM)
    v_low = project(x_norm, w_value).astype(jnp.bfloat16).reshape(seq_grp, width_pair, kv_width)
    q_scale = rms_scale(q_proj)
    q_normed = q_proj * q_scale
    q_rot = (
        rotate(q_normed * q_gain, cosine, sine)
        .astype(jnp.bfloat16)
        .reshape(seq_grp, width_pair, KV_HEADS, groups, HEAD_DIM)
    )
    k_scale = rms_scale(k_proj)
    k_normed = k_proj * k_scale
    k_rot = (
        rotate(k_normed * k_gain, cosine, sine)
        .astype(jnp.bfloat16)
        .reshape(seq_grp, width_pair, kv_width)
    )
    k_all, v_all = (
        lax.all_gather(k_rot, "ctx", axis=1, tiled=True),
        lax.all_gather(v_low, "ctx", axis=1, tiled=True),
    )
    k_all = k_all.reshape(seq_grp, slots, KV_HEADS, HEAD_DIM)
    v_all = v_all.reshape(seq_grp, slots, KV_HEADS, HEAD_DIM)

    def key_slices(first, count):
        k_blk = lax.dynamic_slice_in_dim(k_all, first, count, 1)
        v_blk = lax.dynamic_slice_in_dim(v_all, first, count, 1)
        allowed = block_mask(local_pos, lax.dynamic_slice_in_dim(key_pos, first, count, 0), lengths)
        return (k_blk, v_blk, allowed)

    def forward_step(index, carry):
        top, total, summed = carry
        k_blk, v_blk, allowed = key_slices(index * key_blk, key_blk)
        scores = (
            jnp.einsum("sqhgd,sjhd->sqhgj", q_rot, k_blk, preferred_element_type=jnp.float32)
            * scale
        )
        scores = jnp.where(allowed[:, :, None, None, :], scores, NEG)
        new_top = jnp.maximum(top, jnp.max(scores, axis=-1))
        shrink = jnp.exp(top - new_top)
        probs = jnp.exp(scores - new_top[..., None])
        total = total * shrink + jnp.sum(probs, axis=-1)
        summed = summed * shrink[..., None] + jnp.einsum(
            "sqhgj,sjhd->sqhgd",
            probs.astype(jnp.bfloat16),
            v_blk,
            preferred_element_type=jnp.float32,
        )
        return (new_top, total, summed)

    stat_shape = (seq_grp, width_pair, KV_HEADS, groups)
    start_carry = (
        jnp.full(stat_shape, NEG, jnp.float32),
        jnp.zeros(stat_shape, jnp.float32),
        jnp.zeros(stat_shape + (HEAD_DIM,), jnp.float32),
    )
    top, total, summed = lax.fori_loop(0, key_count, forward_step, start_carry)
    lse = top + jnp.log(total)
    o_low = (summed / total[..., None]).astype(jnp.bfloat16)
    o_rows = o_low.reshape(tok_rows, q_width)
    resid = x_rows + jnp.einsum("tf,fd->td", o_rows, w_out, preferred_element_type=jnp.float32)
    scale_two = rms_scale(resid)
    normed_two = resid * scale_two
    x_norm2 = (normed_two * ffn_gain).astype(jnp.bfloat16)
    grad_out = jnp.where(live_rows, cotangent.astype(jnp.float32).reshape(tok_rows, D), 0.0)
    grad_low = grad_out.astype(jnp.bfloat16)
    pieces = (
        lax.all_gather(gate_weight, ("ctx", "fsdp"), axis=0, tiled=True),
        lax.all_gather(up_weight, ("ctx", "fsdp"), axis=0, tiled=True),
        lax.all_gather(down_weight, ("ctx", "fsdp"), axis=0, tiled=True),
    )
    gate_part = project(x_norm2, pieces[0])
    up_part = project(x_norm2, pieces[1])
    hidden_part = (jax.nn.silu(gate_part) * up_part).astype(jnp.bfloat16)
    out_sum = jnp.einsum("tf,fd->td", hidden_part, pieces[2], preferred_element_type=jnp.float32)
    gate_all = gate_part
    up_all = up_part
    hidden = (jax.nn.silu(gate_all) * up_all).astype(jnp.bfloat16)
    pieces = (
        lax.all_gather(gate_weight, ("ctx", "fsdp"), axis=0, tiled=True),
        lax.all_gather(up_weight, ("ctx", "fsdp"), axis=0, tiled=True),
        lax.all_gather(down_weight, ("ctx", "fsdp"), axis=0, tiled=True),
    )
    count = pieces[0].shape[0]
    gate_part = gate_all
    up_part = up_all
    grad_gate_part, grad_up_part = gate_grads(project(grad_low, pieces[2]), gate_part, up_part)
    grad_sum = jnp.einsum(
        "tf,fd->td", grad_gate_part, pieces[0], preferred_element_type=jnp.float32
    ) + jnp.einsum("tf,fd->td", grad_up_part, pieces[1], preferred_element_type=jnp.float32)
    gate_grad_all = grad_gate_part
    up_grad_all = grad_up_part
    block_out = (
        jnp.where(live_rows, resid + out_sum, 0.0)
        .astype(jnp.bfloat16)
        .reshape(seq_grp, width_pair, D)
    )
    ffn_dev = FF // dev_count
    owners = lax.axis_size(("ctx", "fsdp")) * (3 * ffn_dev) // (3 * ffn_dev)
    first = jnp.int32(0) // (3 * ffn_dev) * ffn_dev
    grad_gate_part = jnp.einsum(
        "tf,td->fd", gate_grad_all, x_norm2, preferred_element_type=jnp.float32
    )
    grad_up_part = jnp.einsum("tf,td->fd", up_grad_all, x_norm2, preferred_element_type=jnp.float32)
    grad_down_part = jnp.einsum("tf,td->fd", hidden, grad_low, preferred_element_type=jnp.float32)
    stacked = jnp.stack(
        [
            grad_gate_part.reshape(owners, ffn_dev, D),
            grad_up_part.reshape(owners, ffn_dev, D),
            grad_down_part.reshape(owners, ffn_dev, D),
        ],
        axis=1,
    )
    ffn_grads = lax.psum_scatter(
        stacked.reshape(lax.axis_size(("ctx", "fsdp")) * (3 * ffn_dev), D),
        ("ctx", "fsdp"),
        scatter_dimension=0,
        tiled=True,
    )
    grad_ffn_gain = jnp.sum(grad_sum * normed_two, axis=0)
    grad_resid = grad_out + rms_back(grad_sum * ffn_gain, normed_two, scale_two)
    grad_attn_low = grad_resid.astype(jnp.bfloat16)
    grad_o_low = (
        project(grad_attn_low, w_out)
        .astype(jnp.bfloat16)
        .reshape(seq_grp, width_pair, KV_HEADS, groups, HEAD_DIM)
    )
    delta = jnp.sum(grad_o_low.astype(jnp.float32) * o_low.astype(jnp.float32), axis=-1)
    dq_zero = jnp.zeros((seq_grp, width_pair, KV_HEADS, groups, HEAD_DIM), jnp.float32)
    kv_cols = seq_grp * 2 * kv_width

    def key_value_grads(probs, grad_scores):
        grad_k_blk = (
            jnp.einsum("sqhgj,sqhgd->jshd", grad_scores, q_rot, preferred_element_type=jnp.float32)
            * scale
        )
        grad_v_blk = jnp.einsum(
            "sqhgj,sqhgd->jshd",
            probs.astype(jnp.bfloat16),
            grad_o_low,
            preferred_element_type=jnp.float32,
        )
        return jnp.stack([grad_k_blk, grad_v_blk], axis=2).reshape(probs.shape[-1], kv_cols)

    def both_step(grad_q, index):
        k_blk, v_blk, allowed = key_slices(index * key_blk, key_blk)
        probs, grad_scores = block_grads(
            q_rot, grad_o_low, lse, delta, k_blk, v_blk, allowed, scale
        )
        grad_q = (
            grad_q
            + jnp.einsum(
                "sqhgj,sjhd->sqhgd", grad_scores, k_blk, preferred_element_type=jnp.float32
            )
            * scale
        )
        return (grad_q, key_value_grads(probs, grad_scores))

    grad_q_rot, kv_blocks = lax.scan(both_step, dq_zero, jnp.arange(key_count))
    kv_grad = lax.psum_scatter(
        kv_blocks.reshape(slots, kv_cols), "ctx", scatter_dimension=0, tiled=True
    )
    kv_grad = jnp.transpose(
        kv_grad.reshape(width_pair, seq_grp, 2, KV_HEADS, HEAD_DIM), (1, 0, 2, 3, 4)
    )
    grad_q_pre = rotate(grad_q_rot.reshape(seq_grp, width_pair, HEADS, HEAD_DIM), cosine, -sine)
    grad_k_pre = rotate(kv_grad[:, :, 0], cosine, -sine)
    grad_q_gain = jnp.sum(grad_q_pre * q_normed, axis=(0, 1, 2))
    grad_k_gain = jnp.sum(grad_k_pre * k_normed, axis=(0, 1, 2))
    grad_q_proj = (
        rms_back(grad_q_pre * q_gain, q_normed, q_scale)
        .reshape(tok_rows, q_width)
        .astype(jnp.bfloat16)
    )
    grad_k_proj = (
        rms_back(grad_k_pre * k_gain, k_normed, k_scale)
        .reshape(tok_rows, kv_width)
        .astype(jnp.bfloat16)
    )
    grad_v_proj = kv_grad[:, :, 1].reshape(tok_rows, kv_width).astype(jnp.bfloat16)
    grad_norm1 = jnp.einsum("tf,fd->td", grad_q_proj, w_query, preferred_element_type=jnp.float32)
    grad_norm1 = grad_norm1 + jnp.einsum(
        "tf,fd->td", grad_k_proj, w_key, preferred_element_type=jnp.float32
    )
    grad_norm1 = grad_norm1 + jnp.einsum(
        "tf,fd->td", grad_v_proj, w_value, preferred_element_type=jnp.float32
    )
    grad_attn_gain = jnp.sum(grad_norm1 * normed_one, axis=0)
    grad_tokens = (grad_resid + rms_back(grad_norm1 * attn_gain, normed_one, scale_one)).reshape(
        seq_grp, width_pair, D
    )
    q_dev = q_width // dev_count
    kv_dev = kv_width // dev_count
    per_dev = 2 * q_dev + 2 * kv_dev
    owners = lax.axis_size(("ctx", "fsdp")) * per_dev // per_dev

    def rows_of(grad_rows, inputs, each):
        return jnp.einsum(
            "tf,td->fd", grad_rows, inputs, preferred_element_type=jnp.float32
        ).reshape(owners, each, D)

    joined = jnp.concatenate(
        [
            rows_of(grad_q_proj, x_norm, q_dev),
            rows_of(grad_k_proj, x_norm, kv_dev),
            rows_of(grad_v_proj, x_norm, kv_dev),
            rows_of(o_rows, grad_attn_low, q_dev),
        ],
        axis=1,
    )
    attn_grads = lax.psum_scatter(
        joined.reshape(lax.axis_size(("ctx", "fsdp")) * per_dev, D),
        ("ctx", "fsdp"),
        scatter_dimension=0,
        tiled=True,
    )
    grad_attn_gain, grad_ffn_gain, grad_q_gain, grad_k_gain = lax.psum(
        (grad_attn_gain, grad_ffn_gain, grad_q_gain, grad_k_gain), ("ctx", "fsdp")
    )
    return (
        block_out,
        grad_tokens,
        attn_grads[:q_dev],
        attn_grads[q_dev : q_dev + kv_dev],
        attn_grads[q_dev + kv_dev : q_dev + 2 * kv_dev],
        attn_grads[q_dev + 2 * kv_dev :],
        ffn_grads[:ffn_dev],
        ffn_grads[ffn_dev : 2 * ffn_dev],
        ffn_grads[2 * ffn_dev :],
        grad_attn_gain,
        grad_ffn_gain,
        grad_q_gain,
        grad_k_gain,
    )


AXES = ("ctx", "fsdp")
RANKS = 16
LANES = 4 * HEAD_DIM
BF16 = jnp.bfloat16
F32 = jnp.float32
NEVER = 1 << 30


def fits_split(mesh):
    return mesh.shape["ctx"] == RANKS and mesh.shape["fsdp"] == 2


CYCLE = ((0, 0), (1, 0), (2, 0), (3, 0), (3, 1), (2, 1), (1, 1), (0, 1))
CHIPS = len(CYCLE)
NEAR = (2, -2, 1, -1, 0)
FAR = (4, 3, -3)


def index_of(z, y, core, x):
    return z * 8 + y * 4 + core * 2 + x


def pairs_of(move):
    places = [(z, y, c, x) for z in range(4) for y in range(2) for c in range(2) for x in range(2)]
    return [(index_of(*place), index_of(*move(*place))) for place in places]


def along_cycle(step):
    def move(z, y, core, x):
        return (*CYCLE[(CYCLE.index((z, y)) + step) % CHIPS], core, x)

    return pairs_of(move)


SWAP_X = pairs_of(lambda z, y, c, x: (z, y, c, 1 - x))
SWAP_CORE = pairs_of(lambda z, y, c, x: (z, y, 1 - c, x))
SWAP_Y = pairs_of(lambda z, y, c, x: (z, 1 - y, c, x))
SWAP_Z0 = pairs_of(lambda z, y, c, x: (z ^ 1, y, c, x))
SWAP_Z1 = pairs_of(lambda z, y, c, x: (z ^ 2, y, c, x))
SWAP_Z = pairs_of(lambda z, y, c, x: (3 - z, y, c, x))
AHEAD = along_cycle(1)
BEHIND = along_cycle(-1)


def block_owners(rank):
    place = jnp.array([CYCLE.index((chip // 2, chip % 2)) for chip in range(CHIPS)], jnp.int32)
    chips = jnp.array([2 * z + y for z, y in CYCLE], jnp.int32)
    around = jnp.array(NEAR + NEAR + FAR + FAR, jnp.int32)
    turn = jnp.array((0,) * 5 + (1,) * 5 + (0,) * 3 + (1,) * 3, jnp.int32)
    return chips[(place[rank // 2] + around) % CHIPS] * 2 + (rank % 2) ^ turn


def send(value, pairs):
    return lax.ppermute(value, AXES, pairs)


def window(moves, inputs=(), work=None):
    values, inputs = lax.optimization_barrier((tuple(v for v, _ in moves), tuple(inputs)))
    come = tuple(send(v, pairs) for v, (_, pairs) in zip(values, moves))
    done = work(*inputs) if work else ()
    return lax.optimization_barrier((come, done))


def idle(run):
    run()


def collect_kernel(starts, *refs):
    count = len(starts)
    pieces, (whole, held, come_sems, leave_sems) = refs[:count], refs[-4:]
    coming, leaving, at = [], [], 0
    for i, (piece, start) in enumerate(zip(pieces, starts)):
        part = held.at[pl.ds(at, piece.shape[0])]
        at += piece.shape[0]
        coming.append(pltpu.make_async_copy(piece, part, come_sems.at[i]))
        place = whole.at[pl.ds(start, piece.shape[0])]
        leaving.append(pltpu.make_async_copy(part, place, leave_sems.at[i]))
    for copy in coming:
        copy.start()
    for come, leave in zip(coming, leaving):
        come.wait()
        leave.start()
    for copy in leaving:
        copy.wait()


def collect(pieces, starts, whole):
    inner = functools.partial(collect_kernel, starts)
    given = isinstance(whole, jax.Array)
    anywhere = pl.BlockSpec(memory_space=pl.ANY)
    rows = sum(piece.shape[0] for piece in pieces)
    return pl.pallas_call(
        inner,
        in_specs=[anywhere] * (len(pieces) + given),
        out_specs=anywhere,
        out_shape=jax.ShapeDtypeStruct(whole.shape, whole.dtype),
        scratch_shapes=[
            pltpu.VMEM((rows, whole.shape[1]), whole.dtype),
            pltpu.SemaphoreType.DMA((len(pieces),)),
            pltpu.SemaphoreType.DMA((len(pieces),)),
        ],
        input_output_aliases={len(pieces): 0} if given else {},
        cost_estimate=cost_of(0.3 * len(pieces)),
        name="collect",
    )(*pieces, *([whole] if given else []))


def gather_blocks(piece, slots):
    rows = piece.shape[0]
    half = rows // 2
    back, front = [piece], [piece]
    near = None
    for step, slot in enumerate(slots):
        leave = (back[-1], front[-1])
        if step == 3:
            leave = (back[-1][:half], front[-1][half:])

        def run(inputs=(), work=None, moves=()):
            both = [(leave[0], AHEAD), (leave[1], BEHIND), *moves]
            come, done = window(both, inputs, work)
            back.append(come[0])
            front.append(come[1])
            return come[2:], done

        if step == 1:
            found = [front[1], back[1], piece]
            early = [send(block, SWAP_CORE) for block in found]
        if step < 2:
            slot(run)
        elif step == 2:
            blocks = [front[2], back[2], *found]

            def join(*blocks_early):
                mine, other = blocks_early[:5], blocks_early[5:]
                other = [send(block, SWAP_CORE) for block in mine[:2]] + list(other)
                starts = tuple(i * rows for i in range(10))
                shape = jax.ShapeDtypeStruct((10 * rows, piece.shape[1]), piece.dtype)
                return collect([*mine, *other], starts, shape)

            near = slot(run, [*blocks, *early], join)
        else:
            slot(run, near)
    return near, (back[4], front[4], front[3], back[3])


def join_far(first, second, third, fourth):
    mine = [first, second, third, fourth]
    half, rows = first.shape[0], third.shape[0]
    starts = (0, half, rows, 2 * rows)
    across = 3 * rows
    return collect(
        mine + [send(block, SWAP_CORE) for block in mine],
        starts + tuple(across + start for start in starts),
        jax.ShapeDtypeStruct((2 * across, first.shape[1]), first.dtype),
    )


def add_low(left, right):
    return (left.astype(F32) + right.astype(F32)).astype(BF16)


def core_sum(rows, weight):
    cut = rows.shape[0] // 2
    come = send(plain(rows[cut:], weight).astype(BF16), SWAP_CORE)
    return (plain(rows[:cut], weight) + come.astype(F32)).astype(BF16)


def scatter_blocks(first, rest, slots=(idle,) * 4):
    rows = first.shape[0] // 3
    half = rows // 2
    state = {"rest": rest}

    def stepper(leave, given, own_work):
        def run(inputs=(), work=None, moves=()):
            both = [(leave[0], AHEAD), (leave[1], BEHIND), *moves]
            count = len(given)

            def all_work(*xs):
                mine = (own_work(*xs[:count]),) if count else ()
                return mine + tuple(work(*xs[count:]) if work else ())

            come, done = window(both, tuple(given) + tuple(inputs), all_work)
            state["come"] = come[:2]
            if count:
                state["rest"] = done[0]
                done = done[1:]
            return come[2:], done

        return run

    given = rest if isinstance(rest, tuple) else ()
    slots[0](stepper((first[:half], first[half:rows]), given, core_sum))
    ahead, behind = first[rows : 2 * rows], first[2 * rows :]
    come, rest = state["come"], state["rest"]
    leave = (
        jnp.concatenate([add_low(ahead[:half], come[0]), ahead[half:]]),
        jnp.concatenate([behind[:half], add_low(behind[half:], come[1])]),
    )
    for step in (1, 2, 3):
        slots[step](stepper(leave, (), None))
        come = state["come"]
        at = (step - 1) * 2 * rows
        if step < 3:
            leave = (
                add_low(rest[at : at + rows], come[0]),
                add_low(rest[at + rows : at + 2 * rows], come[1]),
            )
    return rest[4 * rows :].astype(F32) + come[0].astype(F32) + come[1].astype(F32)


def head_sums():
    row = lax.broadcasted_iota(jnp.int32, (LANES, LANES), 0) // HEAD_DIM
    col = lax.broadcasted_iota(jnp.int32, (LANES, LANES), 1) // HEAD_DIM
    return jnp.where(row == col, 1.0 / HEAD_DIM, 0.0).astype(BF16)


def head_mean(values):
    high = values.astype(BF16)
    rest = (values - high.astype(F32)).astype(BF16)
    sums = head_sums()
    return plain(high, sums) + plain(rest, sums)


def swap_halves(values):
    lane = lax.broadcasted_iota(jnp.int32, values.shape, 1)
    return jnp.where(
        lane % HEAD_DIM < HEAD_DIM // 2,
        pltpu.roll(values, LANES - HEAD_DIM // 2, 1),
        pltpu.roll(values, HEAD_DIM // 2, 1),
    )


def twice(ref):
    return jnp.concatenate([ref[...]] * 2, axis=1)


def dot_lanes(left, right):
    return lax.dot_general(left, right, (((1,), (1,)), ((), ())), preferred_element_type=F32)


def allowed_of(length, pos_col_ref, pos_row_ref):
    col = pos_col_ref[...]
    return jnp.where(col < length, col, NEVER) <= pos_row_ref[...]


def rows_of_ref(ref):
    value = ref[...]
    return value.reshape(-1, value.shape[-1])


def attend_kernel(
    length_ref, proj_ref, cos_ref, sin_ref, gain_ref, pos_col_ref, pos_row_ref,
    out_ref, lse_ref, rot_ref, val_ref,
):
    step = pl.program_id(0)
    block = lse_ref.shape[-1]

    @pl.when(step == 0)
    def _():
        proj = rows_of_ref(proj_ref)
        normed = proj * lax.rsqrt(head_mean(proj * proj) + EPS) * gain_ref[...]
        rotated = normed * twice(cos_ref) + swap_halves(normed) * twice(sin_ref)
        lane = lax.broadcasted_iota(jnp.int32, proj.shape, 1)
        rotated = jnp.where(lane < 2 * HEAD_DIM, rotated * HEAD_DIM**-0.5, rotated)
        rot_ref[...] = jnp.where(lane < 3 * HEAD_DIM, rotated, proj).astype(BF16)
        val_ref[:HEAD_DIM, :] = proj[:, 3 * HEAD_DIM :].T.astype(BF16)
        val_ref[HEAD_DIM:, :] = jnp.ones((16, proj.shape[0]), BF16)

    allowed = allowed_of(length_ref[0], pos_col_ref, pos_row_ref)
    keys = rot_ref[:, 2 * HEAD_DIM : 3 * HEAD_DIM]
    query = rot_ref[pl.ds(pl.multiple_of(step * block, block), block), : 2 * HEAD_DIM]
    outs = []
    for head in range(2):
        scores = dot_lanes(keys, query[:, head * HEAD_DIM : (head + 1) * HEAD_DIM])
        weights = jnp.where(allowed, jnp.exp(scores), 0.0).astype(BF16)
        summed = jnp.dot(val_ref[...], weights, preferred_element_type=F32)
        total = summed[HEAD_DIM : HEAD_DIM + 1]
        outs.append((summed[:HEAD_DIM] / total).T)
        lse_ref[head : head + 1, :] = jnp.log(total)
    out_ref[...] = jnp.concatenate(outs, axis=1).astype(BF16).reshape(out_ref.shape)


def fixed(shape):
    return pl.BlockSpec(shape, lambda i: (0,) * len(shape))


def of_seq(seq, blocks, width, lanes):
    return pl.BlockSpec((blocks, 1, width, lanes), lambda i: (0, seq, 0, 0))


def part_of_seq(seq, blocks, width, lanes):
    return pl.BlockSpec((blocks, 1, width, lanes), lambda i: (i, seq, 0, 0))


def cost_of(microseconds):
    return pl.CostEstimate(
        flops=int(microseconds * 6e8), transcendentals=0, bytes_accessed=int(microseconds * 2.5e6)
    )


STEPS = 4


def attend(seq, proj, cosine, sine, gain, positions, lengths):
    blocks, _, width, _ = proj.shape
    slots = blocks * width
    part = slots // STEPS
    return pl.pallas_call(
        attend_kernel,
        grid=(STEPS,),
        in_specs=[
            pl.BlockSpec(memory_space=pltpu.SMEM),
            of_seq(seq, blocks, width, LANES),
            fixed((slots, LANES // 2)),
            fixed((slots, LANES // 2)),
            fixed((1, LANES)),
            fixed((slots, 1)),
            pl.BlockSpec((1, part), lambda i: (0, i)),
        ],
        out_specs=[
            part_of_seq(0, blocks // STEPS, width, 2 * HEAD_DIM),
            pl.BlockSpec((2, part), lambda i: (0, i)),
            fixed((slots, LANES)),
        ],
        out_shape=[
            jax.ShapeDtypeStruct((blocks, 1, width, 2 * HEAD_DIM), BF16),
            jax.ShapeDtypeStruct((2, slots), F32),
            jax.ShapeDtypeStruct((slots, LANES), BF16),
        ],
        scratch_shapes=[pltpu.VMEM((HEAD_DIM + 16, slots), BF16)],
        cost_estimate=cost_of(8),
        name="attend",
    )(lengths[seq : seq + 1], proj, cosine, sine, gain, positions[:, None], positions[None, :])


def attend_back_kernel(
    length_ref, rot_ref, query_ref, grad_ref, out_ref, lse_ref, pos_col_ref, pos_row_ref,
    dq_ref, dkv_ref,
):
    step = pl.program_id(0)
    allowed = allowed_of(length_ref[0], pos_col_ref, pos_row_ref)
    keys = rot_ref[:, 2 * HEAD_DIM : 3 * HEAD_DIM]
    values = rot_ref[:, 3 * HEAD_DIM :]
    query = query_ref[:, : 2 * HEAD_DIM]
    grad = rows_of_ref(grad_ref)
    product = grad.astype(F32) * rows_of_ref(out_ref).astype(F32)
    ones = jnp.ones((8, HEAD_DIM), F32)
    grad_q, grad_k, grad_v = [], 0.0, 0.0
    for head in range(2):
        cut = slice(head * HEAD_DIM, (head + 1) * HEAD_DIM)
        delta = lax.dot_general(
            ones,
            product[:, cut],
            (((1,), (1,)), ((), ())),
            precision=lax.Precision.HIGHEST,
            preferred_element_type=F32,
        )[:1]
        scores = dot_lanes(keys, query[:, cut])
        probs = jnp.where(allowed, jnp.exp(scores - lse_ref[head : head + 1, :]), 0.0)
        grad_probs = dot_lanes(values, grad[:, cut])
        grad_scores = (probs * (grad_probs - delta)).astype(BF16)
        grad_v += jnp.dot(probs.astype(BF16), grad[:, cut], preferred_element_type=F32)
        grad_k += jnp.dot(grad_scores, query[:, cut], preferred_element_type=F32)
        grad_q.append(
            lax.dot_general(
                grad_scores, keys, (((0,), (0,)), ((), ())), preferred_element_type=F32
            )
        )
    dq_ref[...] = jnp.concatenate(grad_q, axis=1) * HEAD_DIM**-0.5
    both = jnp.concatenate([grad_k, grad_v], axis=1)

    @pl.when(step == 0)
    def _():
        dkv_ref[...] = both

    @pl.when(step > 0)
    def _():
        dkv_ref[...] += both


def attend_back(seq, rotated, grad, out, lse, positions, lengths):
    blocks, _, width, _ = grad.shape
    slots = blocks * width
    part = slots // STEPS
    return pl.pallas_call(
        attend_back_kernel,
        grid=(STEPS,),
        in_specs=[
            pl.BlockSpec(memory_space=pltpu.SMEM),
            fixed((slots, LANES)),
            pl.BlockSpec((part, LANES), lambda i: (i, 0)),
            part_of_seq(seq, blocks // STEPS, width, 2 * HEAD_DIM),
            part_of_seq(0, blocks // STEPS, width, 2 * HEAD_DIM),
            pl.BlockSpec((2, part), lambda i: (0, i)),
            fixed((slots, 1)),
            pl.BlockSpec((1, part), lambda i: (0, i)),
        ],
        out_specs=[
            pl.BlockSpec((part, 2 * HEAD_DIM), lambda i: (i, 0)),
            fixed((slots, 2 * HEAD_DIM)),
        ],
        out_shape=[jax.ShapeDtypeStruct((slots, 2 * HEAD_DIM), F32)] * 2,
        cost_estimate=cost_of(10),
        name="attend_back",
    )(
        lengths[seq : seq + 1], rotated, rotated, grad, out, lse,
        positions[:, None], positions[None, :],
    )


def project_back_kernel(
    dq_ref, dkv_ref, other_ref, proj_ref, cos_ref, sin_ref, gain_ref, grad_ref, sum_ref
):
    slots = dq_ref.shape[0]
    near, far = slots // 16 * len(NEAR), slots // 16 * len(FAR)
    cuts = [(near, near), (0, near), (2 * near + far, far), (2 * near, far)]
    other = jnp.concatenate([other_ref[at : at + size] for at, size in cuts], axis=0)
    grad = jnp.concatenate([dq_ref[...], dkv_ref[...] + other], axis=1)
    proj = rows_of_ref(proj_ref)
    scale_rows = lax.rsqrt(head_mean(proj * proj) + EPS)
    normed = proj * scale_rows
    turned = grad * twice(cos_ref) - swap_halves(grad) * twice(sin_ref)
    gained = turned * gain_ref[...]
    back = scale_rows * (gained - normed * head_mean(gained * normed))
    lane = lax.broadcasted_iota(jnp.int32, proj.shape, 1)
    grad_ref[...] = jnp.where(lane < 3 * HEAD_DIM, back, grad).astype(BF16).reshape(grad_ref.shape)
    sum_ref[...] = jnp.sum((turned * normed).reshape(-1, 8, LANES), axis=0)


def project_back(seq, grad_q, grad_kv, other_kv, proj, cosine, sine, gain):
    blocks, _, width, _ = proj.shape
    slots = blocks * width
    half = fixed((slots, 2 * HEAD_DIM))
    table = fixed((slots, LANES // 2))
    return pl.pallas_call(
        project_back_kernel,
        grid=(1,),
        in_specs=[
            half, half, half, of_seq(seq, blocks, width, LANES), table, table, fixed((1, LANES))
        ],
        out_specs=[of_seq(0, blocks, width, LANES), fixed((8, LANES))],
        out_shape=[
            jax.ShapeDtypeStruct((blocks, 1, width, LANES), BF16),
            jax.ShapeDtypeStruct((8, LANES), F32),
        ],
        cost_estimate=cost_of(4),
        name="project_back",
    )(grad_q, grad_kv, other_kv, proj, cosine, sine, gain)


def dot_rows(left, right):
    return lax.dot_general(left, right, (((0,), (0,)), ((), ())), preferred_element_type=F32)


def plain(left, right):
    return jnp.dot(left, right, preferred_element_type=F32)


def in_order(own, other, index):
    first = index == 0
    return jnp.concatenate([jnp.where(first, own, other), jnp.where(first, other, own)], axis=0)


def split_local(
    tokens, cotangent, q_weight, k_weight, v_weight, o_weight, gate_weight, up_weight,
    down_weight, attn_gain, ffn_gain, q_gain, k_gain, lengths, pair_order,
):
    seqs, width, _ = tokens.shape
    rank = lax.axis_index("ctx")
    side = lax.axis_index("fsdp")
    core = rank % 2
    mine = seqs * width
    q_rows, kv_rows, ff_rows = q_weight.shape[0], k_weight.shape[0], gate_weight.shape[0]

    x_rows = tokens.astype(F32).reshape(mine, D)
    scale_one = rms_scale(x_rows)
    normed_one = x_rows * scale_one
    kept = {}

    owners = block_owners(rank)
    blocks = owners.shape[0]
    within = jnp.arange(width, dtype=jnp.int32)
    half_blk = width // 2

    def positions_of(dealt):
        block_id = jnp.where(
            within[None, :] < half_blk, dealt[:, None], 2 * pair_order.shape[0] - 1 - dealt[:, None]
        )
        return (block_id * half_blk + within[None, :] % half_blk).reshape(-1)

    def tables(found):
        cosine, sine = rope_tables(found)
        return jnp.concatenate([cosine] * 4, axis=1), jnp.concatenate([-sine, sine] * 2, axis=1)

    cut = ff_rows // 2
    ff_own = [w[at : at + cut] for w in (gate_weight, up_weight, down_weight) for at in (0, cut)]
    ff_side = []

    def moving(index):
        return [(ff_own[index], SWAP_X)]

    def slot_positions(run):
        def work(order):
            come = tuple(send(w, SWAP_X) for w in (q_weight, k_weight, v_weight))
            return positions_of(order[owners]), come

        _, (kept["positions"], kept["side"]) = run((pair_order,), work)

    def attention_weights(found, q_side, k_side, v_side):
        kv_own, kv_side = jnp.stack([k_weight, v_weight]), jnp.stack([k_side, v_side])
        kv_half = jnp.concatenate(
            [jnp.where(side == 0, kv_own, kv_side), jnp.where(side == 0, kv_side, kv_own)], axis=1
        )
        kv_core = send(kv_half, SWAP_CORE)
        kv_full = jnp.concatenate(
            [jnp.where(core == 0, kv_half, kv_core), jnp.where(core == 0, kv_core, kv_half)], axis=1
        )
        weights = jnp.concatenate([q_weight, q_side, kv_full[0], kv_full[1]], axis=0)
        return weights, *tables(found)

    def slot_weights(run):
        (o_side,), (kept["w_attn"], *kept["tables"]) = run(
            (kept["positions"], *kept["side"]), attention_weights, [(o_weight, SWAP_X)]
        )
        kept["w_out"] = jnp.concatenate([o_weight, o_side], axis=0)

    def slot_join_move(index):
        def slot(run, blocks, join):
            (come,), (near,) = run(blocks, lambda *xs: (join(*xs),), moving(index))
            ff_side.append(come)
            return near

        return slot

    def slot_project(run, near):
        _, (kept["proj_near"], kept["x_near"]) = run(
            (near, kept["w_attn"]), lambda x, w: (project(x, w), x)
        )

    _, x_late = gather_blocks(
        (normed_one * attn_gain).astype(BF16),
        (slot_positions, slot_weights, slot_join_move(0), slot_project),
    )
    x_near = kept["x_near"]
    positions, (cosine, sine) = kept["positions"], kept["tables"]
    w_attn, w_out = kept["w_attn"], kept["w_out"]
    cut_rows = x_near.shape[0]
    gain_lanes = jnp.concatenate([q_gain, q_gain, k_gain, jnp.ones((HEAD_DIM,), F32)])[None, :]
    my_pos = positions_of(pair_order[rank][None])
    live = (my_pos[None, :] < lengths[:, None]).reshape(mine, 1)
    grad_out = jnp.where(live, cotangent.astype(F32).reshape(mine, D), 0.0)

    heads = []

    def slot_project_far(run):
        def work(near, weight, *late):
            far = join_far(*late)
            rows = jnp.concatenate([near, project(far, weight)], axis=0)
            return rows.reshape(blocks, seqs, width, LANES), far

        (come,), (kept["proj"], kept["x_far"]) = run(
            (kept["proj_near"], w_attn, *x_late), work, moving(1)
        )
        ff_side.append(come)

    def attend_beside(run, seq):
        work = lambda p: attend(seq, p, cosine, sine, gain_lanes, positions, lengths)
        (come,), found = run((kept["proj"],), work, moving(2 + seq))
        ff_side.append(come)
        heads.append(found)

    def slot_out(run, near):
        def work(*outs):
            rows = jnp.concatenate(outs, axis=1).reshape(-1, 2 * HEAD_DIM)
            return rows, core_sum(rows[cut_rows:], w_out)

        _, (kept["out_rows"], kept["first"]) = run([found[0] for found in heads], work)

    def slot_attend_last(run, blocks_near, join):
        attend_beside(run, 1)
        return blocks_near, join

    (grad_blocks, grad_join), grad_late = gather_blocks(
        grad_out.astype(BF16),
        (slot_project_far, lambda run: attend_beside(run, 0), slot_attend_last, slot_out),
    )
    out_rows, proj, x_far = kept["out_rows"], kept["proj"], kept["x_far"]

    def slot_grad_near(run):
        (come,), (kept["grad_near"],) = run(grad_blocks, lambda *xs: (grad_join(*xs),), moving(4))
        ff_side.append(come)

    def slot_grad_far(run):
        (come,), (kept["grad_far"],) = run(grad_late, lambda *xs: (join_far(*xs),), moving(5))
        ff_side.append(come)

    def slot_gate_up_weights(run):
        _, (kept["w_gate_up"],) = run(
            (*ff_own[:4], *ff_side[:4]), lambda *xs: (jnp.concatenate(xs, axis=0),)
        )

    resid = x_rows + scatter_blocks(
        kept["first"],
        (out_rows[:cut_rows], w_out),
        (idle, slot_grad_near, slot_grad_far, slot_gate_up_weights),
    )
    grad_near, grad_far = kept["grad_near"], kept["grad_far"]
    w_gate_up = kept["w_gate_up"]
    w_down = jnp.concatenate([*ff_own[4:], *ff_side[4:]], axis=0)
    scale_two = rms_scale(resid)
    normed_two = resid * scale_two

    def slot_hidden(name, grad):
        def slot(run):
            _, (kept[name],) = run((grad, w_down), lambda g, w: (project(g, w),))

        return slot

    def gates(both, grad_hidden):
        gate_part = jnp.concatenate([both[:, :ff_rows], both[:, 2 * ff_rows : 3 * ff_rows]], axis=1)
        up_part = jnp.concatenate([both[:, ff_rows : 2 * ff_rows], both[:, 3 * ff_rows :]], axis=1)
        hidden = (jax.nn.silu(gate_part) * up_part).astype(BF16)
        gate_low, up_low = gate_grads(grad_hidden, gate_part, up_part)
        grads = [gate_low[:, :ff_rows], up_low[:, :ff_rows], gate_low[:, ff_rows:], up_low[:, ff_rows:]]
        return hidden, jnp.concatenate(grads, axis=1)

    def slot_feed(run, blocks_near, join):
        def work(weight, *found):
            near = join(*found)
            return near, project(near, weight)

        _, near = run((w_gate_up, *blocks_near), work)
        return near

    def slot_gates(run, near):
        kept["x2_near"], both = near
        _, (kept["hidden"], kept["gate_up_low"]) = run((both, kept["hidden_near"]), gates)

    _, x2_late = gather_blocks(
        (normed_two * ffn_gain).astype(BF16),
        (
            slot_hidden("hidden_near", grad_near),
            slot_hidden("hidden_far", grad_far),
            slot_feed,
            slot_gates,
        ),
    )
    x2_near = kept["x2_near"]
    hidden_near, low_near = kept["hidden"], kept["gate_up_low"]
    x2_far = join_far(*x2_late)
    hidden_far, low_far = gates(project(x2_far, w_gate_up), kept["hidden_far"])

    def slot_sums(run):
        work = lambda near, far, weight: (core_sum(far, weight), core_sum(near, weight))
        _, kept["out_parts"] = run((hidden_near, hidden_far, w_down), work)

    def both_parts(*parts):
        near, far, right_near, right_far = parts
        return dot_rows(near, right_near) + dot_rows(far, right_far)

    half_ff = 2 * ff_rows

    def slot_leave(run):
        def work(*parts):
            gate_up = both_parts(parts[0][:, half_ff:], parts[1][:, half_ff:], *parts[2:4])
            return jnp.split(gate_up.astype(BF16), 4)

        _, kept["gate_up_leave"] = run((low_near, low_far, x2_near, x2_far), work)

    def slot_down_leave(run):
        def work(*parts):
            down = both_parts(parts[0][:, ff_rows:], parts[1][:, ff_rows:], *parts[2:4])
            return jnp.split(down.astype(BF16), 2)

        _, kept["down_leave"] = run((hidden_near, hidden_far, grad_near, grad_far), work)

    grad_norm2 = scatter_blocks(
        core_sum(low_far, w_gate_up),
        (low_near, w_gate_up),
        (idle, slot_sums, slot_leave, slot_down_leave),
    )
    pieces = [*kept["gate_up_leave"], *kept["down_leave"]]
    came = []
    grad_ffn_gain = jnp.sum(grad_norm2 * normed_two, axis=0)
    grad_resid = grad_out + rms_back(grad_norm2 * ffn_gain, normed_two, scale_two)

    def slot_gate_up_stay(run):
        def work(*parts):
            return (both_parts(parts[0][:, :half_ff], parts[1][:, :half_ff], *parts[2:4]),)

        (come,), (kept["gate_up"],) = run(
            (low_near, low_far, x2_near, x2_far), work, [(pieces[0], SWAP_X)]
        )
        came.append(come)

    def slot_down_stay(run):
        def work(*parts):
            return (both_parts(parts[0][:, :ff_rows], parts[1][:, :ff_rows], *parts[2:4]),)

        (come,), (kept["down"],) = run(
            (hidden_near, hidden_far, grad_near, grad_far), work, [(pieces[1], SWAP_X)]
        )
        came.append(come)

    def slot_join_aside(run, blocks, join):
        (come,), (near,) = run(blocks, lambda *xs: (join(*xs),), [(pieces[2], SWAP_X)])
        came.append(come)
        return near

    def grad_heads(grad, weight):
        return project(grad, weight).astype(BF16)

    def slot_grad_heads(run, near):
        _, (kept["heads_near"], kept["da_near"]) = run(
            (near, w_out), lambda x, w: (grad_heads(x, w), x)
        )

    _, da_late = gather_blocks(
        grad_resid.astype(BF16),
        (slot_gate_up_stay, slot_down_stay, slot_join_aside, slot_grad_heads),
    )
    da_near = kept["da_near"]
    da_far = join_far(*da_late)

    def slot_grad_o(run):
        def work(near, x, w):
            rows = jnp.concatenate([near, grad_heads(x, w)], axis=0)
            return (rows.reshape(blocks, seqs, width, 2 * HEAD_DIM),)

        _, (kept["grad_o"],) = run((kept["heads_near"], da_far, w_out), work)

    def slot_attend_back(seq):
        def slot(run):
            out, lse, rotated = heads[seq]

            def work(grad, *before):
                come = tuple(send(x, SWAP_CORE) for x in before)
                return attend_back(seq, rotated, grad, out, lse, positions, lengths), come

            before = [kept["back", seq - 1][1]] if seq else []
            (come,), (kept["back", seq], other) = run(
                (kept["grad_o"], *before), work, [(pieces[3 + seq], SWAP_X)]
            )
            came.append(come)
            kept["other"] = other

        return slot

    def slot_project_back(run):
        def work(found, others):
            others = [*others, send(found[-1][1], SWAP_CORE)]
            grads, sums = [], 0.0
            for s, ((grad_q, grad_kv), other_kv) in enumerate(zip(found, others)):
                rows, part = project_back(
                    s, grad_q, grad_kv, other_kv, proj, cosine, sine, gain_lanes
                )
                grads.append(rows)
                sums = sums + jnp.sum(part, axis=0)
            return jnp.concatenate(grads, axis=1).reshape(blocks * mine, LANES), sums

        (come,), (kept["grad_rows"], kept["gain_sums"]) = run(
            ([kept["back", s] for s in range(seqs)], kept["other"]), work, [(pieces[5], SWAP_X)]
        )
        came.append(come)

    out_sum = scatter_blocks(
        *kept["out_parts"],
        (slot_grad_o, slot_attend_back(0), slot_attend_back(1), slot_project_back),
    )
    grad_rows, gain_sums = kept["grad_rows"], kept["gain_sums"]
    row = jnp.arange(LANES)[:, None] // HEAD_DIM
    w_once = jnp.where((row < 2) | (row == 2 + core), w_attn, 0).astype(BF16)

    def slot_attn_grads(run):
        def work(grads, near, far):
            full = both_parts(grads[:cut_rows], grads[cut_rows:], near, far)
            kv_grads = full[2 * q_rows :].reshape(2, 2, 2, kv_rows, D)
            kv_mine = jnp.where(core == 0, kv_grads[:, 0], kv_grads[:, 1])
            kv_stay = jnp.where(side == 0, kv_mine[:, 0], kv_mine[:, 1])
            kv_leave = jnp.where(side == 0, kv_mine[:, 1], kv_mine[:, 0])
            stay = jnp.concatenate([full[:q_rows], kv_stay.reshape(2 * kv_rows, D)])
            leave = jnp.concatenate([full[q_rows : 2 * q_rows], kv_leave.reshape(2 * kv_rows, D)])
            return stay, leave.astype(BF16)

        _, kept["attn"] = run((grad_rows, x_near, x_far), work)

    def slot_out_grads(run):
        def work(rows, near, far):
            stay, leave = jnp.split(both_parts(rows[:cut_rows], rows[cut_rows:], near, far), 2)
            return stay, leave.astype(BF16)

        (kept["attn_come"],), kept["o"] = run(
            (out_rows, da_near, da_far), work, [(kept["attn"][1], SWAP_X)]
        )

    def slot_finish(run):
        def work(attn_stay, attn_come, gate_up, down, f_sum, *xs):
            attn_grads = attn_stay + attn_come.astype(F32)
            owned = jnp.concatenate([q_weight, k_weight, v_weight], axis=0).astype(F32)
            gains = jnp.concatenate(
                [
                    jnp.sum(owned * attn_grads, axis=0) / attn_gain,
                    grad_ffn_gain,
                    gain_sums[:HEAD_DIM] + gain_sums[HEAD_DIM : 2 * HEAD_DIM],
                    0.5 * gain_sums[2 * HEAD_DIM : 3 * HEAD_DIM],
                ]
            )
            gains = gains + send(gains, SWAP_CORE)
            gains = gains + send(gains, SWAP_X)
            gate_up = gate_up + jnp.concatenate(xs[:4]).astype(F32)
            down = down + jnp.concatenate(xs[4:]).astype(F32)
            block = jnp.where(live, resid + f_sum, 0.0).astype(BF16).reshape(seqs, width, D)
            return gains, attn_grads, gate_up, down, block

        (kept["o_come"],), kept["finish"] = run(
            (*kept["attn"][:1], kept["attn_come"], kept["gate_up"], kept["down"], out_sum, *came),
            work,
            [(kept["o"][1], SWAP_X)],
        )

    def slot_gains(run):
        gains = kept["finish"][0]
        (come,), kept["o_grad"] = run(
            (*kept["o"][:1], kept["o_come"]),
            lambda stay, come: (stay + come.astype(F32),),
            [(gains, SWAP_Y)],
        )
        gains = gains + come
        kept["gains"] = (gains + send(gains, SWAP_Z0)) + (
            send(gains, SWAP_Z1) + send(gains, SWAP_Z)
        )

    grad_norm1 = scatter_blocks(
        core_sum(grad_rows[cut_rows:], w_once),
        (grad_rows[:cut_rows], w_once),
        (slot_attn_grads, slot_out_grads, slot_finish, slot_gains),
    )
    _, attn_grads, gate_up_grad, down_grad, block_out = kept["finish"]
    (o_grad,) = kept["o_grad"]
    gains = kept["gains"]
    grad_tokens = (grad_resid + rms_back(grad_norm1 * attn_gain, normed_one, scale_one)).reshape(
        seqs, width, D
    )
    return (
        block_out,
        grad_tokens,
        attn_grads[:q_rows],
        attn_grads[q_rows : q_rows + kv_rows],
        attn_grads[q_rows + kv_rows :],
        o_grad,
        gate_up_grad[:ff_rows],
        gate_up_grad[ff_rows:],
        down_grad,
        gains[:D],
        gains[D : 2 * D],
        gains[2 * D : 2 * D + HEAD_DIM],
        gains[2 * D + HEAD_DIM :],
    )


def solution(mesh):
    body = split_local if fits_split(mesh) else local
    in_specs = (
        P("fsdp", "ctx", None),
        P("fsdp", "ctx", None),
        P(("ctx", "fsdp"), None),
        P(("ctx", "fsdp"), None),
        P(("ctx", "fsdp"), None),
        P(("ctx", "fsdp"), None),
        P(("ctx", "fsdp"), None),
        P(("ctx", "fsdp"), None),
        P(("ctx", "fsdp"), None),
        P(),
        P(),
        P(),
        P(),
        P("fsdp"),
        P(),
    )
    out_specs = (
        P("fsdp", "ctx", None),
        P("fsdp", "ctx", None),
        P(("ctx", "fsdp"), None),
        P(("ctx", "fsdp"), None),
        P(("ctx", "fsdp"), None),
        P(("ctx", "fsdp"), None),
        P(("ctx", "fsdp"), None),
        P(("ctx", "fsdp"), None),
        P(("ctx", "fsdp"), None),
        P(),
        P(),
        P(),
        P(),
    )
    return jax.shard_map(body, mesh=mesh, in_specs=in_specs, out_specs=out_specs, check_vma=False)
```

```python
import functools
import math

import jax
import jax.numpy as jnp
from jax import lax
from jax.experimental import pallas as pl
from jax.experimental.pallas import tpu as pltpu
from jax.sharding import PartitionSpec as P

D = 2048
HEADS = 32
KV_HEADS = 8
HEAD_DIM = 64
FF = 8192


EPS = 1e-05
THETA = 1000000.0
NEG = -1e30


def rms_scale(values):
    return lax.rsqrt(jnp.mean(values * values, axis=-1, keepdims=True) + EPS)


def rms_back(grad_normed, normed, scale_rows):
    return scale_rows * (
        grad_normed - normed * jnp.mean(grad_normed * normed, axis=-1, keepdims=True)
    )


def rope_tables(positions):
    half = HEAD_DIM // 2
    freq = THETA ** (-(jnp.arange(half, dtype=jnp.float32) * 2.0 / HEAD_DIM))
    angle = positions.astype(jnp.float32)[:, None] * freq[None, :]
    return (jnp.cos(angle), jnp.sin(angle))


def rotate(values, cosine, sine):
    half = values.shape[-1] // 2
    first = values[..., :half]
    second = values[..., half:]
    return jnp.concatenate(
        [first * cosine - second * sine, second * cosine + first * sine], axis=-1
    )


def slot_positions(pair_order, width_pair, first, count):
    slot = first + jnp.arange(count, dtype=jnp.int32)
    owner = slot // width_pair
    within = slot % width_pair
    half_blk = width_pair // 2
    pair = pair_order[owner]
    block_id = jnp.where(within < half_blk, pair, 2 * pair_order.shape[0] - 1 - pair)
    return block_id * half_blk + within % half_blk


def block_mask(query_pos, key_part, lengths):
    return (key_part[None, None, :] <= query_pos[None, :, None]) & (
        key_part[None, None, :] < lengths[:, None, None]
    )


def project(inputs, weight):
    return jnp.einsum("td,fd->tf", inputs, weight, preferred_element_type=jnp.float32)


def gate_grads(grad_hidden, gate_part, up_part):
    sigma = jax.nn.sigmoid(gate_part)
    grad_gate = grad_hidden * up_part * sigma * (1.0 + gate_part * (1.0 - sigma))
    grad_up = grad_hidden * gate_part * sigma
    return (grad_gate.astype(jnp.bfloat16), grad_up.astype(jnp.bfloat16))


def block_grads(q_rot, grad_o_low, lse, delta, k_blk, v_blk, allowed, scale):
    scores = (
        jnp.einsum("sqhgd,sjhd->sqhgj", q_rot, k_blk, preferred_element_type=jnp.float32) * scale
    )
    scores = jnp.where(allowed[:, :, None, None, :], scores, NEG)
    probs = jnp.exp(scores - lse[..., None])
    grad_probs = jnp.einsum(
        "sqhgd,sjhd->sqhgj", grad_o_low, v_blk, preferred_element_type=jnp.float32
    )
    grad_scores = (probs * (grad_probs - delta[..., None])).astype(jnp.bfloat16)
    return (probs, grad_scores)


def local(
    tokens,
    cotangent,
    q_weight,
    k_weight,
    v_weight,
    o_weight,
    gate_weight,
    up_weight,
    down_weight,
    attn_gain,
    ffn_gain,
    q_gain,
    k_gain,
    lengths,
    pair_order,
):
    seq_grp = tokens.shape[0]
    width_pair = tokens.shape[1]
    groups = HEADS // KV_HEADS
    q_width = HEADS * HEAD_DIM
    kv_width = KV_HEADS * HEAD_DIM
    scale = HEAD_DIM ** (-0.5)
    tok_rows = seq_grp * width_pair
    slots = width_pair * pair_order.shape[0]
    key_blk = math.gcd(slots, 512)
    key_count = slots // key_blk
    dev_count = lax.axis_size("ctx") * lax.axis_size("fsdp")
    local_pos = slot_positions(
        pair_order, width_pair, lax.axis_index("ctx") * width_pair, width_pair
    )
    key_pos = slot_positions(pair_order, width_pair, 0, slots)
    live_rows = (local_pos[None, :] < lengths[:, None]).reshape(tok_rows, 1)
    cosine, sine = rope_tables(local_pos)
    cosine = cosine[None, :, None, :]
    sine = sine[None, :, None, :]
    x_rows = tokens.astype(jnp.float32).reshape(tok_rows, D)
    scale_one = rms_scale(x_rows)
    normed_one = x_rows * scale_one
    x_norm = (normed_one * attn_gain).astype(jnp.bfloat16)
    w_query, w_key, w_value, w_out = (
        lax.all_gather(q_weight, ("ctx", "fsdp"), axis=0, tiled=True),
        lax.all_gather(k_weight, ("ctx", "fsdp"), axis=0, tiled=True),
        lax.all_gather(v_weight, ("ctx", "fsdp"), axis=0, tiled=True),
        lax.all_gather(o_weight, ("ctx", "fsdp"), axis=0, tiled=True),
    )
    q_proj = project(x_norm, w_query).reshape(seq_grp, width_pair, HEADS, HEAD_DIM)
    k_proj = project(x_norm, w_key).reshape(seq_grp, width_pair, KV_HEADS, HEAD_DIM)
    v_low = project(x_norm, w_value).astype(jnp.bfloat16).reshape(seq_grp, width_pair, kv_width)
    q_scale = rms_scale(q_proj)
    q_normed = q_proj * q_scale
    q_rot = (
        rotate(q_normed * q_gain, cosine, sine)
        .astype(jnp.bfloat16)
        .reshape(seq_grp, width_pair, KV_HEADS, groups, HEAD_DIM)
    )
    k_scale = rms_scale(k_proj)
    k_normed = k_proj * k_scale
    k_rot = (
        rotate(k_normed * k_gain, cosine, sine)
        .astype(jnp.bfloat16)
        .reshape(seq_grp, width_pair, kv_width)
    )
    k_all, v_all = (
        lax.all_gather(k_rot, "ctx", axis=1, tiled=True),
        lax.all_gather(v_low, "ctx", axis=1, tiled=True),
    )
    k_all = k_all.reshape(seq_grp, slots, KV_HEADS, HEAD_DIM)
    v_all = v_all.reshape(seq_grp, slots, KV_HEADS, HEAD_DIM)

    def key_slices(first, count):
        k_blk = lax.dynamic_slice_in_dim(k_all, first, count, 1)
        v_blk = lax.dynamic_slice_in_dim(v_all, first, count, 1)
        allowed = block_mask(local_pos, lax.dynamic_slice_in_dim(key_pos, first, count, 0), lengths)
        return (k_blk, v_blk, allowed)

    def forward_step(index, carry):
        top, total, summed = carry
        k_blk, v_blk, allowed = key_slices(index * key_blk, key_blk)
        scores = (
            jnp.einsum("sqhgd,sjhd->sqhgj", q_rot, k_blk, preferred_element_type=jnp.float32)
            * scale
        )
        scores = jnp.where(allowed[:, :, None, None, :], scores, NEG)
        new_top = jnp.maximum(top, jnp.max(scores, axis=-1))
        shrink = jnp.exp(top - new_top)
        probs = jnp.exp(scores - new_top[..., None])
        total = total * shrink + jnp.sum(probs, axis=-1)
        summed = summed * shrink[..., None] + jnp.einsum(
            "sqhgj,sjhd->sqhgd",
            probs.astype(jnp.bfloat16),
            v_blk,
            preferred_element_type=jnp.float32,
        )
        return (new_top, total, summed)

    stat_shape = (seq_grp, width_pair, KV_HEADS, groups)
    start_carry = (
        jnp.full(stat_shape, NEG, jnp.float32),
        jnp.zeros(stat_shape, jnp.float32),
        jnp.zeros(stat_shape + (HEAD_DIM,), jnp.float32),
    )
    top, total, summed = lax.fori_loop(0, key_count, forward_step, start_carry)
    lse = top + jnp.log(total)
    o_low = (summed / total[..., None]).astype(jnp.bfloat16)
    o_rows = o_low.reshape(tok_rows, q_width)
    resid = x_rows + jnp.einsum("tf,fd->td", o_rows, w_out, preferred_element_type=jnp.float32)
    scale_two = rms_scale(resid)
    normed_two = resid * scale_two
    x_norm2 = (normed_two * ffn_gain).astype(jnp.bfloat16)
    grad_out = jnp.where(live_rows, cotangent.astype(jnp.float32).reshape(tok_rows, D), 0.0)
    grad_low = grad_out.astype(jnp.bfloat16)
    pieces = (
        lax.all_gather(gate_weight, ("ctx", "fsdp"), axis=0, tiled=True),
        lax.all_gather(up_weight, ("ctx", "fsdp"), axis=0, tiled=True),
        lax.all_gather(down_weight, ("ctx", "fsdp"), axis=0, tiled=True),
    )
    gate_part = project(x_norm2, pieces[0])
    up_part = project(x_norm2, pieces[1])
    hidden_part = (jax.nn.silu(gate_part) * up_part).astype(jnp.bfloat16)
    out_sum = jnp.einsum("tf,fd->td", hidden_part, pieces[2], preferred_element_type=jnp.float32)
    gate_all = gate_part
    up_all = up_part
    hidden = (jax.nn.silu(gate_all) * up_all).astype(jnp.bfloat16)
    pieces = (
        lax.all_gather(gate_weight, ("ctx", "fsdp"), axis=0, tiled=True),
        lax.all_gather(up_weight, ("ctx", "fsdp"), axis=0, tiled=True),
        lax.all_gather(down_weight, ("ctx", "fsdp"), axis=0, tiled=True),
    )
    count = pieces[0].shape[0]
    gate_part = gate_all
    up_part = up_all
    grad_gate_part, grad_up_part = gate_grads(project(grad_low, pieces[2]), gate_part, up_part)
    grad_sum = jnp.einsum(
        "tf,fd->td", grad_gate_part, pieces[0], preferred_element_type=jnp.float32
    ) + jnp.einsum("tf,fd->td", grad_up_part, pieces[1], preferred_element_type=jnp.float32)
    gate_grad_all = grad_gate_part
    up_grad_all = grad_up_part
    block_out = (
        jnp.where(live_rows, resid + out_sum, 0.0)
        .astype(jnp.bfloat16)
        .reshape(seq_grp, width_pair, D)
    )
    ffn_dev = FF // dev_count
    owners = lax.axis_size(("ctx", "fsdp")) * (3 * ffn_dev) // (3 * ffn_dev)
    first = jnp.int32(0) // (3 * ffn_dev) * ffn_dev
    grad_gate_part = jnp.einsum(
        "tf,td->fd", gate_grad_all, x_norm2, preferred_element_type=jnp.float32
    )
    grad_up_part = jnp.einsum("tf,td->fd", up_grad_all, x_norm2, preferred_element_type=jnp.float32)
    grad_down_part = jnp.einsum("tf,td->fd", hidden, grad_low, preferred_element_type=jnp.float32)
    stacked = jnp.stack(
        [
            grad_gate_part.reshape(owners, ffn_dev, D),
            grad_up_part.reshape(owners, ffn_dev, D),
            grad_down_part.reshape(owners, ffn_dev, D),
        ],
        axis=1,
    )
    ffn_grads = lax.psum_scatter(
        stacked.reshape(lax.axis_size(("ctx", "fsdp")) * (3 * ffn_dev), D),
        ("ctx", "fsdp"),
        scatter_dimension=0,
        tiled=True,
    )
    grad_ffn_gain = jnp.sum(grad_sum * normed_two, axis=0)
    grad_resid = grad_out + rms_back(grad_sum * ffn_gain, normed_two, scale_two)
    grad_attn_low = grad_resid.astype(jnp.bfloat16)
    grad_o_low = (
        project(grad_attn_low, w_out)
        .astype(jnp.bfloat16)
        .reshape(seq_grp, width_pair, KV_HEADS, groups, HEAD_DIM)
    )
    delta = jnp.sum(grad_o_low.astype(jnp.float32) * o_low.astype(jnp.float32), axis=-1)
    dq_zero = jnp.zeros((seq_grp, width_pair, KV_HEADS, groups, HEAD_DIM), jnp.float32)
    kv_cols = seq_grp * 2 * kv_width

    def key_value_grads(probs, grad_scores):
        grad_k_blk = (
            jnp.einsum("sqhgj,sqhgd->jshd", grad_scores, q_rot, preferred_element_type=jnp.float32)
            * scale
        )
        grad_v_blk = jnp.einsum(
            "sqhgj,sqhgd->jshd",
            probs.astype(jnp.bfloat16),
            grad_o_low,
            preferred_element_type=jnp.float32,
        )
        return jnp.stack([grad_k_blk, grad_v_blk], axis=2).reshape(probs.shape[-1], kv_cols)

    def both_step(grad_q, index):
        k_blk, v_blk, allowed = key_slices(index * key_blk, key_blk)
        probs, grad_scores = block_grads(
            q_rot, grad_o_low, lse, delta, k_blk, v_blk, allowed, scale
        )
        grad_q = (
            grad_q
            + jnp.einsum(
                "sqhgj,sjhd->sqhgd", grad_scores, k_blk, preferred_element_type=jnp.float32
            )
            * scale
        )
        return (grad_q, key_value_grads(probs, grad_scores))

    grad_q_rot, kv_blocks = lax.scan(both_step, dq_zero, jnp.arange(key_count))
    kv_grad = lax.psum_scatter(
        kv_blocks.reshape(slots, kv_cols), "ctx", scatter_dimension=0, tiled=True
    )
    kv_grad = jnp.transpose(
        kv_grad.reshape(width_pair, seq_grp, 2, KV_HEADS, HEAD_DIM), (1, 0, 2, 3, 4)
    )
    grad_q_pre = rotate(grad_q_rot.reshape(seq_grp, width_pair, HEADS, HEAD_DIM), cosine, -sine)
    grad_k_pre = rotate(kv_grad[:, :, 0], cosine, -sine)
    grad_q_gain = jnp.sum(grad_q_pre * q_normed, axis=(0, 1, 2))
    grad_k_gain = jnp.sum(grad_k_pre * k_normed, axis=(0, 1, 2))
    grad_q_proj = (
        rms_back(grad_q_pre * q_gain, q_normed, q_scale)
        .reshape(tok_rows, q_width)
        .astype(jnp.bfloat16)
    )
    grad_k_proj = (
        rms_back(grad_k_pre * k_gain, k_normed, k_scale)
        .reshape(tok_rows, kv_width)
        .astype(jnp.bfloat16)
    )
    grad_v_proj = kv_grad[:, :, 1].reshape(tok_rows, kv_width).astype(jnp.bfloat16)
    grad_norm1 = jnp.einsum("tf,fd->td", grad_q_proj, w_query, preferred_element_type=jnp.float32)
    grad_norm1 = grad_norm1 + jnp.einsum(
        "tf,fd->td", grad_k_proj, w_key, preferred_element_type=jnp.float32
    )
    grad_norm1 = grad_norm1 + jnp.einsum(
        "tf,fd->td", grad_v_proj, w_value, preferred_element_type=jnp.float32
    )
    grad_attn_gain = jnp.sum(grad_norm1 * normed_one, axis=0)
    grad_tokens = (grad_resid + rms_back(grad_norm1 * attn_gain, normed_one, scale_one)).reshape(
        seq_grp, width_pair, D
    )
    q_dev = q_width // dev_count
    kv_dev = kv_width // dev_count
    per_dev = 2 * q_dev + 2 * kv_dev
    owners = lax.axis_size(("ctx", "fsdp")) * per_dev // per_dev

    def rows_of(grad_rows, inputs, each):
        return jnp.einsum(
            "tf,td->fd", grad_rows, inputs, preferred_element_type=jnp.float32
        ).reshape(owners, each, D)

    joined = jnp.concatenate(
        [
            rows_of(grad_q_proj, x_norm, q_dev),
            rows_of(grad_k_proj, x_norm, kv_dev),
            rows_of(grad_v_proj, x_norm, kv_dev),
            rows_of(o_rows, grad_attn_low, q_dev),
        ],
        axis=1,
    )
    attn_grads = lax.psum_scatter(
        joined.reshape(lax.axis_size(("ctx", "fsdp")) * per_dev, D),
        ("ctx", "fsdp"),
        scatter_dimension=0,
        tiled=True,
    )
    grad_attn_gain, grad_ffn_gain, grad_q_gain, grad_k_gain = lax.psum(
        (grad_attn_gain, grad_ffn_gain, grad_q_gain, grad_k_gain), ("ctx", "fsdp")
    )
    return (
        block_out,
        grad_tokens,
        attn_grads[:q_dev],
        attn_grads[q_dev : q_dev + kv_dev],
        attn_grads[q_dev + kv_dev : q_dev + 2 * kv_dev],
        attn_grads[q_dev + 2 * kv_dev :],
        ffn_grads[:ffn_dev],
        ffn_grads[ffn_dev : 2 * ffn_dev],
        ffn_grads[2 * ffn_dev :],
        grad_attn_gain,
        grad_ffn_gain,
        grad_q_gain,
        grad_k_gain,
    )


AXES = ("ctx", "fsdp")
RANKS = 16
LANES = 4 * HEAD_DIM
BF16 = jnp.bfloat16
F32 = jnp.float32
NEVER = 1 << 30


def fits_split(mesh):
    return mesh.shape["ctx"] == RANKS and mesh.shape["fsdp"] == 2


CYCLE = ((0, 0), (1, 0), (2, 0), (3, 0), (3, 1), (2, 1), (1, 1), (0, 1))
CHIPS = len(CYCLE)
NEAR = (2, -2, 1, -1, 0)
FAR = (4, 3, -3)


def index_of(z, y, core, x):
    return z * 8 + y * 4 + core * 2 + x


def pairs_of(move):
    places = [(z, y, c, x) for z in range(4) for y in range(2) for c in range(2) for x in range(2)]
    return [(index_of(*place), index_of(*move(*place))) for place in places]


def along_cycle(step):
    def move(z, y, core, x):
        return (*CYCLE[(CYCLE.index((z, y)) + step) % CHIPS], core, x)

    return pairs_of(move)


SWAP_X = pairs_of(lambda z, y, c, x: (z, y, c, 1 - x))
SWAP_CORE = pairs_of(lambda z, y, c, x: (z, y, 1 - c, x))
SWAP_Y = pairs_of(lambda z, y, c, x: (z, 1 - y, c, x))
SWAP_Z0 = pairs_of(lambda z, y, c, x: (z ^ 1, y, c, x))
SWAP_Z1 = pairs_of(lambda z, y, c, x: (z ^ 2, y, c, x))
SWAP_Z = pairs_of(lambda z, y, c, x: (3 - z, y, c, x))
AHEAD = along_cycle(1)
BEHIND = along_cycle(-1)


def block_owners(rank):
    place = jnp.array([CYCLE.index((chip // 2, chip % 2)) for chip in range(CHIPS)], jnp.int32)
    chips = jnp.array([2 * z + y for z, y in CYCLE], jnp.int32)
    around = jnp.array(NEAR + NEAR + FAR + FAR, jnp.int32)
    turn = jnp.array((0,) * 5 + (1,) * 5 + (0,) * 3 + (1,) * 3, jnp.int32)
    return chips[(place[rank // 2] + around) % CHIPS] * 2 + (rank % 2) ^ turn


def send(value, pairs):
    return lax.ppermute(value, AXES, pairs)


def window(moves, inputs=(), work=None):
    values, inputs = lax.optimization_barrier((tuple(v for v, _ in moves), tuple(inputs)))
    come = tuple(send(v, pairs) for v, (_, pairs) in zip(values, moves))
    done = work(*inputs) if work else ()
    return lax.optimization_barrier((come, done))


def idle(run):
    run()


def collect_kernel(starts, *refs):
    count = len(starts)
    pieces, (whole, held, come_sems, leave_sems) = refs[:count], refs[-4:]
    coming, leaving, at = [], [], 0
    for i, (piece, start) in enumerate(zip(pieces, starts)):
        part = held.at[pl.ds(at, piece.shape[0])]
        at += piece.shape[0]
        coming.append(pltpu.make_async_copy(piece, part, come_sems.at[i]))
        place = whole.at[pl.ds(start, piece.shape[0])]
        leaving.append(pltpu.make_async_copy(part, place, leave_sems.at[i]))
    for copy in coming:
        copy.start()
    for come, leave in zip(coming, leaving):
        come.wait()
        leave.start()
    for copy in leaving:
        copy.wait()


def collect(pieces, starts, whole):
    inner = functools.partial(collect_kernel, starts)
    given = isinstance(whole, jax.Array)
    anywhere = pl.BlockSpec(memory_space=pl.ANY)
    rows = sum(piece.shape[0] for piece in pieces)
    return pl.pallas_call(
        inner,
        in_specs=[anywhere] * (len(pieces) + given),
        out_specs=anywhere,
        out_shape=jax.ShapeDtypeStruct(whole.shape, whole.dtype),
        scratch_shapes=[
            pltpu.VMEM((rows, whole.shape[1]), whole.dtype),
            pltpu.SemaphoreType.DMA((len(pieces),)),
            pltpu.SemaphoreType.DMA((len(pieces),)),
        ],
        input_output_aliases={len(pieces): 0} if given else {},
        cost_estimate=cost_of(0.3 * len(pieces)),
        name="collect",
    )(*pieces, *([whole] if given else []))


def gather_blocks(piece, slots):
    rows = piece.shape[0]
    half = rows // 2
    back, front = [piece], [piece]
    near = None
    for step, slot in enumerate(slots):
        leave = (back[-1], front[-1])
        if step == 3:
            leave = (back[-1][:half], front[-1][half:])

        def run(inputs=(), work=None, moves=()):
            both = [(leave[0], AHEAD), (leave[1], BEHIND), *moves]
            come, done = window(both, inputs, work)
            back.append(come[0])
            front.append(come[1])
            return come[2:], done

        if step == 1:
            found = [front[1], back[1], piece]
            early = [send(block, SWAP_CORE) for block in found]
        if step < 2:
            slot(run)
        elif step == 2:
            blocks = [front[2], back[2], *found]

            def join(*blocks_early):
                mine, other = blocks_early[:5], blocks_early[5:]
                other = [send(block, SWAP_CORE) for block in mine[:2]] + list(other)
                starts = tuple(i * rows for i in range(10))
                shape = jax.ShapeDtypeStruct((10 * rows, piece.shape[1]), piece.dtype)
                return collect([*mine, *other], starts, shape)

            near = slot(run, [*blocks, *early], join)
        else:
            slot(run, near)
    return near, (back[4], front[4], front[3], back[3])


def join_far(first, second, third, fourth):
    mine = [first, second, third, fourth]
    half, rows = first.shape[0], third.shape[0]
    starts = (0, half, rows, 2 * rows)
    across = 3 * rows
    return collect(
        mine + [send(block, SWAP_CORE) for block in mine],
        starts + tuple(across + start for start in starts),
        jax.ShapeDtypeStruct((2 * across, first.shape[1]), first.dtype),
    )


def add_low(left, right):
    return (left.astype(F32) + right.astype(F32)).astype(BF16)


def core_sum(own, other, weight):
    come = send(plain(other, weight).astype(BF16), SWAP_CORE)
    return (plain(own, weight) + come.astype(F32)).astype(BF16)


def scatter_joined(far, near, slots):
    state = {}

    def stepper(leave, parts):
        def run(inputs=(), work=None, moves=(), early=()):
            both = [*early, (leave[0], AHEAD), (leave[1], BEHIND), *moves]

            def all_work(*xs):
                made = (core_sum(*xs[:3]),) if parts else ()
                return made, tuple(work(*xs[len(parts) :]) if work else ())

            come, (made, done) = window(both, tuple(parts) + tuple(inputs), all_work)
            state["come"] = come[len(early) : len(early) + 2]
            if made:
                state["made"] = made[0]
            return come[: len(early)] + come[len(early) + 2 :], done

        return run

    late = isinstance(far, tuple)
    first, rest = far if late else (far[: far.shape[0] // 3], ())
    rows = first.shape[0]
    half = rows // 2
    slots[0](stepper((first[:half], first[half:]), rest))
    come, made = state["come"], state["made"] if late else far[rows:]
    ahead, behind = made[:rows], made[rows:]
    leave = (
        jnp.concatenate([add_low(ahead[:half], come[0]), ahead[half:]]),
        jnp.concatenate([behind[:half], add_low(behind[half:], come[1])]),
    )
    for step in (1, 2, 3):
        slots[step](stepper(leave, near if late and step == 1 else ()))
        come, made = state["come"], state["made"] if late else near
        at = (step - 1) * 2 * rows
        if step < 3:
            leave = (
                add_low(made[at : at + rows], come[0]),
                add_low(made[at + rows : at + 2 * rows], come[1]),
            )
    return made[4 * rows :].astype(F32) + come[0].astype(F32) + come[1].astype(F32)


def scatter_blocks(near, far, weight, slots):
    across, cut = far.shape[0] // 2, near.shape[0] // 2
    rows = across // 3
    first = core_sum(far[:rows], far[across : across + rows], weight)
    rest = (far[rows:across], far[across + rows :], weight)
    return scatter_joined((first, rest), (near[:cut], near[cut:], weight), slots)


def head_sums():
    row = lax.broadcasted_iota(jnp.int32, (LANES, LANES), 0) // HEAD_DIM
    col = lax.broadcasted_iota(jnp.int32, (LANES, LANES), 1) // HEAD_DIM
    return jnp.where(row == col, 1.0 / HEAD_DIM, 0.0).astype(BF16)


def head_mean(values):
    high = values.astype(BF16)
    rest = (values - high.astype(F32)).astype(BF16)
    sums = head_sums()
    return plain(high, sums) + plain(rest, sums)


def swap_halves(values):
    lane = lax.broadcasted_iota(jnp.int32, values.shape, 1)
    return jnp.where(
        lane % HEAD_DIM < HEAD_DIM // 2,
        pltpu.roll(values, LANES - HEAD_DIM // 2, 1),
        pltpu.roll(values, HEAD_DIM // 2, 1),
    )


def twice(ref):
    return jnp.concatenate([ref[...]] * 2, axis=1)


def dot_lanes(left, right):
    return lax.dot_general(left, right, (((1,), (1,)), ((), ())), preferred_element_type=F32)


def allowed_of(length, pos_col_ref, pos_row_ref):
    col = pos_col_ref[...]
    return jnp.where(col < length, col, NEVER) <= pos_row_ref[...]


def rows_of_ref(ref):
    value = ref[...]
    return value.reshape(-1, value.shape[-1])


def attend_kernel(
    length_ref, proj_ref, cos_ref, sin_ref, gain_ref, pos_col_ref, pos_row_ref,
    out_ref, lse_ref, rot_ref, val_ref,
):
    step = pl.program_id(0)
    block = lse_ref.shape[-1]

    @pl.when(step == 0)
    def _():
        proj = rows_of_ref(proj_ref)
        normed = proj * lax.rsqrt(head_mean(proj * proj) + EPS) * gain_ref[...]
        rotated = normed * twice(cos_ref) + swap_halves(normed) * twice(sin_ref)
        lane = lax.broadcasted_iota(jnp.int32, proj.shape, 1)
        rotated = jnp.where(lane < 2 * HEAD_DIM, rotated * HEAD_DIM**-0.5, rotated)
        rot_ref[...] = jnp.where(lane < 3 * HEAD_DIM, rotated, proj).astype(BF16)
        val_ref[:HEAD_DIM, :] = proj[:, 3 * HEAD_DIM :].T.astype(BF16)
        val_ref[HEAD_DIM:, :] = jnp.ones((16, proj.shape[0]), BF16)

    allowed = allowed_of(length_ref[0], pos_col_ref, pos_row_ref)
    keys = rot_ref[:, 2 * HEAD_DIM : 3 * HEAD_DIM]
    query = rot_ref[pl.ds(pl.multiple_of(step * block, block), block), : 2 * HEAD_DIM]
    outs = []
    for head in range(2):
        scores = dot_lanes(keys, query[:, head * HEAD_DIM : (head + 1) * HEAD_DIM])
        weights = jnp.where(allowed, jnp.exp(scores), 0.0).astype(BF16)
        summed = jnp.dot(val_ref[...], weights, preferred_element_type=F32)
        total = summed[HEAD_DIM : HEAD_DIM + 1]
        outs.append((summed[:HEAD_DIM] / total).T)
        lse_ref[head : head + 1, :] = jnp.log(total)
    out_ref[...] = jnp.concatenate(outs, axis=1).astype(BF16).reshape(out_ref.shape)


def fixed(shape):
    return pl.BlockSpec(shape, lambda i: (0,) * len(shape))


def of_seq(seq, blocks, width, lanes):
    return pl.BlockSpec((blocks, 1, width, lanes), lambda i: (0, seq, 0, 0))


def part_of_seq(seq, blocks, width, lanes):
    return pl.BlockSpec((blocks, 1, width, lanes), lambda i: (i, seq, 0, 0))


def cost_of(microseconds):
    return pl.CostEstimate(
        flops=int(microseconds * 6e8), transcendentals=0, bytes_accessed=int(microseconds * 2.5e6)
    )


STEPS = 4


def attend(seq, proj, cosine, sine, gain, positions, lengths):
    blocks, _, width, _ = proj.shape
    slots = blocks * width
    part = slots // STEPS
    return pl.pallas_call(
        attend_kernel,
        grid=(STEPS,),
        in_specs=[
            pl.BlockSpec(memory_space=pltpu.SMEM),
            of_seq(seq, blocks, width, LANES),
            fixed((slots, LANES // 2)),
            fixed((slots, LANES // 2)),
            fixed((1, LANES)),
            fixed((slots, 1)),
            pl.BlockSpec((1, part), lambda i: (0, i)),
        ],
        out_specs=[
            part_of_seq(0, blocks // STEPS, width, 2 * HEAD_DIM),
            pl.BlockSpec((2, part), lambda i: (0, i)),
            fixed((slots, LANES)),
        ],
        out_shape=[
            jax.ShapeDtypeStruct((blocks, 1, width, 2 * HEAD_DIM), BF16),
            jax.ShapeDtypeStruct((2, slots), F32),
            jax.ShapeDtypeStruct((slots, LANES), BF16),
        ],
        scratch_shapes=[pltpu.VMEM((HEAD_DIM + 16, slots), BF16)],
        cost_estimate=cost_of(8),
        name="attend",
    )(lengths[seq : seq + 1], proj, cosine, sine, gain, positions[:, None], positions[None, :])


def attend_back_kernel(
    length_ref, rot_ref, query_ref, grad_ref, out_ref, lse_ref, pos_col_ref, pos_row_ref,
    dq_ref, dkv_ref,
):
    step = pl.program_id(0)
    allowed = allowed_of(length_ref[0], pos_col_ref, pos_row_ref)
    keys = rot_ref[:, 2 * HEAD_DIM : 3 * HEAD_DIM]
    values = rot_ref[:, 3 * HEAD_DIM :]
    query = query_ref[:, : 2 * HEAD_DIM]
    grad = rows_of_ref(grad_ref)
    product = grad.astype(F32) * rows_of_ref(out_ref).astype(F32)
    ones = jnp.ones((8, HEAD_DIM), F32)
    grad_q, grad_k, grad_v = [], 0.0, 0.0
    for head in range(2):
        cut = slice(head * HEAD_DIM, (head + 1) * HEAD_DIM)
        delta = lax.dot_general(
            ones,
            product[:, cut],
            (((1,), (1,)), ((), ())),
            precision=lax.Precision.HIGHEST,
            preferred_element_type=F32,
        )[:1]
        scores = dot_lanes(keys, query[:, cut])
        probs = jnp.where(allowed, jnp.exp(scores - lse_ref[head : head + 1, :]), 0.0)
        grad_probs = dot_lanes(values, grad[:, cut])
        grad_scores = (probs * (grad_probs - delta)).astype(BF16)
        grad_v += jnp.dot(probs.astype(BF16), grad[:, cut], preferred_element_type=F32)
        grad_k += jnp.dot(grad_scores, query[:, cut], preferred_element_type=F32)
        grad_q.append(
            lax.dot_general(
                grad_scores, keys, (((0,), (0,)), ((), ())), preferred_element_type=F32
            )
        )
    dq_ref[...] = jnp.concatenate(grad_q, axis=1) * HEAD_DIM**-0.5
    both = jnp.concatenate([grad_k, grad_v], axis=1)

    @pl.when(step == 0)
    def _():
        dkv_ref[...] = both

    @pl.when(step > 0)
    def _():
        dkv_ref[...] += both


def attend_back(seq, rotated, grad, out, lse, positions, lengths):
    blocks, _, width, _ = grad.shape
    slots = blocks * width
    part = slots // STEPS
    return pl.pallas_call(
        attend_back_kernel,
        grid=(STEPS,),
        in_specs=[
            pl.BlockSpec(memory_space=pltpu.SMEM),
            fixed((slots, LANES)),
            pl.BlockSpec((part, LANES), lambda i: (i, 0)),
            part_of_seq(seq, blocks // STEPS, width, 2 * HEAD_DIM),
            part_of_seq(0, blocks // STEPS, width, 2 * HEAD_DIM),
            pl.BlockSpec((2, part), lambda i: (0, i)),
            fixed((slots, 1)),
            pl.BlockSpec((1, part), lambda i: (0, i)),
        ],
        out_specs=[
            pl.BlockSpec((part, 2 * HEAD_DIM), lambda i: (i, 0)),
            fixed((slots, 2 * HEAD_DIM)),
        ],
        out_shape=[jax.ShapeDtypeStruct((slots, 2 * HEAD_DIM), F32)] * 2,
        cost_estimate=cost_of(10),
        name="attend_back",
    )(
        lengths[seq : seq + 1], rotated, rotated, grad, out, lse,
        positions[:, None], positions[None, :],
    )


def project_back_kernel(
    dq_ref, dkv_ref, other_ref, proj_ref, cos_ref, sin_ref, gain_ref, grad_ref, sum_ref
):
    slots = dq_ref.shape[0]
    near, far = slots // 16 * len(NEAR), slots // 16 * len(FAR)
    cuts = [(near, near), (0, near), (2 * near + far, far), (2 * near, far)]
    other = jnp.concatenate([other_ref[at : at + size] for at, size in cuts], axis=0)
    grad = jnp.concatenate([dq_ref[...], dkv_ref[...] + other], axis=1)
    proj = rows_of_ref(proj_ref)
    scale_rows = lax.rsqrt(head_mean(proj * proj) + EPS)
    normed = proj * scale_rows
    turned = grad * twice(cos_ref) - swap_halves(grad) * twice(sin_ref)
    gained = turned * gain_ref[...]
    back = scale_rows * (gained - normed * head_mean(gained * normed))
    lane = lax.broadcasted_iota(jnp.int32, proj.shape, 1)
    grad_ref[...] = jnp.where(lane < 3 * HEAD_DIM, back, grad).astype(BF16).reshape(grad_ref.shape)
    sum_ref[...] = jnp.sum((turned * normed).reshape(-1, 8, LANES), axis=0)


def project_back(seq, grad_q, grad_kv, other_kv, proj, cosine, sine, gain):
    blocks, _, width, _ = proj.shape
    slots = blocks * width
    half = fixed((slots, 2 * HEAD_DIM))
    table = fixed((slots, LANES // 2))
    return pl.pallas_call(
        project_back_kernel,
        grid=(1,),
        in_specs=[
            half, half, half, of_seq(seq, blocks, width, LANES), table, table, fixed((1, LANES))
        ],
        out_specs=[of_seq(0, blocks, width, LANES), fixed((8, LANES))],
        out_shape=[
            jax.ShapeDtypeStruct((blocks, 1, width, LANES), BF16),
            jax.ShapeDtypeStruct((8, LANES), F32),
        ],
        cost_estimate=cost_of(4),
        name="project_back",
    )(grad_q, grad_kv, other_kv, proj, cosine, sine, gain)


def feed_kernel(input_ref, weight_ref, grad_ref, hidden_ref, low_ref):
    both = dot_lanes(input_ref[...], weight_ref[...])
    width = both.shape[1] // 4
    for part in range(2):
        at = 2 * part * width
        gate_part, up_part = both[:, at : at + width], both[:, at + width : at + 2 * width]
        grad_hidden = grad_ref[:, part * width : (part + 1) * width]
        hidden = jax.nn.silu(gate_part) * up_part
        hidden_ref[:, part * width : (part + 1) * width] = hidden.astype(BF16)
        gate_low, up_low = gate_grads(grad_hidden, gate_part, up_part)
        low_ref[:, at : at + width] = gate_low
        low_ref[:, at + width : at + 2 * width] = up_low


def feed(inputs, weight, grad_hidden):
    rows, units = inputs.shape[0], weight.shape[0]
    part = math.gcd(rows, 256)
    row_block = lambda lanes: pl.BlockSpec((part, lanes), lambda i: (i, 0))
    return pl.pallas_call(
        feed_kernel,
        grid=(rows // part,),
        in_specs=[row_block(inputs.shape[1]), fixed(weight.shape), row_block(units // 2)],
        out_specs=[row_block(units // 2), row_block(units)],
        out_shape=[
            jax.ShapeDtypeStruct((rows, units // 2), BF16),
            jax.ShapeDtypeStruct((rows, units), BF16),
        ],
        cost_estimate=cost_of(2),
        name="feed",
    )(inputs, weight, grad_hidden)


def dot_rows(left, right):
    return lax.dot_general(left, right, (((0,), (0,)), ((), ())), preferred_element_type=F32)


def plain(left, right):
    return jnp.dot(left, right, preferred_element_type=F32)


def in_order(own, other, index):
    first = index == 0
    return jnp.concatenate([jnp.where(first, own, other), jnp.where(first, other, own)], axis=0)


def split_local(
    tokens, cotangent, q_weight, k_weight, v_weight, o_weight, gate_weight, up_weight,
    down_weight, attn_gain, ffn_gain, q_gain, k_gain, lengths, pair_order,
):
    seqs, width, _ = tokens.shape
    rank = lax.axis_index("ctx")
    side = lax.axis_index("fsdp")
    core = rank % 2
    mine = seqs * width
    q_rows, kv_rows, ff_rows = q_weight.shape[0], k_weight.shape[0], gate_weight.shape[0]

    x_rows = tokens.astype(F32).reshape(mine, D)
    scale_one = rms_scale(x_rows)
    normed_one = x_rows * scale_one
    kept = {}

    owners = block_owners(rank)
    blocks = owners.shape[0]
    within = jnp.arange(width, dtype=jnp.int32)
    half_blk = width // 2

    def positions_of(dealt):
        block_id = jnp.where(
            within[None, :] < half_blk, dealt[:, None], 2 * pair_order.shape[0] - 1 - dealt[:, None]
        )
        return (block_id * half_blk + within[None, :] % half_blk).reshape(-1)

    def tables(found):
        cosine, sine = rope_tables(found)
        return jnp.concatenate([cosine] * 4, axis=1), jnp.concatenate([-sine, sine] * 2, axis=1)

    cut = ff_rows // 2
    ff_own = [w[at : at + cut] for w in (gate_weight, up_weight, down_weight) for at in (0, cut)]
    ff_side = []

    def moving(index):
        return [(ff_own[index], SWAP_X)]

    def slot_positions(run):
        def work(order):
            come = tuple(send(w, SWAP_X) for w in (q_weight, k_weight, v_weight))
            return positions_of(order[owners]), come

        _, (kept["positions"], kept["side"]) = run((pair_order,), work)

    def attention_weights(found, q_side, k_side, v_side):
        kv_own, kv_side = jnp.stack([k_weight, v_weight]), jnp.stack([k_side, v_side])
        kv_half = jnp.concatenate(
            [jnp.where(side == 0, kv_own, kv_side), jnp.where(side == 0, kv_side, kv_own)], axis=1
        )
        kv_core = send(kv_half, SWAP_CORE)
        kv_full = jnp.concatenate(
            [jnp.where(core == 0, kv_half, kv_core), jnp.where(core == 0, kv_core, kv_half)], axis=1
        )
        weights = jnp.concatenate([q_weight, q_side, kv_full[0], kv_full[1]], axis=0)
        return weights, *tables(found)

    def slot_weights(run):
        (o_side,), (kept["w_attn"], *kept["tables"]) = run(
            (kept["positions"], *kept["side"]), attention_weights, [(o_weight, SWAP_X)]
        )
        kept["w_out"] = jnp.concatenate([o_weight, o_side], axis=0)

    def slot_join_move(index):
        def slot(run, blocks, join):
            (come,), (near,) = run(blocks, lambda *xs: (join(*xs),), moving(index))
            ff_side.append(come)
            return near

        return slot

    def slot_project(run, near):
        _, (kept["proj_near"], kept["x_near"]) = run(
            (near, kept["w_attn"]), lambda x, w: (project(x, w), x)
        )

    _, x_late = gather_blocks(
        (normed_one * attn_gain).astype(BF16),
        (slot_positions, slot_weights, slot_join_move(0), slot_project),
    )
    x_near = kept["x_near"]
    positions, (cosine, sine) = kept["positions"], kept["tables"]
    w_attn, w_out = kept["w_attn"], kept["w_out"]
    cut_rows = x_near.shape[0]
    gain_lanes = jnp.concatenate([q_gain, q_gain, k_gain, jnp.ones((HEAD_DIM,), F32)])[None, :]
    my_pos = positions_of(pair_order[rank][None])
    live = (my_pos[None, :] < lengths[:, None]).reshape(mine, 1)
    grad_out = jnp.where(live, cotangent.astype(F32).reshape(mine, D), 0.0)

    heads = []

    def slot_project_far(run):
        def work(near, weight, *late):
            far = join_far(*late)
            rows = jnp.concatenate([near, project(far, weight)], axis=0)
            return rows.reshape(blocks, seqs, width, LANES), far

        (come,), (kept["proj"], kept["x_far"]) = run(
            (kept["proj_near"], w_attn, *x_late), work, moving(1)
        )
        ff_side.append(come)

    def attend_beside(run, seq):
        work = lambda p: attend(seq, p, cosine, sine, gain_lanes, positions, lengths)
        (come,), found = run((kept["proj"],), work, moving(2 + seq))
        ff_side.append(come)
        heads.append(found)

    def slot_out(run, near):
        def work(*outs):
            rows = jnp.concatenate(outs, axis=1).reshape(-1, 2 * HEAD_DIM)
            return (rows,)

        _, (kept["out_rows"],) = run([found[0] for found in heads], work)

    def slot_attend_last(run, blocks_near, join):
        attend_beside(run, 1)
        return blocks_near, join

    (grad_blocks, grad_join), grad_late = gather_blocks(
        grad_out.astype(BF16),
        (slot_project_far, lambda run: attend_beside(run, 0), slot_attend_last, slot_out),
    )
    out_rows, proj, x_far = kept["out_rows"], kept["proj"], kept["x_far"]

    def slot_grad_near(run):
        (come,), (kept["grad_near"],) = run(grad_blocks, lambda *xs: (grad_join(*xs),), moving(5))
        ff_side.append(come)

    def slot_grad_far(run):
        (come,), (kept["grad_far"],) = run(grad_late, lambda *xs: (join_far(*xs),), moving(4))
        ff_side.append(come)

    def slot_gate_up_weights(run):
        _, (kept["w_gate_up"],) = run(
            (*ff_own[:4], *ff_side[:4]), lambda *xs: (jnp.concatenate(xs, axis=0),)
        )

    resid = x_rows + scatter_blocks(
        out_rows[:cut_rows],
        out_rows[cut_rows:],
        w_out,
        (idle, slot_grad_far, slot_grad_near, slot_gate_up_weights),
    )
    grad_near, grad_far = kept["grad_near"], kept["grad_far"]
    w_gate_up = kept["w_gate_up"]
    w_down = jnp.concatenate([*ff_own[4:], *ff_side[4:]], axis=0)
    scale_two = rms_scale(resid)
    normed_two = resid * scale_two

    def slot_hidden(name, grad):
        def slot(run):
            _, (kept[name],) = run((grad, w_down), lambda g, w: (project(g, w),))

        return slot

    def slot_feed(run, blocks_near, join):
        def work(weight, grad_hidden, *found):
            near = join(*found)
            return near, *feed(near, weight, grad_hidden)

        _, near = run((w_gate_up, kept["hidden_near"], *blocks_near), work)
        return near

    def slot_keep(run, near):
        kept["x2_near"], kept["hidden"], kept["gate_up_low"] = near
        run()

    _, x2_late = gather_blocks(
        (normed_two * ffn_gain).astype(BF16),
        (
            slot_hidden("hidden_near", grad_near),
            slot_hidden("hidden_far", grad_far),
            slot_feed,
            slot_keep,
        ),
    )
    x2_near = kept["x2_near"]
    hidden_near, low_near = kept["hidden"], kept["gate_up_low"]
    x2_far = join_far(*x2_late)
    hidden_far, low_far = feed(x2_far, w_gate_up, kept["hidden_far"])

    across = hidden_far.shape[0] // 2

    def slot_sums(run):
        def work(near, far, weight):
            cut = near.shape[0] // 2
            far = core_sum(far[:across], far[across:], weight)
            return far, core_sum(near[:cut], near[cut:], weight)

        _, kept["out_parts"] = run((hidden_near, hidden_far, w_down), work)

    def both_parts(*parts):
        near, far, right_near, right_far = parts
        return dot_rows(near, right_near) + dot_rows(far, right_far)

    half_ff = 2 * ff_rows

    def slot_leave(run):
        def work(*parts):
            gate_up = both_parts(parts[0][:, half_ff:], parts[1][:, half_ff:], *parts[2:4])
            return jnp.split(gate_up.astype(BF16), 4)

        _, kept["gate_up_leave"] = run((low_near, low_far, x2_near, x2_far), work)

    grad_norm2 = scatter_blocks(
        low_near, low_far, w_gate_up, (idle, idle, slot_sums, slot_leave)
    )
    came = []
    grad_ffn_gain = jnp.sum(grad_norm2 * normed_two, axis=0)
    grad_resid = grad_out + rms_back(grad_norm2 * ffn_gain, normed_two, scale_two)

    def slot_downs(run):
        def work(*parts):
            leave = both_parts(parts[0][:, ff_rows:], parts[1][:, ff_rows:], *parts[2:4])
            stay = both_parts(parts[0][:, :ff_rows], parts[1][:, :ff_rows], *parts[2:4])
            return stay, *jnp.split(leave.astype(BF16), 2)

        (come,), (kept["down"], *kept["down_leave"]) = run(
            (hidden_near, hidden_far, grad_near, grad_far),
            work,
            [(kept["gate_up_leave"][0], SWAP_X)],
        )
        came.append(come)

    def slot_gate_up_stay(run):
        def work(*parts):
            return (both_parts(parts[0][:, :half_ff], parts[1][:, :half_ff], *parts[2:4]),)

        (come,), (kept["gate_up"],) = run(
            (low_near, low_far, x2_near, x2_far), work, [(kept["gate_up_leave"][1], SWAP_X)]
        )
        came.append(come)

    def slot_join_aside(run, blocks, join):
        (come,), (near,) = run(blocks, lambda *xs: (join(*xs),), [(kept["gate_up_leave"][2], SWAP_X)])
        came.append(come)
        return near

    def grad_heads(grad, weight):
        return project(grad, weight).astype(BF16)

    def slot_grad_heads(run, near):
        _, (kept["heads_near"], kept["da_near"]) = run(
            (near, w_out), lambda x, w: (grad_heads(x, w), x)
        )

    _, da_late = gather_blocks(
        grad_resid.astype(BF16),
        (slot_downs, slot_gate_up_stay, slot_join_aside, slot_grad_heads),
    )
    da_near = kept["da_near"]
    da_far = join_far(*da_late)
    pieces = [*kept["gate_up_leave"], *kept["down_leave"]]

    def slot_grad_o(run):
        def work(near, x, w):
            rows = jnp.concatenate([near, grad_heads(x, w)], axis=0)
            return (rows.reshape(blocks, seqs, width, 2 * HEAD_DIM),)

        _, (kept["grad_o"],) = run((kept["heads_near"], da_far, w_out), work)

    def slot_attend_back(seq):
        def slot(run):
            out, lse, rotated = heads[seq]

            def work(grad, *before):
                come = tuple(send(x, SWAP_CORE) for x in before)
                return attend_back(seq, rotated, grad, out, lse, positions, lengths), come

            before = [kept["back", seq - 1][1]] if seq else []
            (come,), (kept["back", seq], other) = run(
                (kept["grad_o"], *before), work, [(pieces[3 + seq], SWAP_X)]
            )
            came.append(come)
            kept["other"] = other

        return slot

    def slot_project_back(run):
        def work(found, others):
            others = [*others, send(found[-1][1], SWAP_CORE)]
            grads, sums = [], 0.0
            for s, ((grad_q, grad_kv), other_kv) in enumerate(zip(found, others)):
                rows, part = project_back(
                    s, grad_q, grad_kv, other_kv, proj, cosine, sine, gain_lanes
                )
                grads.append(rows)
                sums = sums + jnp.sum(part, axis=0)
            return jnp.concatenate(grads, axis=1).reshape(blocks * mine, LANES), sums

        (come,), (kept["grad_rows"], kept["gain_sums"]) = run(
            ([kept["back", s] for s in range(seqs)], kept["other"]), work, [(pieces[5], SWAP_X)]
        )
        came.append(come)

    out_sum = scatter_joined(
        *kept["out_parts"],
        (slot_grad_o, slot_attend_back(0), slot_attend_back(1), slot_project_back),
    )
    grad_rows, gain_sums = kept["grad_rows"], kept["gain_sums"]
    row = jnp.arange(LANES)[:, None] // HEAD_DIM
    w_once = jnp.where((row < 2) | (row == 2 + core), w_attn, 0).astype(BF16)

    def slot_attn_grads(run):
        def work(grads, near, far):
            full = both_parts(grads[:cut_rows], grads[cut_rows:], near, far)
            kv_grads = full[2 * q_rows :].reshape(2, 2, 2, kv_rows, D)
            kv_mine = jnp.where(core == 0, kv_grads[:, 0], kv_grads[:, 1])
            kv_stay = jnp.where(side == 0, kv_mine[:, 0], kv_mine[:, 1])
            kv_leave = jnp.where(side == 0, kv_mine[:, 1], kv_mine[:, 0])
            stay = jnp.concatenate([full[:q_rows], kv_stay.reshape(2 * kv_rows, D)])
            leave = jnp.concatenate([full[q_rows : 2 * q_rows], kv_leave.reshape(2 * kv_rows, D)])
            return stay, leave.astype(BF16)

        _, kept["attn"] = run((grad_rows, x_near, x_far), work)

    def slot_out_grads(run):
        def work(rows, near, far):
            stay, leave = jnp.split(both_parts(rows[:cut_rows], rows[cut_rows:], near, far), 2)
            return stay, leave.astype(BF16)

        (kept["attn_come"],), kept["o"] = run(
            (out_rows, da_near, da_far), work, [(kept["attn"][1], SWAP_X)]
        )

    def slot_finish(run):
        def work(attn_stay, attn_come, gate_up, down, f_sum, *xs):
            attn_grads = attn_stay + attn_come.astype(F32)
            owned = jnp.concatenate([q_weight, k_weight, v_weight], axis=0).astype(F32)
            gains = jnp.concatenate(
                [
                    jnp.sum(owned * attn_grads, axis=0) / attn_gain,
                    grad_ffn_gain,
                    gain_sums[:HEAD_DIM] + gain_sums[HEAD_DIM : 2 * HEAD_DIM],
                    0.5 * gain_sums[2 * HEAD_DIM : 3 * HEAD_DIM],
                ]
            )
            gains = gains + send(gains, SWAP_CORE)
            gains = gains + send(gains, SWAP_X)
            gate_up = gate_up + jnp.concatenate(xs[:4]).astype(F32)
            down = down + jnp.concatenate(xs[4:]).astype(F32)
            block = jnp.where(live, resid + f_sum, 0.0).astype(BF16).reshape(seqs, width, D)
            return gains, attn_grads, gate_up, down, block

        (kept["o_come"],), kept["finish"] = run(
            (*kept["attn"][:1], kept["attn_come"], kept["gate_up"], kept["down"], out_sum, *came),
            work,
            [(kept["o"][1], SWAP_X)],
        )

    def slot_gains(run):
        gains = kept["finish"][0]
        (come,), kept["o_grad"] = run(
            (*kept["o"][:1], kept["o_come"]),
            lambda stay, come: (stay + come.astype(F32),),
            early=[(gains, SWAP_Y)],
        )
        gains = gains + come
        kept["gains"] = (gains + send(gains, SWAP_Z0)) + (
            send(gains, SWAP_Z1) + send(gains, SWAP_Z)
        )

    grad_norm1 = scatter_blocks(
        grad_rows[:cut_rows],
        grad_rows[cut_rows:],
        w_once,
        (slot_attn_grads, slot_out_grads, slot_finish, slot_gains),
    )
    _, attn_grads, gate_up_grad, down_grad, block_out = kept["finish"]
    (o_grad,) = kept["o_grad"]
    gains = kept["gains"]
    grad_tokens = (grad_resid + rms_back(grad_norm1 * attn_gain, normed_one, scale_one)).reshape(
        seqs, width, D
    )
    return (
        block_out,
        grad_tokens,
        attn_grads[:q_rows],
        attn_grads[q_rows : q_rows + kv_rows],
        attn_grads[q_rows + kv_rows :],
        o_grad,
        gate_up_grad[:ff_rows],
        gate_up_grad[ff_rows:],
        down_grad,
        gains[:D],
        gains[D : 2 * D],
        gains[2 * D : 2 * D + HEAD_DIM],
        gains[2 * D + HEAD_DIM :],
    )


def solution(mesh):
    body = split_local if fits_split(mesh) else local
    in_specs = (
        P("fsdp", "ctx", None),
        P("fsdp", "ctx", None),
        P(("ctx", "fsdp"), None),
        P(("ctx", "fsdp"), None),
        P(("ctx", "fsdp"), None),
        P(("ctx", "fsdp"), None),
        P(("ctx", "fsdp"), None),
        P(("ctx", "fsdp"), None),
        P(("ctx", "fsdp"), None),
        P(),
        P(),
        P(),
        P(),
        P("fsdp"),
        P(),
    )
    out_specs = (
        P("fsdp", "ctx", None),
        P("fsdp", "ctx", None),
        P(("ctx", "fsdp"), None),
        P(("ctx", "fsdp"), None),
        P(("ctx", "fsdp"), None),
        P(("ctx", "fsdp"), None),
        P(("ctx", "fsdp"), None),
        P(("ctx", "fsdp"), None),
        P(("ctx", "fsdp"), None),
        P(),
        P(),
        P(),
        P(),
    )
    return jax.shard_map(body, mesh=mesh, in_specs=in_specs, out_specs=out_specs, check_vma=False)
```

```python
import functools
import math

import jax
import jax.numpy as jnp
from jax import lax
from jax.experimental import pallas as pl
from jax.experimental.pallas import tpu as pltpu
from jax.sharding import PartitionSpec as P

D = 2048
HEADS = 32
KV_HEADS = 8
HEAD_DIM = 64
FF = 8192


EPS = 1e-05
THETA = 1000000.0
NEG = -1e30


def rms_scale(values):
    return lax.rsqrt(jnp.mean(values * values, axis=-1, keepdims=True) + EPS)


def rms_back(grad_normed, normed, scale_rows):
    return scale_rows * (
        grad_normed - normed * jnp.mean(grad_normed * normed, axis=-1, keepdims=True)
    )


def rope_tables(positions):
    half = HEAD_DIM // 2
    freq = THETA ** (-(jnp.arange(half, dtype=jnp.float32) * 2.0 / HEAD_DIM))
    angle = positions.astype(jnp.float32)[:, None] * freq[None, :]
    return (jnp.cos(angle), jnp.sin(angle))


def rotate(values, cosine, sine):
    half = values.shape[-1] // 2
    first = values[..., :half]
    second = values[..., half:]
    return jnp.concatenate(
        [first * cosine - second * sine, second * cosine + first * sine], axis=-1
    )


def slot_positions(pair_order, width_pair, first, count):
    slot = first + jnp.arange(count, dtype=jnp.int32)
    owner = slot // width_pair
    within = slot % width_pair
    half_blk = width_pair // 2
    pair = pair_order[owner]
    block_id = jnp.where(within < half_blk, pair, 2 * pair_order.shape[0] - 1 - pair)
    return block_id * half_blk + within % half_blk


def block_mask(query_pos, key_part, lengths):
    return (key_part[None, None, :] <= query_pos[None, :, None]) & (
        key_part[None, None, :] < lengths[:, None, None]
    )


def project(inputs, weight):
    return jnp.einsum("td,fd->tf", inputs, weight, preferred_element_type=jnp.float32)


def gate_grads(grad_hidden, gate_part, up_part):
    sigma = jax.nn.sigmoid(gate_part)
    grad_gate = grad_hidden * up_part * sigma * (1.0 + gate_part * (1.0 - sigma))
    grad_up = grad_hidden * gate_part * sigma
    return (grad_gate.astype(jnp.bfloat16), grad_up.astype(jnp.bfloat16))


def block_grads(q_rot, grad_o_low, lse, delta, k_blk, v_blk, allowed, scale):
    scores = (
        jnp.einsum("sqhgd,sjhd->sqhgj", q_rot, k_blk, preferred_element_type=jnp.float32) * scale
    )
    scores = jnp.where(allowed[:, :, None, None, :], scores, NEG)
    probs = jnp.exp(scores - lse[..., None])
    grad_probs = jnp.einsum(
        "sqhgd,sjhd->sqhgj", grad_o_low, v_blk, preferred_element_type=jnp.float32
    )
    grad_scores = (probs * (grad_probs - delta[..., None])).astype(jnp.bfloat16)
    return (probs, grad_scores)


def local(
    tokens,
    cotangent,
    q_weight,
    k_weight,
    v_weight,
    o_weight,
    gate_weight,
    up_weight,
    down_weight,
    attn_gain,
    ffn_gain,
    q_gain,
    k_gain,
    lengths,
    pair_order,
):
    seq_grp = tokens.shape[0]
    width_pair = tokens.shape[1]
    groups = HEADS // KV_HEADS
    q_width = HEADS * HEAD_DIM
    kv_width = KV_HEADS * HEAD_DIM
    scale = HEAD_DIM ** (-0.5)
    tok_rows = seq_grp * width_pair
    slots = width_pair * pair_order.shape[0]
    key_blk = math.gcd(slots, 512)
    key_count = slots // key_blk
    dev_count = lax.axis_size("ctx") * lax.axis_size("fsdp")
    local_pos = slot_positions(
        pair_order, width_pair, lax.axis_index("ctx") * width_pair, width_pair
    )
    key_pos = slot_positions(pair_order, width_pair, 0, slots)
    live_rows = (local_pos[None, :] < lengths[:, None]).reshape(tok_rows, 1)
    cosine, sine = rope_tables(local_pos)
    cosine = cosine[None, :, None, :]
    sine = sine[None, :, None, :]
    x_rows = tokens.astype(jnp.float32).reshape(tok_rows, D)
    scale_one = rms_scale(x_rows)
    normed_one = x_rows * scale_one
    x_norm = (normed_one * attn_gain).astype(jnp.bfloat16)
    w_query, w_key, w_value, w_out = (
        lax.all_gather(q_weight, ("ctx", "fsdp"), axis=0, tiled=True),
        lax.all_gather(k_weight, ("ctx", "fsdp"), axis=0, tiled=True),
        lax.all_gather(v_weight, ("ctx", "fsdp"), axis=0, tiled=True),
        lax.all_gather(o_weight, ("ctx", "fsdp"), axis=0, tiled=True),
    )
    q_proj = project(x_norm, w_query).reshape(seq_grp, width_pair, HEADS, HEAD_DIM)
    k_proj = project(x_norm, w_key).reshape(seq_grp, width_pair, KV_HEADS, HEAD_DIM)
    v_low = project(x_norm, w_value).astype(jnp.bfloat16).reshape(seq_grp, width_pair, kv_width)
    q_scale = rms_scale(q_proj)
    q_normed = q_proj * q_scale
    q_rot = (
        rotate(q_normed * q_gain, cosine, sine)
        .astype(jnp.bfloat16)
        .reshape(seq_grp, width_pair, KV_HEADS, groups, HEAD_DIM)
    )
    k_scale = rms_scale(k_proj)
    k_normed = k_proj * k_scale
    k_rot = (
        rotate(k_normed * k_gain, cosine, sine)
        .astype(jnp.bfloat16)
        .reshape(seq_grp, width_pair, kv_width)
    )
    k_all, v_all = (
        lax.all_gather(k_rot, "ctx", axis=1, tiled=True),
        lax.all_gather(v_low, "ctx", axis=1, tiled=True),
    )
    k_all = k_all.reshape(seq_grp, slots, KV_HEADS, HEAD_DIM)
    v_all = v_all.reshape(seq_grp, slots, KV_HEADS, HEAD_DIM)

    def key_slices(first, count):
        k_blk = lax.dynamic_slice_in_dim(k_all, first, count, 1)
        v_blk = lax.dynamic_slice_in_dim(v_all, first, count, 1)
        allowed = block_mask(local_pos, lax.dynamic_slice_in_dim(key_pos, first, count, 0), lengths)
        return (k_blk, v_blk, allowed)

    def forward_step(index, carry):
        top, total, summed = carry
        k_blk, v_blk, allowed = key_slices(index * key_blk, key_blk)
        scores = (
            jnp.einsum("sqhgd,sjhd->sqhgj", q_rot, k_blk, preferred_element_type=jnp.float32)
            * scale
        )
        scores = jnp.where(allowed[:, :, None, None, :], scores, NEG)
        new_top = jnp.maximum(top, jnp.max(scores, axis=-1))
        shrink = jnp.exp(top - new_top)
        probs = jnp.exp(scores - new_top[..., None])
        total = total * shrink + jnp.sum(probs, axis=-1)
        summed = summed * shrink[..., None] + jnp.einsum(
            "sqhgj,sjhd->sqhgd",
            probs.astype(jnp.bfloat16),
            v_blk,
            preferred_element_type=jnp.float32,
        )
        return (new_top, total, summed)

    stat_shape = (seq_grp, width_pair, KV_HEADS, groups)
    start_carry = (
        jnp.full(stat_shape, NEG, jnp.float32),
        jnp.zeros(stat_shape, jnp.float32),
        jnp.zeros(stat_shape + (HEAD_DIM,), jnp.float32),
    )
    top, total, summed = lax.fori_loop(0, key_count, forward_step, start_carry)
    lse = top + jnp.log(total)
    o_low = (summed / total[..., None]).astype(jnp.bfloat16)
    o_rows = o_low.reshape(tok_rows, q_width)
    resid = x_rows + jnp.einsum("tf,fd->td", o_rows, w_out, preferred_element_type=jnp.float32)
    scale_two = rms_scale(resid)
    normed_two = resid * scale_two
    x_norm2 = (normed_two * ffn_gain).astype(jnp.bfloat16)
    grad_out = jnp.where(live_rows, cotangent.astype(jnp.float32).reshape(tok_rows, D), 0.0)
    grad_low = grad_out.astype(jnp.bfloat16)
    pieces = (
        lax.all_gather(gate_weight, ("ctx", "fsdp"), axis=0, tiled=True),
        lax.all_gather(up_weight, ("ctx", "fsdp"), axis=0, tiled=True),
        lax.all_gather(down_weight, ("ctx", "fsdp"), axis=0, tiled=True),
    )
    gate_part = project(x_norm2, pieces[0])
    up_part = project(x_norm2, pieces[1])
    hidden_part = (jax.nn.silu(gate_part) * up_part).astype(jnp.bfloat16)
    out_sum = jnp.einsum("tf,fd->td", hidden_part, pieces[2], preferred_element_type=jnp.float32)
    gate_all = gate_part
    up_all = up_part
    hidden = (jax.nn.silu(gate_all) * up_all).astype(jnp.bfloat16)
    pieces = (
        lax.all_gather(gate_weight, ("ctx", "fsdp"), axis=0, tiled=True),
        lax.all_gather(up_weight, ("ctx", "fsdp"), axis=0, tiled=True),
        lax.all_gather(down_weight, ("ctx", "fsdp"), axis=0, tiled=True),
    )
    count = pieces[0].shape[0]
    gate_part = gate_all
    up_part = up_all
    grad_gate_part, grad_up_part = gate_grads(project(grad_low, pieces[2]), gate_part, up_part)
    grad_sum = jnp.einsum(
        "tf,fd->td", grad_gate_part, pieces[0], preferred_element_type=jnp.float32
    ) + jnp.einsum("tf,fd->td", grad_up_part, pieces[1], preferred_element_type=jnp.float32)
    gate_grad_all = grad_gate_part
    up_grad_all = grad_up_part
    block_out = (
        jnp.where(live_rows, resid + out_sum, 0.0)
        .astype(jnp.bfloat16)
        .reshape(seq_grp, width_pair, D)
    )
    ffn_dev = FF // dev_count
    owners = lax.axis_size(("ctx", "fsdp")) * (3 * ffn_dev) // (3 * ffn_dev)
    first = jnp.int32(0) // (3 * ffn_dev) * ffn_dev
    grad_gate_part = jnp.einsum(
        "tf,td->fd", gate_grad_all, x_norm2, preferred_element_type=jnp.float32
    )
    grad_up_part = jnp.einsum("tf,td->fd", up_grad_all, x_norm2, preferred_element_type=jnp.float32)
    grad_down_part = jnp.einsum("tf,td->fd", hidden, grad_low, preferred_element_type=jnp.float32)
    stacked = jnp.stack(
        [
            grad_gate_part.reshape(owners, ffn_dev, D),
            grad_up_part.reshape(owners, ffn_dev, D),
            grad_down_part.reshape(owners, ffn_dev, D),
        ],
        axis=1,
    )
    ffn_grads = lax.psum_scatter(
        stacked.reshape(lax.axis_size(("ctx", "fsdp")) * (3 * ffn_dev), D),
        ("ctx", "fsdp"),
        scatter_dimension=0,
        tiled=True,
    )
    grad_ffn_gain = jnp.sum(grad_sum * normed_two, axis=0)
    grad_resid = grad_out + rms_back(grad_sum * ffn_gain, normed_two, scale_two)
    grad_attn_low = grad_resid.astype(jnp.bfloat16)
    grad_o_low = (
        project(grad_attn_low, w_out)
        .astype(jnp.bfloat16)
        .reshape(seq_grp, width_pair, KV_HEADS, groups, HEAD_DIM)
    )
    delta = jnp.sum(grad_o_low.astype(jnp.float32) * o_low.astype(jnp.float32), axis=-1)
    dq_zero = jnp.zeros((seq_grp, width_pair, KV_HEADS, groups, HEAD_DIM), jnp.float32)
    kv_cols = seq_grp * 2 * kv_width

    def key_value_grads(probs, grad_scores):
        grad_k_blk = (
            jnp.einsum("sqhgj,sqhgd->jshd", grad_scores, q_rot, preferred_element_type=jnp.float32)
            * scale
        )
        grad_v_blk = jnp.einsum(
            "sqhgj,sqhgd->jshd",
            probs.astype(jnp.bfloat16),
            grad_o_low,
            preferred_element_type=jnp.float32,
        )
        return jnp.stack([grad_k_blk, grad_v_blk], axis=2).reshape(probs.shape[-1], kv_cols)

    def both_step(grad_q, index):
        k_blk, v_blk, allowed = key_slices(index * key_blk, key_blk)
        probs, grad_scores = block_grads(
            q_rot, grad_o_low, lse, delta, k_blk, v_blk, allowed, scale
        )
        grad_q = (
            grad_q
            + jnp.einsum(
                "sqhgj,sjhd->sqhgd", grad_scores, k_blk, preferred_element_type=jnp.float32
            )
            * scale
        )
        return (grad_q, key_value_grads(probs, grad_scores))

    grad_q_rot, kv_blocks = lax.scan(both_step, dq_zero, jnp.arange(key_count))
    kv_grad = lax.psum_scatter(
        kv_blocks.reshape(slots, kv_cols), "ctx", scatter_dimension=0, tiled=True
    )
    kv_grad = jnp.transpose(
        kv_grad.reshape(width_pair, seq_grp, 2, KV_HEADS, HEAD_DIM), (1, 0, 2, 3, 4)
    )
    grad_q_pre = rotate(grad_q_rot.reshape(seq_grp, width_pair, HEADS, HEAD_DIM), cosine, -sine)
    grad_k_pre = rotate(kv_grad[:, :, 0], cosine, -sine)
    grad_q_gain = jnp.sum(grad_q_pre * q_normed, axis=(0, 1, 2))
    grad_k_gain = jnp.sum(grad_k_pre * k_normed, axis=(0, 1, 2))
    grad_q_proj = (
        rms_back(grad_q_pre * q_gain, q_normed, q_scale)
        .reshape(tok_rows, q_width)
        .astype(jnp.bfloat16)
    )
    grad_k_proj = (
        rms_back(grad_k_pre * k_gain, k_normed, k_scale)
        .reshape(tok_rows, kv_width)
        .astype(jnp.bfloat16)
    )
    grad_v_proj = kv_grad[:, :, 1].reshape(tok_rows, kv_width).astype(jnp.bfloat16)
    grad_norm1 = jnp.einsum("tf,fd->td", grad_q_proj, w_query, preferred_element_type=jnp.float32)
    grad_norm1 = grad_norm1 + jnp.einsum(
        "tf,fd->td", grad_k_proj, w_key, preferred_element_type=jnp.float32
    )
    grad_norm1 = grad_norm1 + jnp.einsum(
        "tf,fd->td", grad_v_proj, w_value, preferred_element_type=jnp.float32
    )
    grad_attn_gain = jnp.sum(grad_norm1 * normed_one, axis=0)
    grad_tokens = (grad_resid + rms_back(grad_norm1 * attn_gain, normed_one, scale_one)).reshape(
        seq_grp, width_pair, D
    )
    q_dev = q_width // dev_count
    kv_dev = kv_width // dev_count
    per_dev = 2 * q_dev + 2 * kv_dev
    owners = lax.axis_size(("ctx", "fsdp")) * per_dev // per_dev

    def rows_of(grad_rows, inputs, each):
        return jnp.einsum(
            "tf,td->fd", grad_rows, inputs, preferred_element_type=jnp.float32
        ).reshape(owners, each, D)

    joined = jnp.concatenate(
        [
            rows_of(grad_q_proj, x_norm, q_dev),
            rows_of(grad_k_proj, x_norm, kv_dev),
            rows_of(grad_v_proj, x_norm, kv_dev),
            rows_of(o_rows, grad_attn_low, q_dev),
        ],
        axis=1,
    )
    attn_grads = lax.psum_scatter(
        joined.reshape(lax.axis_size(("ctx", "fsdp")) * per_dev, D),
        ("ctx", "fsdp"),
        scatter_dimension=0,
        tiled=True,
    )
    grad_attn_gain, grad_ffn_gain, grad_q_gain, grad_k_gain = lax.psum(
        (grad_attn_gain, grad_ffn_gain, grad_q_gain, grad_k_gain), ("ctx", "fsdp")
    )
    return (
        block_out,
        grad_tokens,
        attn_grads[:q_dev],
        attn_grads[q_dev : q_dev + kv_dev],
        attn_grads[q_dev + kv_dev : q_dev + 2 * kv_dev],
        attn_grads[q_dev + 2 * kv_dev :],
        ffn_grads[:ffn_dev],
        ffn_grads[ffn_dev : 2 * ffn_dev],
        ffn_grads[2 * ffn_dev :],
        grad_attn_gain,
        grad_ffn_gain,
        grad_q_gain,
        grad_k_gain,
    )


AXES = ("ctx", "fsdp")
RANKS = 16
LANES = 4 * HEAD_DIM
BF16 = jnp.bfloat16
F32 = jnp.float32
NEVER = 1 << 30


def fits_split(mesh):
    return mesh.shape["ctx"] == RANKS and mesh.shape["fsdp"] == 2


CYCLE = ((0, 0), (1, 0), (2, 0), (3, 0), (3, 1), (2, 1), (1, 1), (0, 1))
CHIPS = len(CYCLE)
NEAR = (2, -2, 1, -1, 0)
FAR = (4, 3, -3)


def index_of(z, y, core, x):
    return z * 8 + y * 4 + core * 2 + x


def pairs_of(move):
    places = [(z, y, c, x) for z in range(4) for y in range(2) for c in range(2) for x in range(2)]
    return [(index_of(*place), index_of(*move(*place))) for place in places]


def along_cycle(step):
    def move(z, y, core, x):
        return (*CYCLE[(CYCLE.index((z, y)) + step) % CHIPS], core, x)

    return pairs_of(move)


SWAP_X = pairs_of(lambda z, y, c, x: (z, y, c, 1 - x))
SWAP_CORE = pairs_of(lambda z, y, c, x: (z, y, 1 - c, x))
SWAP_Y = pairs_of(lambda z, y, c, x: (z, 1 - y, c, x))
SWAP_Z0 = pairs_of(lambda z, y, c, x: (z ^ 1, y, c, x))
SWAP_Z1 = pairs_of(lambda z, y, c, x: (z ^ 2, y, c, x))
SWAP_Z = pairs_of(lambda z, y, c, x: (3 - z, y, c, x))
AHEAD = along_cycle(1)
BEHIND = along_cycle(-1)


def block_owners(rank):
    place = jnp.array([CYCLE.index((chip // 2, chip % 2)) for chip in range(CHIPS)], jnp.int32)
    chips = jnp.array([2 * z + y for z, y in CYCLE], jnp.int32)
    around = jnp.array(NEAR + NEAR + FAR + FAR, jnp.int32)
    turn = jnp.array((0,) * 5 + (1,) * 5 + (0,) * 3 + (1,) * 3, jnp.int32)
    return chips[(place[rank // 2] + around) % CHIPS] * 2 + (rank % 2) ^ turn


def send(value, pairs):
    return lax.ppermute(value, AXES, pairs)


def window(moves, inputs=(), work=None):
    values, inputs = lax.optimization_barrier((tuple(v for v, _ in moves), tuple(inputs)))
    come = tuple(send(v, pairs) for v, (_, pairs) in zip(values, moves))
    done = work(*inputs) if work else ()
    return lax.optimization_barrier((come, done))


def idle(run):
    run()


def collect_kernel(starts, *refs):
    count = len(starts)
    pieces, (whole, held, come_sems, leave_sems) = refs[:count], refs[-4:]
    coming, leaving, at = [], [], 0
    for i, (piece, start) in enumerate(zip(pieces, starts)):
        part = held.at[pl.ds(at, piece.shape[0])]
        at += piece.shape[0]
        coming.append(pltpu.make_async_copy(piece, part, come_sems.at[i]))
        place = whole.at[pl.ds(start, piece.shape[0])]
        leaving.append(pltpu.make_async_copy(part, place, leave_sems.at[i]))
    for copy in coming:
        copy.start()
    for come, leave in zip(coming, leaving):
        come.wait()
        leave.start()
    for copy in leaving:
        copy.wait()


def collect(pieces, starts, whole):
    inner = functools.partial(collect_kernel, starts)
    given = isinstance(whole, jax.Array)
    anywhere = pl.BlockSpec(memory_space=pl.ANY)
    rows = sum(piece.shape[0] for piece in pieces)
    return pl.pallas_call(
        inner,
        in_specs=[anywhere] * (len(pieces) + given),
        out_specs=anywhere,
        out_shape=jax.ShapeDtypeStruct(whole.shape, whole.dtype),
        scratch_shapes=[
            pltpu.VMEM((rows, whole.shape[1]), whole.dtype),
            pltpu.SemaphoreType.DMA((len(pieces),)),
            pltpu.SemaphoreType.DMA((len(pieces),)),
        ],
        input_output_aliases={len(pieces): 0} if given else {},
        cost_estimate=cost_of(0.3 * len(pieces)),
        name="collect",
    )(*pieces, *([whole] if given else []))


def gather_blocks(piece, slots):
    rows = piece.shape[0]
    half = rows // 2
    back, front = [piece], [piece]
    near = None
    for step, slot in enumerate(slots):
        leave = (back[-1], front[-1])
        if step == 3:
            leave = (back[-1][:half], front[-1][half:])

        def run(inputs=(), work=None, moves=()):
            both = [(leave[0], AHEAD), (leave[1], BEHIND), *moves]
            come, done = window(both, inputs, work)
            back.append(come[0])
            front.append(come[1])
            return come[2:], done

        if step == 1:
            found = [front[1], back[1], piece]
            early = [send(block, SWAP_CORE) for block in found]
        if step < 2:
            slot(run)
        elif step == 2:
            blocks = [front[2], back[2], *found]

            def join(*blocks_early):
                mine, other = blocks_early[:5], blocks_early[5:]
                other = [send(block, SWAP_CORE) for block in mine[:2]] + list(other)
                starts = tuple(i * rows for i in range(10))
                shape = jax.ShapeDtypeStruct((10 * rows, piece.shape[1]), piece.dtype)
                return collect([*mine, *other], starts, shape)

            near = slot(run, [*blocks, *early], join)
        else:
            slot(run, near)
    return near, (back[4], front[4], front[3], back[3])


def join_far(first, second, third, fourth):
    mine = [first, second, third, fourth]
    half, rows = first.shape[0], third.shape[0]
    starts = (0, half, rows, 2 * rows)
    across = 3 * rows
    return collect(
        mine + [send(block, SWAP_CORE) for block in mine],
        starts + tuple(across + start for start in starts),
        jax.ShapeDtypeStruct((2 * across, first.shape[1]), first.dtype),
    )


def add_low(left, right):
    return (left.astype(F32) + right.astype(F32)).astype(BF16)


def core_sum(rows, weight):
    cut = rows.shape[0] // 2
    come = send(plain(rows[cut:], weight).astype(BF16), SWAP_CORE)
    return (plain(rows[:cut], weight) + come.astype(F32)).astype(BF16)


def scatter_blocks(first, rest, slots=(idle,) * 4):
    rows = first.shape[0] // 3
    half = rows // 2
    state = {"rest": rest}

    def stepper(leave, given, own_work):
        def run(inputs=(), work=None, moves=(), early=()):
            both = [*early, (leave[0], AHEAD), (leave[1], BEHIND), *moves]
            count = len(given)

            def all_work(*xs):
                mine = (own_work(*xs[:count]),) if count else ()
                return mine + tuple(work(*xs[count:]) if work else ())

            come, done = window(both, tuple(given) + tuple(inputs), all_work)
            come, state["come"] = [*come[: len(early)], *come[len(early) + 2 :]], come[len(early) :]
            if count:
                state["rest"] = done[0]
                done = done[1:]
            return come, done

        return run

    given = rest if isinstance(rest, tuple) else ()
    slots[0](stepper((first[:half], first[half:rows]), given, core_sum))
    ahead, behind = first[rows : 2 * rows], first[2 * rows :]
    come, rest = state["come"], state["rest"]
    leave = (
        jnp.concatenate([add_low(ahead[:half], come[0]), ahead[half:]]),
        jnp.concatenate([behind[:half], add_low(behind[half:], come[1])]),
    )
    for step in (1, 2, 3):
        slots[step](stepper(leave, (), None))
        come = state["come"]
        at = (step - 1) * 2 * rows
        if step < 3:
            leave = (
                add_low(rest[at : at + rows], come[0]),
                add_low(rest[at + rows : at + 2 * rows], come[1]),
            )
    return rest[4 * rows :].astype(F32) + come[0].astype(F32) + come[1].astype(F32)


def head_sums():
    row = lax.broadcasted_iota(jnp.int32, (LANES, LANES), 0) // HEAD_DIM
    col = lax.broadcasted_iota(jnp.int32, (LANES, LANES), 1) // HEAD_DIM
    return jnp.where(row == col, 1.0 / HEAD_DIM, 0.0).astype(BF16)


def head_mean(values):
    high = values.astype(BF16)
    rest = (values - high.astype(F32)).astype(BF16)
    sums = head_sums()
    return plain(high, sums) + plain(rest, sums)


def swap_halves(values):
    lane = lax.broadcasted_iota(jnp.int32, values.shape, 1)
    return jnp.where(
        lane % HEAD_DIM < HEAD_DIM // 2,
        pltpu.roll(values, LANES - HEAD_DIM // 2, 1),
        pltpu.roll(values, HEAD_DIM // 2, 1),
    )


def twice(ref):
    return jnp.concatenate([ref[...]] * 2, axis=1)


def dot_lanes(left, right):
    return lax.dot_general(left, right, (((1,), (1,)), ((), ())), preferred_element_type=F32)


def allowed_of(length, pos_col_ref, pos_row_ref):
    col = pos_col_ref[...]
    return jnp.where(col < length, col, NEVER) <= pos_row_ref[...]


def rows_of_ref(ref):
    value = ref[...]
    return value.reshape(-1, value.shape[-1])


def attend_kernel(
    length_ref, proj_ref, cos_ref, sin_ref, gain_ref, pos_col_ref, pos_row_ref,
    out_ref, lse_ref, rot_ref, val_ref,
):
    step = pl.program_id(0)
    block = lse_ref.shape[-1]

    @pl.when(step == 0)
    def _():
        proj = rows_of_ref(proj_ref)
        normed = proj * lax.rsqrt(head_mean(proj * proj) + EPS) * gain_ref[...]
        rotated = normed * twice(cos_ref) + swap_halves(normed) * twice(sin_ref)
        lane = lax.broadcasted_iota(jnp.int32, proj.shape, 1)
        rotated = jnp.where(lane < 2 * HEAD_DIM, rotated * HEAD_DIM**-0.5, rotated)
        rot_ref[...] = jnp.where(lane < 3 * HEAD_DIM, rotated, proj).astype(BF16)
        val_ref[:HEAD_DIM, :] = proj[:, 3 * HEAD_DIM :].T.astype(BF16)
        val_ref[HEAD_DIM:, :] = jnp.ones((16, proj.shape[0]), BF16)

    allowed = allowed_of(length_ref[0], pos_col_ref, pos_row_ref)
    keys = rot_ref[:, 2 * HEAD_DIM : 3 * HEAD_DIM]
    query = rot_ref[pl.ds(pl.multiple_of(step * block, block), block), : 2 * HEAD_DIM]
    outs = []
    for head in range(2):
        scores = dot_lanes(keys, query[:, head * HEAD_DIM : (head + 1) * HEAD_DIM])
        weights = jnp.where(allowed, jnp.exp(scores), 0.0).astype(BF16)
        summed = jnp.dot(val_ref[...], weights, preferred_element_type=F32)
        total = summed[HEAD_DIM : HEAD_DIM + 1]
        outs.append((summed[:HEAD_DIM] / total).T)
        lse_ref[head : head + 1, :] = jnp.log(total)
    out_ref[...] = jnp.concatenate(outs, axis=1).astype(BF16).reshape(out_ref.shape)


def fixed(shape):
    return pl.BlockSpec(shape, lambda i: (0,) * len(shape))


def of_seq(seq, blocks, width, lanes):
    return pl.BlockSpec((blocks, 1, width, lanes), lambda i: (0, seq, 0, 0))


def part_of_seq(seq, blocks, width, lanes):
    return pl.BlockSpec((blocks, 1, width, lanes), lambda i: (i, seq, 0, 0))


def cost_of(microseconds):
    return pl.CostEstimate(
        flops=int(microseconds * 6e8), transcendentals=0, bytes_accessed=int(microseconds * 2.5e6)
    )


STEPS = 4


def attend(seq, proj, cosine, sine, gain, positions, lengths):
    blocks, _, width, _ = proj.shape
    slots = blocks * width
    part = slots // STEPS
    return pl.pallas_call(
        attend_kernel,
        grid=(STEPS,),
        in_specs=[
            pl.BlockSpec(memory_space=pltpu.SMEM),
            of_seq(seq, blocks, width, LANES),
            fixed((slots, LANES // 2)),
            fixed((slots, LANES // 2)),
            fixed((1, LANES)),
            fixed((slots, 1)),
            pl.BlockSpec((1, part), lambda i: (0, i)),
        ],
        out_specs=[
            part_of_seq(0, blocks // STEPS, width, 2 * HEAD_DIM),
            pl.BlockSpec((2, part), lambda i: (0, i)),
            fixed((slots, LANES)),
        ],
        out_shape=[
            jax.ShapeDtypeStruct((blocks, 1, width, 2 * HEAD_DIM), BF16),
            jax.ShapeDtypeStruct((2, slots), F32),
            jax.ShapeDtypeStruct((slots, LANES), BF16),
        ],
        scratch_shapes=[pltpu.VMEM((HEAD_DIM + 16, slots), BF16)],
        cost_estimate=cost_of(8),
        name="attend",
    )(lengths[seq : seq + 1], proj, cosine, sine, gain, positions[:, None], positions[None, :])


def attend_back_kernel(
    length_ref, rot_ref, query_ref, grad_ref, out_ref, lse_ref, pos_col_ref, pos_row_ref,
    dq_ref, dkv_ref,
):
    step = pl.program_id(0)
    allowed = allowed_of(length_ref[0], pos_col_ref, pos_row_ref)
    keys = rot_ref[:, 2 * HEAD_DIM : 3 * HEAD_DIM]
    values = rot_ref[:, 3 * HEAD_DIM :]
    query = query_ref[:, : 2 * HEAD_DIM]
    grad = rows_of_ref(grad_ref)
    product = grad.astype(F32) * rows_of_ref(out_ref).astype(F32)
    ones = jnp.ones((8, HEAD_DIM), F32)
    grad_q, grad_k, grad_v = [], 0.0, 0.0
    for head in range(2):
        cut = slice(head * HEAD_DIM, (head + 1) * HEAD_DIM)
        delta = lax.dot_general(
            ones,
            product[:, cut],
            (((1,), (1,)), ((), ())),
            precision=lax.Precision.HIGHEST,
            preferred_element_type=F32,
        )[:1]
        scores = dot_lanes(keys, query[:, cut])
        probs = jnp.where(allowed, jnp.exp(scores - lse_ref[head : head + 1, :]), 0.0)
        grad_probs = dot_lanes(values, grad[:, cut])
        grad_scores = (probs * (grad_probs - delta)).astype(BF16)
        grad_v += jnp.dot(probs.astype(BF16), grad[:, cut], preferred_element_type=F32)
        grad_k += jnp.dot(grad_scores, query[:, cut], preferred_element_type=F32)
        grad_q.append(
            lax.dot_general(
                grad_scores, keys, (((0,), (0,)), ((), ())), preferred_element_type=F32
            )
        )
    dq_ref[...] = jnp.concatenate(grad_q, axis=1) * HEAD_DIM**-0.5
    both = jnp.concatenate([grad_k, grad_v], axis=1)

    @pl.when(step == 0)
    def _():
        dkv_ref[...] = both

    @pl.when(step > 0)
    def _():
        dkv_ref[...] += both


def attend_back(seq, rotated, grad, out, lse, positions, lengths):
    blocks, _, width, _ = grad.shape
    slots = blocks * width
    part = slots // STEPS
    return pl.pallas_call(
        attend_back_kernel,
        grid=(STEPS,),
        in_specs=[
            pl.BlockSpec(memory_space=pltpu.SMEM),
            fixed((slots, LANES)),
            pl.BlockSpec((part, LANES), lambda i: (i, 0)),
            part_of_seq(seq, blocks // STEPS, width, 2 * HEAD_DIM),
            part_of_seq(0, blocks // STEPS, width, 2 * HEAD_DIM),
            pl.BlockSpec((2, part), lambda i: (0, i)),
            fixed((slots, 1)),
            pl.BlockSpec((1, part), lambda i: (0, i)),
        ],
        out_specs=[
            pl.BlockSpec((part, 2 * HEAD_DIM), lambda i: (i, 0)),
            fixed((slots, 2 * HEAD_DIM)),
        ],
        out_shape=[jax.ShapeDtypeStruct((slots, 2 * HEAD_DIM), F32)] * 2,
        cost_estimate=cost_of(10),
        name="attend_back",
    )(
        lengths[seq : seq + 1], rotated, rotated, grad, out, lse,
        positions[:, None], positions[None, :],
    )


def project_back_kernel(
    dq_ref, dkv_ref, other_ref, proj_ref, cos_ref, sin_ref, gain_ref, grad_ref, sum_ref
):
    slots = dq_ref.shape[0]
    near, far = slots // 16 * len(NEAR), slots // 16 * len(FAR)
    cuts = [(near, near), (0, near), (2 * near + far, far), (2 * near, far)]
    other = jnp.concatenate([other_ref[at : at + size] for at, size in cuts], axis=0)
    grad = jnp.concatenate([dq_ref[...], dkv_ref[...] + other], axis=1)
    proj = rows_of_ref(proj_ref)
    scale_rows = lax.rsqrt(head_mean(proj * proj) + EPS)
    normed = proj * scale_rows
    turned = grad * twice(cos_ref) - swap_halves(grad) * twice(sin_ref)
    gained = turned * gain_ref[...]
    back = scale_rows * (gained - normed * head_mean(gained * normed))
    lane = lax.broadcasted_iota(jnp.int32, proj.shape, 1)
    grad_ref[...] = jnp.where(lane < 3 * HEAD_DIM, back, grad).astype(BF16).reshape(grad_ref.shape)
    sum_ref[...] = jnp.sum((turned * normed).reshape(-1, 8, LANES), axis=0)


def project_back(seq, grad_q, grad_kv, other_kv, proj, cosine, sine, gain):
    blocks, _, width, _ = proj.shape
    slots = blocks * width
    half = fixed((slots, 2 * HEAD_DIM))
    table = fixed((slots, LANES // 2))
    return pl.pallas_call(
        project_back_kernel,
        grid=(1,),
        in_specs=[
            half, half, half, of_seq(seq, blocks, width, LANES), table, table, fixed((1, LANES))
        ],
        out_specs=[of_seq(0, blocks, width, LANES), fixed((8, LANES))],
        out_shape=[
            jax.ShapeDtypeStruct((blocks, 1, width, LANES), BF16),
            jax.ShapeDtypeStruct((8, LANES), F32),
        ],
        cost_estimate=cost_of(4),
        name="project_back",
    )(grad_q, grad_kv, other_kv, proj, cosine, sine, gain)


def feed_kernel(input_ref, weight_ref, grad_ref, hidden_ref, low_ref, *sum_refs):
    weight = weight_ref[...]
    both = dot_lanes(input_ref[...], weight)
    width = both.shape[1] // 4
    for part in range(2):
        at = 2 * part * width
        gate_part, up_part = both[:, at : at + width], both[:, at + width : at + 2 * width]
        grad_hidden = grad_ref[:, part * width : (part + 1) * width]
        hidden = jax.nn.silu(gate_part) * up_part
        hidden_ref[:, part * width : (part + 1) * width] = hidden.astype(BF16)
        gate_low, up_low = gate_grads(grad_hidden, gate_part, up_part)
        low_ref[:, at : at + width] = gate_low
        low_ref[:, at + width : at + 2 * width] = up_low
    if sum_refs:
        sums = plain(low_ref[...], weight).astype(BF16)
        for step, sum_ref in enumerate(sum_refs):

            @pl.when(pl.program_id(0) == step)
            def _(sum_ref=sum_ref):
                sum_ref[...] = sums


def feed(inputs, weight, grad_hidden, steps, with_sums=False):
    rows, units = inputs.shape[0], weight.shape[0]
    part = rows // steps
    row_block = lambda lanes: pl.BlockSpec((part, lanes), lambda i: (i, 0))
    sums = [jax.ShapeDtypeStruct((part, weight.shape[1]), BF16)] * (steps if with_sums else 0)
    return pl.pallas_call(
        feed_kernel,
        grid=(steps,),
        in_specs=[row_block(inputs.shape[1]), fixed(weight.shape), row_block(units // 2)],
        out_specs=[row_block(units // 2), row_block(units)] + [fixed(x.shape) for x in sums],
        out_shape=[
            jax.ShapeDtypeStruct((rows, units // 2), BF16),
            jax.ShapeDtypeStruct((rows, units), BF16),
            *sums,
        ],
        cost_estimate=cost_of(2),
        name="feed",
    )(inputs, weight, grad_hidden)


def dot_rows(left, right):
    return lax.dot_general(left, right, (((0,), (0,)), ((), ())), preferred_element_type=F32)


def plain(left, right):
    return jnp.dot(left, right, preferred_element_type=F32)


def in_order(own, other, index):
    first = index == 0
    return jnp.concatenate([jnp.where(first, own, other), jnp.where(first, other, own)], axis=0)


def split_local(
    tokens, cotangent, q_weight, k_weight, v_weight, o_weight, gate_weight, up_weight,
    down_weight, attn_gain, ffn_gain, q_gain, k_gain, lengths, pair_order,
):
    seqs, width, _ = tokens.shape
    rank = lax.axis_index("ctx")
    side = lax.axis_index("fsdp")
    core = rank % 2
    mine = seqs * width
    q_rows, kv_rows, ff_rows = q_weight.shape[0], k_weight.shape[0], gate_weight.shape[0]

    x_rows = tokens.astype(F32).reshape(mine, D)
    scale_one = rms_scale(x_rows)
    normed_one = x_rows * scale_one
    kept = {}

    owners = block_owners(rank)
    blocks = owners.shape[0]
    within = jnp.arange(width, dtype=jnp.int32)
    half_blk = width // 2

    def positions_of(dealt):
        block_id = jnp.where(
            within[None, :] < half_blk, dealt[:, None], 2 * pair_order.shape[0] - 1 - dealt[:, None]
        )
        return (block_id * half_blk + within[None, :] % half_blk).reshape(-1)

    def tables(found):
        cosine, sine = rope_tables(found)
        return jnp.concatenate([cosine] * 4, axis=1), jnp.concatenate([-sine, sine] * 2, axis=1)

    cut = ff_rows // 2
    ff_own = [w[at : at + cut] for w in (gate_weight, up_weight, down_weight) for at in (0, cut)]
    ff_side = []

    def moving(index):
        return [(ff_own[index], SWAP_X)]

    def slot_positions(run):
        def work(order):
            come = tuple(send(w, SWAP_X) for w in (q_weight, k_weight, v_weight))
            return positions_of(order[owners]), come

        _, (kept["positions"], kept["side"]) = run((pair_order,), work)

    def attention_weights(found, q_side, k_side, v_side):
        kv_own, kv_side = jnp.stack([k_weight, v_weight]), jnp.stack([k_side, v_side])
        kv_half = jnp.concatenate(
            [jnp.where(side == 0, kv_own, kv_side), jnp.where(side == 0, kv_side, kv_own)], axis=1
        )
        kv_core = send(kv_half, SWAP_CORE)
        kv_full = jnp.concatenate(
            [jnp.where(core == 0, kv_half, kv_core), jnp.where(core == 0, kv_core, kv_half)], axis=1
        )
        weights = jnp.concatenate([q_weight, q_side, kv_full[0], kv_full[1]], axis=0)
        return weights, *tables(found)

    def slot_weights(run):
        (o_side,), (kept["w_attn"], *kept["tables"]) = run(
            (kept["positions"], *kept["side"]), attention_weights, [(o_weight, SWAP_X)]
        )
        kept["w_out"] = jnp.concatenate([o_weight, o_side], axis=0)

    def slot_join_move(index):
        def slot(run, blocks, join):
            (come,), (near,) = run(blocks, lambda *xs: (join(*xs),), moving(index))
            ff_side.append(come)
            return near

        return slot

    def slot_project(run, near):
        _, (kept["proj_near"], kept["x_near"]) = run(
            (near, kept["w_attn"]), lambda x, w: (project(x, w), x)
        )

    _, x_late = gather_blocks(
        (normed_one * attn_gain).astype(BF16),
        (slot_positions, slot_weights, slot_join_move(0), slot_project),
    )
    x_near = kept["x_near"]
    positions, (cosine, sine) = kept["positions"], kept["tables"]
    w_attn, w_out = kept["w_attn"], kept["w_out"]
    cut_rows = x_near.shape[0]
    gain_lanes = jnp.concatenate([q_gain, q_gain, k_gain, jnp.ones((HEAD_DIM,), F32)])[None, :]
    my_pos = positions_of(pair_order[rank][None])
    live = (my_pos[None, :] < lengths[:, None]).reshape(mine, 1)
    grad_out = jnp.where(live, cotangent.astype(F32).reshape(mine, D), 0.0)

    heads = []

    def slot_project_far(run):
        def work(near, weight, *late):
            far = join_far(*late)
            rows = jnp.concatenate([near, project(far, weight)], axis=0)
            return rows.reshape(blocks, seqs, width, LANES), far

        (come,), (kept["proj"], kept["x_far"]) = run(
            (kept["proj_near"], w_attn, *x_late), work, moving(1)
        )
        ff_side.append(come)

    def attend_beside(run, seq):
        work = lambda p: attend(seq, p, cosine, sine, gain_lanes, positions, lengths)
        (come,), found = run((kept["proj"],), work, moving(2 + seq))
        ff_side.append(come)
        heads.append(found)

    def slot_out(run, near):
        def work(*outs):
            rows = jnp.concatenate(outs, axis=1).reshape(-1, 2 * HEAD_DIM)
            return rows, core_sum(rows[cut_rows:], w_out)

        _, (kept["out_rows"], kept["first"]) = run([found[0] for found in heads], work)

    def slot_attend_last(run, blocks_near, join):
        attend_beside(run, 1)
        return blocks_near, join

    (grad_blocks, grad_join), grad_late = gather_blocks(
        grad_out.astype(BF16),
        (slot_project_far, lambda run: attend_beside(run, 0), slot_attend_last, slot_out),
    )
    out_rows, proj, x_far = kept["out_rows"], kept["proj"], kept["x_far"]

    def slot_grad_near(run):
        (come,), (kept["grad_near"],) = run(grad_blocks, lambda *xs: (grad_join(*xs),), moving(4))
        ff_side.append(come)

    def slot_grad_far(run):
        (come,), (kept["grad_far"],) = run(grad_late, lambda *xs: (join_far(*xs),), moving(5))
        ff_side.append(come)

    def slot_gate_up_weights(run):
        _, (kept["w_gate_up"],) = run(
            (*ff_own[:4], *ff_side[:4]), lambda *xs: (jnp.concatenate(xs, axis=0),)
        )

    resid = x_rows + scatter_blocks(
        kept["first"],
        (out_rows[:cut_rows], w_out),
        (idle, slot_grad_near, slot_grad_far, slot_gate_up_weights),
    )
    grad_near, grad_far = kept["grad_near"], kept["grad_far"]
    w_gate_up = kept["w_gate_up"]
    w_down = jnp.concatenate([*ff_own[4:], *ff_side[4:]], axis=0)
    scale_two = rms_scale(resid)
    normed_two = resid * scale_two

    def slot_hidden(name, grad):
        def slot(run):
            _, (kept[name],) = run((grad, w_down), lambda g, w: (project(g, w),))

        return slot

    def slot_feed(run, blocks_near, join):
        def work(weight, grad_hidden, *found):
            near = join(*found)
            return near, *feed(near, weight, grad_hidden, 4)

        _, near = run((w_gate_up, kept["hidden_near"], *blocks_near), work)
        return near

    def slot_near_sums(run, near):
        work = lambda x, hidden, low, w: (x, hidden, low, core_sum(low, w))
        _, (kept["x2_near"], kept["hidden"], kept["gate_up_low"], kept["near_sums"]) = run(
            (*near, w_gate_up), work
        )

    _, x2_late = gather_blocks(
        (normed_two * ffn_gain).astype(BF16),
        (
            slot_hidden("hidden_near", grad_near),
            slot_hidden("hidden_far", grad_far),
            slot_feed,
            slot_near_sums,
        ),
    )
    x2_near = kept["x2_near"]
    hidden_near, low_near = kept["hidden"], kept["gate_up_low"]
    x2_far = join_far(*x2_late)
    hidden_far, low_far, sums_mine, sums_other = feed(
        x2_far, w_gate_up, kept["hidden_far"], 2, with_sums=True
    )

    def slot_sums(run):
        work = lambda near, far, weight: (core_sum(far, weight), core_sum(near, weight))
        _, kept["out_parts"] = run((hidden_near, hidden_far, w_down), work)

    def both_parts(*parts):
        near, far, right_near, right_far = parts
        return dot_rows(near, right_near) + dot_rows(far, right_far)

    half_ff = 2 * ff_rows

    def slot_leave(run):
        def work(*parts):
            gate_up = both_parts(parts[0][:, half_ff:], parts[1][:, half_ff:], *parts[2:4])
            return jnp.split(gate_up.astype(BF16), 4)

        _, kept["gate_up_leave"] = run((low_near, low_far, x2_near, x2_far), work)

    def slot_down_leave(run):
        def work(*parts):
            down = both_parts(parts[0][:, ff_rows:], parts[1][:, ff_rows:], *parts[2:4])
            return jnp.split(down.astype(BF16), 2)

        _, kept["down_leave"] = run((hidden_near, hidden_far, grad_near, grad_far), work)

    grad_norm2 = scatter_blocks(
        add_low(sums_mine, send(sums_other, SWAP_CORE)),
        kept["near_sums"],
        (idle, slot_sums, slot_leave, slot_down_leave),
    )
    pieces = [*kept["gate_up_leave"], *kept["down_leave"]]
    came = []
    grad_ffn_gain = jnp.sum(grad_norm2 * normed_two, axis=0)
    grad_resid = grad_out + rms_back(grad_norm2 * ffn_gain, normed_two, scale_two)

    def slot_gate_up_stay(run):
        def work(*parts):
            return (both_parts(parts[0][:, :half_ff], parts[1][:, :half_ff], *parts[2:4]),)

        (come,), (kept["gate_up"],) = run(
            (low_near, low_far, x2_near, x2_far), work, [(pieces[0], SWAP_X)]
        )
        came.append(come)

    def slot_down_stay(run):
        def work(*parts):
            return (both_parts(parts[0][:, :ff_rows], parts[1][:, :ff_rows], *parts[2:4]),)

        (come,), (kept["down"],) = run(
            (hidden_near, hidden_far, grad_near, grad_far), work, [(pieces[1], SWAP_X)]
        )
        came.append(come)

    def slot_join_aside(run, blocks, join):
        (come,), (near,) = run(blocks, lambda *xs: (join(*xs),), [(pieces[2], SWAP_X)])
        came.append(come)
        return near

    def grad_heads(grad, weight):
        return project(grad, weight).astype(BF16)

    def slot_grad_heads(run, near):
        _, (kept["heads_near"], kept["da_near"]) = run(
            (near, w_out), lambda x, w: (grad_heads(x, w), x)
        )

    _, da_late = gather_blocks(
        grad_resid.astype(BF16),
        (slot_gate_up_stay, slot_down_stay, slot_join_aside, slot_grad_heads),
    )
    da_near = kept["da_near"]
    da_far = join_far(*da_late)

    def slot_grad_o(run):
        def work(near, x, w):
            rows = jnp.concatenate([near, grad_heads(x, w)], axis=0)
            return (rows.reshape(blocks, seqs, width, 2 * HEAD_DIM),)

        _, (kept["grad_o"],) = run((kept["heads_near"], da_far, w_out), work)

    def slot_attend_back(seq):
        def slot(run):
            out, lse, rotated = heads[seq]

            def work(grad, *before):
                come = tuple(send(x, SWAP_CORE) for x in before)
                return attend_back(seq, rotated, grad, out, lse, positions, lengths), come

            before = [kept["back", seq - 1][1]] if seq else []
            (come,), (kept["back", seq], other) = run(
                (kept["grad_o"], *before), work, [(pieces[3 + seq], SWAP_X)]
            )
            came.append(come)
            kept["other"] = other

        return slot

    def slot_project_back(run):
        def work(found, others):
            others = [*others, send(found[-1][1], SWAP_CORE)]
            grads, sums = [], 0.0
            for s, ((grad_q, grad_kv), other_kv) in enumerate(zip(found, others)):
                rows, part = project_back(
                    s, grad_q, grad_kv, other_kv, proj, cosine, sine, gain_lanes
                )
                grads.append(rows)
                sums = sums + jnp.sum(part, axis=0)
            return jnp.concatenate(grads, axis=1).reshape(blocks * mine, LANES), sums

        (come,), (kept["grad_rows"], kept["gain_sums"]) = run(
            ([kept["back", s] for s in range(seqs)], kept["other"]), work, [(pieces[5], SWAP_X)]
        )
        came.append(come)

    out_sum = scatter_blocks(
        *kept["out_parts"],
        (slot_grad_o, slot_attend_back(0), slot_attend_back(1), slot_project_back),
    )
    grad_rows, gain_sums = kept["grad_rows"], kept["gain_sums"]
    row = jnp.arange(LANES)[:, None] // HEAD_DIM
    w_once = jnp.where((row < 2) | (row == 2 + core), w_attn, 0).astype(BF16)

    def slot_attn_grads(run):
        def work(grads, near, far):
            full = both_parts(grads[:cut_rows], grads[cut_rows:], near, far)
            kv_grads = full[2 * q_rows :].reshape(2, 2, 2, kv_rows, D)
            kv_mine = jnp.where(core == 0, kv_grads[:, 0], kv_grads[:, 1])
            kv_stay = jnp.where(side == 0, kv_mine[:, 0], kv_mine[:, 1])
            kv_leave = jnp.where(side == 0, kv_mine[:, 1], kv_mine[:, 0])
            stay = jnp.concatenate([full[:q_rows], kv_stay.reshape(2 * kv_rows, D)])
            leave = jnp.concatenate([full[q_rows : 2 * q_rows], kv_leave.reshape(2 * kv_rows, D)])
            return stay, leave.astype(BF16)

        _, kept["attn"] = run((grad_rows, x_near, x_far), work)

    def slot_out_grads(run):
        def work(rows, near, far):
            stay, leave = jnp.split(both_parts(rows[:cut_rows], rows[cut_rows:], near, far), 2)
            return stay, leave.astype(BF16)

        (kept["attn_come"],), kept["o"] = run(
            (out_rows, da_near, da_far), work, [(kept["attn"][1], SWAP_X)]
        )

    def slot_finish(run):
        def work(attn_stay, attn_come, gate_up, down, f_sum, *xs):
            attn_grads = attn_stay + attn_come.astype(F32)
            owned = jnp.concatenate([q_weight, k_weight, v_weight], axis=0).astype(F32)
            gains = jnp.concatenate(
                [
                    jnp.sum(owned * attn_grads, axis=0) / attn_gain,
                    grad_ffn_gain,
                    gain_sums[:HEAD_DIM] + gain_sums[HEAD_DIM : 2 * HEAD_DIM],
                    0.5 * gain_sums[2 * HEAD_DIM : 3 * HEAD_DIM],
                ]
            )
            gains = gains + send(gains, SWAP_CORE)
            gains = gains + send(gains, SWAP_X)
            gate_up = gate_up + jnp.concatenate(xs[:4]).astype(F32)
            down = down + jnp.concatenate(xs[4:]).astype(F32)
            block = jnp.where(live, resid + f_sum, 0.0).astype(BF16).reshape(seqs, width, D)
            return gains, attn_grads, gate_up, down, block

        (kept["o_come"],), kept["finish"] = run(
            (*kept["attn"][:1], kept["attn_come"], kept["gate_up"], kept["down"], out_sum, *came),
            work,
            [(kept["o"][1], SWAP_X)],
        )

    def slot_gains(run):
        gains = kept["finish"][0]
        (come,), kept["o_grad"] = run(
            (*kept["o"][:1], kept["o_come"]),
            lambda stay, come: (stay + come.astype(F32),),
            early=[(gains, SWAP_Y)],
        )
        gains = gains + come
        kept["gains"] = (gains + send(gains, SWAP_Z0)) + (
            send(gains, SWAP_Z1) + send(gains, SWAP_Z)
        )

    grad_norm1 = scatter_blocks(
        core_sum(grad_rows[cut_rows:], w_once),
        (grad_rows[:cut_rows], w_once),
        (slot_attn_grads, slot_out_grads, slot_finish, slot_gains),
    )
    _, attn_grads, gate_up_grad, down_grad, block_out = kept["finish"]
    (o_grad,) = kept["o_grad"]
    gains = kept["gains"]
    grad_tokens = (grad_resid + rms_back(grad_norm1 * attn_gain, normed_one, scale_one)).reshape(
        seqs, width, D
    )
    return (
        block_out,
        grad_tokens,
        attn_grads[:q_rows],
        attn_grads[q_rows : q_rows + kv_rows],
        attn_grads[q_rows + kv_rows :],
        o_grad,
        gate_up_grad[:ff_rows],
        gate_up_grad[ff_rows:],
        down_grad,
        gains[:D],
        gains[D : 2 * D],
        gains[2 * D : 2 * D + HEAD_DIM],
        gains[2 * D + HEAD_DIM :],
    )


def solution(mesh):
    body = split_local if fits_split(mesh) else local
    in_specs = (
        P("fsdp", "ctx", None),
        P("fsdp", "ctx", None),
        P(("ctx", "fsdp"), None),
        P(("ctx", "fsdp"), None),
        P(("ctx", "fsdp"), None),
        P(("ctx", "fsdp"), None),
        P(("ctx", "fsdp"), None),
        P(("ctx", "fsdp"), None),
        P(("ctx", "fsdp"), None),
        P(),
        P(),
        P(),
        P(),
        P("fsdp"),
        P(),
    )
    out_specs = (
        P("fsdp", "ctx", None),
        P("fsdp", "ctx", None),
        P(("ctx", "fsdp"), None),
        P(("ctx", "fsdp"), None),
        P(("ctx", "fsdp"), None),
        P(("ctx", "fsdp"), None),
        P(("ctx", "fsdp"), None),
        P(("ctx", "fsdp"), None),
        P(("ctx", "fsdp"), None),
        P(),
        P(),
        P(),
        P(),
    )
    return jax.shard_map(body, mesh=mesh, in_specs=in_specs, out_specs=out_specs, check_vma=False)
```
